32 devices in a mesh: section: 2 (over y), group: 4 (over x, core), expert: 4 (over z).
Axes of the slice: x: 2, y: 2, z: 4, core: 2. Of those that a mesh axis runs over, the one named last changes fastest.
Arguments:
- inputs: bfloat16 [2, 16, 128, 1536], P(None, ('group', 'expert')), may hold values from -6 to 6
- cotangent: bfloat16 [2, 16, 128, 1536], P(None, ('group', 'expert')), may hold values from -6 to 6
- segment_ids: int32 [2, 16, 128], P(None, ('group', 'expert')), may hold values from 0 to 63, as said below
- live_first: int32 [2, 16, 2], P(None, ('group', 'expert')), may hold values from 0 to 1, as said below
- routes: int32 [2, 2, 16, 128, 8], P('section', None, ('group', 'expert')), may hold values from 0 to 19, all different within a row; in each aligned block of 128 rows (0 to 127, 128 to 255, ..., all dimensions but the last counted through in order) at most 64 rows name the same one
- gain_attn: bfloat16 [2, 1536], P('section', ('group', 'expert')), may hold values from 0.5 to 1.5
- gain_moe: bfloat16 [2, 1536], P('section', ('group', 'expert')), may hold values from 0.5 to 1.5
- w_query: bfloat16 [2, 1536, 1536], P('section', ('group', 'expert')), may hold values from -0.15625 to 0.15625
- key_weight: bfloat16 [2, 1536, 512], P('section', ('group', 'expert')), may hold values from -0.15625 to 0.15625
- value_weight: bfloat16 [2, 1536, 512], P('section', ('group', 'expert')), may hold values from -0.15625 to 0.15625
- w_out: bfloat16 [2, 1536, 1536], P('section', None, ('group', 'expert')), may hold values from -0.625 to 0.625
- w_router: bfloat16 [2, 1536, 20], P('section', ('group', 'expert')), may hold values from -0.076171875 to 0.076171875
- w_gate: bfloat16 [2, 20, 1536, 512], P('section', 'expert'), may hold values from -0.15625 to 0.15625
- w_up: bfloat16 [2, 20, 1536, 512], P('section', 'expert'), may hold values from -0.15625 to 0.15625
- w_down: bfloat16 [2, 20, 512, 1536], P('section', 'expert'), may hold values from -1 to 1
Outputs:
- layer_out: bfloat16 [2, 2, 16, 128, 1536], P('section', None, ('group', 'expert'))
- input_grad: float32 [2, 2, 16, 128, 1536], P('section', None, ('group', 'expert'))
- gain_attn_grad: float32 [2, 1536], P('section', ('group', 'expert'))
- gain_moe_grad: float32 [2, 1536], P('section', ('group', 'expert'))
- w_query_grad: float32 [2, 1536, 1536], P('section', ('group', 'expert'))
- w_key_grad: float32 [2, 1536, 512], P('section', ('group', 'expert'))
- w_value_grad: float32 [2, 1536, 512], P('section', ('group', 'expert'))
- w_out_grad: float32 [2, 1536, 1536], P('section', None, ('group', 'expert'))
- w_router_grad: float32 [2, 1536, 20], P('section', ('group', 'expert'))
- w_gate_grad: float32 [2, 20, 1536, 512], P('section', 'expert', 'group')
- w_up_grad: float32 [2, 20, 1536, 512], P('section', 'expert', 'group')
- w_down_grad: float32 [2, 20, 512, 1536], P('section', 'expert', None, 'group')
The draws below stay inside these ranges and needn't reach their ends.
Inputs may be any that keep to these rules, and one draw needn't show every extreme that they name: `segment_ids`: within each sequence the numbers start at 0 at its first position, never fall, and rise by one where a new document starts; in each micro-batch some sequence reaches 63, and document lengths run from a few positions to the whole sequence. `live_first`: for each query block of 64 positions: the index of the block that holds the start of the document of the query block's first position. `routes`: in the 128 tokens of one sequence of one micro-batch and layer, no expert is named more than 64 times, a bound that some block reaches; a token names 8 different experts.
All inputs are finite; a program needn't handle non-finite values.
Results may differ from the reference program's by a relative error of at most 0.023.
Values may be sent and summed in bfloat16 or wider, within the bound.
A program may use at most 320 MiB of HBM per device.

```python
import math
import jax
import jax.numpy as jnp
import numpy as np
from jax import lax

MODEL_WIDTH = 1536
QUERY_HEADS = 24
KEY_VALUE_HEADS = 8
HEAD_SIZE = 64
FFE = 512
TOPK = 8
MB = 2
BLK = 64
SEQ = 128
EXPERTS = 20
SEQS = 16
CAP = 64
N_SECTION = 2


def document_ids(key):
    level_key = jax.random.fold_in(key, 7)
    flag_key = jax.random.fold_in(key, 8)
    pick_key = jax.random.fold_in(key, 9)
    levels = jax.random.randint(level_key, (MB, SEQS, 1), 1, 5)
    threshold = 4096 // jnp.power(4, levels)
    ticket = jax.random.randint(flag_key, (MB, SEQS, SEQ), 0, 4096)
    position = jnp.arange(SEQ, dtype=jnp.int32)
    chosen = jax.random.randint(pick_key, (MB, 1, 1), 0, SEQS)
    seq_number = jnp.arange(SEQS, dtype=jnp.int32)[None, :, None]
    dense_docs = (seq_number == chosen) & (position % 2 == 0)[None, None, :]
    doc_flags = (ticket < threshold) | (position == 0)[None, None, :] | dense_docs
    counted = jnp.cumsum(doc_flags.astype(jnp.int32), axis=-1) - 1
    return jnp.minimum(counted, SEQ // 2 - 1).astype(jnp.int32)


def draw_segment_ids(key, part):
    return document_ids(key)


def draw_live_first(key, part):
    doc_ids = document_ids(key)
    position = jnp.arange(SEQ, dtype=jnp.int32)
    previous = jnp.concatenate([doc_ids[:, :, :1], doc_ids[:, :, :-1]], axis=-1)
    doc_flags = (doc_ids != previous) | (position == 0)[None, None, :]
    starts = lax.cummax(jnp.where(doc_flags, position[None, None, :], 0), axis=2)
    return (starts[:, :, ::BLK] // BLK).astype(jnp.int32)


def shard_levels(stream_key, extent, split, low, largest):
    def one(axis_at, blocks):
        heights = jax.random.uniform(jax.random.fold_in(jax.random.fold_in(stream_key, 6), axis_at), (blocks,), jnp.float32, low / len(split), largest / len(split))
        return jnp.repeat(jnp.exp(heights), extent[axis_at] // blocks).reshape((-1,) + (1,) * (len(extent) - axis_at - 1))

    level = one(*split[0])
    for cut in split[1:]:
        level = level * one(*cut)
    return level


def routed_block(rng, own, number, rows, number_of, top, most, lean):
    ranking = jax.random.permutation(rng, number_of)
    crowded, ordinary = load_shares(number_of, rows * top, most, lean, True), load_shares(number_of, rows * top, most, lean, False)
    places = jnp.arange(number_of)

    def named(lengths, rotation):
        used = int((lengths > 0).sum())
        fixed = max(1, used // 4)
        moved = fixed + (places - fixed + rotation * (used - fixed)) % max(1, number_of - fixed)
        return jnp.zeros((number_of,), jnp.int32).at[ranking[jnp.where(places < fixed, places, moved)]].set(jnp.asarray(lengths, jnp.int32))

    lengths = jnp.where(number % 4 == 0, named(crowded, number // 4), named(ordinary, number - number // 4 - 1))
    mixed = jax.random.permutation(jax.random.fold_in(own, 3), number_of)
    giver, taker = mixed[0:number_of // 2 * 2:2], mixed[1:number_of // 2 * 2:2]
    slack = jnp.minimum(lengths[giver] - 1, most - lengths[taker]) // 2
    slack = jnp.where((giver == ranking[0]) | (taker == ranking[0]) | (lengths[taker] == 0), 0, jnp.maximum(slack, 0))
    moved = jax.random.randint(jax.random.fold_in(own, 4), (number_of // 2,), 0, 1 << 20) % (slack + 1)
    lengths = lengths.at[giver].add(-moved).at[taker].add(moved)
    members = jnp.searchsorted(jnp.cumsum(lengths), jnp.arange(rows * top), side="right").astype(jnp.int32)
    table = members.reshape(top, rows).T
    table = table[jax.random.permutation(jax.random.fold_in(own, 1), rows)]
    rotation = jax.random.randint(jax.random.fold_in(own, 2), (rows, 1), 0, top)
    return jnp.take_along_axis(table, (jnp.arange(top)[None, :] + rotation) % top, axis=1)


def load_shares(count, total, limit, skew, full):
    weights = [(1 << 20) // math.isqrt(standing ** skew) + 1 for standing in range(1, count + 1)]
    largest = limit if full else min(limit, max(-(-total // count), total * weights[0] // sum(weights)))
    least = 1 if total - largest >= count - 1 else 0
    given, spare = [largest] + [least] * (count - 1), total - largest - least * (count - 1)
    while spare > 0:
        candidates = [i for i in range(1, count) if given[i] < largest] or [i for i in range(1, count) if given[i] < limit]
        pool, budget = sum([weights[i] for i in candidates]), spare
        for i in candidates:
            addition = min(limit - given[i], max(1, budget * weights[i] // pool), spare)
            given[i] = given[i] + addition
            spare = spare - addition
    return np.array(given)


def bell_draw(stream_key, dims, deviation, most, split=(), kind=jnp.bfloat16):
    values = deviation * jax.random.normal(stream_key, dims, jnp.float32)
    if split:
        values = values * shard_levels(stream_key, dims, split, -0.22, 0.18)
    return jnp.clip(values, -most, most).astype(kind)


def setup_inputs(seed: int = 0) -> dict:
    key_list = jax.random.split(jax.random.key(seed), 16)
    inputs = bell_draw(key_list[0], (MB, SEQS, SEQ, MODEL_WIDTH), 1.0, 6.0, ((1, 16),))
    cotangent = bell_draw(key_list[1], (MB, SEQS, SEQ, MODEL_WIDTH), 1.0, 6.0, ((1, 16),))
    segment_ids = draw_segment_ids(jax.random.fold_in(key_list[15], 71), 0)
    live_first = draw_live_first(jax.random.fold_in(key_list[15], 71), 0)
    routes_keys = jax.random.split(jax.random.fold_in(key_list[4], 1), N_SECTION * MB * SEQS * SEQ // SEQ)
    routes_turns = jax.random.permutation(jax.random.fold_in(key_list[4], 3), N_SECTION * MB * SEQS * SEQ // SEQ)
    routes = jax.vmap(lambda own, number: routed_block(jax.random.fold_in(key_list[4], 2), own, number, SEQ, EXPERTS, TOPK, CAP, 1))(routes_keys, routes_turns).reshape((N_SECTION, MB, SEQS, SEQ, TOPK))
    gain_attn = jnp.clip(1.0 + 0.1 * jax.random.normal(key_list[5], (N_SECTION, MODEL_WIDTH), jnp.float32), 0.5, 1.5).astype(jnp.bfloat16)
    gain_moe = jnp.clip(1.0 + 0.1 * jax.random.normal(key_list[6], (N_SECTION, MODEL_WIDTH), jnp.float32), 0.5, 1.5).astype(jnp.bfloat16)
    w_query = bell_draw(key_list[7], (N_SECTION, MODEL_WIDTH, QUERY_HEADS * HEAD_SIZE), MODEL_WIDTH ** -0.5, 0.15625, ((0, 2), (1, 16)))
    key_weight = bell_draw(key_list[8], (N_SECTION, MODEL_WIDTH, KEY_VALUE_HEADS * HEAD_SIZE), MODEL_WIDTH ** -0.5, 0.15625, ((0, 2), (1, 16)))
    value_weight = bell_draw(key_list[9], (N_SECTION, MODEL_WIDTH, KEY_VALUE_HEADS * HEAD_SIZE), MODEL_WIDTH ** -0.5, 0.15625, ((0, 2), (1, 16)))
    w_out = bell_draw(key_list[10], (N_SECTION, QUERY_HEADS * HEAD_SIZE, MODEL_WIDTH), (QUERY_HEADS * HEAD_SIZE // 16) ** -0.5, 0.625, ((0, 2), (2, 16)))
    w_router = bell_draw(key_list[11], (N_SECTION, MODEL_WIDTH, EXPERTS), (0.5 * MODEL_WIDTH ** -0.5), 0.076171875, ((0, 2), (1, 16)))
    w_gate = bell_draw(key_list[12], (N_SECTION, EXPERTS, MODEL_WIDTH, FFE), MODEL_WIDTH ** -0.5, 0.15625, ((0, 2), (1, 4)))
    w_up = bell_draw(key_list[13], (N_SECTION, EXPERTS, MODEL_WIDTH, FFE), MODEL_WIDTH ** -0.5, 0.15625, ((0, 2), (1, 4)))
    w_down = bell_draw(key_list[14], (N_SECTION, EXPERTS, FFE, MODEL_WIDTH), (FFE // 16) ** -0.5, 1.0, ((0, 2), (1, 4)))
    return dict(inputs=inputs, cotangent=cotangent, segment_ids=segment_ids, live_first=live_first, routes=routes, gain_attn=gain_attn, gain_moe=gain_moe, w_query=w_query, key_weight=key_weight, value_weight=value_weight, w_out=w_out, w_router=w_router, w_gate=w_gate, w_up=w_up, w_down=w_down)


@jax.custom_vjp
def low_precision(v):
    return lax.optimization_barrier(v.astype(jnp.bfloat16)).astype(jnp.float32)

@jax.custom_vjp
def low_precision_backward(v):
    return v

def low_keep(v):
    return (low_precision(v), None)

def low_pass(kept, grad):
    return (grad,)

def back_keep(v):
    return (v, None)

def back_low(kept, grad):
    return (low_precision(grad),)
low_precision.defvjp(low_keep, low_pass)
low_precision_backward.defvjp(back_keep, back_low)
EPS = 1e-06
THETA = 10000.0
NEG_FILL = -1e+30
HIGH_PRECISION = lax.Precision.HIGHEST

def rotate_halves(values, direction):
    sequence_length = values.shape[-3]
    half_size = values.shape[-1] // 2
    frequency = THETA ** (-jnp.arange(half_size, dtype=jnp.float32) * 2.0 / values.shape[-1])
    angles = jnp.arange(sequence_length, dtype=jnp.float32)[:, None] * frequency[None, :]
    cosine = jnp.cos(angles)[:, None, :]
    sine_val = direction * jnp.sin(angles)[:, None, :]
    first_half = values[..., :half_size]
    second_half = values[..., half_size:]
    return jnp.concatenate([first_half * cosine - second_half * sine_val, second_half * cosine + first_half * sine_val], axis=-1)

def rms_norm(values, gain_vec):
    return values * lax.rsqrt(lax.optimization_barrier(jnp.mean(values * values, axis=-1, keepdims=True)) + EPS) * gain_vec

def build_mask(seg_now, live_now):
    position = jnp.arange(seg_now.shape[0], dtype=jnp.int32)
    causal = position[None, :] <= position[:, None]
    same_doc = seg_now[:, None] == seg_now[None, :]
    first_block = jnp.repeat(live_now, BLK)[:, None]
    reaches = position[None, :] // BLK >= first_block
    return causal & same_doc & reaches

def attend(pieces):
    query_rows, key_heads_split, value_heads_split, seg_now, live_now = pieces
    sequence_length = query_rows.shape[0]
    grouped_heads = query_rows.reshape(sequence_length, KEY_VALUE_HEADS, QUERY_HEADS // KEY_VALUE_HEADS, HEAD_SIZE)
    raw_scores = jnp.einsum('qhgd,khd->hgqk', grouped_heads, key_heads_split, precision=HIGH_PRECISION)
    scores = low_precision_backward(raw_scores) * HEAD_SIZE ** (-0.5)
    allowed = build_mask(seg_now, live_now)
    scores = jnp.where(allowed[None, None], scores, NEG_FILL)
    probs = jax.nn.softmax(scores, axis=-1)
    mixed_heads = jnp.einsum('hgqk,khd->qhgd', low_precision(probs), value_heads_split, precision=HIGH_PRECISION)
    return mixed_heads.reshape(sequence_length, QUERY_HEADS * HEAD_SIZE)

def layer(layer_params, tokens, seg_all, live_all, route_all):
    attn_gain, moe_gain, query_mat, key_matrix, value_matrix, out_mat, router_mat, gate_mat, up_mat, down_mat = layer_params
    item_count, sequence_length, features = tokens.shape
    flat_in = tokens.reshape(item_count * sequence_length, features)
    normed_input = low_precision(rms_norm(flat_in, attn_gain))
    query_rows = low_precision(rotate_halves(low_precision_backward(jnp.dot(normed_input, query_mat, precision=HIGH_PRECISION)).reshape(item_count, sequence_length, QUERY_HEADS, HEAD_SIZE), 1.0))
    key_heads_split = low_precision(rotate_halves(low_precision_backward(jnp.dot(normed_input, key_matrix, precision=HIGH_PRECISION)).reshape(item_count, sequence_length, KEY_VALUE_HEADS, HEAD_SIZE), 1.0))
    value_heads_split = low_precision(low_precision_backward(jnp.dot(normed_input, value_matrix, precision=HIGH_PRECISION))).reshape(item_count, sequence_length, KEY_VALUE_HEADS, HEAD_SIZE)
    mixed_heads = lax.map(jax.checkpoint(attend), (query_rows, key_heads_split, value_heads_split, seg_all, live_all))
    mixed_heads = low_precision(low_precision_backward(mixed_heads.reshape(item_count * sequence_length, QUERY_HEADS * HEAD_SIZE)))
    hidden = flat_in + low_precision_backward(jnp.dot(mixed_heads, out_mat, precision=HIGH_PRECISION))
    moe_in = low_precision(rms_norm(hidden, moe_gain))
    logits = low_precision_backward(jnp.dot(moe_in, router_mat, precision=HIGH_PRECISION))
    experts_total = router_mat.shape[1]
    route_flat = route_all.reshape(item_count * sequence_length, TOPK)
    choose = route_flat[:, :, None] == jnp.arange(experts_total, dtype=jnp.int32)[None, None, :]
    picked = lax.optimization_barrier(jnp.sum(jnp.where(choose, logits[:, None, :], 0.0), axis=-1))
    gate_probs = jax.nn.softmax(picked, axis=-1)
    one_hot = choose.reshape(item_count, sequence_length * TOPK, experts_total).astype(jnp.int32)
    before = jnp.cumsum(one_hot, axis=1) - one_hot
    slot_num = lax.optimization_barrier(jnp.sum(before * one_hot, axis=-1))
    expert_of = route_all.reshape(item_count, sequence_length * TOPK).astype(jnp.int32)
    seq_index = jnp.arange(item_count, dtype=jnp.int32)[:, None]
    slot_place = ((expert_of * item_count + seq_index) * CAP + slot_num).reshape(-1).astype(jnp.int32)
    total_rows = item_count * sequence_length * TOPK
    buffer_size = experts_total * item_count * CAP
    source = jnp.full((buffer_size,), total_rows, jnp.int32).at[slot_place].set(jnp.arange(total_rows, dtype=jnp.int32))
    rows_in = low_precision_backward(jnp.repeat(moe_in, TOPK, axis=0))
    padded = jnp.concatenate([rows_in, jnp.zeros((1, features), jnp.float32)], axis=0)
    buffer = padded[source].reshape(experts_total, item_count * CAP, features)
    gate_pre = low_precision_backward(jnp.einsum('erd,edf->erf', buffer, gate_mat, precision=HIGH_PRECISION))
    up_pre = low_precision_backward(jnp.einsum('erd,edf->erf', buffer, up_mat, precision=HIGH_PRECISION))
    inner_act = low_precision(jax.nn.silu(gate_pre) * up_pre)
    produced = low_precision(low_precision_backward(jnp.einsum('erf,efd->erd', inner_act, down_mat, precision=HIGH_PRECISION)))
    back_rows = produced.reshape(buffer_size, features)[slot_place].reshape(item_count * sequence_length, TOPK, features)
    moe_out = lax.optimization_barrier(jnp.sum(gate_probs[:, :, None] * back_rows, axis=1))
    return (hidden + moe_out).reshape(item_count, sequence_length, features)

def forward(params, first_in, shift_zero, seg_all, live_all, route_all):
    current = first_in
    results = []
    for section_num in range(N_SECTION):
        layer_params = tuple((weight[section_num] for weight in params))
        section_out = low_precision(low_precision_backward(layer(layer_params, current, seg_all, live_all, route_all[section_num])))
        results.append(section_out)
        current = section_out + shift_zero
    return jnp.stack(results)

def reference(inputs, cotangent, segment_ids, live_first, routes, gain_attn, gain_moe, w_query, key_weight, value_weight, w_out, w_router, w_gate, w_up, w_down):
    item_count = MB * SEQS
    first_in = inputs.astype(jnp.float32).reshape(item_count, SEQ, MODEL_WIDTH)
    seg_all = segment_ids.reshape(item_count, SEQ).astype(jnp.int32)
    live_all = live_first.reshape(item_count, SEQ // BLK).astype(jnp.int32)
    route_all = routes.reshape(N_SECTION, item_count, SEQ, TOPK).astype(jnp.int32)
    params = tuple((weight.astype(jnp.float32) for weight in (gain_attn, gain_moe, w_query, key_weight, value_weight, w_out, w_router, w_gate, w_up, w_down)))
    shift_zero = jnp.zeros((item_count, SEQ, MODEL_WIDTH), jnp.float32)

    def run_layers(params_in, first_val, zero_val):
        return forward(params_in, first_val, zero_val, seg_all, live_all, route_all)
    stacked, pullback = jax.vjp(run_layers, params, first_in, shift_zero)
    cot_all = jnp.stack([jnp.zeros((item_count, SEQ, MODEL_WIDTH), jnp.float32), cotangent.astype(jnp.float32).reshape(item_count, SEQ, MODEL_WIDTH)])
    param_grads, first_grad, shift_grad = pullback(cot_all)
    layer_out = stacked.astype(jnp.bfloat16).reshape(N_SECTION, MB, SEQS, SEQ, MODEL_WIDTH)
    input_grad = jnp.stack([first_grad, shift_grad]).reshape(N_SECTION, MB, SEQS, SEQ, MODEL_WIDTH)
    return (layer_out, input_grad, param_grads[0], param_grads[1], param_grads[2], param_grads[3], param_grads[4], param_grads[5], param_grads[6], param_grads[7], param_grads[8], param_grads[9])
```

```python
import functools

import jax
import jax.numpy as jnp
from jax import lax
from jax.experimental import pallas as pl
from jax.experimental.pallas import tpu as pltpu
from jax.sharding import PartitionSpec as P

QUERY_HEADS = 24
KEY_VALUE_HEADS = 8
HEAD_SIZE = 64
BLK = 64
EPS = 1e-06
THETA = 10000.0
NEG_FILL = -1e30
BF = jnp.bfloat16
F32 = jnp.float32
MESH = pl.DeviceIdType.MESH
LANES = 128
TILE = 512
QW = QUERY_HEADS * HEAD_SIZE
KW = KEY_VALUE_HEADS * HEAD_SIZE
QKV = QW + 2 * KW
GAIN_MOE_ROW = 126
GAIN_ATTN_ROW = 127
VMEM_LIMIT = 60 * 1024 * 1024
HEAD_PAIRS = KEY_VALUE_HEADS // 2
TILES_PER_PAIR = QUERY_HEADS // KEY_VALUE_HEADS


def dot(a, b, ca=1, cb=0):
    return lax.dot_general(a, b, (((ca,), (cb,)), ((), ())), preferred_element_type=F32)


def iota(shape, axis):
    return lax.broadcasted_iota(jnp.int32, shape, axis)


def rope(z, cos, sin, direction):
    width = z.shape[1]
    half = HEAD_SIZE // 2
    first = iota(z.shape, 1) % HEAD_SIZE < half
    partner = jnp.where(first, pltpu.roll(z, width - half, 1), pltpu.roll(z, half, 1))
    signed = jnp.where(first, -direction, direction) * partner
    reps = width // LANES
    return z * jnp.concatenate([cos] * reps, axis=1) + signed * jnp.concatenate([sin] * reps, axis=1)


def lane_masks(t):
    low = iota((t, LANES), 1) < HEAD_SIZE
    return low, jnp.logical_not(low)


def swapped(z):
    return pltpu.roll(z.astype(F32), HEAD_SIZE, 1).astype(BF)


def head_plan():
    return [(r, half, (2 * r + half) // TILES_PER_PAIR != half) for r in range(TILES_PER_PAIR) for half in range(2)]


def pick(z, half, masks):
    return jnp.where(masks[half], z, jnp.zeros_like(z))


def attn_fwd_kernel(x_ref, w_ref, cos_ref, sin_ref, meta_ref, segr_ref, qkv_ref, p_ref, o_ref, h_ref, b_ref, wrt_ref):
    t, d = x_ref.shape
    aux = jnp.transpose(w_ref[:, QKV + QW :].astype(F32))
    wrt_ref[...] = aux.astype(BF)
    gain_attn = aux[GAIN_ATTN_ROW : GAIN_ATTN_ROW + 1]
    gain_moe = aux[GAIN_MOE_ROW : GAIN_MOE_ROW + 1]
    x = x_ref[...].astype(F32)
    r1 = lax.rsqrt(jnp.mean(x * x, axis=1, keepdims=True) + EPS)
    a = (x * r1 * gain_attn).astype(BF)
    cos, sin = cos_ref[...], sin_ref[...]
    for n in range(QKV // TILE):
        cols = slice(n * TILE, (n + 1) * TILE)
        y = dot(a, w_ref[:, cols])
        if n * TILE < QW + KW:
            y = rope(y, cos, sin, 1.0)
        qkv_ref[:, cols] = y.astype(BF)
    i, j = iota((t, t), 0), iota((t, t), 1)
    allowed = (j <= i) & (meta_ref[:, 0:1] == segr_ref[0:1, :]) & (j // BLK >= meta_ref[:, 1:2])
    masks = lane_masks(t)

    def pair(m, carry):
        def lanes(base):
            return pl.ds(pl.multiple_of(base, LANES), LANES)

        kp = qkv_ref[:, lanes(QW + m * LANES)]
        vp = qkv_ref[:, lanes(QW + KW + m * LANES)]
        ks, vs = swapped(kp), swapped(vp)
        parts = {}
        for r, half, swap in head_plan():
            q = pick(qkv_ref[:, lanes((m * TILES_PER_PAIR + r) * LANES)], half, masks)
            s = dot(q, ks if swap else kp, 1, 1) * HEAD_SIZE ** (-0.5)
            s = jnp.where(allowed, s, NEG_FILL)
            e = jnp.exp(s - jnp.max(s, axis=1, keepdims=True))
            p = e / jnp.sum(e, axis=1, keepdims=True)
            p_ref[m * 2 * TILES_PER_PAIR + 2 * r + half] = p
            part = dot(p.astype(BF), pick(vs if swap else vp, half, masks))
            parts[half] = part
            if half == 1:
                o_ref[:, lanes((m * TILES_PER_PAIR + r) * LANES)] = (parts[0] + parts[1]).astype(BF)
        return carry

    lax.fori_loop(0, HEAD_PAIRS, pair, 0)
    o = o_ref[...]
    for n in range(d // TILE):
        rows = slice(n * TILE, (n + 1) * TILE)
        h_ref[:, rows] = x_ref[:, rows].astype(F32) + dot(o, w_ref[rows, QKV : QKV + QW], 1, 1)
    h = h_ref[...]
    r2 = lax.rsqrt(jnp.mean(h * h, axis=1, keepdims=True) + EPS)
    b_ref[...] = (h * r2 * gain_moe).astype(BF)


def vmem(n):
    return [pl.BlockSpec(memory_space=pltpu.VMEM)] * n


def attn_fwd(x, w, cos, sin, meta, segr):
    t, d = x.shape
    sds = jax.ShapeDtypeStruct
    return pl.pallas_call(
        attn_fwd_kernel,
        out_shape=(
            sds((t, QKV), BF),
            sds((QUERY_HEADS, t, t), F32),
            sds((t, QW), BF),
            sds((t, d), F32),
            sds((t, d), BF),
            sds((LANES, d), BF),
        ),
        in_specs=vmem(6),
        out_specs=tuple(vmem(6)),
        compiler_params=pltpu.CompilerParams(vmem_limit_bytes=VMEM_LIMIT),
        cost_estimate=pl.CostEstimate(flops=2 * t * d * 4096, bytes_accessed=w.size * 2, transcendentals=QUERY_HEADS * t * t),
    )(x, w, cos, sin, meta, segr)


def gates_of(rt, wrt, b, e_pad):
    t = rt.shape[1]
    experts = iota((e_pad, t), 0)
    chosen = experts == rt[0:1]
    for k in range(1, rt.shape[0]):
        chosen = chosen | (experts == rt[k : k + 1])
    logits = jnp.where(chosen, dot(wrt[0:e_pad], b, 1, 1), NEG_FILL)
    e = jnp.where(chosen, jnp.exp(logits - jnp.max(logits, axis=0, keepdims=True)), 0.0)
    return e / jnp.sum(e, axis=0, keepdims=True)


def attn_bwd_kernel(
    e_pad, gy_ref, h_ref, x_ref, w_ref, qkv_ref, p_ref, o_ref, b_ref, wrt_ref, back_ref, dg_ref, rt_ref, cos_ref, sin_ref,
    dx_ref, dd_ref, do_ref, dqkv_ref, dh_ref, lt_ref,
):
    t, d = x_ref.shape
    gain_attn = wrt_ref[GAIN_ATTN_ROW - 7 :, :].astype(F32)[7:8]
    gain_moe = wrt_ref[GAIN_ATTN_ROW - 7 :, :].astype(F32)[6:7]
    b = b_ref[...]
    gates = gates_of(rt_ref[...], wrt_ref, b, e_pad)
    dg = dg_ref[...]
    dl = (gates * (dg - jnp.sum(gates * dg, axis=0, keepdims=True)))
    dlb = dl.astype(BF)
    db = dot(dlb, wrt_ref[0:e_pad, :], 0, 0)
    for z in range(back_ref.shape[0]):
        db = db + back_ref[z].astype(F32)
    h = h_ref[...]
    r2 = lax.rsqrt(jnp.mean(h * h, axis=1, keepdims=True) + EPS)
    grad_moe = jnp.sum(db * h * r2, axis=0, keepdims=True)
    dn = db * gain_moe
    dh = gy_ref[...].astype(F32) + r2 * dn - h * (r2 * r2 * r2) * jnp.mean(dn * h, axis=1, keepdims=True)
    dh_ref[...] = dh
    dhb = dh.astype(BF)
    for n in range(QW // TILE):
        cols = slice(n * TILE, (n + 1) * TILE)
        do_ref[:, cols] = dot(dhb, w_ref[:, QKV + n * TILE : QKV + (n + 1) * TILE]).astype(BF)
    masks = lane_masks(t)
    cos, sin = cos_ref[...], sin_ref[...]

    def pair(m, carry):
        def lanes(base):
            return pl.ds(pl.multiple_of(base, LANES), LANES)

        kp = qkv_ref[:, lanes(QW + m * LANES)]
        vp = qkv_ref[:, lanes(QW + KW + m * LANES)]
        ks, vs = swapped(kp), swapped(vp)
        zero = jnp.zeros((t, LANES), F32)
        dk = {False: zero, True: zero}
        dv = {False: zero, True: zero}
        dq = zero
        for r, half, swap in head_plan():
            tile = lanes((m * TILES_PER_PAIR + r) * LANES)
            q = pick(qkv_ref[:, tile], half, masks)
            do = pick(do_ref[:, tile], half, masks)
            p = p_ref[m * 2 * TILES_PER_PAIR + 2 * r + half]
            dp = dot(do, vs if swap else vp, 1, 1)
            dv[swap] = dv[swap] + dot(p.astype(BF), do, 0, 0)
            dt = p * (dp - jnp.sum(p * dp, axis=1, keepdims=True)) * HEAD_SIZE ** (-0.5)
            dt = dt.astype(BF)
            dk[swap] = dk[swap] + dot(dt, q, 0, 0)
            part = dot(dt, pick(ks if swap else kp, half, masks))
            dq = part if half == 0 else dq + part
            if half == 1:
                dqkv_ref[:, tile] = rope(dq, cos, sin, -1.0).astype(BF)
        dk_all = dk[False] + pltpu.roll(dk[True], HEAD_SIZE, 1)
        dv_all = dv[False] + pltpu.roll(dv[True], HEAD_SIZE, 1)
        dqkv_ref[:, lanes(QW + m * LANES)] = rope(dk_all, cos, sin, -1.0).astype(BF)
        dqkv_ref[:, lanes(QW + KW + m * LANES)] = dv_all.astype(BF)
        return carry

    lax.fori_loop(0, HEAD_PAIRS, pair, 0)
    x = x_ref[...].astype(F32)
    r1 = lax.rsqrt(jnp.mean(x * x, axis=1, keepdims=True) + EPS)
    dqkv = dqkv_ref[...]
    for n in range(d // TILE):
        rows = slice(n * TILE, (n + 1) * TILE)
        dx_ref[:, rows] = dot(dqkv, w_ref[rows, 0:QKV], 1, 1)
    da = dx_ref[...]
    grad_attn = jnp.sum(da * x * r1, axis=0, keepdims=True)
    dag = da * gain_attn
    dx_ref[...] = dh_ref[...] + r1 * dag - x * (r1 * r1 * r1) * jnp.mean(dag * x, axis=1, keepdims=True)
    lt_ref[...] = jnp.transpose(x * r1 * gain_attn).astype(BF)
    for n in range(QKV // TILE):
        cols = slice(n * TILE, (n + 1) * TILE)
        dd_ref[:, cols] = dot(lt_ref[...], dqkv_ref[:, cols]).astype(BF)
    lt_ref[...] = jnp.transpose(dh_ref[...]).astype(BF)
    for n in range(QW // TILE):
        cols = slice(n * TILE, (n + 1) * TILE)
        dd_ref[:, QKV + n * TILE : QKV + (n + 1) * TILE] = dot(lt_ref[...], o_ref[:, cols]).astype(BF)
    lt_ref[...] = jnp.transpose(b_ref[...].astype(F32)).astype(BF)
    row = iota((LANES, d), 0)
    grads = jnp.where(row == GAIN_MOE_ROW, grad_moe, jnp.where(row == GAIN_ATTN_ROW, grad_attn, 0.0))
    dl_full = jnp.concatenate([dl, jnp.zeros((LANES - e_pad, t), F32)], axis=0)
    dl_rows = jnp.transpose(dl_full).astype(BF)
    dd_ref[:, QKV + QW :] = (dot(lt_ref[...], dl_rows) + jnp.transpose(grads)).astype(BF)


def attn_bwd(gy, h, x, w, qkv, p, o, b, wrt, back, dg, rt, cos, sin):
    t, d = x.shape
    sds = jax.ShapeDtypeStruct
    return pl.pallas_call(
        functools.partial(attn_bwd_kernel, dg.shape[0]),
        out_shape=(sds((t, d), F32), sds(w.shape, BF)),
        in_specs=vmem(14),
        out_specs=tuple(vmem(2)),
        scratch_shapes=[
            pltpu.VMEM((t, QW), BF),
            pltpu.VMEM((t, QKV), BF),
            pltpu.VMEM((t, d), F32),
            pltpu.VMEM((d, t), BF),
        ],
        compiler_params=pltpu.CompilerParams(vmem_limit_bytes=VMEM_LIMIT),
        cost_estimate=pl.CostEstimate(flops=4 * t * d * 4096, bytes_accessed=w.size * 4, transcendentals=0),
    )(gy, h, x, w, qkv, p, o, b, wrt, back, dg, rt, cos, sin)


def one_hot(pos_row, cap):
    return jnp.where(iota((cap, pos_row.shape[1]), 0) == pos_row, 1.0, 0.0)


def all_hots(pos, per, cap):
    return jnp.concatenate([one_hot(pos[j : j + 1], cap) for j in range(per)], axis=0)


def slots_of(rt, first, per):
    t = rt.shape[1]
    experts = iota((16, t), 0)
    mine = jnp.where(experts < per, experts + first, -1)
    chosen = mine == rt[0:1]
    for k in range(1, rt.shape[0]):
        chosen = chosen | (mine == rt[k : k + 1])
    earlier = jnp.where(iota((t, t), 0) < iota((t, t), 1), 1.0, 0.0).astype(BF)
    before = dot(jnp.where(chosen, 1.0, 0.0).astype(BF), earlier)
    return jnp.where(chosen, before.astype(jnp.int32), -1)[0:8]


def streamed(count, copies, body):
    for c in copies(0, 0):
        c.start()

    def step(b, carry):
        slot = lax.rem(b, 2)

        @pl.when(b + 1 < count)
        def _():
            for c in copies(b + 1, lax.rem(b + 1, 2)):
                c.start()

        for c in copies(b, slot):
            c.wait()
        body(b, slot)
        return carry

    lax.fori_loop(0, count, step, 0)


def combine(count, per, cap, pos_ref, rows_ref, out_hbm, obuf, osem):
    def copy(b, slot):
        return pltpu.make_async_copy(obuf.at[slot], out_hbm.at[b], osem.at[slot])

    def step(b, carry):
        slot = lax.rem(b, 2)

        @pl.when(b >= 2)
        def _():
            copy(b - 2, slot).wait()

        back = jnp.transpose(all_hots(pos_ref[b], per, cap)).astype(BF)
        at = pl.ds(pl.multiple_of(b * cap, cap), cap)
        rows = jnp.concatenate([rows_ref[j, at, :] for j in range(per)], axis=0)
        obuf[slot] = dot(back, rows).astype(BF)
        copy(b, slot).start()
        return carry

    lax.fori_loop(0, count, step, 0)
    copy(count - 2, (count - 2) % 2).wait()
    copy(count - 1, (count - 1) % 2).wait()


def chunk_gates(c, j, chunk, cap, pos_ref, gate_ref):
    hots, gates = [], []
    for bb in range(chunk // cap):
        b = c * (chunk // cap) + bb
        hot = one_hot(pos_ref[b, pl.ds(j, 1), :], cap)
        hots.append(hot)
        gates.append(jnp.sum(hot * gate_ref[b, pl.ds(j, 1), :], axis=1, keepdims=True))
    return hots, jnp.concatenate(gates, axis=0)


def experts_fwd_kernel(
    layer, e_pad, cap, rt_ref, wrt_ref, wg_ref, wu_ref, wd_ref, b_hbm,
    gp_ref, up_ref, pos_ref, gate_ref, out_hbm, x_scr, y_scr, all_gates, bbuf, obuf, bsem, osem,
):
    per, rows, d = x_scr.shape
    count = rt_ref.shape[0]
    chunk = 256
    j = pl.program_id(0)
    first = lax.axis_index("expert") * per

    @pl.when(lax.axis_index("section") == layer)
    def _():
        @pl.when(j == 0)
        def _():
            def prepare(b, slot):
                rt = rt_ref[b]
                block = bbuf[slot]
                pos = slots_of(rt, first, per)
                pos_ref[b] = pos
                all_gates[...] = gates_of(rt, wrt_ref, block, e_pad)
                gate_ref[b] = jnp.concatenate(
                    [all_gates[pl.ds(first + k, 1), :] for k in range(per)] + [jnp.zeros((8 - per, rt.shape[1]), F32)], axis=0
                )
                x = dot(all_hots(pos, per, cap).astype(BF), block).astype(BF)
                at = pl.ds(pl.multiple_of(b * cap, cap), cap)
                for k in range(per):
                    x_scr[k, at, :] = x[k * cap : (k + 1) * cap]

            streamed(count, lambda b, slot: [pltpu.make_async_copy(b_hbm.at[b], bbuf.at[slot], bsem.at[slot])], prepare)

        def part(c, carry):
            at = pl.ds(pl.multiple_of(c * chunk, chunk), chunk)
            x = x_scr[j, at, :]
            gp = dot(x, wg_ref[0])
            up = dot(x, wu_ref[0])
            gp_ref[0, at, :] = gp
            up_ref[0, at, :] = up
            hid = (gp / (1.0 + jnp.exp(-gp)) * up).astype(BF)
            _, gate = chunk_gates(c, j, chunk, cap, pos_ref, gate_ref)
            y_scr[j, at, :] = (dot(hid, wd_ref[0]) * gate).astype(BF)
            return carry

        lax.fori_loop(0, rows // chunk, part, 0)

        @pl.when(j == per - 1)
        def _():
            combine(count, per, cap, pos_ref, y_scr, out_hbm, obuf, osem)


def any_spec():
    return pl.BlockSpec(memory_space=pl.ANY)


def fixed(shape):
    return pl.BlockSpec(shape, lambda j: (0,) * len(shape))


def experts_fwd(layer, e_pad, cap, rt, wrt, wg, wu, wd, blocks):
    count, t, d = blocks.shape
    per, _, f = wg.shape
    rows = count * cap
    sds = jax.ShapeDtypeStruct
    return pl.pallas_call(
        functools.partial(experts_fwd_kernel, layer, e_pad, cap),
        grid=(per,),
        out_shape=(
            sds((per, rows, f), F32),
            sds((per, rows, f), F32),
            sds((count, 8, t), jnp.int32),
            sds((count, 8, t), F32),
            sds((count, t, d), BF),
        ),
        in_specs=[
            fixed(rt.shape),
            fixed(wrt.shape),
            pl.BlockSpec((1, d, f), lambda j: (j, 0, 0)),
            pl.BlockSpec((1, d, f), lambda j: (j, 0, 0)),
            pl.BlockSpec((1, f, d), lambda j: (j, 0, 0)),
            any_spec(),
        ],
        out_specs=(
            pl.BlockSpec((1, rows, f), lambda j: (j, 0, 0)),
            pl.BlockSpec((1, rows, f), lambda j: (j, 0, 0)),
            fixed((count, 8, t)),
            fixed((count, 8, t)),
            any_spec(),
        ),
        scratch_shapes=[
            pltpu.VMEM((per, rows, d), BF),
            pltpu.VMEM((per, rows, d), BF),
            pltpu.VMEM((e_pad, t), F32),
            pltpu.VMEM((2, t, d), BF),
            pltpu.VMEM((2, t, d), BF),
            pltpu.SemaphoreType.DMA((2,)),
            pltpu.SemaphoreType.DMA((2,)),
        ],
        compiler_params=pltpu.CompilerParams(vmem_limit_bytes=VMEM_LIMIT),
        cost_estimate=pl.CostEstimate(flops=6 * per * rows * d * f, bytes_accessed=6 * per * d * f, transcendentals=per * rows * f),
    )(rt, wrt, wg, wu, wd, blocks)


def experts_bwd_kernel(
    layer, cap, pos_ref, gate_ref, wg_ref, wu_ref, wd_ref, gp_ref, up_ref, b_hbm, gy_hbm,
    dw_ref, dg_ref, out_hbm, x_scr, y_scr, dgp_scr, dup_scr, hid_scr, bbuf, gbuf, obuf, bsem, gsem, osem,
):
    per, rows, d = x_scr.shape
    count = pos_ref.shape[0]
    parts = dw_ref.shape[0]
    piece = d // parts
    chunk = 256
    j = pl.program_id(0)

    @pl.when(lax.axis_index("section") == layer)
    def _():
        @pl.when(j == 0)
        def _():
            def prepare(b, slot):
                hots = all_hots(pos_ref[b], per, cap).astype(BF)
                x = dot(hots, bbuf[slot]).astype(BF)
                y = dot(hots, gbuf[slot]).astype(BF)
                at = pl.ds(pl.multiple_of(b * cap, cap), cap)
                for k in range(per):
                    x_scr[k, at, :] = x[k * cap : (k + 1) * cap]
                    y_scr[k, at, :] = y[k * cap : (k + 1) * cap]

            streamed(
                count,
                lambda b, slot: [
                    pltpu.make_async_copy(b_hbm.at[b], bbuf.at[slot], bsem.at[slot]),
                    pltpu.make_async_copy(gy_hbm.at[b], gbuf.at[slot], gsem.at[slot]),
                ],
                prepare,
            )
            dg_ref[...] = jnp.zeros_like(dg_ref)

        def part(c, carry):
            at = pl.ds(pl.multiple_of(c * chunk, chunk), chunk)
            raw = dot(y_scr[j, at, :], wd_ref[0], 1, 1)
            gp, up = gp_ref[0, at, :], up_ref[0, at, :]
            sg = 1.0 / (1.0 + jnp.exp(-gp))
            silu = gp * sg
            hid = silu * up
            hots, gate = chunk_gates(c, j, chunk, cap, pos_ref, gate_ref)
            dgate = jnp.sum(hid.astype(BF).astype(F32) * raw, axis=1, keepdims=True)
            for bb in range(chunk // cap):
                b = c * (chunk // cap) + bb
                dg_ref[b, pl.ds(j, 1), :] = jnp.sum(hots[bb] * dgate[bb * cap : (bb + 1) * cap], axis=0, keepdims=True)
            dh = raw * gate
            dgp_scr[at, :] = (dh * up * sg * (1.0 + gp * (1.0 - sg))).astype(BF)
            dup_scr[at, :] = (dh * silu).astype(BF)
            hid_scr[at, :] = (hid * gate).astype(BF)
            return carry

        lax.fori_loop(0, rows // chunk, part, 0)

        def weights(g, carry):
            cols = pl.ds(pl.multiple_of(g * piece, LANES), piece)
            x = x_scr[j, :, cols]
            dw_ref[g, 0, 0] = dot(x, dgp_scr[...], 0, 0).astype(BF)
            dw_ref[g, 0, 1] = dot(x, dup_scr[...], 0, 0).astype(BF)
            dw_ref[g, 0, 2] = dot(y_scr[j, :, cols], hid_scr[...], 0, 0).astype(BF)
            return carry

        if piece % LANES == 0:
            lax.fori_loop(0, parts, weights, 0)
        else:
            wide = LANES
            while wide % piece:
                wide += LANES
            for g0 in range(0, d, wide):
                x = x_scr[j, :, g0 : g0 + wide]
                y = y_scr[j, :, g0 : g0 + wide]
                for n, (left, right) in enumerate(((x, dgp_scr), (x, dup_scr), (y, hid_scr))):
                    full = dot(left, right[...], 0, 0).astype(BF)
                    for i in range(wide // piece):
                        dw_ref[g0 // piece + i, 0, n] = full[i * piece : (i + 1) * piece]

        def rows_back(c, carry):
            at = pl.ds(pl.multiple_of(c * chunk, chunk), chunk)
            y_scr[j, at, :] = (dot(dgp_scr[at, :], wg_ref[0], 1, 1) + dot(dup_scr[at, :], wu_ref[0], 1, 1)).astype(BF)
            return carry

        lax.fori_loop(0, rows // chunk, rows_back, 0)

        @pl.when(j == per - 1)
        def _():
            combine(count, per, cap, pos_ref, y_scr, out_hbm, obuf, osem)


def experts_bwd(layer, cap, groups, pos, gate, wg, wu, wd, gp, up, blocks, grads):
    count, t, d = blocks.shape
    per, _, f = wg.shape
    rows = count * cap
    sds = jax.ShapeDtypeStruct
    return pl.pallas_call(
        functools.partial(experts_bwd_kernel, layer, cap),
        grid=(per,),
        out_shape=(
            sds((groups, per, 3, d // groups, f), BF),
            sds((count, 8, t), F32),
            sds((count, t, d), BF),
        ),
        in_specs=[
            fixed(pos.shape),
            fixed(gate.shape),
            pl.BlockSpec((1, d, f), lambda j: (j, 0, 0)),
            pl.BlockSpec((1, d, f), lambda j: (j, 0, 0)),
            pl.BlockSpec((1, f, d), lambda j: (j, 0, 0)),
            pl.BlockSpec((1, rows, f), lambda j: (j, 0, 0)),
            pl.BlockSpec((1, rows, f), lambda j: (j, 0, 0)),
            any_spec(),
            any_spec(),
        ],
        out_specs=(
            pl.BlockSpec((groups, 1, 3, d // groups, f), lambda j: (0, j, 0, 0, 0)),
            fixed((count, 8, t)),
            any_spec(),
        ),
        scratch_shapes=[
            pltpu.VMEM((per, rows, d), BF),
            pltpu.VMEM((per, rows, d), BF),
            pltpu.VMEM((rows, f), BF),
            pltpu.VMEM((rows, f), BF),
            pltpu.VMEM((rows, f), BF),
            pltpu.VMEM((2, t, d), BF),
            pltpu.VMEM((2, t, d), BF),
            pltpu.VMEM((2, t, d), BF),
            pltpu.SemaphoreType.DMA((2,)),
            pltpu.SemaphoreType.DMA((2,)),
            pltpu.SemaphoreType.DMA((2,)),
        ],
        compiler_params=pltpu.CompilerParams(vmem_limit_bytes=VMEM_LIMIT),
        cost_estimate=pl.CostEstimate(flops=12 * per * rows * d * f, bytes_accessed=12 * per * d * f, transcendentals=per * rows * f),
    )(pos, gate, wg, wu, wd, gp, up, blocks, grads)


def meet(n, with_cross):
    s, z = lax.axis_index("section"), lax.axis_index("expert")
    barrier = pltpu.get_barrier_semaphore()
    for k in range(1, n):
        pl.semaphore_signal(barrier, inc=1, device_id={"expert": lax.rem(z + k, n)}, device_id_type=MESH)
    for k in range(n if with_cross else 1):
        pl.semaphore_signal(
            barrier, inc=1, device_id={"section": 1 - s, "expert": lax.rem(z + k, n)}, device_id_type=MESH
        )
    pl.semaphore_wait(barrier, 2 * n - 1 if with_cross else n)


def spread_kernel(layer, n, x_ref, o_ref, send_sem, recv_sem, local_sem):
    s, z = lax.axis_index("section"), lax.axis_index("expert")
    meet(n, True)

    def copy(k, source_section):
        return pltpu.make_async_remote_copy(
            src_ref=x_ref,
            dst_ref=o_ref.at[source_section, z],
            send_sem=send_sem.at[k],
            recv_sem=recv_sem.at[source_section, k],
            device_id={"section": layer, "expert": lax.rem(z + k, n)},
            device_id_type=MESH,
        )

    order = sorted(range(n), key=lambda k: (k == 0, abs(k - n // 2)))

    @pl.when(s == layer)
    def _():
        own = pltpu.make_async_copy(x_ref, o_ref.at[layer, z], local_sem)
        own.start()
        sends = [copy(k, layer) for k in order if k]
        for c in sends:
            c.start()
        own.wait()
        for c in sends:
            c.wait()
        for k in range(n):
            copy(k, 1 - layer).wait_recv()

    @pl.when(s != layer)
    def _():
        sends = [copy(k, 1 - layer) for k in order]
        for c in sends:
            c.start()
        for c in sends:
            c.wait_send()


def spread(layer, cid, x):
    n = lax.axis_size("expert")
    return pl.pallas_call(
        functools.partial(spread_kernel, layer, n),
        out_shape=jax.ShapeDtypeStruct((2, n) + x.shape, x.dtype),
        in_specs=[any_spec()],
        out_specs=any_spec(),
        scratch_shapes=[
            pltpu.SemaphoreType.DMA((n,)),
            pltpu.SemaphoreType.DMA((2, n)),
            pltpu.SemaphoreType.DMA,
        ],
        compiler_params=pltpu.CompilerParams(collective_id=cid, has_side_effects=True),
    )(x)


def collect_kernel(layer, n, arrays, *refs):
    srcs, outs, relays = refs[:arrays], refs[arrays : 2 * arrays], refs[2 * arrays : 3 * arrays]
    relay_send, relay_recv, send_sem, recv_sem, local_sem = refs[3 * arrays :]
    s, z = lax.axis_index("section"), lax.axis_index("expert")
    meet(n, False)

    def hop(a, to):
        return pltpu.make_async_remote_copy(
            src_ref=srcs[a].at[1 - layer, to],
            dst_ref=relays[a].at[to],
            send_sem=relay_send.at[a, to],
            recv_sem=relay_recv.at[a, to],
            device_id={"section": 1 - s},
            device_id_type=MESH,
        )

    def give(a, source, k):
        return pltpu.make_async_remote_copy(
            src_ref=source,
            dst_ref=outs[a].at[z],
            send_sem=send_sem.at[a, k],
            recv_sem=recv_sem.at[a, k],
            device_id={"expert": lax.rem(z + k, n)},
            device_id_type=MESH,
        )

    order = sorted(range(n), key=lambda k: (k == 0, abs(k - n // 2)))

    @pl.when(s == layer)
    def _():
        for k in order:
            for a in range(arrays):
                hop(a, lax.rem(z + k, n)).start()
        for k in order:
            for a in range(arrays):
                if k:
                    give(a, srcs[a].at[layer, lax.rem(z + k, n)], k).start()
                else:
                    pltpu.make_async_copy(srcs[a].at[layer, z], outs[a].at[z], local_sem.at[a]).start()
        for k in order:
            for a in range(arrays):
                hop(a, lax.rem(z + k, n)).wait_send()

    @pl.when(s != layer)
    def _():
        for k in order:
            to = lax.rem(z + k, n)
            for a in range(arrays):
                hop(a, to).wait_recv()
                if k:
                    give(a, relays[a].at[to], k).start()
                else:
                    pltpu.make_async_copy(relays[a].at[z], outs[a].at[z], local_sem.at[a]).start()

    for a in range(arrays):
        for k in order:
            if k:
                give(a, relays[a].at[lax.rem(z + k, n)], k).wait()
            else:
                pltpu.make_async_copy(relays[a].at[z], outs[a].at[z], local_sem.at[a]).wait()


def collect(layer, cid, *arrays):
    n = lax.axis_size("expert")
    count = len(arrays)
    return pl.pallas_call(
        functools.partial(collect_kernel, layer, n, count),
        out_shape=tuple(jax.ShapeDtypeStruct(a.shape[1:], a.dtype) for a in arrays),
        in_specs=[any_spec()] * count,
        out_specs=tuple([any_spec()] * count),
        scratch_shapes=[pltpu.VMEM(a.shape[1:], a.dtype) for a in arrays]
        + [
            pltpu.SemaphoreType.DMA((count, n)),
            pltpu.SemaphoreType.DMA((count, n)),
            pltpu.SemaphoreType.DMA((count, n)),
            pltpu.SemaphoreType.DMA((count, n)),
            pltpu.SemaphoreType.DMA((count,)),
        ],
        compiler_params=pltpu.CompilerParams(collective_id=cid, has_side_effects=True),
    )(*arrays)


def swap_sections(value):
    return lax.ppermute(value, "section", [(0, 1), (1, 0)])


def rope_tables(t):
    half = HEAD_SIZE // 2
    frequency = THETA ** (-jnp.arange(half, dtype=F32) * 2.0 / HEAD_SIZE)
    angles = jnp.arange(t, dtype=F32)[:, None] * frequency[None, :]
    reps = LANES // half
    return jnp.tile(jnp.cos(angles), (1, reps)), jnp.tile(jnp.sin(angles), (1, reps))


def local(
    inputs, cotangent, segment_ids, live_first, routes, gain_attn, gain_moe,
    w_query, key_weight, value_weight, w_out, w_router, w_gate, w_up, w_down,
):
    s = lax.axis_index("section")
    n = lax.axis_size("expert")
    groups = lax.axis_size("group")
    t, d = inputs.shape[2:]
    top = routes.shape[-1]
    per = w_gate.shape[1]
    experts = per * n
    e_pad = -(-experts // 16) * 16
    cap = t * top * 5 // (4 * experts)
    wg, wu, wd = w_gate[0], w_up[0], w_down[0]
    at_zero = s == 0

    shard = w_query.shape[1]
    aux = jnp.concatenate(
        [
            w_router[0],
            jnp.zeros((shard, GAIN_MOE_ROW - experts), BF),
            gain_moe[0][:, None],
            gain_attn[0][:, None],
        ],
        axis=1,
    )
    packed = jnp.concatenate([w_query[0], key_weight[0], value_weight[0], w_out[0].T, aux], axis=1)
    other = swap_sections(packed)
    shards = (jnp.where(at_zero, packed, other), jnp.where(at_zero, other, packed))
    first_weights = lax.all_gather(shards[0], ("group", "expert"), axis=0, tiled=True)

    x0 = lax.dynamic_index_in_dim(inputs[:, 0], s, 0, keepdims=False)
    cot = lax.dynamic_index_in_dim(cotangent[:, 0], s, 0, keepdims=False)
    seg = lax.dynamic_index_in_dim(segment_ids[:, 0], s, 0, keepdims=False)
    live = lax.dynamic_index_in_dim(live_first[:, 0], s, 0, keepdims=False)
    meta = jnp.stack([seg, jnp.repeat(live, BLK)], axis=1)
    meta = jnp.pad(meta, ((0, 0), (0, LANES - 2)))
    segr = jnp.broadcast_to(seg[None, :], (8, t))
    cos, sin = rope_tables(t)

    rt = jnp.swapaxes(routes[0, :, 0], 1, 2)
    rt_mine = lax.dynamic_index_in_dim(rt, s, 0, keepdims=False)
    rt_theirs = swap_sections(lax.dynamic_index_in_dim(rt, 1 - s, 0, keepdims=False))
    rt_tokens = (jnp.where(at_zero, rt_mine, rt_theirs), jnp.where(at_zero, rt_theirs, rt_mine))
    rt_all = lax.all_gather(rt, "expert", axis=1, tiled=False).reshape(2 * n, top, t)

    def flat(z):
        return z.reshape((2 * n,) + z.shape[2:])

    def paired(z):
        return z.reshape((2, n) + z.shape[1:])

    gy1 = flat(spread(1, 1, cot))

    qkv0, p0, o0, h0, b0, wrt0 = attn_fwd(x0, first_weights, cos, sin, meta, segr)
    second_weights = lax.all_gather(shards[1], ("group", "expert"), axis=0, tiled=True)
    b0_all = flat(spread(0, 2, b0))
    gp0, up0, pos0, gate0, part0 = experts_fwd(0, e_pad, cap, rt_all, wrt0, wg, wu, wd, b0_all)
    (back0,) = collect(0, 3, paired(part0))
    x1 = (h0 + jnp.sum(back0.astype(F32), axis=0)).astype(BF)

    qkv1, p1, o1, h1, b1, wrt1 = attn_fwd(x1, second_weights, cos, sin, meta, segr)
    b1_all = flat(spread(1, 4, b1))
    gp1, up1, pos1, gate1, part1 = experts_fwd(1, e_pad, cap, rt_all, wrt1, wg, wu, wd, b1_all)
    dw1, dg1, dpart1 = experts_bwd(1, cap, groups, pos1, gate1, wg, wu, wd, gp1, up1, b1_all, gy1)
    dback1, dgate1 = collect(1, 5, paired(dpart1), paired(dg1))

    def gates_back(dg):
        dg = dg[:, :per].reshape(experts, t)
        return jnp.pad(dg, ((0, e_pad - experts), (0, 0)))

    dx1, dd1 = attn_bwd(cot, h1, x1, second_weights, qkv1, p1, o1, b1, wrt1, dback1, gates_back(dgate1), rt_tokens[1], cos, sin)
    gy0 = dx1.astype(BF)

    gy0_all = flat(spread(0, 6, gy0))
    dw0, dg0, dpart0 = experts_bwd(0, cap, groups, pos0, gate0, wg, wu, wd, gp0, up0, b0_all, gy0_all)
    dback0, dgate0 = collect(0, 7, paired(dpart0), paired(dg0))
    dw = jnp.where(at_zero, dw0, dw1)
    dw = lax.psum_scatter(dw, "group", scatter_dimension=0, tiled=True)[0].astype(F32)
    dx0, dd0 = attn_bwd(gy0, h0, x0, first_weights, qkv0, p0, o0, b0, wrt0, dback0, gates_back(dgate0), rt_tokens[0], cos, sin)

    part1, _ = lax.optimization_barrier((part1, dback0))
    (back1,) = collect(1, 8, paired(part1))
    y1 = (h1 + jnp.sum(back1.astype(F32), axis=0)).astype(BF)

    ds1 = lax.psum_scatter(dd1, ("group", "expert"), scatter_dimension=0, tiled=True)
    ds0 = lax.psum_scatter(dd0, ("group", "expert"), scatter_dimension=0, tiled=True)
    kept = jnp.where(at_zero, ds0, ds1)
    dense = kept.astype(F32) + swap_sections(jnp.where(at_zero, ds1, ds0)).astype(F32)

    kept_out = jnp.where(at_zero, x1, y1)
    swapped_out = swap_sections(jnp.where(at_zero, y1, x1))
    layer_out = jnp.where(at_zero, jnp.stack([kept_out, swapped_out]), jnp.stack([swapped_out, kept_out]))
    kept_in = jnp.where(at_zero, dx0, dx1)
    swapped_in = swap_sections(jnp.where(at_zero, dx1, dx0))
    input_grad = jnp.where(at_zero, jnp.stack([kept_in, swapped_in]), jnp.stack([swapped_in, kept_in]))

    return (
        layer_out[None, :, None],
        input_grad[None, :, None],
        dense[:, QKV + QW + GAIN_ATTN_ROW][None],
        dense[:, QKV + QW + GAIN_MOE_ROW][None],
        dense[None, :, 0:QW],
        dense[None, :, QW : QW + KW],
        dense[None, :, QW + KW : QKV],
        dense[:, QKV : QKV + QW].T[None],
        dense[None, :, QKV + QW : QKV + QW + experts],
        dw[None, :, 0],
        dw[None, :, 1],
        jnp.swapaxes(dw[:, 2], 1, 2)[None],
    )


def solution(mesh):
    return jax.shard_map(
        local,
        mesh=mesh,
        in_specs=(
            P(None, ("group", "expert"), None, None),
            P(None, ("group", "expert"), None, None),
            P(None, ("group", "expert"), None),
            P(None, ("group", "expert"), None),
            P("section", None, ("group", "expert"), None, None),
            P("section", ("group", "expert")),
            P("section", ("group", "expert")),
            P("section", ("group", "expert"), None),
            P("section", ("group", "expert"), None),
            P("section", ("group", "expert"), None),
            P("section", None, ("group", "expert")),
            P("section", ("group", "expert"), None),
            P("section", "expert", None, None),
            P("section", "expert", None, None),
            P("section", "expert", None, None),
        ),
        out_specs=(
            P("section", None, ("group", "expert"), None, None),
            P("section", None, ("group", "expert"), None, None),
            P("section", ("group", "expert")),
            P("section", ("group", "expert")),
            P("section", ("group", "expert"), None),
            P("section", ("group", "expert"), None),
            P("section", ("group", "expert"), None),
            P("section", None, ("group", "expert")),
            P("section", ("group", "expert"), None),
            P("section", "expert", "group", None),
            P("section", "expert", "group", None),
            P("section", "expert", None, "group"),
        ),
        check_vma=False,
    )
```

```python
import functools

import jax
import jax.numpy as jnp
from jax import lax
from jax.experimental import pallas as pl
from jax.experimental.pallas import tpu as pltpu
from jax.sharding import PartitionSpec as P

QUERY_HEADS = 24
KEY_VALUE_HEADS = 8
HEAD_SIZE = 64
BLK = 64
EPS = 1e-06
THETA = 10000.0
NEG_FILL = -1e30
BF = jnp.bfloat16
F32 = jnp.float32
MESH = pl.DeviceIdType.MESH
LANES = 128
TILE = 512
QW = QUERY_HEADS * HEAD_SIZE
KW = KEY_VALUE_HEADS * HEAD_SIZE
QKV = QW + 2 * KW
GAIN_MOE_ROW = 126
GAIN_ATTN_ROW = 127
VMEM_LIMIT = 60 * 1024 * 1024
HEAD_PAIRS = KEY_VALUE_HEADS // 2
TILES_PER_PAIR = QUERY_HEADS // KEY_VALUE_HEADS


def dot(a, b, ca=1, cb=0):
    return lax.dot_general(a, b, (((ca,), (cb,)), ((), ())), preferred_element_type=F32)


def iota(shape, axis):
    return lax.broadcasted_iota(jnp.int32, shape, axis)


def rope(z, cos, sin, direction):
    width = z.shape[1]
    half = HEAD_SIZE // 2
    first = iota(z.shape, 1) % HEAD_SIZE < half
    partner = jnp.where(first, pltpu.roll(z, width - half, 1), pltpu.roll(z, half, 1))
    signed = jnp.where(first, -direction, direction) * partner
    reps = width // LANES
    return z * jnp.concatenate([cos] * reps, axis=1) + signed * jnp.concatenate([sin] * reps, axis=1)


def lane_masks(t):
    low = iota((t, LANES), 1) < HEAD_SIZE
    return low, jnp.logical_not(low)


def swapped(z):
    return pltpu.roll(z.astype(F32), HEAD_SIZE, 1).astype(BF)


def head_plan():
    return [(r, half, (2 * r + half) // TILES_PER_PAIR != half) for r in range(TILES_PER_PAIR) for half in range(2)]


def pick(z, half, masks):
    return jnp.where(masks[half], z, jnp.zeros_like(z))


def attn_fwd_kernel(x_ref, w_ref, cos_ref, sin_ref, meta_ref, segr_ref, qkv_ref, p_ref, o_ref, h_ref, b_ref, wrt_ref):
    t, d = x_ref.shape
    aux = jnp.transpose(w_ref[:, QKV + QW :].astype(F32))
    wrt_ref[...] = aux.astype(BF)
    gain_attn = aux[GAIN_ATTN_ROW : GAIN_ATTN_ROW + 1]
    gain_moe = aux[GAIN_MOE_ROW : GAIN_MOE_ROW + 1]
    x = x_ref[...].astype(F32)
    r1 = lax.rsqrt(jnp.mean(x * x, axis=1, keepdims=True) + EPS)
    a = (x * r1 * gain_attn).astype(BF)
    cos, sin = cos_ref[...], sin_ref[...]
    for n in range(QKV // TILE):
        cols = slice(n * TILE, (n + 1) * TILE)
        y = dot(a, w_ref[:, cols])
        if n * TILE < QW + KW:
            y = rope(y, cos, sin, 1.0)
        qkv_ref[:, cols] = y.astype(BF)
    i, j = iota((t, t), 0), iota((t, t), 1)
    allowed = (j <= i) & (meta_ref[:, 0:1] == segr_ref[0:1, :]) & (j // BLK >= meta_ref[:, 1:2])
    masks = lane_masks(t)

    def pair(m, carry):
        def lanes(base):
            return pl.ds(pl.multiple_of(base, LANES), LANES)

        kp = qkv_ref[:, lanes(QW + m * LANES)]
        vp = qkv_ref[:, lanes(QW + KW + m * LANES)]
        ks, vs = swapped(kp), swapped(vp)
        parts = {}
        for r, half, swap in head_plan():
            q = pick(qkv_ref[:, lanes((m * TILES_PER_PAIR + r) * LANES)], half, masks)
            s = dot(q, ks if swap else kp, 1, 1) * HEAD_SIZE ** (-0.5)
            s = jnp.where(allowed, s, NEG_FILL)
            e = jnp.exp(s - jnp.max(s, axis=1, keepdims=True))
            p = e / jnp.sum(e, axis=1, keepdims=True)
            p_ref[m * 2 * TILES_PER_PAIR + 2 * r + half] = p
            part = dot(p.astype(BF), pick(vs if swap else vp, half, masks))
            parts[half] = part
            if half == 1:
                o_ref[:, lanes((m * TILES_PER_PAIR + r) * LANES)] = (parts[0] + parts[1]).astype(BF)
        return carry

    lax.fori_loop(0, HEAD_PAIRS, pair, 0)
    o = o_ref[...]
    for n in range(d // TILE):
        rows = slice(n * TILE, (n + 1) * TILE)
        h_ref[:, rows] = x_ref[:, rows].astype(F32) + dot(o, w_ref[rows, QKV : QKV + QW], 1, 1)
    h = h_ref[...]
    r2 = lax.rsqrt(jnp.mean(h * h, axis=1, keepdims=True) + EPS)
    b_ref[...] = (h * r2 * gain_moe).astype(BF)


def vmem(n):
    return [pl.BlockSpec(memory_space=pltpu.VMEM)] * n


def attn_fwd(x, w, cos, sin, meta, segr):
    t, d = x.shape
    sds = jax.ShapeDtypeStruct
    return pl.pallas_call(
        attn_fwd_kernel,
        out_shape=(
            sds((t, QKV), BF),
            sds((QUERY_HEADS, t, t), F32),
            sds((t, QW), BF),
            sds((t, d), F32),
            sds((t, d), BF),
            sds((LANES, d), BF),
        ),
        in_specs=vmem(6),
        out_specs=tuple(vmem(6)),
        compiler_params=pltpu.CompilerParams(vmem_limit_bytes=VMEM_LIMIT),
        cost_estimate=pl.CostEstimate(flops=2 * t * d * 4096, bytes_accessed=w.size * 2, transcendentals=QUERY_HEADS * t * t),
    )(x, w, cos, sin, meta, segr)


def gates_of(rt, wrt, b, e_pad):
    t = rt.shape[1]
    experts = iota((e_pad, t), 0)
    chosen = experts == rt[0:1]
    for k in range(1, rt.shape[0]):
        chosen = chosen | (experts == rt[k : k + 1])
    logits = jnp.where(chosen, dot(wrt[0:e_pad], b, 1, 1), NEG_FILL)
    e = jnp.where(chosen, jnp.exp(logits - jnp.max(logits, axis=0, keepdims=True)), 0.0)
    return e / jnp.sum(e, axis=0, keepdims=True)


def attn_bwd_kernel(
    e_pad, gy_ref, h_ref, x_ref, w_ref, qkv_ref, p_ref, o_ref, b_ref, wrt_ref, back_ref, dg_ref, rt_ref, cos_ref, sin_ref,
    dx_ref, dd_ref, do_ref, dqkv_ref, dh_ref, lt_ref,
):
    t, d = x_ref.shape
    gain_attn = wrt_ref[GAIN_ATTN_ROW - 7 :, :].astype(F32)[7:8]
    gain_moe = wrt_ref[GAIN_ATTN_ROW - 7 :, :].astype(F32)[6:7]
    b = b_ref[...]
    gates = gates_of(rt_ref[...], wrt_ref, b, e_pad)
    dg = dg_ref[...]
    dl = (gates * (dg - jnp.sum(gates * dg, axis=0, keepdims=True)))
    dlb = dl.astype(BF)
    db = dot(dlb, wrt_ref[0:e_pad, :], 0, 0)
    for z in range(back_ref.shape[0]):
        db = db + back_ref[z].astype(F32)
    h = h_ref[...]
    r2 = lax.rsqrt(jnp.mean(h * h, axis=1, keepdims=True) + EPS)
    grad_moe = jnp.sum(db * h * r2, axis=0, keepdims=True)
    dn = db * gain_moe
    dh = gy_ref[...].astype(F32) + r2 * dn - h * (r2 * r2 * r2) * jnp.mean(dn * h, axis=1, keepdims=True)
    dh_ref[...] = dh
    dhb = dh.astype(BF)
    for n in range(QW // TILE):
        cols = slice(n * TILE, (n + 1) * TILE)
        do_ref[:, cols] = dot(dhb, w_ref[:, QKV + n * TILE : QKV + (n + 1) * TILE]).astype(BF)
    masks = lane_masks(t)
    cos, sin = cos_ref[...], sin_ref[...]

    def pair(m, carry):
        def lanes(base):
            return pl.ds(pl.multiple_of(base, LANES), LANES)

        kp = qkv_ref[:, lanes(QW + m * LANES)]
        vp = qkv_ref[:, lanes(QW + KW + m * LANES)]
        ks, vs = swapped(kp), swapped(vp)
        zero = jnp.zeros((t, LANES), F32)
        dk = {False: zero, True: zero}
        dv = {False: zero, True: zero}
        dq = zero
        for r, half, swap in head_plan():
            tile = lanes((m * TILES_PER_PAIR + r) * LANES)
            q = pick(qkv_ref[:, tile], half, masks)
            do = pick(do_ref[:, tile], half, masks)
            p = p_ref[m * 2 * TILES_PER_PAIR + 2 * r + half]
            dp = dot(do, vs if swap else vp, 1, 1)
            dv[swap] = dv[swap] + dot(p.astype(BF), do, 0, 0)
            dt = p * (dp - jnp.sum(p * dp, axis=1, keepdims=True)) * HEAD_SIZE ** (-0.5)
            dt = dt.astype(BF)
            dk[swap] = dk[swap] + dot(dt, q, 0, 0)
            part = dot(dt, pick(ks if swap else kp, half, masks))
            dq = part if half == 0 else dq + part
            if half == 1:
                dqkv_ref[:, tile] = rope(dq, cos, sin, -1.0).astype(BF)
        dk_all = dk[False] + pltpu.roll(dk[True], HEAD_SIZE, 1)
        dv_all = dv[False] + pltpu.roll(dv[True], HEAD_SIZE, 1)
        dqkv_ref[:, lanes(QW + m * LANES)] = rope(dk_all, cos, sin, -1.0).astype(BF)
        dqkv_ref[:, lanes(QW + KW + m * LANES)] = dv_all.astype(BF)
        return carry

    lax.fori_loop(0, HEAD_PAIRS, pair, 0)
    x = x_ref[...].astype(F32)
    r1 = lax.rsqrt(jnp.mean(x * x, axis=1, keepdims=True) + EPS)
    dqkv = dqkv_ref[...]
    for n in range(d // TILE):
        rows = slice(n * TILE, (n + 1) * TILE)
        dx_ref[:, rows] = dot(dqkv, w_ref[rows, 0:QKV], 1, 1)
    da = dx_ref[...]
    grad_attn = jnp.sum(da * x * r1, axis=0, keepdims=True)
    dag = da * gain_attn
    dx_ref[...] = dh_ref[...] + r1 * dag - x * (r1 * r1 * r1) * jnp.mean(dag * x, axis=1, keepdims=True)
    lt_ref[...] = jnp.transpose(x * r1 * gain_attn).astype(BF)
    for n in range(QKV // TILE):
        cols = slice(n * TILE, (n + 1) * TILE)
        dd_ref[:, cols] = dot(lt_ref[...], dqkv_ref[:, cols]).astype(BF)
    lt_ref[...] = jnp.transpose(dh_ref[...]).astype(BF)
    for n in range(QW // TILE):
        cols = slice(n * TILE, (n + 1) * TILE)
        dd_ref[:, QKV + n * TILE : QKV + (n + 1) * TILE] = dot(lt_ref[...], o_ref[:, cols]).astype(BF)
    lt_ref[...] = jnp.transpose(b_ref[...].astype(F32)).astype(BF)
    row = iota((LANES, d), 0)
    grads = jnp.where(row == GAIN_MOE_ROW, grad_moe, jnp.where(row == GAIN_ATTN_ROW, grad_attn, 0.0))
    dl_full = jnp.concatenate([dl, jnp.zeros((LANES - e_pad, t), F32)], axis=0)
    dl_rows = jnp.transpose(dl_full).astype(BF)
    dd_ref[:, QKV + QW :] = (dot(lt_ref[...], dl_rows) + jnp.transpose(grads)).astype(BF)


def attn_bwd(gy, h, x, w, qkv, p, o, b, wrt, back, dg, rt, cos, sin):
    t, d = x.shape
    sds = jax.ShapeDtypeStruct
    return pl.pallas_call(
        functools.partial(attn_bwd_kernel, dg.shape[0]),
        out_shape=(sds((t, d), F32), sds(w.shape, BF)),
        in_specs=vmem(14),
        out_specs=tuple(vmem(2)),
        scratch_shapes=[
            pltpu.VMEM((t, QW), BF),
            pltpu.VMEM((t, QKV), BF),
            pltpu.VMEM((t, d), F32),
            pltpu.VMEM((d, t), BF),
        ],
        compiler_params=pltpu.CompilerParams(vmem_limit_bytes=VMEM_LIMIT),
        cost_estimate=pl.CostEstimate(flops=4 * t * d * 4096, bytes_accessed=w.size * 4, transcendentals=0),
    )(gy, h, x, w, qkv, p, o, b, wrt, back, dg, rt, cos, sin)


def one_hot(pos_row, cap):
    return jnp.where(iota((cap, pos_row.shape[1]), 0) == pos_row, 1.0, 0.0)


def all_hots(pos, per, cap):
    return jnp.concatenate([one_hot(pos[j : j + 1], cap) for j in range(per)], axis=0)


def slots_of(rt, first, per):
    t = rt.shape[1]
    experts = iota((16, t), 0)
    mine = jnp.where(experts < per, experts + first, -1)
    chosen = mine == rt[0:1]
    for k in range(1, rt.shape[0]):
        chosen = chosen | (mine == rt[k : k + 1])
    earlier = jnp.where(iota((t, t), 0) < iota((t, t), 1), 1.0, 0.0).astype(BF)
    before = dot(jnp.where(chosen, 1.0, 0.0).astype(BF), earlier)
    return jnp.where(chosen, before.astype(jnp.int32), -1)[0:8]


def streamed(count, copies, body):
    for c in copies(0, 0):
        c.start()

    def step(b, carry):
        slot = lax.rem(b, 2)

        @pl.when(b + 1 < count)
        def _():
            for c in copies(b + 1, lax.rem(b + 1, 2)):
                c.start()

        for c in copies(b, slot):
            c.wait()
        body(b, slot)
        return carry

    lax.fori_loop(0, count, step, 0)


def combine(count, per, cap, pos_ref, rows_ref, out_hbm, obuf, osem):
    def copy(b, slot):
        return pltpu.make_async_copy(obuf.at[slot], out_hbm.at[b], osem.at[slot])

    def step(b, carry):
        slot = lax.rem(b, 2)

        @pl.when(b >= 2)
        def _():
            copy(b - 2, slot).wait()

        back = jnp.transpose(all_hots(pos_ref[b], per, cap)).astype(BF)
        at = pl.ds(pl.multiple_of(b * cap, cap), cap)
        rows = jnp.concatenate([rows_ref[j, at, :] for j in range(per)], axis=0)
        obuf[slot] = dot(back, rows).astype(BF)
        copy(b, slot).start()
        return carry

    lax.fori_loop(0, count, step, 0)
    copy(count - 2, (count - 2) % 2).wait()
    copy(count - 1, (count - 1) % 2).wait()


def chunk_gates(c, j, chunk, cap, pos_ref, gate_ref):
    hots, gates = [], []
    for bb in range(chunk // cap):
        b = c * (chunk // cap) + bb
        hot = one_hot(pos_ref[b, pl.ds(j, 1), :], cap)
        hots.append(hot)
        gates.append(jnp.sum(hot * gate_ref[b, pl.ds(j, 1), :], axis=1, keepdims=True))
    return hots, jnp.concatenate(gates, axis=0)


def experts_fwd_kernel(
    layer, e_pad, cap, rt_ref, wrt_ref, wg_ref, wu_ref, wd_ref, b_hbm,
    gp_ref, up_ref, pos_ref, gate_ref, out_hbm, x_scr, y_scr, all_gates, bbuf, obuf, bsem, osem,
):
    per, rows, d = x_scr.shape
    count = rt_ref.shape[0]
    chunk = 256
    j = pl.program_id(0)
    first = lax.axis_index("expert") * per

    @pl.when(lax.axis_index("section") == layer)
    def _():
        @pl.when(j == 0)
        def _():
            def prepare(b, slot):
                rt = rt_ref[b]
                block = bbuf[slot]
                pos = slots_of(rt, first, per)
                pos_ref[b] = pos
                all_gates[...] = gates_of(rt, wrt_ref, block, e_pad)
                gate_ref[b] = jnp.concatenate(
                    [all_gates[pl.ds(first + k, 1), :] for k in range(per)] + [jnp.zeros((8 - per, rt.shape[1]), F32)], axis=0
                )
                x = dot(all_hots(pos, per, cap).astype(BF), block).astype(BF)
                at = pl.ds(pl.multiple_of(b * cap, cap), cap)
                for k in range(per):
                    x_scr[k, at, :] = x[k * cap : (k + 1) * cap]

            streamed(count, lambda b, slot: [pltpu.make_async_copy(b_hbm.at[b], bbuf.at[slot], bsem.at[slot])], prepare)

        def part(c, carry):
            at = pl.ds(pl.multiple_of(c * chunk, chunk), chunk)
            x = x_scr[j, at, :]
            gp = dot(x, wg_ref[0])
            up = dot(x, wu_ref[0])
            gp_ref[0, at, :] = gp
            up_ref[0, at, :] = up
            hid = (gp / (1.0 + jnp.exp(-gp)) * up).astype(BF)
            _, gate = chunk_gates(c, j, chunk, cap, pos_ref, gate_ref)
            y_scr[j, at, :] = (dot(hid, wd_ref[0]) * gate).astype(BF)
            return carry

        lax.fori_loop(0, rows // chunk, part, 0)

        @pl.when(j == per - 1)
        def _():
            combine(count, per, cap, pos_ref, y_scr, out_hbm, obuf, osem)


def any_spec():
    return pl.BlockSpec(memory_space=pl.ANY)


def fixed(shape):
    return pl.BlockSpec(shape, lambda j: (0,) * len(shape))


def experts_fwd(layer, e_pad, cap, rt, wrt, wg, wu, wd, blocks):
    count, t, d = blocks.shape
    per, _, f = wg.shape
    rows = count * cap
    sds = jax.ShapeDtypeStruct
    return pl.pallas_call(
        functools.partial(experts_fwd_kernel, layer, e_pad, cap),
        grid=(per,),
        out_shape=(
            sds((per, rows, f), F32),
            sds((per, rows, f), F32),
            sds((count, 8, t), jnp.int32),
            sds((count, 8, t), F32),
            sds((count, t, d), BF),
        ),
        in_specs=[
            fixed(rt.shape),
            fixed(wrt.shape),
            pl.BlockSpec((1, d, f), lambda j: (j, 0, 0)),
            pl.BlockSpec((1, d, f), lambda j: (j, 0, 0)),
            pl.BlockSpec((1, f, d), lambda j: (j, 0, 0)),
            any_spec(),
        ],
        out_specs=(
            pl.BlockSpec((1, rows, f), lambda j: (j, 0, 0)),
            pl.BlockSpec((1, rows, f), lambda j: (j, 0, 0)),
            fixed((count, 8, t)),
            fixed((count, 8, t)),
            any_spec(),
        ),
        scratch_shapes=[
            pltpu.VMEM((per, rows, d), BF),
            pltpu.VMEM((per, rows, d), BF),
            pltpu.VMEM((e_pad, t), F32),
            pltpu.VMEM((2, t, d), BF),
            pltpu.VMEM((2, t, d), BF),
            pltpu.SemaphoreType.DMA((2,)),
            pltpu.SemaphoreType.DMA((2,)),
        ],
        compiler_params=pltpu.CompilerParams(vmem_limit_bytes=VMEM_LIMIT),
        cost_estimate=pl.CostEstimate(flops=6 * per * rows * d * f, bytes_accessed=6 * per * d * f, transcendentals=per * rows * f),
    )(rt, wrt, wg, wu, wd, blocks)


def experts_bwd_kernel(
    layer, cap, pos_ref, gate_ref, wg_ref, wu_ref, wd_ref, gp_ref, up_ref, b_hbm, gy_hbm,
    even_ref, odd_ref, evend_ref, oddd_ref, dg_ref, out_hbm, x_scr, y_scr, dgp_scr, dup_scr, hid_scr, bbuf, gbuf, obuf, bsem, gsem, osem,
):
    per, rows, d = x_scr.shape
    count = pos_ref.shape[0]
    parts = even_ref.shape[0]
    piece = even_ref.shape[3]
    chunk = 256
    j = pl.program_id(0)

    @pl.when(lax.axis_index("section") == layer)
    def _():
        @pl.when(j == 0)
        def _():
            def prepare(b, slot):
                hots = all_hots(pos_ref[b], per, cap).astype(BF)
                x = dot(hots, bbuf[slot]).astype(BF)
                y = dot(hots, gbuf[slot]).astype(BF)
                at = pl.ds(pl.multiple_of(b * cap, cap), cap)
                for k in range(per):
                    x_scr[k, at, :] = x[k * cap : (k + 1) * cap]
                    y_scr[k, at, :] = y[k * cap : (k + 1) * cap]

            streamed(
                count,
                lambda b, slot: [
                    pltpu.make_async_copy(b_hbm.at[b], bbuf.at[slot], bsem.at[slot]),
                    pltpu.make_async_copy(gy_hbm.at[b], gbuf.at[slot], gsem.at[slot]),
                ],
                prepare,
            )
            dg_ref[...] = jnp.zeros_like(dg_ref)

        def part(c, carry):
            at = pl.ds(pl.multiple_of(c * chunk, chunk), chunk)
            raw = dot(y_scr[j, at, :], wd_ref[0], 1, 1)
            gp, up = gp_ref[0, at, :], up_ref[0, at, :]
            sg = 1.0 / (1.0 + jnp.exp(-gp))
            silu = gp * sg
            hid = silu * up
            hots, gate = chunk_gates(c, j, chunk, cap, pos_ref, gate_ref)
            dgate = jnp.sum(hid.astype(BF).astype(F32) * raw, axis=1, keepdims=True)
            for bb in range(chunk // cap):
                b = c * (chunk // cap) + bb
                dg_ref[b, pl.ds(j, 1), :] = jnp.sum(hots[bb] * dgate[bb * cap : (bb + 1) * cap], axis=0, keepdims=True)
            dh = raw * gate
            dgp_scr[at, :] = (dh * up * sg * (1.0 + gp * (1.0 - sg))).astype(BF)
            dup_scr[at, :] = (dh * silu).astype(BF)
            hid_scr[at, :] = (hid * gate).astype(BF)
            return carry

        lax.fori_loop(0, rows // chunk, part, 0)

        odd = lax.rem(lax.axis_index("group"), 2)
        place = lax.axis_index("group") // 2
        for q in range(parts):
            cols = slice(2 * q * piece, 2 * (q + 1) * piece)
            at = lax.bitwise_xor(place, q)
            for n, right in ((0, dgp_scr), (1, dup_scr)):
                full = dot(x_scr[j, :, cols], right[...], 0, 0).astype(BF)
                for parity, (low, high) in ((0, (even_ref, odd_ref)), (1, (odd_ref, even_ref))):

                    @pl.when(odd == parity)
                    def _(low=low, high=high):
                        low[at, n, 0] = full[:piece]
                        high[at, n, 0] = full[piece:]

            full = dot(hid_scr[...], y_scr[j, :, cols], 0, 0).astype(BF)
            for parity, (low, high) in ((0, (evend_ref, oddd_ref)), (1, (oddd_ref, evend_ref))):

                @pl.when(odd == parity)
                def _(low=low, high=high):
                    low[at, 0] = full[:, :piece]
                    high[at, 0] = full[:, piece:]

        def rows_back(c, carry):
            at = pl.ds(pl.multiple_of(c * chunk, chunk), chunk)
            y_scr[j, at, :] = (dot(dgp_scr[at, :], wg_ref[0], 1, 1) + dot(dup_scr[at, :], wu_ref[0], 1, 1)).astype(BF)
            return carry

        lax.fori_loop(0, rows // chunk, rows_back, 0)

        @pl.when(j == per - 1)
        def _():
            combine(count, per, cap, pos_ref, y_scr, out_hbm, obuf, osem)


def experts_bwd(layer, cap, groups, pos, gate, wg, wu, wd, gp, up, blocks, grads):
    count, t, d = blocks.shape
    per, _, f = wg.shape
    rows = count * cap
    sds = jax.ShapeDtypeStruct
    return pl.pallas_call(
        functools.partial(experts_bwd_kernel, layer, cap),
        grid=(per,),
        out_shape=(
            sds((groups // 2, 2, per, d // groups, f), BF),
            sds((groups // 2, 2, per, d // groups, f), BF),
            sds((groups // 2, per, f, d // groups), BF),
            sds((groups // 2, per, f, d // groups), BF),
            sds((count, 8, t), F32),
            sds((count, t, d), BF),
        ),
        in_specs=[
            fixed(pos.shape),
            fixed(gate.shape),
            pl.BlockSpec((1, d, f), lambda j: (j, 0, 0)),
            pl.BlockSpec((1, d, f), lambda j: (j, 0, 0)),
            pl.BlockSpec((1, f, d), lambda j: (j, 0, 0)),
            pl.BlockSpec((1, rows, f), lambda j: (j, 0, 0)),
            pl.BlockSpec((1, rows, f), lambda j: (j, 0, 0)),
            any_spec(),
            any_spec(),
        ],
        out_specs=(
            pl.BlockSpec((groups // 2, 2, 1, d // groups, f), lambda j: (0, 0, j, 0, 0)),
            pl.BlockSpec((groups // 2, 2, 1, d // groups, f), lambda j: (0, 0, j, 0, 0)),
            pl.BlockSpec((groups // 2, 1, f, d // groups), lambda j: (0, j, 0, 0)),
            pl.BlockSpec((groups // 2, 1, f, d // groups), lambda j: (0, j, 0, 0)),
            fixed((count, 8, t)),
            any_spec(),
        ),
        scratch_shapes=[
            pltpu.VMEM((per, rows, d), BF),
            pltpu.VMEM((per, rows, d), BF),
            pltpu.VMEM((rows, f), BF),
            pltpu.VMEM((rows, f), BF),
            pltpu.VMEM((rows, f), BF),
            pltpu.VMEM((2, t, d), BF),
            pltpu.VMEM((2, t, d), BF),
            pltpu.VMEM((2, t, d), BF),
            pltpu.SemaphoreType.DMA((2,)),
            pltpu.SemaphoreType.DMA((2,)),
            pltpu.SemaphoreType.DMA((2,)),
        ],
        compiler_params=pltpu.CompilerParams(vmem_limit_bytes=VMEM_LIMIT),
        cost_estimate=pl.CostEstimate(flops=12 * per * rows * d * f, bytes_accessed=12 * per * d * f, transcendentals=per * rows * f),
    )(pos, gate, wg, wu, wd, gp, up, blocks, grads)


def meet(n, with_cross):
    s, z = lax.axis_index("section"), lax.axis_index("expert")
    barrier = pltpu.get_barrier_semaphore()
    for k in range(1, n):
        pl.semaphore_signal(barrier, inc=1, device_id={"expert": lax.rem(z + k, n)}, device_id_type=MESH)
    for k in range(n if with_cross else 1):
        pl.semaphore_signal(
            barrier, inc=1, device_id={"section": 1 - s, "expert": lax.rem(z + k, n)}, device_id_type=MESH
        )
    pl.semaphore_wait(barrier, 2 * n - 1 if with_cross else n)


def spread_kernel(layer, n, x_ref, o_ref, send_sem, recv_sem, local_sem):
    s, z = lax.axis_index("section"), lax.axis_index("expert")
    meet(n, True)

    def copy(k, source_section):
        return pltpu.make_async_remote_copy(
            src_ref=x_ref,
            dst_ref=o_ref.at[source_section, z],
            send_sem=send_sem.at[k],
            recv_sem=recv_sem.at[source_section, k],
            device_id={"section": layer, "expert": lax.rem(z + k, n)},
            device_id_type=MESH,
        )

    order = sorted(range(n), key=lambda k: (k == 0, abs(k - n // 2)))

    @pl.when(s == layer)
    def _():
        own = pltpu.make_async_copy(x_ref, o_ref.at[layer, z], local_sem)
        own.start()
        sends = [copy(k, layer) for k in order if k]
        for c in sends:
            c.start()
        own.wait()
        for c in sends:
            c.wait()
        for k in range(n):
            copy(k, 1 - layer).wait_recv()

    @pl.when(s != layer)
    def _():
        sends = [copy(k, 1 - layer) for k in order]
        for c in sends:
            c.start()
        for c in sends:
            c.wait_send()


def spread(layer, cid, x):
    n = lax.axis_size("expert")
    return pl.pallas_call(
        functools.partial(spread_kernel, layer, n),
        out_shape=jax.ShapeDtypeStruct((2, n) + x.shape, x.dtype),
        in_specs=[any_spec()],
        out_specs=any_spec(),
        scratch_shapes=[
            pltpu.SemaphoreType.DMA((n,)),
            pltpu.SemaphoreType.DMA((2, n)),
            pltpu.SemaphoreType.DMA,
        ],
        compiler_params=pltpu.CompilerParams(collective_id=cid, has_side_effects=True),
    )(x)


def collect_kernel(layer, n, arrays, *refs):
    srcs, outs, relays = refs[:arrays], refs[arrays : 2 * arrays], refs[2 * arrays : 3 * arrays]
    relay_send, relay_recv, send_sem, recv_sem, local_sem = refs[3 * arrays :]
    s, z = lax.axis_index("section"), lax.axis_index("expert")
    meet(n, False)

    def hop(a, to):
        return pltpu.make_async_remote_copy(
            src_ref=srcs[a].at[1 - layer, to],
            dst_ref=relays[a].at[to],
            send_sem=relay_send.at[a, to],
            recv_sem=relay_recv.at[a, to],
            device_id={"section": 1 - s},
            device_id_type=MESH,
        )

    def give(a, source, k):
        return pltpu.make_async_remote_copy(
            src_ref=source,
            dst_ref=outs[a].at[z],
            send_sem=send_sem.at[a, k],
            recv_sem=recv_sem.at[a, k],
            device_id={"expert": lax.rem(z + k, n)},
            device_id_type=MESH,
        )

    order = sorted(range(n), key=lambda k: (k == 0, abs(k - n // 2)))

    @pl.when(s == layer)
    def _():
        for k in order:
            for a in range(arrays):
                hop(a, lax.rem(z + k, n)).start()
        for k in order:
            for a in range(arrays):
                if k:
                    give(a, srcs[a].at[layer, lax.rem(z + k, n)], k).start()
                else:
                    pltpu.make_async_copy(srcs[a].at[layer, z], outs[a].at[z], local_sem.at[a]).start()
        for k in order:
            for a in range(arrays):
                hop(a, lax.rem(z + k, n)).wait_send()

    @pl.when(s != layer)
    def _():
        for k in order:
            to = lax.rem(z + k, n)
            for a in range(arrays):
                hop(a, to).wait_recv()
                if k:
                    give(a, relays[a].at[to], k).start()
                else:
                    pltpu.make_async_copy(relays[a].at[z], outs[a].at[z], local_sem.at[a]).start()

    for a in range(arrays):
        for k in order:
            if k:
                give(a, relays[a].at[lax.rem(z + k, n)], k).wait()
            else:
                pltpu.make_async_copy(relays[a].at[z], outs[a].at[z], local_sem.at[a]).wait()


def collect(layer, cid, *arrays):
    n = lax.axis_size("expert")
    count = len(arrays)
    return pl.pallas_call(
        functools.partial(collect_kernel, layer, n, count),
        out_shape=tuple(jax.ShapeDtypeStruct(a.shape[1:], a.dtype) for a in arrays),
        in_specs=[any_spec()] * count,
        out_specs=tuple([any_spec()] * count),
        scratch_shapes=[pltpu.VMEM(a.shape[1:], a.dtype) for a in arrays]
        + [
            pltpu.SemaphoreType.DMA((count, n)),
            pltpu.SemaphoreType.DMA((count, n)),
            pltpu.SemaphoreType.DMA((count, n)),
            pltpu.SemaphoreType.DMA((count, n)),
            pltpu.SemaphoreType.DMA((count,)),
        ],
        compiler_params=pltpu.CompilerParams(collective_id=cid, has_side_effects=True),
    )(*arrays)


def top_bit(q):
    return q.bit_length() - 1


def finish_kernel(
    n, dd0, dd1, egu0, ogu0, ed0, od0, egu1, ogu1, ed1, od1,
    dense_out, gate_out, up_out, down_out,
    core_gu, core_dn, hop_gu, hop_dn, core_dd, hop_y, hop_z, hop_x, dd_buf, gu_buf, dn_buf, gu_f32, dn_f32,
    s_core_gu, r_core_gu, s_core_dn, r_core_dn, s_hop_gu, r_hop_gu, s_hop_dn, r_hop_dn,
    s_core_dd, r_core_dd, s_y, r_y, s_z, r_z, s_x, r_x, l_dd, l_gu, l_dn, o_gu, o_dn,
):
    s, g, z = lax.axis_index("section"), lax.axis_index("group"), lax.axis_index("expert")
    pairs, cgu = core_gu.shape[:2]
    cdn = core_dn.shape[1]
    levels = top_bit(pairs)
    units = pairs * n
    remote = functools.partial(pltpu.make_async_remote_copy, device_id_type=MESH)
    twin = {"group": lax.bitwise_xor(g, 1)}
    other = {"section": 1 - s}

    def across(k):
        return {"group": lax.bitwise_xor(g, 2 << k)}

    barrier = pltpu.get_barrier_semaphore()
    peers = [twin, other] + [across(k) for k in range(levels)] + [{"expert": lax.rem(z + k, n)} for k in range(1, n)]
    for peer in peers:
        pl.semaphore_signal(barrier, inc=1, device_id=peer, device_id_type=MESH)
    pl.semaphore_wait(barrier, len(peers))

    def by_section(action):
        @pl.when(s == 0)
        def _():
            action(dd0, dd1, egu0, ogu0, ed0, od0)

        @pl.when(s != 0)
        def _():
            action(dd1, dd0, egu1, ogu1, ed1, od1)

    def unit(i):
        return pairs - 1 - i // n, lax.rem(z + 1 + lax.rem(i, n), n)

    def shard(i, core):
        q, place = unit(i)
        return (lax.bitwise_xor(g // 2, q) * 2 + core) * n + place

    core = lax.rem(g, 2)

    def core_dd_copy(kind, i, source):
        return remote(
            src_ref=source.at[shard(i, 1 - core)],
            dst_ref=core_dd.at[kind, i],
            send_sem=s_core_dd.at[kind, i],
            recv_sem=r_core_dd.at[kind, i],
            device_id=twin,
        )

    def core_chunk(source, dest, ssem, rsem, q, c):
        return remote(
            src_ref=source.at[q, c], dst_ref=dest.at[q, c], send_sem=ssem.at[q, c], recv_sem=rsem.at[q, c], device_id=twin
        )

    def core_gu_copy(source, q, c):
        return core_chunk(source, core_gu, s_core_gu, r_core_gu, q, c)

    def core_dn_copy(source, q, c):
        return core_chunk(source, core_dn, s_core_dn, r_core_dn, q, c)

    def send_all(own, away, egu, ogu, ed, od):
        @pl.loop(0, units)
        def _(i):
            core_dd_copy(0, i, away).start()

            @pl.when(i < cgu)
            def _():
                core_gu_copy(ogu, pairs - 1, i).start()

            @pl.when(i < cdn)
            def _():
                core_dn_copy(od, pairs - 1, i).start()

        for i in range(units, max(cgu, cdn)):
            if i < cgu:
                core_gu_copy(ogu, pairs - 1, i).start()
            if i < cdn:
                core_dn_copy(od, pairs - 1, i).start()

        @pl.loop(0, units)
        def _(i):
            core_dd_copy(1, i, own).start()

        for q in reversed(range(pairs - 1)):

            @pl.loop(0, cgu)
            def _(c):
                core_gu_copy(ogu, q, c).start()

            @pl.loop(0, cdn)
            def _(c):
                core_dn_copy(od, q, c).start()

    by_section(send_all)

    def load(buf, sem, slot, source):
        return pltpu.make_async_copy(source, buf.at[slot], sem.at[slot])

    def dd_load(i, slot, source):
        return load(dd_buf, l_dd, slot, source.at[shard(i, core)])

    def hop(dest, ssem, rsem, source, k, q, c):
        return remote(
            src_ref=source.at[q, c],
            dst_ref=dest.at[k, q - (1 << k), c],
            send_sem=ssem.at[k, q - (1 << k), c],
            recv_sem=rsem.at[k, q - (1 << k), c],
            device_id=across(k),
        )

    def gu_hop(k, q, c):
        return hop(hop_gu, s_hop_gu, r_hop_gu, core_gu, k, q, c)

    def dn_hop(k, q, c):
        return hop(hop_dn, s_hop_dn, r_hop_dn, core_dn, k, q, c)

    def y_copy(i):
        return remote(src_ref=core_dd.at[0, i], dst_ref=hop_y.at[i], send_sem=s_y.at[i], recv_sem=r_y.at[i], device_id=other)

    def z_copy(q, k, i):
        return remote(
            src_ref=core_dd.at[1, i],
            dst_ref=hop_z.at[k - 1, q],
            send_sem=s_z.at[k - 1, q],
            recv_sem=r_z.at[k - 1, q],
            device_id={"expert": lax.rem(z + k, n)},
        )

    def x_copy(k, q, i):
        return remote(
            src_ref=core_dd.at[1, i],
            dst_ref=hop_x.at[k, q - (1 << k)],
            send_sem=s_x.at[k, q - (1 << k)],
            recv_sem=r_x.at[k, q - (1 << k)],
            device_id=across(k),
        )

    def chunk_start(i, slot, q, egu, ed):
        @pl.when(i < cgu)
        def _():
            load(gu_buf, l_gu, slot, egu.at[q, i]).start()

        @pl.when(i < cdn)
        def _():
            load(dn_buf, l_dn, slot, ed.at[q, i]).start()

    def expert_sum(hops, rsem, dest, core_r, buf, sem, slot, even, q, c, hop_copy):
        load(buf, sem, slot, even.at[q, c]).wait()
        core_r(q, c).wait_recv()
        total = buf[slot].astype(F32) + dest[q, c].astype(F32)
        for k in range(top_bit(q) + 1 if q else 0, levels):
            hop_copy(k, q + (1 << k), c).wait_recv()
            total = total + hops[k, q, c].astype(F32)
        return total

    def gu_sum(slot, q, c):
        return expert_sum(hop_gu, r_hop_gu, core_gu, functools.partial(core_gu_copy, ogu0), gu_buf, l_gu, slot, egu0, q, c, gu_hop)

    def dn_sum(slot, q, c):
        return expert_sum(hop_dn, r_hop_dn, core_dn, functools.partial(core_dn_copy, od0), dn_buf, l_dn, slot, ed0, q, c, dn_hop)

    def stepped(count, start, body):
        start(0, 0)

        def step(i, carry):
            @pl.when(i + 1 < count)
            def _():
                start(i + 1, lax.rem(i + 1, 2))

            body(i, lax.rem(i, 2))
            return carry

        lax.fori_loop(0, count, step, 0)

    for q in reversed(range(1, pairs)):
        dense_too = q == pairs - 1
        steps = max(units, cgu, cdn) if dense_too else max(cgu, cdn)

        def start(i, slot):
            def go(own, away, egu, ogu, ed, od):
                if dense_too:

                    @pl.when(i < units)
                    def _():
                        dd_load(i, slot, away).start()

                chunk_start(i, slot, q, egu, ed)

            by_section(go)

        def body(i, slot):
            if dense_too:

                @pl.when(i < units)
                def _():
                    dd_load(i, slot, dd0).wait()
                    core_dd_copy(0, i, dd0).wait_recv()
                    core_dd[0, i] = core_dd[0, i] + dd_buf[slot]
                    y_copy(i).start()

            @pl.when(i < cgu)
            def _():
                core_gu[q, i] = gu_sum(slot, q, i).astype(BF)
                gu_hop(top_bit(q), q, i).start()

            @pl.when(i < cdn)
            def _():
                core_dn[q, i] = dn_sum(slot, q, i).astype(BF)
                dn_hop(top_bit(q), q, i).start()

        stepped(steps, start, body)

    def gu_out_copy(c, slot, to=gate_out):
        return pltpu.make_async_copy(gu_f32.at[slot], to.at[lax.rem(c, cgu // 2)], o_gu.at[slot])

    def dn_out_copy(c, slot):
        return pltpu.make_async_copy(dn_f32.at[slot], down_out.at[c], o_dn.at[slot])

    def dense_sum(q):
        i = (pairs - 1 - q) * n + n - 1
        total = core_dd[1, i].astype(F32)
        for k in range(1, n):
            z_copy(q, k, i).wait_recv()
            total = total + hop_z[k - 1, q].astype(F32)
        for k in range(top_bit(q) + 1 if q else 0, levels):
            x_copy(k, q + (1 << k), i).wait_recv()
            total = total + hop_x[k, q].astype(F32)
        return i, total

    def pass_on(q):
        i, total = dense_sum(q)
        core_dd[1, i] = total.astype(BF)
        x_copy(top_bit(q), q, i).start()

    steps = max(units, cgu, cdn)

    def start(i, slot):
        def go(own, away, egu, ogu, ed, od):
            @pl.when(i < units)
            def _():
                dd_load(i, slot, own).start()

            chunk_start(i, slot, 0, egu, ed)

        by_section(go)

    def body(i, slot):
        @pl.when(i < units)
        def _():
            dd_load(i, slot, dd0).wait()
            core_dd_copy(1, i, dd0).wait_recv()
            y_copy(i).wait_recv()
            core_dd[1, i] = (core_dd[1, i].astype(F32) + dd_buf[slot].astype(F32) + hop_y[i].astype(F32)).astype(BF)
            q, _ = unit(i)
            k = lax.rem(i, n) + 1

            @pl.when(k < n)
            def _():
                z_copy(q, k, i).start()

        for q in range(1, pairs):

            @pl.when(i == (pairs - q) * n + min(2, n - 1))
            def _():
                pass_on(q)

        @pl.when(i < cgu)
        def _():
            @pl.when(i >= 2)
            def _():
                gu_out_copy(i - 2, slot).wait()

            gu_f32[slot] = gu_sum(slot, 0, i)

            @pl.when(i < cgu // 2)
            def _():
                gu_out_copy(i, slot).start()

            @pl.when(i >= cgu // 2)
            def _():
                gu_out_copy(i, slot, up_out).start()

        @pl.when(i < cdn)
        def _():
            @pl.when(i >= 2)
            def _():
                dn_out_copy(i - 2, slot).wait()

            dn_f32[slot] = dn_sum(slot, 0, i)
            dn_out_copy(i, slot).start()

    stepped(steps, start, body)
    _, total = dense_sum(0)
    dense_out[...] = total
    for c in (cgu - 2, cgu - 1):
        gu_out_copy(c, c % 2).wait()
    for c in (cdn - 2, cdn - 1):
        dn_out_copy(c, c % 2).wait()

    @pl.loop(0, units)
    def _(i):
        core_dd_copy(0, i, dd0).wait_send()
        core_dd_copy(1, i, dd0).wait_send()
        y_copy(i).wait_send()
        q, _ = unit(i)
        k = lax.rem(i, n) + 1

        @pl.when(k < n)
        def _():
            z_copy(q, k, i).wait_send()

    for q in range(pairs):
        if q:
            x_copy(top_bit(q), q, (pairs - 1 - q) * n + n - 1).wait_send()

        @pl.loop(0, cgu)
        def _(c):
            core_gu_copy(ogu0, q, c).wait_send()
            if q:
                gu_hop(top_bit(q), q, c).wait_send()

        @pl.loop(0, cdn)
        def _(c):
            core_dn_copy(od0, q, c).wait_send()
            if q:
                dn_hop(top_bit(q), q, c).wait_send()


def finish(cid, dd0, dd1, experts0, experts1):
    n, groups = lax.axis_size("expert"), lax.axis_size("group")
    pairs, levels = groups // 2, top_bit(groups // 2)
    width = dd0.shape[1]
    rows = dd0.shape[0] // (groups * n)
    dd0, dd1 = (v.reshape(groups * n, rows, width) for v in (dd0, dd1))

    def chunked(arrays):
        gu_even, gu_odd, dn_even, dn_odd = arrays
        flat = (pairs, -1) + gu_even.shape[3:]
        return gu_even.reshape(flat), gu_odd.reshape(flat), dn_even, dn_odd

    experts0, experts1 = chunked(experts0), chunked(experts1)
    gu, dn = experts0[0].shape[1:], experts0[2].shape[1:]
    units = pairs * n
    dma = pltpu.SemaphoreType.DMA
    sds = jax.ShapeDtypeStruct
    half = max(1, pairs // 2)

    def both(shape):
        return [dma(shape), dma(shape)]

    return pl.pallas_call(
        functools.partial(finish_kernel, n),
        out_shape=(sds((rows, width), F32), sds((gu[0] // 2,) + gu[1:], F32), sds((gu[0] // 2,) + gu[1:], F32), sds(dn, F32)),
        in_specs=[any_spec()] * 10,
        out_specs=(pl.BlockSpec(memory_space=pltpu.VMEM), any_spec(), any_spec(), any_spec()),
        scratch_shapes=[
            pltpu.VMEM((pairs,) + gu, BF),
            pltpu.VMEM((pairs,) + dn, BF),
            pltpu.VMEM((levels, half) + gu, BF),
            pltpu.VMEM((levels, half) + dn, BF),
            pltpu.VMEM((2, units, rows, width), BF),
            pltpu.VMEM((units, rows, width), BF),
            pltpu.VMEM((n - 1, pairs, rows, width), BF),
            pltpu.VMEM((levels, half, rows, width), BF),
            pltpu.VMEM((2, rows, width), BF),
            pltpu.VMEM((2,) + gu[1:], BF),
            pltpu.VMEM((2,) + dn[1:], BF),
            pltpu.VMEM((2,) + gu[1:], F32),
            pltpu.VMEM((2,) + dn[1:], F32),
        ]
        + both((pairs, gu[0]))
        + both((pairs, dn[0]))
        + both((levels, half, gu[0]))
        + both((levels, half, dn[0]))
        + both((2, units))
        + both((units,))
        + both((n - 1, pairs))
        + both((levels, half))
        + [dma((2,))] * 5,
        compiler_params=pltpu.CompilerParams(collective_id=cid, has_side_effects=True, vmem_limit_bytes=VMEM_LIMIT),
    )(dd0, dd1, *experts0, *experts1)


def swap_sections(value):
    return lax.ppermute(value, "section", [(0, 1), (1, 0)])


def rope_tables(t):
    half = HEAD_SIZE // 2
    frequency = THETA ** (-jnp.arange(half, dtype=F32) * 2.0 / HEAD_SIZE)
    angles = jnp.arange(t, dtype=F32)[:, None] * frequency[None, :]
    reps = LANES // half
    return jnp.tile(jnp.cos(angles), (1, reps)), jnp.tile(jnp.sin(angles), (1, reps))


def local(
    inputs, cotangent, segment_ids, live_first, routes, gain_attn, gain_moe,
    w_query, key_weight, value_weight, w_out, w_router, w_gate, w_up, w_down,
):
    s = lax.axis_index("section")
    n = lax.axis_size("expert")
    groups = lax.axis_size("group")
    t, d = inputs.shape[2:]
    top = routes.shape[-1]
    per = w_gate.shape[1]
    experts = per * n
    e_pad = -(-experts // 16) * 16
    cap = t * top * 5 // (4 * experts)
    wg, wu, wd = w_gate[0], w_up[0], w_down[0]
    at_zero = s == 0

    shard = w_query.shape[1]
    aux = jnp.concatenate(
        [
            w_router[0],
            jnp.zeros((shard, GAIN_MOE_ROW - experts), BF),
            gain_moe[0][:, None],
            gain_attn[0][:, None],
        ],
        axis=1,
    )
    packed = jnp.concatenate([w_query[0], key_weight[0], value_weight[0], w_out[0].T, aux], axis=1)
    other = swap_sections(packed)
    shards = (jnp.where(at_zero, packed, other), jnp.where(at_zero, other, packed))
    first_weights = lax.all_gather(shards[0], ("group", "expert"), axis=0, tiled=True)

    x0 = lax.dynamic_index_in_dim(inputs[:, 0], s, 0, keepdims=False)
    cot = lax.dynamic_index_in_dim(cotangent[:, 0], s, 0, keepdims=False)
    seg = lax.dynamic_index_in_dim(segment_ids[:, 0], s, 0, keepdims=False)
    live = lax.dynamic_index_in_dim(live_first[:, 0], s, 0, keepdims=False)
    meta = jnp.stack([seg, jnp.repeat(live, BLK)], axis=1)
    meta = jnp.pad(meta, ((0, 0), (0, LANES - 2)))
    segr = jnp.broadcast_to(seg[None, :], (8, t))
    cos, sin = rope_tables(t)

    rt = jnp.swapaxes(routes[0, :, 0], 1, 2)
    rt_mine = lax.dynamic_index_in_dim(rt, s, 0, keepdims=False)
    rt_theirs = swap_sections(lax.dynamic_index_in_dim(rt, 1 - s, 0, keepdims=False))
    rt_tokens = (jnp.where(at_zero, rt_mine, rt_theirs), jnp.where(at_zero, rt_theirs, rt_mine))
    rt_all = lax.all_gather(rt, "expert", axis=1, tiled=False).reshape(2 * n, top, t)

    def flat(z):
        return z.reshape((2 * n,) + z.shape[2:])

    def paired(z):
        return z.reshape((2, n) + z.shape[1:])

    gy1 = flat(spread(1, 1, cot))

    qkv0, p0, o0, h0, b0, wrt0 = attn_fwd(x0, first_weights, cos, sin, meta, segr)
    second_weights = lax.all_gather(shards[1], ("group", "expert"), axis=0, tiled=True)
    b0_all = flat(spread(0, 2, b0))
    gp0, up0, pos0, gate0, part0 = experts_fwd(0, e_pad, cap, rt_all, wrt0, wg, wu, wd, b0_all)
    (back0,) = collect(0, 3, paired(part0))
    x1 = (h0 + jnp.sum(back0.astype(F32), axis=0)).astype(BF)

    qkv1, p1, o1, h1, b1, wrt1 = attn_fwd(x1, second_weights, cos, sin, meta, segr)
    b1_all = flat(spread(1, 4, b1))
    gp1, up1, pos1, gate1, part1 = experts_fwd(1, e_pad, cap, rt_all, wrt1, wg, wu, wd, b1_all)
    ge1, go1, de1, do1, dg1, dpart1 = experts_bwd(1, cap, groups, pos1, gate1, wg, wu, wd, gp1, up1, b1_all, gy1)
    dback1, dgate1 = collect(1, 5, paired(dpart1), paired(dg1))

    def gates_back(dg):
        dg = dg[:, :per].reshape(experts, t)
        return jnp.pad(dg, ((0, e_pad - experts), (0, 0)))

    dx1, dd1 = attn_bwd(cot, h1, x1, second_weights, qkv1, p1, o1, b1, wrt1, dback1, gates_back(dgate1), rt_tokens[1], cos, sin)
    gy0 = dx1.astype(BF)

    gy0_all = flat(spread(0, 6, gy0))
    gy0_all, part1 = lax.optimization_barrier((gy0_all, part1))
    crossed = lax.ppermute(paired(part1)[0], "section", [(1, 0)])
    ge0, go0, de0, do0, dg0, dpart0 = experts_bwd(0, cap, groups, pos0, gate0, wg, wu, wd, gp0, up0, b0_all, gy0_all)
    dback0, dgate0 = collect(0, 7, paired(dpart0), paired(dg0))
    dback0, part1, crossed = lax.optimization_barrier((dback0, part1, crossed))
    back1 = lax.all_to_all(jnp.where(at_zero, crossed, paired(part1)[1]), "expert", split_axis=0, concat_axis=0, tiled=True)
    y1 = (h1 + jnp.sum(back1.astype(F32), axis=0)).astype(BF)
    dx0, dd0 = attn_bwd(gy0, h0, x0, first_weights, qkv0, p0, o0, b0, wrt0, dback0, gates_back(dgate0), rt_tokens[0], cos, sin)

    dense, gate_grad, up_grad, down = finish(9, dd0, dd1, (ge0, go0, de0, do0), (ge1, go1, de1, do1))

    kept_out = jnp.where(at_zero, x1, y1)
    swapped_out = swap_sections(jnp.where(at_zero, y1, x1))
    layer_out = jnp.where(at_zero, jnp.stack([kept_out, swapped_out]), jnp.stack([swapped_out, kept_out]))
    kept_in = jnp.where(at_zero, dx0, dx1)
    swapped_in = swap_sections(jnp.where(at_zero, dx1, dx0))
    input_grad = jnp.where(at_zero, jnp.stack([kept_in, swapped_in]), jnp.stack([swapped_in, kept_in]))

    return (
        layer_out[None, :, None],
        input_grad[None, :, None],
        dense[:, QKV + QW + GAIN_ATTN_ROW][None],
        dense[:, QKV + QW + GAIN_MOE_ROW][None],
        dense[None, :, 0:QW],
        dense[None, :, QW : QW + KW],
        dense[None, :, QW + KW : QKV],
        dense[:, QKV : QKV + QW].T[None],
        dense[None, :, QKV + QW : QKV + QW + experts],
        gate_grad[None],
        up_grad[None],
        down[None],
    )


def solution(mesh):
    return jax.shard_map(
        local,
        mesh=mesh,
        in_specs=(
            P(None, ("group", "expert"), None, None),
            P(None, ("group", "expert"), None, None),
            P(None, ("group", "expert"), None),
            P(None, ("group", "expert"), None),
            P("section", None, ("group", "expert"), None, None),
            P("section", ("group", "expert")),
            P("section", ("group", "expert")),
            P("section", ("group", "expert"), None),
            P("section", ("group", "expert"), None),
            P("section", ("group", "expert"), None),
            P("section", None, ("group", "expert")),
            P("section", ("group", "expert"), None),
            P("section", "expert", None, None),
            P("section", "expert", None, None),
            P("section", "expert", None, None),
        ),
        out_specs=(
            P("section", None, ("group", "expert"), None, None),
            P("section", None, ("group", "expert"), None, None),
            P("section", ("group", "expert")),
            P("section", ("group", "expert")),
            P("section", ("group", "expert"), None),
            P("section", ("group", "expert"), None),
            P("section", ("group", "expert"), None),
            P("section", None, ("group", "expert")),
            P("section", ("group", "expert"), None),
            P("section", "expert", "group", None),
            P("section", "expert", "group", None),
            P("section", "expert", None, "group"),
        ),
        check_vma=False,
    )
```

```python
import functools

import jax
import jax.numpy as jnp
from jax import lax
from jax.experimental import pallas as pl
from jax.experimental.pallas import tpu as pltpu
from jax.sharding import PartitionSpec as P

QUERY_HEADS = 24
KEY_VALUE_HEADS = 8
HEAD_SIZE = 64
BLK = 64
EPS = 1e-06
THETA = 10000.0
NEG_FILL = -1e30
BF = jnp.bfloat16
F32 = jnp.float32
MESH = pl.DeviceIdType.MESH
LANES = 128
TILE = 512
QW = QUERY_HEADS * HEAD_SIZE
KW = KEY_VALUE_HEADS * HEAD_SIZE
QKV = QW + 2 * KW
GAIN_MOE_ROW = 126
GAIN_ATTN_ROW = 127
VMEM_LIMIT = 60 * 1024 * 1024
HEAD_PAIRS = KEY_VALUE_HEADS // 2
TILES_PER_PAIR = QUERY_HEADS // KEY_VALUE_HEADS


def dot(a, b, ca=1, cb=0):
    return lax.dot_general(a, b, (((ca,), (cb,)), ((), ())), preferred_element_type=F32)


def iota(shape, axis):
    return lax.broadcasted_iota(jnp.int32, shape, axis)


def rope(z, cos, sin, direction):
    width = z.shape[1]
    half = HEAD_SIZE // 2
    first = iota(z.shape, 1) % HEAD_SIZE < half
    partner = jnp.where(first, pltpu.roll(z, width - half, 1), pltpu.roll(z, half, 1))
    signed = jnp.where(first, -direction, direction) * partner
    reps = width // LANES
    return z * jnp.concatenate([cos] * reps, axis=1) + signed * jnp.concatenate([sin] * reps, axis=1)


def lane_masks(t):
    low = iota((t, LANES), 1) < HEAD_SIZE
    return low, jnp.logical_not(low)


def swapped(z):
    return pltpu.roll(z.astype(F32), HEAD_SIZE, 1).astype(BF)


def head_plan():
    return [(r, half, (2 * r + half) // TILES_PER_PAIR != half) for r in range(TILES_PER_PAIR) for half in range(2)]


def pick(z, half, masks):
    return jnp.where(masks[half], z, jnp.zeros_like(z))


def attn_fwd_kernel(x_ref, w_ref, cos_ref, sin_ref, meta_ref, segr_ref, qkv_ref, p_ref, o_ref, h_ref, b_ref, wrt_ref):
    t, d = x_ref.shape
    aux = jnp.transpose(w_ref[:, QKV + QW :].astype(F32))
    wrt_ref[...] = aux.astype(BF)
    gain_attn = aux[GAIN_ATTN_ROW : GAIN_ATTN_ROW + 1]
    gain_moe = aux[GAIN_MOE_ROW : GAIN_MOE_ROW + 1]
    x = x_ref[...].astype(F32)
    r1 = lax.rsqrt(jnp.mean(x * x, axis=1, keepdims=True) + EPS)
    a = (x * r1 * gain_attn).astype(BF)
    cos, sin = cos_ref[...], sin_ref[...]
    for n in range(QKV // TILE):
        cols = slice(n * TILE, (n + 1) * TILE)
        y = dot(a, w_ref[:, cols])
        if n * TILE < QW + KW:
            y = rope(y, cos, sin, 1.0)
        qkv_ref[:, cols] = y.astype(BF)
    i, j = iota((t, t), 0), iota((t, t), 1)
    allowed = (j <= i) & (meta_ref[:, 0:1] == segr_ref[0:1, :]) & (j // BLK >= meta_ref[:, 1:2])
    masks = lane_masks(t)

    def pair(m, carry):
        def lanes(base):
            return pl.ds(pl.multiple_of(base, LANES), LANES)

        kp = qkv_ref[:, lanes(QW + m * LANES)]
        vp = qkv_ref[:, lanes(QW + KW + m * LANES)]
        ks, vs = swapped(kp), swapped(vp)
        parts = {}
        for r, half, swap in head_plan():
            q = pick(qkv_ref[:, lanes((m * TILES_PER_PAIR + r) * LANES)], half, masks)
            s = dot(q, ks if swap else kp, 1, 1) * HEAD_SIZE ** (-0.5)
            s = jnp.where(allowed, s, NEG_FILL)
            e = jnp.exp(s - jnp.max(s, axis=1, keepdims=True))
            p = e / jnp.sum(e, axis=1, keepdims=True)
            p_ref[m * 2 * TILES_PER_PAIR + 2 * r + half] = p
            part = dot(p.astype(BF), pick(vs if swap else vp, half, masks))
            parts[half] = part
            if half == 1:
                o_ref[:, lanes((m * TILES_PER_PAIR + r) * LANES)] = (parts[0] + parts[1]).astype(BF)
        return carry

    lax.fori_loop(0, HEAD_PAIRS, pair, 0)
    o = o_ref[...]
    for n in range(d // TILE):
        rows = slice(n * TILE, (n + 1) * TILE)
        h_ref[:, rows] = x_ref[:, rows].astype(F32) + dot(o, w_ref[rows, QKV : QKV + QW], 1, 1)
    h = h_ref[...]
    r2 = lax.rsqrt(jnp.mean(h * h, axis=1, keepdims=True) + EPS)
    b_ref[...] = (h * r2 * gain_moe).astype(BF)


def vmem(n):
    return [pl.BlockSpec(memory_space=pltpu.VMEM)] * n


def attn_fwd(x, w, cos, sin, meta, segr):
    t, d = x.shape
    sds = jax.ShapeDtypeStruct
    return pl.pallas_call(
        attn_fwd_kernel,
        out_shape=(
            sds((t, QKV), BF),
            sds((QUERY_HEADS, t, t), F32),
            sds((t, QW), BF),
            sds((t, d), F32),
            sds((t, d), BF),
            sds((LANES, d), BF),
        ),
        in_specs=vmem(6),
        out_specs=tuple(vmem(6)),
        compiler_params=pltpu.CompilerParams(vmem_limit_bytes=VMEM_LIMIT),
        cost_estimate=pl.CostEstimate(flops=2 * t * d * 4096, bytes_accessed=w.size * 2, transcendentals=QUERY_HEADS * t * t),
    )(x, w, cos, sin, meta, segr)


def gates_of(rt, wrt, b, e_pad):
    t = rt.shape[1]
    experts = iota((e_pad, t), 0)
    chosen = experts == rt[0:1]
    for k in range(1, rt.shape[0]):
        chosen = chosen | (experts == rt[k : k + 1])
    logits = jnp.where(chosen, dot(wrt[0:e_pad], b, 1, 1), NEG_FILL)
    e = jnp.where(chosen, jnp.exp(logits - jnp.max(logits, axis=0, keepdims=True)), 0.0)
    return e / jnp.sum(e, axis=0, keepdims=True)


def attn_bwd_kernel(
    e_pad, gy_ref, h_ref, x_ref, w_ref, qkv_ref, p_ref, o_ref, b_ref, wrt_ref, back_ref, dg_ref, rt_ref, cos_ref, sin_ref,
    dx_ref, dd_ref, do_ref, dqkv_ref, dh_ref, lt_ref,
):
    t, d = x_ref.shape
    gain_attn = wrt_ref[GAIN_ATTN_ROW - 7 :, :].astype(F32)[7:8]
    gain_moe = wrt_ref[GAIN_ATTN_ROW - 7 :, :].astype(F32)[6:7]
    b = b_ref[...]
    gates = gates_of(rt_ref[...], wrt_ref, b, e_pad)
    dg = dg_ref[...]
    dl = (gates * (dg - jnp.sum(gates * dg, axis=0, keepdims=True)))
    dlb = dl.astype(BF)
    db = dot(dlb, wrt_ref[0:e_pad, :], 0, 0)
    for z in range(back_ref.shape[0]):
        db = db + back_ref[z].astype(F32)
    h = h_ref[...]
    r2 = lax.rsqrt(jnp.mean(h * h, axis=1, keepdims=True) + EPS)
    grad_moe = jnp.sum(db * h * r2, axis=0, keepdims=True)
    dn = db * gain_moe
    dh = gy_ref[...].astype(F32) + r2 * dn - h * (r2 * r2 * r2) * jnp.mean(dn * h, axis=1, keepdims=True)
    dh_ref[...] = dh
    dhb = dh.astype(BF)
    for n in range(QW // TILE):
        cols = slice(n * TILE, (n + 1) * TILE)
        do_ref[:, cols] = dot(dhb, w_ref[:, QKV + n * TILE : QKV + (n + 1) * TILE]).astype(BF)
    masks = lane_masks(t)
    cos, sin = cos_ref[...], sin_ref[...]

    def pair(m, carry):
        def lanes(base):
            return pl.ds(pl.multiple_of(base, LANES), LANES)

        kp = qkv_ref[:, lanes(QW + m * LANES)]
        vp = qkv_ref[:, lanes(QW + KW + m * LANES)]
        ks, vs = swapped(kp), swapped(vp)
        zero = jnp.zeros((t, LANES), F32)
        dk = {False: zero, True: zero}
        dv = {False: zero, True: zero}
        dq = zero
        for r, half, swap in head_plan():
            tile = lanes((m * TILES_PER_PAIR + r) * LANES)
            q = pick(qkv_ref[:, tile], half, masks)
            do = pick(do_ref[:, tile], half, masks)
            p = p_ref[m * 2 * TILES_PER_PAIR + 2 * r + half]
            dp = dot(do, vs if swap else vp, 1, 1)
            dv[swap] = dv[swap] + dot(p.astype(BF), do, 0, 0)
            dt = p * (dp - jnp.sum(p * dp, axis=1, keepdims=True)) * HEAD_SIZE ** (-0.5)
            dt = dt.astype(BF)
            dk[swap] = dk[swap] + dot(dt, q, 0, 0)
            part = dot(dt, pick(ks if swap else kp, half, masks))
            dq = part if half == 0 else dq + part
            if half == 1:
                dqkv_ref[:, tile] = rope(dq, cos, sin, -1.0).astype(BF)
        dk_all = dk[False] + pltpu.roll(dk[True], HEAD_SIZE, 1)
        dv_all = dv[False] + pltpu.roll(dv[True], HEAD_SIZE, 1)
        dqkv_ref[:, lanes(QW + m * LANES)] = rope(dk_all, cos, sin, -1.0).astype(BF)
        dqkv_ref[:, lanes(QW + KW + m * LANES)] = dv_all.astype(BF)
        return carry

    lax.fori_loop(0, HEAD_PAIRS, pair, 0)
    x = x_ref[...].astype(F32)
    r1 = lax.rsqrt(jnp.mean(x * x, axis=1, keepdims=True) + EPS)
    dqkv = dqkv_ref[...]
    for n in range(d // TILE):
        rows = slice(n * TILE, (n + 1) * TILE)
        dx_ref[:, rows] = dot(dqkv, w_ref[rows, 0:QKV], 1, 1)
    da = dx_ref[...]
    grad_attn = jnp.sum(da * x * r1, axis=0, keepdims=True)
    dag = da * gain_attn
    dx_ref[...] = dh_ref[...] + r1 * dag - x * (r1 * r1 * r1) * jnp.mean(dag * x, axis=1, keepdims=True)
    lt_ref[...] = jnp.transpose(x * r1 * gain_attn).astype(BF)
    for n in range(QKV // TILE):
        cols = slice(n * TILE, (n + 1) * TILE)
        dd_ref[:, cols] = dot(lt_ref[...], dqkv_ref[:, cols]).astype(BF)
    lt_ref[...] = jnp.transpose(dh_ref[...]).astype(BF)
    for n in range(QW // TILE):
        cols = slice(n * TILE, (n + 1) * TILE)
        dd_ref[:, QKV + n * TILE : QKV + (n + 1) * TILE] = dot(lt_ref[...], o_ref[:, cols]).astype(BF)
    lt_ref[...] = jnp.transpose(b_ref[...].astype(F32)).astype(BF)
    row = iota((LANES, d), 0)
    grads = jnp.where(row == GAIN_MOE_ROW, grad_moe, jnp.where(row == GAIN_ATTN_ROW, grad_attn, 0.0))
    dl_full = jnp.concatenate([dl, jnp.zeros((LANES - e_pad, t), F32)], axis=0)
    dl_rows = jnp.transpose(dl_full).astype(BF)
    dd_ref[:, QKV + QW :] = (dot(lt_ref[...], dl_rows) + jnp.transpose(grads)).astype(BF)


def attn_bwd(gy, h, x, w, qkv, p, o, b, wrt, back, dg, rt, cos, sin):
    t, d = x.shape
    sds = jax.ShapeDtypeStruct
    return pl.pallas_call(
        functools.partial(attn_bwd_kernel, dg.shape[0]),
        out_shape=(sds((t, d), F32), sds(w.shape, BF)),
        in_specs=vmem(14),
        out_specs=tuple(vmem(2)),
        scratch_shapes=[
            pltpu.VMEM((t, QW), BF),
            pltpu.VMEM((t, QKV), BF),
            pltpu.VMEM((t, d), F32),
            pltpu.VMEM((d, t), BF),
        ],
        compiler_params=pltpu.CompilerParams(vmem_limit_bytes=VMEM_LIMIT),
        cost_estimate=pl.CostEstimate(flops=4 * t * d * 4096, bytes_accessed=w.size * 4, transcendentals=0),
    )(gy, h, x, w, qkv, p, o, b, wrt, back, dg, rt, cos, sin)


def one_hot(pos_row, cap):
    return jnp.where(iota((cap, pos_row.shape[1]), 0) == pos_row, 1.0, 0.0)


def all_hots(pos, per, cap):
    return jnp.concatenate([one_hot(pos[j : j + 1], cap) for j in range(per)], axis=0)


def all_hots_back(pos, per, cap):
    width = per * cap
    expert = jnp.where(iota((8, width), 1) // cap == iota((8, width), 0), 1.0, 0.0).astype(BF)
    wide = dot(pos.astype(F32).astype(BF), expert, 0, 0)
    slot = (iota((1, width), 1) % cap).astype(F32)
    return jnp.where(wide == slot, 1.0, 0.0).astype(BF)


def slots_of(rt, first, per):
    t = rt.shape[1]
    experts = iota((16, t), 0)
    mine = jnp.where(experts < per, experts + first, -1)
    chosen = mine == rt[0:1]
    for k in range(1, rt.shape[0]):
        chosen = chosen | (mine == rt[k : k + 1])
    earlier = jnp.where(iota((t, t), 0) < iota((t, t), 1), 1.0, 0.0).astype(BF)
    before = dot(jnp.where(chosen, 1.0, 0.0).astype(BF), earlier)
    return jnp.where(chosen, before.astype(jnp.int32), -1)[0:8]


def streamed(count, copies, body):
    for c in copies(0, 0):
        c.start()

    def step(b, carry):
        slot = lax.rem(b, 2)

        @pl.when(b + 1 < count)
        def _():
            for c in copies(b + 1, lax.rem(b + 1, 2)):
                c.start()

        for c in copies(b, slot):
            c.wait()
        body(b, slot)
        return carry

    lax.fori_loop(0, count, step, 0)


def combine(count, per, cap, pos_ref, rows_ref, out_hbm, obuf, osem):
    def copy(b, slot):
        return pltpu.make_async_copy(obuf.at[slot], out_hbm.at[b], osem.at[slot])

    def step(b, carry):
        slot = lax.rem(b, 2)

        @pl.when(b >= 2)
        def _():
            copy(b - 2, slot).wait()

        back = all_hots_back(pos_ref[b], per, cap)
        at = pl.ds(pl.multiple_of(b * cap, cap), cap)
        rows = jnp.concatenate([rows_ref[j, at, :] for j in range(per)], axis=0)
        obuf[slot] = dot(back, rows).astype(BF)
        copy(b, slot).start()
        return carry

    lax.fori_loop(0, count, step, 0)
    copy(count - 2, (count - 2) % 2).wait()
    copy(count - 1, (count - 1) % 2).wait()


def chunk_gates(c, j, chunk, cap, pos_ref, gate_ref):
    hots, gates = [], []
    for bb in range(chunk // cap):
        b = c * (chunk // cap) + bb
        hot = one_hot(pos_ref[b, pl.ds(j, 1), :], cap)
        hots.append(hot)
        gates.append(jnp.sum(hot * gate_ref[b, pl.ds(j, 1), :], axis=1, keepdims=True))
    return hots, jnp.concatenate(gates, axis=0)


def experts_fwd_kernel(
    layer, e_pad, cap, rt_ref, wrt_ref, wg_ref, wu_ref, wd_ref, b_hbm,
    gp_ref, up_ref, pos_ref, gate_ref, out_hbm, x_scr, y_scr, all_gates, bbuf, obuf, bsem, osem,
):
    per, rows, d = x_scr.shape
    count = rt_ref.shape[0]
    chunk = 256
    j = pl.program_id(0)
    first = lax.axis_index("expert") * per

    @pl.when(lax.axis_index("section") == layer)
    def _():
        @pl.when(j == 0)
        def _():
            def prepare(b, slot):
                rt = rt_ref[b]
                block = bbuf[slot]
                pos = slots_of(rt, first, per)
                pos_ref[b] = pos
                all_gates[...] = gates_of(rt, wrt_ref, block, e_pad)
                gate_ref[b] = jnp.concatenate(
                    [all_gates[pl.ds(first + k, 1), :] for k in range(per)] + [jnp.zeros((8 - per, rt.shape[1]), F32)], axis=0
                )
                x = dot(all_hots(pos, per, cap).astype(BF), block).astype(BF)
                at = pl.ds(pl.multiple_of(b * cap, cap), cap)
                for k in range(per):
                    x_scr[k, at, :] = x[k * cap : (k + 1) * cap]

            streamed(count, lambda b, slot: [pltpu.make_async_copy(b_hbm.at[b], bbuf.at[slot], bsem.at[slot])], prepare)

        def part(c, carry):
            at = pl.ds(pl.multiple_of(c * chunk, chunk), chunk)
            x = x_scr[j, at, :]
            gp = dot(x, wg_ref[0])
            up = dot(x, wu_ref[0])
            gp_ref[0, at, :] = gp.astype(BF)
            up_ref[0, at, :] = up.astype(BF)
            hid = (gp / (1.0 + jnp.exp(-gp)) * up).astype(BF)
            _, gate = chunk_gates(c, j, chunk, cap, pos_ref, gate_ref)
            y_scr[j, at, :] = (dot(hid, wd_ref[0]) * gate).astype(BF)
            return carry

        lax.fori_loop(0, rows // chunk, part, 0)

        @pl.when(j == per - 1)
        def _():
            combine(count, per, cap, pos_ref, y_scr, out_hbm, obuf, osem)


def any_spec():
    return pl.BlockSpec(memory_space=pl.ANY)


def fixed(shape):
    return pl.BlockSpec(shape, lambda j: (0,) * len(shape))


def experts_fwd(layer, e_pad, cap, rt, wrt, wg, wu, wd, blocks):
    count, t, d = blocks.shape
    per, _, f = wg.shape
    rows = count * cap
    sds = jax.ShapeDtypeStruct
    return pl.pallas_call(
        functools.partial(experts_fwd_kernel, layer, e_pad, cap),
        grid=(per,),
        out_shape=(
            sds((per, rows, f), BF),
            sds((per, rows, f), BF),
            sds((count, 8, t), jnp.int32),
            sds((count, 8, t), F32),
            sds((count, t, d), BF),
        ),
        in_specs=[
            fixed(rt.shape),
            fixed(wrt.shape),
            pl.BlockSpec((1, d, f), lambda j: (j, 0, 0)),
            pl.BlockSpec((1, d, f), lambda j: (j, 0, 0)),
            pl.BlockSpec((1, f, d), lambda j: (j, 0, 0)),
            any_spec(),
        ],
        out_specs=(
            pl.BlockSpec((1, rows, f), lambda j: (j, 0, 0)),
            pl.BlockSpec((1, rows, f), lambda j: (j, 0, 0)),
            fixed((count, 8, t)),
            fixed((count, 8, t)),
            any_spec(),
        ),
        scratch_shapes=[
            pltpu.VMEM((per, rows, d), BF),
            pltpu.VMEM((per, rows, d), BF),
            pltpu.VMEM((e_pad, t), F32),
            pltpu.VMEM((2, t, d), BF),
            pltpu.VMEM((2, t, d), BF),
            pltpu.SemaphoreType.DMA((2,)),
            pltpu.SemaphoreType.DMA((2,)),
        ],
        compiler_params=pltpu.CompilerParams(vmem_limit_bytes=VMEM_LIMIT),
        cost_estimate=pl.CostEstimate(flops=6 * per * rows * d * f, bytes_accessed=6 * per * d * f, transcendentals=per * rows * f),
    )(rt, wrt, wg, wu, wd, blocks)


def gather_rows(count, per, cap, pos_ref, b_hbm, gy_hbm, x_scr, y_scr, bbuf, gbuf, bsem, gsem):
    def prepare(b, slot):
        hots = all_hots(pos_ref[b], per, cap).astype(BF)
        at = pl.ds(pl.multiple_of(b * cap, cap), cap)
        for source, dest in ((bbuf, x_scr), (gbuf, y_scr)):
            if dest is not None:
                rows = dot(hots, source[slot]).astype(BF)
                for k in range(per):
                    dest[k, at, :] = rows[k * cap : (k + 1) * cap]

    def copies(b, slot):
        both = [pltpu.make_async_copy(gy_hbm.at[b], gbuf.at[slot], gsem.at[slot])]
        if x_scr is not None:
            both.append(pltpu.make_async_copy(b_hbm.at[b], bbuf.at[slot], bsem.at[slot]))
        return both

    streamed(count, copies, prepare)


def experts_bwd_kernel(
    layer, cap, pos_ref, gate_ref, wg_ref, wu_ref, wd_ref, gp_ref, up_ref, gy_hbm,
    dgp_ref, dup_ref, hid_ref, dg_ref, out_hbm, y_scr, gbuf, obuf, gsem, osem,
):
    per, rows, d = y_scr.shape
    count = pos_ref.shape[0]
    chunk = 256
    j = pl.program_id(0)

    @pl.when(lax.axis_index("section") == layer)
    def _():
        @pl.when(j == 0)
        def _():
            gather_rows(count, per, cap, pos_ref, None, gy_hbm, None, y_scr, None, gbuf, None, gsem)
            dg_ref[...] = jnp.zeros_like(dg_ref)

        def part(c, carry):
            at = pl.ds(pl.multiple_of(c * chunk, chunk), chunk)
            raw = dot(y_scr[j, at, :], wd_ref[0], 1, 1)
            gp, up = gp_ref[0, at, :].astype(F32), up_ref[0, at, :].astype(F32)
            sg = 1.0 / (1.0 + jnp.exp(-gp))
            silu = gp * sg
            hid = silu * up
            hots, gate = chunk_gates(c, j, chunk, cap, pos_ref, gate_ref)
            dgate = jnp.sum(hid.astype(BF).astype(F32) * raw, axis=1, keepdims=True)
            for bb in range(chunk // cap):
                b = c * (chunk // cap) + bb
                dg_ref[b, pl.ds(j, 1), :] = jnp.sum(hots[bb] * dgate[bb * cap : (bb + 1) * cap], axis=0, keepdims=True)
            dh = raw * gate
            dgp = (dh * up * sg * (1.0 + gp * (1.0 - sg))).astype(BF)
            dup = (dh * silu).astype(BF)
            dgp_ref[0, at, :] = dgp
            dup_ref[0, at, :] = dup
            hid_ref[0, at, :] = (hid * gate).astype(BF)
            y_scr[j, at, :] = (dot(dgp, wg_ref[0], 1, 1) + dot(dup, wu_ref[0], 1, 1)).astype(BF)
            return carry

        lax.fori_loop(0, rows // chunk, part, 0)

        @pl.when(j == per - 1)
        def _():
            combine(count, per, cap, pos_ref, y_scr, out_hbm, obuf, osem)


def experts_bwd(layer, cap, pos, gate, wg, wu, wd, gp, up, grads):
    count, t, d = grads.shape
    per, _, f = wg.shape
    rows = count * cap
    sds = jax.ShapeDtypeStruct
    by_expert = pl.BlockSpec((1, rows, f), lambda j: (j, 0, 0))
    return pl.pallas_call(
        functools.partial(experts_bwd_kernel, layer, cap),
        grid=(per,),
        out_shape=(sds((per, rows, f), BF),) * 3 + (sds((count, 8, t), F32), sds((count, t, d), BF)),
        in_specs=[
            fixed(pos.shape),
            fixed(gate.shape),
            pl.BlockSpec((1, d, f), lambda j: (j, 0, 0)),
            pl.BlockSpec((1, d, f), lambda j: (j, 0, 0)),
            pl.BlockSpec((1, f, d), lambda j: (j, 0, 0)),
            by_expert,
            by_expert,
            any_spec(),
        ],
        out_specs=(by_expert, by_expert, by_expert, fixed((count, 8, t)), any_spec()),
        scratch_shapes=[
            pltpu.VMEM((per, rows, d), BF),
            pltpu.VMEM((2, t, d), BF),
            pltpu.VMEM((2, t, d), BF),
            pltpu.SemaphoreType.DMA((2,)),
            pltpu.SemaphoreType.DMA((2,)),
        ],
        compiler_params=pltpu.CompilerParams(vmem_limit_bytes=VMEM_LIMIT),
        cost_estimate=pl.CostEstimate(flops=6 * per * rows * d * f, bytes_accessed=8 * per * d * f, transcendentals=per * rows * f),
    )(pos, gate, wg, wu, wd, gp, up, grads)


def weight_grads(
    cap, pos_ref, b_hbm, gy_hbm, dgp_hbm, dup_hbm, hid_hbm, outs, x_scr, y_scr, bbuf, gbuf, act_buf, gu_buf, dn_buf,
    bsem, gsem, act_sem, gu_sem, dn_sem,
):
    even, odd, even_dn, odd_dn = outs
    per, rows, d = x_scr.shape
    count = pos_ref.shape[0]
    parts, piece = gu_buf.shape[1] // 2, gu_buf.shape[3]
    g = lax.axis_index("group")
    parity, place = lax.rem(g, 2), g // 2
    gather_rows(count, per, cap, pos_ref, b_hbm, gy_hbm, x_scr, y_scr, bbuf, gbuf, bsem, gsem)

    def acts(j, slot):
        return [
            pltpu.make_async_copy(source.at[j], act_buf.at[slot, n], act_sem.at[slot, n])
            for n, source in enumerate((dgp_hbm, dup_hbm, hid_hbm))
        ]

    def outgoing(j, slot):
        half = pl.ds(0, parts), pl.ds(parts, parts)
        return [
            pltpu.make_async_copy(gu_buf.at[slot, half[0]], even.at[:, :, j], gu_sem.at[slot, 0]),
            pltpu.make_async_copy(gu_buf.at[slot, half[1]], odd.at[:, :, j], gu_sem.at[slot, 1]),
            pltpu.make_async_copy(dn_buf.at[slot, half[0]], even_dn.at[:, j], dn_sem.at[slot, 0]),
            pltpu.make_async_copy(dn_buf.at[slot, half[1]], odd_dn.at[:, j], dn_sem.at[slot, 1]),
        ]

    def body(j, slot):
        @pl.when(j >= 2)
        def _():
            for c in outgoing(j - 2, slot):
                c.wait()

        for q in range(parts):
            cols = slice(2 * q * piece, 2 * (q + 1) * piece)
            at = lax.bitwise_xor(place, q)
            low, high = parity * parts + at, (1 - parity) * parts + at
            for n in range(2):
                full = dot(x_scr[j, :, cols], act_buf[slot, n], 0, 0).astype(BF)
                gu_buf[slot, low, n] = full[:piece]
                gu_buf[slot, high, n] = full[piece:]
            full = dot(act_buf[slot, 2], y_scr[j, :, cols], 0, 0).astype(BF)
            dn_buf[slot, low] = full[:, :piece]
            dn_buf[slot, high] = full[:, piece:]
        for c in outgoing(j, slot):
            c.start()

    streamed(per, acts, body)
    for j in (per - 2, per - 1):
        for c in outgoing(j, j % 2):
            c.wait()


def meet(n, with_cross):
    s, z = lax.axis_index("section"), lax.axis_index("expert")
    barrier = pltpu.get_barrier_semaphore()
    for k in range(1, n):
        pl.semaphore_signal(barrier, inc=1, device_id={"expert": lax.rem(z + k, n)}, device_id_type=MESH)
    for k in range(n if with_cross else 1):
        pl.semaphore_signal(
            barrier, inc=1, device_id={"section": 1 - s, "expert": lax.rem(z + k, n)}, device_id_type=MESH
        )
    pl.semaphore_wait(barrier, 2 * n - 1 if with_cross else n)


def spread_kernel(layer, n, x_ref, o_ref, send_sem, recv_sem, local_sem):
    s, z = lax.axis_index("section"), lax.axis_index("expert")
    meet(n, True)

    def copy(k, source_section):
        return pltpu.make_async_remote_copy(
            src_ref=x_ref,
            dst_ref=o_ref.at[source_section, z],
            send_sem=send_sem.at[k],
            recv_sem=recv_sem.at[source_section, k],
            device_id={"section": layer, "expert": lax.rem(z + k, n)},
            device_id_type=MESH,
        )

    order = sorted(range(n), key=lambda k: (k == 0, abs(k - n // 2)))

    @pl.when(s == layer)
    def _():
        own = pltpu.make_async_copy(x_ref, o_ref.at[layer, z], local_sem)
        own.start()
        sends = [copy(k, layer) for k in order if k]
        for c in sends:
            c.start()
        own.wait()
        for c in sends:
            c.wait()
        for k in range(n):
            copy(k, 1 - layer).wait_recv()

    @pl.when(s != layer)
    def _():
        sends = [copy(k, 1 - layer) for k in order]
        for c in sends:
            c.start()
        for c in sends:
            c.wait_send()


def spread(layer, cid, x):
    n = lax.axis_size("expert")
    return pl.pallas_call(
        functools.partial(spread_kernel, layer, n),
        out_shape=jax.ShapeDtypeStruct((2, n) + x.shape, x.dtype),
        in_specs=vmem(1),
        out_specs=any_spec(),
        scratch_shapes=[
            pltpu.SemaphoreType.DMA((n,)),
            pltpu.SemaphoreType.DMA((2, n)),
            pltpu.SemaphoreType.DMA,
        ],
        compiler_params=pltpu.CompilerParams(collective_id=cid, has_side_effects=True),
    )(x)


def collect_kernel(layer, n, arrays, cap, *refs):
    srcs, refs = refs[:arrays], refs[arrays:]
    work_in, refs = (refs[:6], refs[6:]) if cap else ((), refs)
    outs, refs = refs[:arrays], refs[arrays:]
    work_out, refs = (refs[:4], refs[4:]) if cap else ((), refs)
    relays, refs = refs[:arrays], refs[arrays:]
    relay_send, relay_recv, send_sem, recv_sem, local_sem = refs[:5]
    s, z = lax.axis_index("section"), lax.axis_index("expert")
    meet(n, False)

    def hop(a, to):
        return pltpu.make_async_remote_copy(
            src_ref=srcs[a].at[1 - layer, to],
            dst_ref=relays[a].at[to],
            send_sem=relay_send.at[a, to],
            recv_sem=relay_recv.at[a, to],
            device_id={"section": 1 - s},
            device_id_type=MESH,
        )

    def give(a, source, k):
        return pltpu.make_async_remote_copy(
            src_ref=source,
            dst_ref=outs[a].at[z],
            send_sem=send_sem.at[a, k],
            recv_sem=recv_sem.at[a, k],
            device_id={"expert": lax.rem(z + k, n)},
            device_id_type=MESH,
        )

    order = sorted(range(n), key=lambda k: (k == 0, abs(k - n // 2)))

    @pl.when(s == layer)
    def _():
        for k in order:
            for a in range(arrays):
                hop(a, lax.rem(z + k, n)).start()
        for k in order:
            for a in range(arrays):
                if k:
                    give(a, srcs[a].at[layer, lax.rem(z + k, n)], k).start()
                else:
                    pltpu.make_async_copy(srcs[a].at[layer, z], outs[a].at[z], local_sem.at[a]).start()
        if cap:
            weight_grads(cap, *work_in, work_out, *refs[5:])
        for k in order:
            for a in range(arrays):
                hop(a, lax.rem(z + k, n)).wait_send()

    @pl.when(s != layer)
    def _():
        for k in order:
            to = lax.rem(z + k, n)
            for a in range(arrays):
                hop(a, to).wait_recv()
                if k:
                    give(a, relays[a].at[to], k).start()
                else:
                    pltpu.make_async_copy(relays[a].at[z], outs[a].at[z], local_sem.at[a]).start()

    for a in range(arrays):
        for k in order:
            if k:
                give(a, relays[a].at[lax.rem(z + k, n)], k).wait()
            else:
                pltpu.make_async_copy(relays[a].at[z], outs[a].at[z], local_sem.at[a]).wait()


def collect(layer, cid, arrays, work=None):
    n, groups = lax.axis_size("expert"), lax.axis_size("group")
    count = len(arrays)
    sds = jax.ShapeDtypeStruct
    dma = pltpu.SemaphoreType.DMA
    outs = [sds(a.shape[1:], a.dtype) for a in arrays]
    scratch = [pltpu.VMEM(a.shape[1:], a.dtype) for a in arrays]
    scratch += [dma((count, n)), dma((count, n)), dma((count, n)), dma((count, n)), dma((count,))]
    in_specs = [any_spec()] * count
    extra = ()
    if work:
        extra = work[1:]
        pos, blocks, _, dgp = extra[:4]
        t, d = blocks.shape[1:]
        per, rows, f = dgp.shape
        piece = d // groups
        outs += [sds((groups // 2, 2, per, piece, f), BF)] * 2 + [sds((groups // 2, per, f, piece), BF)] * 2
        in_specs += vmem(1) + [any_spec()] * 5
        scratch += [
            pltpu.VMEM((per, rows, d), BF),
            pltpu.VMEM((per, rows, d), BF),
            pltpu.VMEM((2, t, d), BF),
            pltpu.VMEM((2, t, d), BF),
            pltpu.VMEM((2, 3, rows, f), BF),
            pltpu.VMEM((2, groups, 2, piece, f), BF),
            pltpu.VMEM((2, groups, f, piece), BF),
            dma((2,)),
            dma((2,)),
            dma((2, 3)),
            dma((2, 2)),
            dma((2, 2)),
        ]
    return pl.pallas_call(
        functools.partial(collect_kernel, layer, n, count, work[0] if work else 0),
        out_shape=tuple(outs),
        in_specs=in_specs,
        out_specs=tuple([any_spec()] * len(outs)),
        scratch_shapes=scratch,
        compiler_params=pltpu.CompilerParams(
            collective_id=cid, has_side_effects=True, vmem_limit_bytes=VMEM_LIMIT if work else 16 * 1024 * 1024
        ),
    )(*arrays, *extra)


def top_bit(q):
    return q.bit_length() - 1


def finish_kernel(
    n, dd0, dd1, egu0, ogu0, ed0, od0, egu1, ogu1, ed1, od1,
    dense_out, gate_out, up_out, down_out,
    core_gu, core_dn, hop_gu, hop_dn, core_dd, hop_y, hop_z, hop_x, dd_buf, gu_buf, dn_buf, gu_f32, dn_f32,
    s_core_gu, r_core_gu, s_core_dn, r_core_dn, s_hop_gu, r_hop_gu, s_hop_dn, r_hop_dn,
    s_core_dd, r_core_dd, s_y, r_y, s_z, r_z, s_x, r_x, l_dd, l_gu, l_dn, o_gu, o_dn,
):
    s, g, z = lax.axis_index("section"), lax.axis_index("group"), lax.axis_index("expert")
    pairs, cgu = core_gu.shape[:2]
    cdn = core_dn.shape[1]
    levels = top_bit(pairs)
    units = pairs * n
    remote = functools.partial(pltpu.make_async_remote_copy, device_id_type=MESH)
    twin = {"group": lax.bitwise_xor(g, 1)}
    other = {"section": 1 - s}

    def across(k):
        return {"group": lax.bitwise_xor(g, 2 << k)}

    barrier = pltpu.get_barrier_semaphore()
    peers = [twin, other] + [across(k) for k in range(levels)] + [{"expert": lax.rem(z + k, n)} for k in range(1, n)]
    for peer in peers:
        pl.semaphore_signal(barrier, inc=1, device_id=peer, device_id_type=MESH)
    pl.semaphore_wait(barrier, len(peers))

    def by_section(action):
        @pl.when(s == 0)
        def _():
            action(dd0, dd1, egu0, ogu0, ed0, od0)

        @pl.when(s != 0)
        def _():
            action(dd1, dd0, egu1, ogu1, ed1, od1)

    def unit(i):
        return pairs - 1 - i // n, lax.rem(z + 1 + lax.rem(i, n), n)

    def shard(i, core):
        q, place = unit(i)
        return (lax.bitwise_xor(g // 2, q) * 2 + core) * n + place

    core = lax.rem(g, 2)

    def core_dd_copy(kind, i, source):
        return remote(
            src_ref=source.at[shard(i, 1 - core)],
            dst_ref=core_dd.at[kind, i],
            send_sem=s_core_dd.at[kind, i],
            recv_sem=r_core_dd.at[kind, i],
            device_id=twin,
        )

    def core_chunk(source, dest, ssem, rsem, q, c):
        return remote(
            src_ref=source.at[q, c], dst_ref=dest.at[q, c], send_sem=ssem.at[q, c], recv_sem=rsem.at[q, c], device_id=twin
        )

    def core_gu_copy(source, q, c):
        return core_chunk(source, core_gu, s_core_gu, r_core_gu, q, c)

    def core_dn_copy(source, q, c):
        return core_chunk(source, core_dn, s_core_dn, r_core_dn, q, c)

    def send_all(own, away, egu, ogu, ed, od):
        @pl.loop(0, units)
        def _(i):
            core_dd_copy(0, i, away).start()

            @pl.when(i < cgu)
            def _():
                core_gu_copy(ogu, pairs - 1, i).start()

            @pl.when(i < cdn)
            def _():
                core_dn_copy(od, pairs - 1, i).start()

        for i in range(units, max(cgu, cdn)):
            if i < cgu:
                core_gu_copy(ogu, pairs - 1, i).start()
            if i < cdn:
                core_dn_copy(od, pairs - 1, i).start()

        @pl.loop(0, units)
        def _(i):
            core_dd_copy(1, i, own).start()

        for q in reversed(range(pairs - 1)):

            @pl.loop(0, cgu)
            def _(c):
                core_gu_copy(ogu, q, c).start()

            @pl.loop(0, cdn)
            def _(c):
                core_dn_copy(od, q, c).start()

    by_section(send_all)

    def load(buf, sem, slot, source):
        return pltpu.make_async_copy(source, buf.at[slot], sem.at[slot])

    def dd_load(i, slot, source):
        return load(dd_buf, l_dd, slot, source.at[shard(i, core)])

    def hop(dest, ssem, rsem, source, k, q, c):
        return remote(
            src_ref=source.at[q, c],
            dst_ref=dest.at[k, q - (1 << k), c],
            send_sem=ssem.at[k, q - (1 << k), c],
            recv_sem=rsem.at[k, q - (1 << k), c],
            device_id=across(k),
        )

    def gu_hop(k, q, c):
        return hop(hop_gu, s_hop_gu, r_hop_gu, core_gu, k, q, c)

    def dn_hop(k, q, c):
        return hop(hop_dn, s_hop_dn, r_hop_dn, core_dn, k, q, c)

    def y_copy(i):
        return remote(src_ref=core_dd.at[0, i], dst_ref=hop_y.at[i], send_sem=s_y.at[i], recv_sem=r_y.at[i], device_id=other)

    def z_copy(q, k, i):
        return remote(
            src_ref=core_dd.at[1, i],
            dst_ref=hop_z.at[k - 1, q],
            send_sem=s_z.at[k - 1, q],
            recv_sem=r_z.at[k - 1, q],
            device_id={"expert": lax.rem(z + k, n)},
        )

    def x_copy(k, q, i):
        return remote(
            src_ref=core_dd.at[1, i],
            dst_ref=hop_x.at[k, q - (1 << k)],
            send_sem=s_x.at[k, q - (1 << k)],
            recv_sem=r_x.at[k, q - (1 << k)],
            device_id=across(k),
        )

    def chunk_start(i, slot, q, egu, ed):
        @pl.when(i < cgu)
        def _():
            load(gu_buf, l_gu, slot, egu.at[q, i]).start()

        @pl.when(i < cdn)
        def _():
            load(dn_buf, l_dn, slot, ed.at[q, i]).start()

    def expert_sum(hops, rsem, dest, core_r, buf, sem, slot, even, q, c, hop_copy):
        load(buf, sem, slot, even.at[q, c]).wait()
        core_r(q, c).wait_recv()
        total = buf[slot].astype(F32) + dest[q, c].astype(F32)
        for k in range(top_bit(q) + 1 if q else 0, levels):
            hop_copy(k, q + (1 << k), c).wait_recv()
            total = total + hops[k, q, c].astype(F32)
        return total

    def gu_sum(slot, q, c):
        return expert_sum(hop_gu, r_hop_gu, core_gu, functools.partial(core_gu_copy, ogu0), gu_buf, l_gu, slot, egu0, q, c, gu_hop)

    def dn_sum(slot, q, c):
        return expert_sum(hop_dn, r_hop_dn, core_dn, functools.partial(core_dn_copy, od0), dn_buf, l_dn, slot, ed0, q, c, dn_hop)

    def stepped(count, start, body):
        start(0, 0)

        def step(i, carry):
            @pl.when(i + 1 < count)
            def _():
                start(i + 1, lax.rem(i + 1, 2))

            body(i, lax.rem(i, 2))
            return carry

        lax.fori_loop(0, count, step, 0)

    for q in reversed(range(1, pairs)):
        dense_too = q == pairs - 1
        steps = max(units, cgu, cdn) if dense_too else max(cgu, cdn)

        def start(i, slot):
            def go(own, away, egu, ogu, ed, od):
                if dense_too:

                    @pl.when(i < units)
                    def _():
                        dd_load(i, slot, away).start()

                chunk_start(i, slot, q, egu, ed)

            by_section(go)

        def body(i, slot):
            if dense_too:

                @pl.when(i < units)
                def _():
                    dd_load(i, slot, dd0).wait()
                    core_dd_copy(0, i, dd0).wait_recv()
                    core_dd[0, i] = core_dd[0, i] + dd_buf[slot]
                    y_copy(i).start()

            @pl.when(i < cgu)
            def _():
                core_gu[q, i] = gu_sum(slot, q, i).astype(BF)
                gu_hop(top_bit(q), q, i).start()

            @pl.when(i < cdn)
            def _():
                core_dn[q, i] = dn_sum(slot, q, i).astype(BF)
                dn_hop(top_bit(q), q, i).start()

        stepped(steps, start, body)

    def gu_out_copy(c, slot, to=gate_out):
        return pltpu.make_async_copy(gu_f32.at[slot], to.at[lax.rem(c, cgu // 2)], o_gu.at[slot])

    def dn_out_copy(c, slot):
        return pltpu.make_async_copy(dn_f32.at[slot], down_out.at[c], o_dn.at[slot])

    def dense_sum(q):
        i = (pairs - 1 - q) * n + n - 1
        total = core_dd[1, i].astype(F32)
        for k in range(1, n):
            z_copy(q, k, i).wait_recv()
            total = total + hop_z[k - 1, q].astype(F32)
        for k in range(top_bit(q) + 1 if q else 0, levels):
            x_copy(k, q + (1 << k), i).wait_recv()
            total = total + hop_x[k, q].astype(F32)
        return i, total

    def pass_on(q):
        i, total = dense_sum(q)
        core_dd[1, i] = total.astype(BF)
        x_copy(top_bit(q), q, i).start()

    steps = max(units, cgu, cdn)

    def start(i, slot):
        def go(own, away, egu, ogu, ed, od):
            @pl.when(i < units)
            def _():
                dd_load(i, slot, own).start()

            chunk_start(i, slot, 0, egu, ed)

        by_section(go)

    def body(i, slot):
        @pl.when(i < units)
        def _():
            dd_load(i, slot, dd0).wait()
            core_dd_copy(1, i, dd0).wait_recv()
            y_copy(i).wait_recv()
            core_dd[1, i] = (core_dd[1, i].astype(F32) + dd_buf[slot].astype(F32) + hop_y[i].astype(F32)).astype(BF)
            q, _ = unit(i)
            k = lax.rem(i, n) + 1

            @pl.when(k < n)
            def _():
                z_copy(q, k, i).start()

        for q in range(1, pairs):

            @pl.when(i == (pairs - q) * n + min(2, n - 1))
            def _():
                pass_on(q)

        @pl.when(i < cgu)
        def _():
            @pl.when(i >= 2)
            def _():
                gu_out_copy(i - 2, slot).wait()

            gu_f32[slot] = gu_sum(slot, 0, i)

            @pl.when(i < cgu // 2)
            def _():
                gu_out_copy(i, slot).start()

            @pl.when(i >= cgu // 2)
            def _():
                gu_out_copy(i, slot, up_out).start()

        @pl.when(i < cdn)
        def _():
            @pl.when(i >= 2)
            def _():
                dn_out_copy(i - 2, slot).wait()

            dn_f32[slot] = dn_sum(slot, 0, i)
            dn_out_copy(i, slot).start()

    stepped(steps, start, body)
    _, total = dense_sum(0)
    dense_out[...] = total
    for c in (cgu - 2, cgu - 1):
        gu_out_copy(c, c % 2).wait()
    for c in (cdn - 2, cdn - 1):
        dn_out_copy(c, c % 2).wait()

    @pl.loop(0, units)
    def _(i):
        core_dd_copy(0, i, dd0).wait_send()
        core_dd_copy(1, i, dd0).wait_send()
        y_copy(i).wait_send()
        q, _ = unit(i)
        k = lax.rem(i, n) + 1

        @pl.when(k < n)
        def _():
            z_copy(q, k, i).wait_send()

    for q in range(pairs):
        if q:
            x_copy(top_bit(q), q, (pairs - 1 - q) * n + n - 1).wait_send()

        @pl.loop(0, cgu)
        def _(c):
            core_gu_copy(ogu0, q, c).wait_send()
            if q:
                gu_hop(top_bit(q), q, c).wait_send()

        @pl.loop(0, cdn)
        def _(c):
            core_dn_copy(od0, q, c).wait_send()
            if q:
                dn_hop(top_bit(q), q, c).wait_send()


def finish(cid, dd0, dd1, experts0, experts1):
    n, groups = lax.axis_size("expert"), lax.axis_size("group")
    pairs, levels = groups // 2, top_bit(groups // 2)
    width = dd0.shape[1]
    rows = dd0.shape[0] // (groups * n)
    dd0, dd1 = (v.reshape(groups * n, rows, width) for v in (dd0, dd1))

    def chunked(arrays):
        gu_even, gu_odd, dn_even, dn_odd = arrays
        flat = (pairs, -1) + gu_even.shape[3:]
        return gu_even.reshape(flat), gu_odd.reshape(flat), dn_even, dn_odd

    experts0, experts1 = chunked(experts0), chunked(experts1)
    gu, dn = experts0[0].shape[1:], experts0[2].shape[1:]
    units = pairs * n
    dma = pltpu.SemaphoreType.DMA
    sds = jax.ShapeDtypeStruct
    half = max(1, pairs // 2)

    def both(shape):
        return [dma(shape), dma(shape)]

    return pl.pallas_call(
        functools.partial(finish_kernel, n),
        out_shape=(sds((rows, width), F32), sds((gu[0] // 2,) + gu[1:], F32), sds((gu[0] // 2,) + gu[1:], F32), sds(dn, F32)),
        in_specs=[any_spec()] * 10,
        out_specs=(pl.BlockSpec(memory_space=pltpu.VMEM), any_spec(), any_spec(), any_spec()),
        scratch_shapes=[
            pltpu.VMEM((pairs,) + gu, BF),
            pltpu.VMEM((pairs,) + dn, BF),
            pltpu.VMEM((levels, half) + gu, BF),
            pltpu.VMEM((levels, half) + dn, BF),
            pltpu.VMEM((2, units, rows, width), BF),
            pltpu.VMEM((units, rows, width), BF),
            pltpu.VMEM((n - 1, pairs, rows, width), BF),
            pltpu.VMEM((levels, half, rows, width), BF),
            pltpu.VMEM((2, rows, width), BF),
            pltpu.VMEM((2,) + gu[1:], BF),
            pltpu.VMEM((2,) + dn[1:], BF),
            pltpu.VMEM((2,) + gu[1:], F32),
            pltpu.VMEM((2,) + dn[1:], F32),
        ]
        + both((pairs, gu[0]))
        + both((pairs, dn[0]))
        + both((levels, half, gu[0]))
        + both((levels, half, dn[0]))
        + both((2, units))
        + both((units,))
        + both((n - 1, pairs))
        + both((levels, half))
        + [dma((2,))] * 5,
        compiler_params=pltpu.CompilerParams(collective_id=cid, has_side_effects=True, vmem_limit_bytes=VMEM_LIMIT),
    )(dd0, dd1, *experts0, *experts1)


def low_bit(q):
    return top_bit(q & -q)


def open_kernel(
    n, groups, pieces, w_ref, cot_ref, rt_ref, w_out, gy_out, rt_out, rt_side,
    s_right, r_right, s_left, r_left, s_group, r_group, s_y, r_y, s_cross, r_cross, s_rt, r_rt, s_side, r_side, local_sem,
):
    s, g, z = lax.axis_index("section"), lax.axis_index("group"), lax.axis_index("expert")
    remote = functools.partial(pltpu.make_async_remote_copy, device_id_type=MESH)
    rows = w_ref.shape[0] // pieces
    bits = top_bit(groups)
    other = {"section": 1 - s}
    barrier = pltpu.get_barrier_semaphore()
    peers = [other] + [{"group": lax.bitwise_xor(g, 1 << b)} for b in range(bits)] + [{"expert": lax.rem(z + k, n)} for k in range(1, n)]
    for peer in peers:
        pl.semaphore_signal(barrier, inc=1, device_id=peer, device_id_type=MESH)
    pl.semaphore_wait(barrier, len(peers))
    sent = []

    def launch(cond, make):
        sent.append((cond, make))
        if cond is None:
            make().start()
        else:

            @pl.when(cond)
            def _():
                make().start()

    def part(q, zz, c):
        return w_out.at[lax.bitwise_xor(g, q) * n + zz, pl.ds(c * rows, rows)] if c < pieces else gy_out.at[s, zz]

    def chain(to, zz, t, c, ssem, rsem):
        return remote(src_ref=part(0, zz, c), dst_ref=part(0, zz, c), send_sem=ssem.at[t, c], recv_sem=rsem.at[t, c], device_id={"expert": to})

    def right(t, c):
        return chain(z + 1, z - t, t, c, s_right, r_right)

    def left(t, c):
        return chain(z - 1, z + t, t, c, s_left, r_left)

    def over(q, b, zz, c):
        at = q | (1 << b)
        return remote(
            src_ref=part(q, zz, c), dst_ref=part(q, zz, c), send_sem=s_group.at[at, zz, c], recv_sem=r_group.at[at, zz, c],
            device_id={"group": lax.bitwise_xor(g, 1 << b)},
        )

    def hop(c):
        at = pl.ds(c * rows, rows)
        return remote(
            src_ref=w_ref.at[at], dst_ref=w_out.at[g * n + z, at], send_sem=s_y.at[c], recv_sem=r_y.at[c], device_id=other
        )

    def cross(zz):
        return remote(src_ref=gy_out.at[0, zz], dst_ref=gy_out.at[0, zz], send_sem=s_cross.at[zz], recv_sem=r_cross.at[zz], device_id=other)

    def route(m, k):
        return remote(
            src_ref=rt_ref.at[m], dst_ref=rt_out.at[m, z], send_sem=s_rt.at[m, k], recv_sem=r_rt.at[m, k],
            device_id={"expert": lax.rem(z + k, n)},
        )

    def side():
        return remote(src_ref=rt_ref.at[1 - s], dst_ref=rt_side, send_sem=s_side, recv_sem=r_side, device_id=other)

    launch(s == 0, functools.partial(hop, 0))
    launch(None, side)
    own = [pltpu.make_async_copy(cot_ref, gy_out.at[s, z], local_sem.at[0])]
    own += [pltpu.make_async_copy(rt_ref.at[m], rt_out.at[m, z], local_sem.at[1 + m]) for m in range(2)]

    def keep():
        return pltpu.make_async_copy(w_ref, w_out.at[g * n + z], local_sem.at[3])

    for copy in own:
        copy.start()

    @pl.when(s == 0)
    def _():
        keep().start()
        keep().wait()

    def spread_out(cond, zz, c):
        if c < pieces:
            for b in reversed(range(bits)):
                launch(cond, functools.partial(over, 0, b, zz, c))
        else:
            launch((s == 0) if cond is None else ((s == 0) & cond), functools.partial(cross, zz))

    def pass_along(t, c):
        if t == 0:
            if c < pieces:

                @pl.when(s != 0)
                def _():
                    hop(c).wait_recv()
            else:
                own[0].wait()
            launch(z < n - 1, functools.partial(right, t, c))
            launch(z > 0, functools.partial(left, t, c))
            spread_out(None, z, c)
            if c + 1 < pieces:

                @pl.when(s == 0)
                def _():
                    hop(c).wait_send()
                    hop(c + 1).start()
        else:
            from_left, from_right = z >= t, z + t < n

            @pl.when(from_left)
            def _():
                right(t - 1, c).wait_recv()

            launch(from_left & (z < n - 1), functools.partial(right, t, c))
            spread_out(from_left, z - t, c)

            @pl.when(from_right)
            def _():
                left(t - 1, c).wait_recv()

            launch(from_right & (z > 0), functools.partial(left, t, c))
            spread_out(from_right, z + t, c)

    def forward(q, k):
        zz = lax.rem(z + k, n)
        for c in range(pieces):
            over(q & (q - 1), low_bit(q), zz, c).wait_recv()
            for b in reversed(range(low_bit(q))):
                launch(None, functools.partial(over, q, b, zz, c))

    for t in range(n):
        for c in range(pieces):
            pass_along(t, c)
        if t == 0:
            for m in range(2):
                for k in range(1, n):
                    launch(None, functools.partial(route, m, k))
    pending = [(q, k) for q in sorted(range(1, groups), key=lambda q: -low_bit(q)) for k in range(n)]
    for t in range(n):
        pass_along(t, pieces)
        forward(*pending.pop(0))
    for q, k in pending:
        forward(q, k)

    @pl.when(s != 0)
    def _():
        for zz in range(n):
            cross(zz).wait_recv()

    side().wait_recv()
    for m in range(2):
        own[1 + m].wait()
        for k in range(1, n):
            route(m, k).wait_recv()
    @pl.when(s == 0)
    def _():
        if pieces > 1:
            hop(pieces - 1).wait_send()

    for cond, make in sent[(1 if pieces > 1 else 0) :]:
        if cond is None:
            make().wait_send()
        else:

            @pl.when(cond)
            def _(make=make):
                make().wait_send()


def open_up(cid, packed, cot, rt):
    n, groups = lax.axis_size("expert"), lax.axis_size("group")
    sh = packed.shape[0]
    pieces = 3 if sh % 48 == 0 else 1
    dma = pltpu.SemaphoreType.DMA
    sds = jax.ShapeDtypeStruct

    def both(shape):
        return [dma(shape), dma(shape)]

    w, gy, rt_all, rt_side = pl.pallas_call(
        functools.partial(open_kernel, n, groups, pieces),
        out_shape=(sds((groups * n,) + packed.shape, BF), sds((2, n) + cot.shape, BF), sds((2, n) + rt.shape[1:], rt.dtype), sds(rt.shape[1:], rt.dtype)),
        in_specs=vmem(3),
        out_specs=(any_spec(), any_spec(), any_spec(), any_spec()),
        scratch_shapes=both((n, pieces + 1)) + both((n, pieces + 1)) + both((groups, n, pieces)) + both((pieces,)) + both((n,)) + both((2, n)) + [dma, dma] + [dma((4,))],
        compiler_params=pltpu.CompilerParams(collective_id=cid, has_side_effects=True),
    )(packed, cot, rt)
    return w.reshape(groups * n * sh, -1), gy, rt_all, rt_side


def swap_sections(value):
    return lax.ppermute(value, "section", [(0, 1), (1, 0)])


def rope_tables(t):
    half = HEAD_SIZE // 2
    frequency = THETA ** (-jnp.arange(half, dtype=F32) * 2.0 / HEAD_SIZE)
    angles = jnp.arange(t, dtype=F32)[:, None] * frequency[None, :]
    reps = LANES // half
    return jnp.tile(jnp.cos(angles), (1, reps)), jnp.tile(jnp.sin(angles), (1, reps))


def local(
    inputs, cotangent, segment_ids, live_first, routes, gain_attn, gain_moe,
    w_query, key_weight, value_weight, w_out, w_router, w_gate, w_up, w_down,
):
    s = lax.axis_index("section")
    n = lax.axis_size("expert")
    groups = lax.axis_size("group")
    t, d = inputs.shape[2:]
    top = routes.shape[-1]
    per = w_gate.shape[1]
    experts = per * n
    e_pad = -(-experts // 16) * 16
    cap = t * top * 5 // (4 * experts)
    wg, wu, wd = w_gate[0], w_up[0], w_down[0]
    at_zero = s == 0

    shard = w_query.shape[1]
    aux = jnp.concatenate(
        [
            w_router[0],
            jnp.zeros((shard, GAIN_MOE_ROW - experts), BF),
            gain_moe[0][:, None],
            gain_attn[0][:, None],
        ],
        axis=1,
    )
    packed = jnp.concatenate([w_query[0], key_weight[0], value_weight[0], w_out[0].T, aux], axis=1)
    other = lax.ppermute(packed, "section", [(1, 0)])
    second_shard = jnp.where(at_zero, other, packed)

    x0 = lax.dynamic_index_in_dim(inputs[:, 0], s, 0, keepdims=False)
    cot = lax.dynamic_index_in_dim(cotangent[:, 0], s, 0, keepdims=False)
    seg = lax.dynamic_index_in_dim(segment_ids[:, 0], s, 0, keepdims=False)
    live = lax.dynamic_index_in_dim(live_first[:, 0], s, 0, keepdims=False)
    meta = jnp.stack([seg, jnp.repeat(live, BLK)], axis=1)
    meta = jnp.pad(meta, ((0, 0), (0, LANES - 2)))
    segr = jnp.broadcast_to(seg[None, :], (8, t))
    cos, sin = rope_tables(t)

    rt = jnp.swapaxes(routes[0, :, 0], 1, 2)
    rt_mine = lax.dynamic_index_in_dim(rt, s, 0, keepdims=False)

    def flat(z):
        return z.reshape((2 * n,) + z.shape[2:])

    def paired(z):
        return z.reshape((2, n) + z.shape[1:])

    first_weights, gy1, rt_all, rt_theirs = open_up(1, packed, cot, rt)
    rt_tokens = (jnp.where(at_zero, rt_mine, rt_theirs), jnp.where(at_zero, rt_theirs, rt_mine))
    gy1, rt_all = flat(gy1), flat(rt_all)

    qkv0, p0, o0, h0, b0, wrt0 = attn_fwd(x0, first_weights, cos, sin, meta, segr)
    second_shard, b0 = lax.optimization_barrier((second_shard, b0))
    second_weights = lax.all_gather(second_shard, ("group", "expert"), axis=0, tiled=True)
    b0_all = flat(spread(0, 2, b0))
    gp0, up0, pos0, gate0, part0 = experts_fwd(0, e_pad, cap, rt_all, wrt0, wg, wu, wd, b0_all)
    (back0,) = collect(0, 3, (paired(part0),))
    x1 = (h0 + jnp.sum(back0.astype(F32), axis=0)).astype(BF)

    qkv1, p1, o1, h1, b1, wrt1 = attn_fwd(x1, second_weights, cos, sin, meta, segr)
    b1_all = flat(spread(1, 4, b1))
    gp1, up1, pos1, gate1, part1 = experts_fwd(1, e_pad, cap, rt_all, wrt1, wg, wu, wd, b1_all)
    dgp1, dup1, hid1, dg1, dpart1 = experts_bwd(1, cap, pos1, gate1, wg, wu, wd, gp1, up1, gy1)
    dback1, dgate1, *dw1 = collect(1, 5, (paired(dpart1), paired(dg1)), (cap, pos1, b1_all, gy1, dgp1, dup1, hid1))

    def gates_back(dg):
        dg = dg[:, :per].reshape(experts, t)
        return jnp.pad(dg, ((0, e_pad - experts), (0, 0)))

    dx1, dd1 = attn_bwd(cot, h1, x1, second_weights, qkv1, p1, o1, b1, wrt1, dback1, gates_back(dgate1), rt_tokens[1], cos, sin)
    gy0 = dx1.astype(BF)

    gy0_all = flat(spread(0, 6, gy0))
    gy0_all, part1 = lax.optimization_barrier((gy0_all, part1))
    crossed = lax.ppermute(paired(part1)[0], "section", [(1, 0)])
    dgp0, dup0, hid0, dg0, dpart0 = experts_bwd(0, cap, pos0, gate0, wg, wu, wd, gp0, up0, gy0_all)
    dback0, dgate0, *dw0 = collect(0, 7, (paired(dpart0), paired(dg0)), (cap, pos0, b0_all, gy0_all, dgp0, dup0, hid0))
    dback0, part1, crossed = lax.optimization_barrier((dback0, part1, crossed))
    back1 = lax.all_to_all(jnp.where(at_zero, crossed, paired(part1)[1]), "expert", split_axis=0, concat_axis=0, tiled=True)
    y1 = (h1 + jnp.sum(back1.astype(F32), axis=0)).astype(BF)
    dx0, dd0 = attn_bwd(gy0, h0, x0, first_weights, qkv0, p0, o0, b0, wrt0, dback0, gates_back(dgate0), rt_tokens[0], cos, sin)

    dense, gate_grad, up_grad, down = finish(9, dd0, dd1, dw0, dw1)

    kept_out = jnp.where(at_zero, x1, y1)
    swapped_out = swap_sections(jnp.where(at_zero, y1, x1))
    layer_out = jnp.where(at_zero, jnp.stack([kept_out, swapped_out]), jnp.stack([swapped_out, kept_out]))
    kept_in = jnp.where(at_zero, dx0, dx1)
    swapped_in = swap_sections(jnp.where(at_zero, dx1, dx0))
    input_grad = jnp.where(at_zero, jnp.stack([kept_in, swapped_in]), jnp.stack([swapped_in, kept_in]))

    return (
        layer_out[None, :, None],
        input_grad[None, :, None],
        dense[:, QKV + QW + GAIN_ATTN_ROW][None],
        dense[:, QKV + QW + GAIN_MOE_ROW][None],
        dense[None, :, 0:QW],
        dense[None, :, QW : QW + KW],
        dense[None, :, QW + KW : QKV],
        dense[:, QKV : QKV + QW].T[None],
        dense[None, :, QKV + QW : QKV + QW + experts],
        gate_grad[None],
        up_grad[None],
        down[None],
    )


def solution(mesh):
    return jax.shard_map(
        local,
        mesh=mesh,
        in_specs=(
            P(None, ("group", "expert"), None, None),
            P(None, ("group", "expert"), None, None),
            P(None, ("group", "expert"), None),
            P(None, ("group", "expert"), None),
            P("section", None, ("group", "expert"), None, None),
            P("section", ("group", "expert")),
            P("section", ("group", "expert")),
            P("section", ("group", "expert"), None),
            P("section", ("group", "expert"), None),
            P("section", ("group", "expert"), None),
            P("section", None, ("group", "expert")),
            P("section", ("group", "expert"), None),
            P("section", "expert", None, None),
            P("section", "expert", None, None),
            P("section", "expert", None, None),
        ),
        out_specs=(
            P("section", None, ("group", "expert"), None, None),
            P("section", None, ("group", "expert"), None, None),
            P("section", ("group", "expert")),
            P("section", ("group", "expert")),
            P("section", ("group", "expert"), None),
            P("section", ("group", "expert"), None),
            P("section", ("group", "expert"), None),
            P("section", None, ("group", "expert")),
            P("section", ("group", "expert"), None),
            P("section", "expert", "group", None),
            P("section", "expert", "group", None),
            P("section", "expert", None, "group"),
        ),
        check_vma=False,
    )
```

```python
import functools
import types

import jax
import jax.numpy as jnp
from jax import lax
from jax.experimental import pallas as pl
from jax.experimental.pallas import tpu as pltpu
from jax.sharding import PartitionSpec as P

QUERY_HEADS = 24
KEY_VALUE_HEADS = 8
HEAD_SIZE = 64
BLK = 64
EPS = 1e-06
THETA = 10000.0
NEG_FILL = -1e30
BF = jnp.bfloat16
F32 = jnp.float32
MESH = pl.DeviceIdType.MESH
LANES = 128
TILE = 512
QW = QUERY_HEADS * HEAD_SIZE
KW = KEY_VALUE_HEADS * HEAD_SIZE
QKV = QW + 2 * KW
GAIN_MOE_ROW = 126
GAIN_ATTN_ROW = 127
VMEM_LIMIT = 60 * 1024 * 1024
HEAD_PAIRS = KEY_VALUE_HEADS // 2
TILES_PER_PAIR = QUERY_HEADS // KEY_VALUE_HEADS


def dot(a, b, ca=1, cb=0):
    return lax.dot_general(a, b, (((ca,), (cb,)), ((), ())), preferred_element_type=F32)


def iota(shape, axis):
    return lax.broadcasted_iota(jnp.int32, shape, axis)


def rope(z, cos, sin, direction):
    width = z.shape[1]
    half = HEAD_SIZE // 2
    first = iota(z.shape, 1) % HEAD_SIZE < half
    partner = jnp.where(first, pltpu.roll(z, width - half, 1), pltpu.roll(z, half, 1))
    signed = jnp.where(first, -direction, direction) * partner
    reps = width // LANES
    return z * jnp.concatenate([cos] * reps, axis=1) + signed * jnp.concatenate([sin] * reps, axis=1)


def lane_masks(t):
    low = iota((t, LANES), 1) < HEAD_SIZE
    return low, jnp.logical_not(low)


def swapped(z):
    return pltpu.roll(z.astype(F32), HEAD_SIZE, 1).astype(BF)


def head_plan():
    return [(r, half, (2 * r + half) // TILES_PER_PAIR != half) for r in range(TILES_PER_PAIR) for half in range(2)]


def pick(z, half, masks):
    return jnp.where(masks[half], z, jnp.zeros_like(z))


def attn_fwd_kernel(x_ref, w_ref, cos_ref, sin_ref, meta_ref, segr_ref, qkv_ref, p_ref, o_ref, h_ref, b_ref, wrt_ref):
    t, d = x_ref.shape
    aux = jnp.transpose(w_ref[:, QKV + QW :].astype(F32))
    wrt_ref[...] = aux.astype(BF)
    gain_attn = aux[GAIN_ATTN_ROW : GAIN_ATTN_ROW + 1]
    gain_moe = aux[GAIN_MOE_ROW : GAIN_MOE_ROW + 1]
    x = x_ref[...].astype(F32)
    r1 = lax.rsqrt(jnp.mean(x * x, axis=1, keepdims=True) + EPS)
    a = (x * r1 * gain_attn).astype(BF)
    cos, sin = cos_ref[...], sin_ref[...]
    for n in range(QKV // TILE):
        cols = slice(n * TILE, (n + 1) * TILE)
        y = dot(a, w_ref[:, cols])
        if n * TILE < QW + KW:
            y = rope(y, cos, sin, 1.0)
        qkv_ref[:, cols] = y.astype(BF)
    i, j = iota((t, t), 0), iota((t, t), 1)
    allowed = (j <= i) & (meta_ref[:, 0:1] == segr_ref[0:1, :]) & (j // BLK >= meta_ref[:, 1:2])
    masks = lane_masks(t)

    def pair(m, carry):
        def lanes(base):
            return pl.ds(pl.multiple_of(base, LANES), LANES)

        kp = qkv_ref[:, lanes(QW + m * LANES)]
        vp = qkv_ref[:, lanes(QW + KW + m * LANES)]
        ks, vs = swapped(kp), swapped(vp)
        parts = {}
        for r, half, swap in head_plan():
            q = pick(qkv_ref[:, lanes((m * TILES_PER_PAIR + r) * LANES)], half, masks)
            s = dot(q, ks if swap else kp, 1, 1) * HEAD_SIZE ** (-0.5)
            s = jnp.where(allowed, s, NEG_FILL)
            e = jnp.exp(s - jnp.max(s, axis=1, keepdims=True))
            p = e / jnp.sum(e, axis=1, keepdims=True)
            p_ref[m * 2 * TILES_PER_PAIR + 2 * r + half] = p
            part = dot(p.astype(BF), pick(vs if swap else vp, half, masks))
            parts[half] = part
            if half == 1:
                o_ref[:, lanes((m * TILES_PER_PAIR + r) * LANES)] = (parts[0] + parts[1]).astype(BF)
        return carry

    lax.fori_loop(0, HEAD_PAIRS, pair, 0)
    o = o_ref[...]
    for n in range(d // TILE):
        rows = slice(n * TILE, (n + 1) * TILE)
        h_ref[:, rows] = x_ref[:, rows].astype(F32) + dot(o, w_ref[rows, QKV : QKV + QW], 1, 1)
    h = h_ref[...]
    r2 = lax.rsqrt(jnp.mean(h * h, axis=1, keepdims=True) + EPS)
    b_ref[...] = (h * r2 * gain_moe).astype(BF)


def vmem(n):
    return [pl.BlockSpec(memory_space=pltpu.VMEM)] * n


def attn_fwd(x, w, cos, sin, meta, segr):
    t, d = x.shape
    sds = jax.ShapeDtypeStruct
    return pl.pallas_call(
        attn_fwd_kernel,
        out_shape=(
            sds((t, QKV), BF),
            sds((QUERY_HEADS, t, t), F32),
            sds((t, QW), BF),
            sds((t, d), F32),
            sds((t, d), BF),
            sds((LANES, d), BF),
        ),
        in_specs=vmem(6),
        out_specs=tuple(vmem(6)),
        compiler_params=pltpu.CompilerParams(vmem_limit_bytes=VMEM_LIMIT),
        cost_estimate=pl.CostEstimate(flops=2 * t * d * 4096, bytes_accessed=w.size * 2, transcendentals=QUERY_HEADS * t * t),
    )(x, w, cos, sin, meta, segr)


def gates_of(rt, wrt, b, e_pad):
    t = rt.shape[1]
    experts = iota((e_pad, t), 0)
    chosen = experts == rt[0:1]
    for k in range(1, rt.shape[0]):
        chosen = chosen | (experts == rt[k : k + 1])
    logits = jnp.where(chosen, dot(wrt[0:e_pad], b, 1, 1), NEG_FILL)
    e = jnp.where(chosen, jnp.exp(logits - jnp.max(logits, axis=0, keepdims=True)), 0.0)
    return e / jnp.sum(e, axis=0, keepdims=True)


def attn_bwd_kernel(
    e_pad, gy_ref, h_ref, x_ref, w_ref, qkv_ref, p_ref, o_ref, b_ref, wrt_ref, back_ref, dg_ref, rt_ref, cos_ref, sin_ref,
    dx_ref, dd_ref, do_ref, dqkv_ref, dh_ref, lt_ref,
):
    t, d = x_ref.shape
    gain_attn = wrt_ref[GAIN_ATTN_ROW - 7 :, :].astype(F32)[7:8]
    gain_moe = wrt_ref[GAIN_ATTN_ROW - 7 :, :].astype(F32)[6:7]
    b = b_ref[...]
    gates = gates_of(rt_ref[...], wrt_ref, b, e_pad)
    dg = dg_ref[...]
    dl = (gates * (dg - jnp.sum(gates * dg, axis=0, keepdims=True)))
    dlb = dl.astype(BF)
    db = dot(dlb, wrt_ref[0:e_pad, :], 0, 0)
    for z in range(back_ref.shape[0]):
        db = db + back_ref[z].astype(F32)
    h = h_ref[...]
    r2 = lax.rsqrt(jnp.mean(h * h, axis=1, keepdims=True) + EPS)
    grad_moe = jnp.sum(db * h * r2, axis=0, keepdims=True)
    dn = db * gain_moe
    dh = gy_ref[...].astype(F32) + r2 * dn - h * (r2 * r2 * r2) * jnp.mean(dn * h, axis=1, keepdims=True)
    dh_ref[...] = dh
    dhb = dh.astype(BF)
    for n in range(QW // TILE):
        cols = slice(n * TILE, (n + 1) * TILE)
        do_ref[:, cols] = dot(dhb, w_ref[:, QKV + n * TILE : QKV + (n + 1) * TILE]).astype(BF)
    masks = lane_masks(t)
    cos, sin = cos_ref[...], sin_ref[...]

    def pair(m, carry):
        def lanes(base):
            return pl.ds(pl.multiple_of(base, LANES), LANES)

        kp = qkv_ref[:, lanes(QW + m * LANES)]
        vp = qkv_ref[:, lanes(QW + KW + m * LANES)]
        ks, vs = swapped(kp), swapped(vp)
        zero = jnp.zeros((t, LANES), F32)
        dk = {False: zero, True: zero}
        dv = {False: zero, True: zero}
        dq = zero
        for r, half, swap in head_plan():
            tile = lanes((m * TILES_PER_PAIR + r) * LANES)
            q = pick(qkv_ref[:, tile], half, masks)
            do = pick(do_ref[:, tile], half, masks)
            p = p_ref[m * 2 * TILES_PER_PAIR + 2 * r + half]
            dp = dot(do, vs if swap else vp, 1, 1)
            dv[swap] = dv[swap] + dot(p.astype(BF), do, 0, 0)
            dt = p * (dp - jnp.sum(p * dp, axis=1, keepdims=True)) * HEAD_SIZE ** (-0.5)
            dt = dt.astype(BF)
            dk[swap] = dk[swap] + dot(dt, q, 0, 0)
            part = dot(dt, pick(ks if swap else kp, half, masks))
            dq = part if half == 0 else dq + part
            if half == 1:
                dqkv_ref[:, tile] = rope(dq, cos, sin, -1.0).astype(BF)
        dk_all = dk[False] + pltpu.roll(dk[True], HEAD_SIZE, 1)
        dv_all = dv[False] + pltpu.roll(dv[True], HEAD_SIZE, 1)
        dqkv_ref[:, lanes(QW + m * LANES)] = rope(dk_all, cos, sin, -1.0).astype(BF)
        dqkv_ref[:, lanes(QW + KW + m * LANES)] = dv_all.astype(BF)
        return carry

    lax.fori_loop(0, HEAD_PAIRS, pair, 0)
    x = x_ref[...].astype(F32)
    r1 = lax.rsqrt(jnp.mean(x * x, axis=1, keepdims=True) + EPS)
    dqkv = dqkv_ref[...]
    for n in range(d // TILE):
        rows = slice(n * TILE, (n + 1) * TILE)
        dx_ref[:, rows] = dot(dqkv, w_ref[rows, 0:QKV], 1, 1)
    da = dx_ref[...]
    grad_attn = jnp.sum(da * x * r1, axis=0, keepdims=True)
    dag = da * gain_attn
    dx_ref[...] = dh_ref[...] + r1 * dag - x * (r1 * r1 * r1) * jnp.mean(dag * x, axis=1, keepdims=True)
    lt_ref[...] = jnp.transpose(x * r1 * gain_attn).astype(BF)
    for n in range(QKV // TILE):
        cols = slice(n * TILE, (n + 1) * TILE)
        dd_ref[:, cols] = dot(lt_ref[...], dqkv_ref[:, cols]).astype(BF)
    lt_ref[...] = jnp.transpose(dh_ref[...]).astype(BF)
    for n in range(QW // TILE):
        cols = slice(n * TILE, (n + 1) * TILE)
        dd_ref[:, QKV + n * TILE : QKV + (n + 1) * TILE] = dot(lt_ref[...], o_ref[:, cols]).astype(BF)
    lt_ref[...] = jnp.transpose(b_ref[...].astype(F32)).astype(BF)
    row = iota((LANES, d), 0)
    grads = jnp.where(row == GAIN_MOE_ROW, grad_moe, jnp.where(row == GAIN_ATTN_ROW, grad_attn, 0.0))
    dl_full = jnp.concatenate([dl, jnp.zeros((LANES - e_pad, t), F32)], axis=0)
    dl_rows = jnp.transpose(dl_full).astype(BF)
    dd_ref[:, QKV + QW :] = (dot(lt_ref[...], dl_rows) + jnp.transpose(grads)).astype(BF)


def attn_bwd(gy, h, x, w, qkv, p, o, b, wrt, back, dg, rt, cos, sin):
    t, d = x.shape
    sds = jax.ShapeDtypeStruct
    return pl.pallas_call(
        functools.partial(attn_bwd_kernel, dg.shape[0]),
        out_shape=(sds((t, d), F32), sds(w.shape, BF)),
        in_specs=vmem(14),
        out_specs=tuple(vmem(2)),
        scratch_shapes=[
            pltpu.VMEM((t, QW), BF),
            pltpu.VMEM((t, QKV), BF),
            pltpu.VMEM((t, d), F32),
            pltpu.VMEM((d, t), BF),
        ],
        compiler_params=pltpu.CompilerParams(vmem_limit_bytes=VMEM_LIMIT),
        cost_estimate=pl.CostEstimate(flops=4 * t * d * 4096, bytes_accessed=w.size * 4, transcendentals=0),
    )(gy, h, x, w, qkv, p, o, b, wrt, back, dg, rt, cos, sin)


def one_hot(pos_row, cap):
    return jnp.where(iota((cap, pos_row.shape[1]), 0) == pos_row, 1.0, 0.0)


def all_hots(pos, per, cap):
    return jnp.concatenate([one_hot(pos[j : j + 1], cap) for j in range(per)], axis=0)


def all_hots_back(pos, per, cap):
    width = per * cap
    expert = jnp.where(iota((8, width), 1) // cap == iota((8, width), 0), 1.0, 0.0).astype(BF)
    wide = dot(pos.astype(F32).astype(BF), expert, 0, 0)
    slot = (iota((1, width), 1) % cap).astype(F32)
    return jnp.where(wide == slot, 1.0, 0.0).astype(BF)


def slots_of(rt, first, per):
    t = rt.shape[1]
    experts = iota((16, t), 0)
    mine = jnp.where(experts < per, experts + first, -1)
    chosen = mine == rt[0:1]
    for k in range(1, rt.shape[0]):
        chosen = chosen | (mine == rt[k : k + 1])
    earlier = jnp.where(iota((t, t), 0) < iota((t, t), 1), 1.0, 0.0).astype(BF)
    before = dot(jnp.where(chosen, 1.0, 0.0).astype(BF), earlier)
    return jnp.where(chosen, before.astype(jnp.int32), -1)[0:8]


def streamed(count, copies, body, primed=False):
    if not primed:
        for c in copies(0, 0):
            c.start()

    def step(b, carry):
        slot = lax.rem(b, 2)

        @pl.when(b + 1 < count)
        def _():
            for c in copies(b + 1, lax.rem(b + 1, 2)):
                c.start()

        for c in copies(b, slot):
            c.wait()
        body(b, slot)
        return carry

    lax.fori_loop(0, count, step, 0)


def combine(base, count, per, cap, pos_ref, rows_ref, out_hbm, obuf, osem):
    def copy(b, slot):
        return pltpu.make_async_copy(obuf.at[slot], out_hbm.at[b], osem.at[slot])

    def step(b, carry):
        slot = lax.rem(b, 2)

        @pl.when(b >= 2)
        def _():
            copy(b - 2, slot).wait()

        back = all_hots_back(pos_ref[base + b], per, cap)
        at = pl.ds(pl.multiple_of((base + b) * cap, cap), cap)
        rows = jnp.concatenate([rows_ref[j, at, :] for j in range(per)], axis=0)
        obuf[slot] = dot(back, rows).astype(BF)
        copy(b, slot).start()
        return carry

    lax.fori_loop(0, count, step, 0)
    copy(count - 2, (count - 2) % 2).wait()
    copy(count - 1, (count - 1) % 2).wait()


def chunk_gates(c, j, chunk, cap, pos_ref, gate_ref):
    hots, gates = [], []
    for bb in range(chunk // cap):
        b = c * (chunk // cap) + bb
        hot = one_hot(pos_ref[b, pl.ds(j, 1), :], cap)
        hots.append(hot)
        gates.append(jnp.sum(hot * gate_ref[b, pl.ds(j, 1), :], axis=1, keepdims=True))
    return hots, jnp.concatenate(gates, axis=0)


def any_spec():
    return pl.BlockSpec(memory_space=pl.ANY)


def put_rows(hots, block, b, per, cap, dest):
    at = pl.ds(pl.multiple_of(b * cap, cap), cap)
    rows = dot(hots, block).astype(BF)
    for k in range(per):
        dest[k, at, :] = rows[k * cap : (k + 1) * cap]


def gather_from(count, per, cap, pos, source, dest, buf, sem):
    def body(b, slot):
        put_rows(all_hots(pos[b], per, cap).astype(BF), buf[slot], b, per, cap, dest)

    streamed(count, lambda b, slot: [pltpu.make_async_copy(source.at[b], buf.at[slot], sem.at[slot])], body)


def weight_grads(r, per):
    parts, piece = r.even.shape[0], r.even.shape[3]
    g = lax.axis_index("group")
    parity, place = lax.rem(g, 2), g // 2

    def outgoing(j, at, slot):
        return [
            pltpu.make_async_copy(r.gu_buf.at[slot, 0], r.even.at[at, :, j], r.gu_sem.at[slot, 0]),
            pltpu.make_async_copy(r.gu_buf.at[slot, 1], r.odd.at[at, :, j], r.gu_sem.at[slot, 1]),
            pltpu.make_async_copy(r.dn_buf.at[slot, 0], r.even_dn.at[at, j], r.dn_sem.at[slot, 0]),
            pltpu.make_async_copy(r.dn_buf.at[slot, 1], r.odd_dn.at[at, j], r.dn_sem.at[slot, 1]),
        ]

    def finished(slot):
        for c in outgoing(0, 0, slot):
            c.wait()

    def body(j, carry):
        for q in range(parts):
            slot = q % 2
            if q >= 2:
                finished(slot)
            else:

                @pl.when(j > 0)
                def _():
                    finished(slot)

            cols = slice(2 * q * piece, 2 * (q + 1) * piece)
            for m in range(2):
                full = dot(r.x_scr[j, :, cols], r.act[m, j], 0, 0).astype(BF)
                r.gu_buf[slot, parity, m] = full[:piece]
                r.gu_buf[slot, 1 - parity, m] = full[piece:]
            full = dot(r.act[2, j], r.y_scr[j, :, cols], 0, 0).astype(BF)
            r.dn_buf[slot, parity] = full[:, :piece]
            r.dn_buf[slot, 1 - parity] = full[:, piece:]
            for c in outgoing(j, lax.bitwise_xor(place, q), slot):
                c.start()
        return carry

    lax.fori_loop(0, per, body, 0)
    for slot in range(2):
        finished(slot)


def meet(n, with_cross):
    s, z = lax.axis_index("section"), lax.axis_index("expert")
    barrier = pltpu.get_barrier_semaphore()
    for k in range(1, n):
        pl.semaphore_signal(barrier, inc=1, device_id={"expert": lax.rem(z + k, n)}, device_id_type=MESH)
    for k in range(n if with_cross else 1):
        pl.semaphore_signal(
            barrier, inc=1, device_id={"section": 1 - s, "expert": lax.rem(z + k, n)}, device_id_type=MESH
        )
    pl.semaphore_wait(barrier, 2 * n - 1 if with_cross else n)


def moe_kernel(layer, mode, n, e_pad, cap, names, *refs):
    r = types.SimpleNamespace(**dict(zip(names, refs)))
    forward, backward = mode != "bwd", mode != "fwd"
    s, z = lax.axis_index("section"), lax.axis_index("expert")
    here = s == layer
    count = 2 * n
    per, rows, d = r.y_scr.shape
    first = z * per
    chunk = 256
    remote = functools.partial(pltpu.make_async_remote_copy, device_id_type=MESH)
    other = {"section": 1 - s}
    meet(n, False)
    r.blk[s, z] = r.own[...]

    def weights(j, slot):
        both = [
            pltpu.make_async_copy(r.wg.at[j], r.wg_buf.at[slot], r.w_sem.at[slot, 0]),
            pltpu.make_async_copy(r.wu.at[j], r.wu_buf.at[slot], r.w_sem.at[slot, 1]),
            pltpu.make_async_copy(r.wd.at[j], r.wd_buf.at[slot], r.w_sem.at[slot, 2]),
        ]
        if mode == "bwd":
            both.append(pltpu.make_async_copy(r.gp.at[j], r.gp_buf.at[slot], r.gp_sem.at[slot, 0]))
            both.append(pltpu.make_async_copy(r.up.at[j], r.gp_buf.at[2 + slot], r.gp_sem.at[slot, 1]))
        return both

    def chain(to, zz, t, ssem, rsem):
        return remote(
            src_ref=r.blk.at[s, zz], dst_ref=r.blk.at[s, zz], send_sem=ssem.at[t], recv_sem=rsem.at[t], device_id={"expert": to}
        )

    def right(t):
        return chain(z + 1, z - t, t, r.s_right, r.r_right)

    def left(t):
        return chain(z - 1, z + t, t, r.s_left, r.r_left)

    def cross(zz):
        return remote(
            src_ref=r.blk.at[s, zz], dst_ref=r.blk.at[s, zz], send_sem=r.s_cross.at[zz], recv_sem=r.r_cross.at[zz], device_id=other
        )

    def prepare(section, zz):
        b = section * n + zz
        block = r.blk[section, zz]
        if forward:
            rt = r.rt[b]
            pos = slots_of(rt, first, per)
            r.pos[b] = pos
            r.gates[...] = gates_of(rt, r.wrt, block, e_pad)
            r.gate[b] = jnp.concatenate(
                [r.gates[pl.ds(first + k, 1), :] for k in range(per)] + [jnp.zeros((8 - per, rt.shape[1]), F32)], axis=0
            )
            put_rows(all_hots(pos, per, cap).astype(BF), block, b, per, cap, r.x_scr)
        else:
            put_rows(all_hots(r.pos[b], per, cap).astype(BF), block, b, per, cap, r.y_scr)

    @pl.when(here)
    def _():
        for c in weights(0, 0):
            c.start()

    @pl.loop(0, n + 1)
    def _(t):
        from_left = (t < n) & (z >= t)
        from_right = (t < n) & (z + t < n)

        @pl.when(from_left & (t > 0))
        def _():
            right(t - 1).wait_recv()

        @pl.when(from_left & (z < n - 1))
        def _():
            right(t).start()

        @pl.when(from_left & jnp.logical_not(here))
        def _():
            cross(z - t).start()

        @pl.when(from_right & (t > 0))
        def _():
            left(t - 1).wait_recv()

        @pl.when(from_right & (z > 0))
        def _():
            left(t).start()

        @pl.when(from_right & (t > 0) & jnp.logical_not(here))
        def _():
            cross(z + t).start()

        @pl.when(here)
        def _():
            if mode == "both":

                @pl.when(t == 0)
                def _():
                    @pl.loop(0, count)
                    def _(b):
                        r.pos[b] = slots_of(r.rt[b], first, per)

                    gather_from(count, per, cap, r.pos, r.gy, r.y_scr, r.row_buf, r.row_sem)

            u = t - 1

            @pl.when((u >= 0) & (z >= u))
            def _():
                cross(z - u).wait_recv()

            @pl.when((u > 0) & (z + u < n))
            def _():
                cross(z + u).wait_recv()

            def candidate(m, carry):
                on_left = lax.rem(m, 2) == 0
                far = t - m // 2
                zz = jnp.where(on_left, z - far, z + far)
                valid = (far >= 0) & (far < n) & (zz >= 0) & (zz < n) & (on_left | (far > 0))

                @pl.when(valid)
                def _():
                    prepare(jnp.where(m >= 2, 1 - layer, layer), zz)

                return carry

            lax.fori_loop(0, 4, candidate, 0)

    srcs = (r.pbuf, r.dg) if backward else (r.pbuf,)
    outs = (r.back, r.dgate) if backward else (r.back,)
    relays = (r.relay, r.dg_relay) if backward else (r.relay,)
    arrays = range(len(srcs))

    def hop(a, to):
        return remote(
            src_ref=srcs[a].at[1 - layer, to],
            dst_ref=relays[a].at[to],
            send_sem=r.s_hop.at[a, to],
            recv_sem=r.r_hop.at[a, to],
            device_id=other,
        )

    def give(a, source, k):
        return remote(
            src_ref=source,
            dst_ref=outs[a].at[z],
            send_sem=r.s_give.at[a, k],
            recv_sem=r.r_give.at[a, k],
            device_id={"expert": lax.rem(z + k, n)},
        )

    def keep(a, source):
        return pltpu.make_async_copy(source, outs[a].at[z], r.keep_sem.at[a])

    def saved(j, slot):
        return [
            pltpu.make_async_copy(r.gp_buf.at[slot], r.gp.at[j], r.gp_sem.at[slot, 0]),
            pltpu.make_async_copy(r.gp_buf.at[2 + slot], r.up.at[j], r.gp_sem.at[slot, 1]),
        ]

    def expert(j, slot):
        if mode == "fwd":

            @pl.when(j >= 2)
            def _():
                for c in saved(j - 2, slot):
                    c.wait()

        def part(c, carry):
            at = pl.ds(pl.multiple_of(c * chunk, chunk), chunk)
            if forward:
                x = r.x_scr[j, at, :]
                gp = dot(x, r.wg_buf[slot])
                up = dot(x, r.wu_buf[slot])
            else:
                gp, up = r.gp_buf[slot, at, :].astype(F32), r.gp_buf[2 + slot, at, :].astype(F32)
            sg = 1.0 / (1.0 + jnp.exp(-gp))
            silu = gp * sg
            hid = silu * up
            hots, gate = chunk_gates(c, j, chunk, cap, r.pos, r.gate)
            if not backward:
                r.gp_buf[slot, at, :] = gp.astype(BF)
                r.gp_buf[2 + slot, at, :] = up.astype(BF)
                r.y_scr[j, at, :] = (dot(hid.astype(BF), r.wd_buf[slot]) * gate).astype(BF)
                return carry
            raw = dot(r.y_scr[j, at, :], r.wd_buf[slot], 1, 1)
            dgate = jnp.sum(hid.astype(BF).astype(F32) * raw, axis=1, keepdims=True)
            for bb in range(chunk // cap):
                b = c * (chunk // cap) + bb
                r.dg[b // n, lax.rem(b, n), pl.ds(j, 1), :] = jnp.sum(
                    hots[bb] * dgate[bb * cap : (bb + 1) * cap], axis=0, keepdims=True
                )
            dh = raw * gate
            dgp = (dh * up * sg * (1.0 + gp * (1.0 - sg))).astype(BF)
            dup = (dh * silu).astype(BF)
            r.act[0, j, at, :] = dgp
            r.act[1, j, at, :] = dup
            r.act[2, j, at, :] = (hid * gate).astype(BF)
            r.y_scr[j, at, :] = (dot(dgp, r.wg_buf[slot], 1, 1) + dot(dup, r.wu_buf[slot], 1, 1)).astype(BF)
            return carry

        lax.fori_loop(0, rows // chunk, part, 0)
        if mode == "fwd":
            for c in saved(j, slot):
                c.start()

    def summed(b, source):
        at = pl.ds(pl.multiple_of(b * cap, cap), cap)
        stacked = jnp.concatenate([source[j, at, :] for j in range(per)], axis=0)
        return dot(all_hots_back(r.pos[b], per, cap), stacked).astype(BF)

    @pl.when(here)
    def _():
        if backward:
            r.dg[...] = jnp.zeros_like(r.dg)
        if mode == "fwd":
            keep_blocks = pltpu.make_async_copy(r.blk, r.blocks, r.row_sem.at[0])
            keep_blocks.start()
        streamed(per, weights, expert, primed=True)

        def emit(i, carry):
            to = lax.rem(z + i + 1, n)
            section = jnp.where(i < n, 1 - layer, layer)
            r.pbuf[section, to] = summed(section * n + to, r.y_scr)

            @pl.when(i < n)
            def _():
                for a in arrays:
                    hop(a, to).start()

            @pl.when((i >= n) & (to != z))
            def _():
                for a in arrays:
                    give(a, srcs[a].at[layer, to], i + 1 - n).start()

            return carry

        lax.fori_loop(0, 2 * n, emit, 0)
        for a in arrays:
            keep(a, srcs[a].at[layer, z]).start()
        if mode == "fwd":
            for j in (per - 2, per - 1):
                for c in saved(j, j % 2):
                    c.wait()
            keep_blocks.wait()
        if mode == "bwd":

            @pl.loop(0, count)
            def _(b):
                put_rows(all_hots(r.pos[b], per, cap).astype(BF), r.blk[b // n, lax.rem(b, n)], b, per, cap, r.y_scr)

            gather_from(count, per, cap, r.pos, r.blocks, r.x_scr, r.row_buf, r.row_sem)
        if mode == "both":
            gather_from(count, per, cap, r.pos, r.gy, r.y_scr, r.row_buf, r.row_sem)
        if backward:
            weight_grads(r, per)
        if mode == "both":
            def output(j, slot):
                @pl.loop(0, rows // chunk)
                def _(c):
                    at = pl.ds(pl.multiple_of(c * chunk, chunk), chunk)
                    r.x_scr[j, at, :] = dot(r.act[2, j, at, :], r.wd_buf[slot]).astype(BF)

            streamed(per, lambda j, slot: weights(j, slot)[2:], output)
            combine(0, n, per, cap, r.pos, r.x_scr, r.part0, r.row_buf, r.row_sem)
            combine(n, n, per, cap, r.pos, r.x_scr, r.part1, r.row_buf, r.row_sem)
        for to in range(n):
            for a in arrays:
                hop(a, to).wait_send()

    @pl.when(jnp.logical_not(here))
    def _():
        @pl.loop(1, n + 1)
        def _(k):
            to = lax.rem(lax.rem(k, n) + z, n)
            for a in arrays:
                hop(a, to).wait_recv()

            @pl.when(k < n)
            def _():
                for a in arrays:
                    give(a, relays[a].at[to], k).start()

        for a in arrays:
            keep(a, relays[a].at[z]).start()
        for zz in range(n):
            cross(zz).wait_send()

    for a in arrays:
        keep(a, relays[a].at[z]).wait()
        for k in range(1, n):
            give(a, relays[a].at[lax.rem(z + k, n)], k).wait()
    for t in range(n):

        @pl.when((z >= t) & (z < n - 1))
        def _():
            right(t).wait_send()

        @pl.when((z + t < n) & (z > 0))
        def _():
            left(t).wait_send()


def moe(layer, mode, cid, e_pad, cap, own, wg, wu, wd, **given):
    n, groups = lax.axis_size("expert"), lax.axis_size("group")
    count = 2 * n
    t, d = own.shape
    per, _, f = wg.shape
    rows = count * cap
    piece = d // groups
    sds = jax.ShapeDtypeStruct
    dma = pltpu.SemaphoreType.DMA
    vm, hbm = pl.BlockSpec(memory_space=pltpu.VMEM), any_spec()
    on_chip = ("own", "rt", "wrt", "pos", "gate")
    ins = dict(own=own, wg=wg, wu=wu, wd=wd, **given)
    outs = dict(back=sds((n, t, d), BF))
    scratch = dict(
        blk=pltpu.VMEM((2, n, t, d), BF),
        y_scr=pltpu.VMEM((per, rows, d), BF),
        wg_buf=pltpu.VMEM((2, d, f), BF),
        wu_buf=pltpu.VMEM((2, d, f), BF),
        wd_buf=pltpu.VMEM((2, f, d), BF),
        pbuf=pltpu.VMEM((2, n, t, d), BF),
        relay=pltpu.VMEM((n, t, d), BF),
        x_scr=pltpu.VMEM((per, rows, d), BF),
        row_buf=pltpu.VMEM((2, t, d), BF),
        row_sem=dma((2,)),
        w_sem=dma((2, 3)),
        keep_sem=dma((2,)),
    )
    for name in ("right", "left", "cross"):
        scratch["s_" + name] = dma((n,))
        scratch["r_" + name] = dma((n,))
    for name in ("hop", "give"):
        scratch["s_" + name] = dma((2, n))
        scratch["r_" + name] = dma((2, n))
    if mode != "both":
        scratch["gp_buf"] = pltpu.VMEM((4, rows, f), BF)
        scratch["gp_sem"] = dma((2, 2))
    if mode != "bwd":
        scratch["gates"] = pltpu.VMEM((e_pad, t), F32)
    if mode == "fwd":
        del scratch["row_buf"]
        outs.update(pos=sds((count, 8, t), jnp.int32), gate=sds((count, 8, t), F32))
        outs.update(gp=sds((per, rows, f), BF), up=sds((per, rows, f), BF), blocks=sds((2, n, t, d), BF))
    else:
        outs["dgate"] = sds((n, 8, t), F32)
        outs["even"] = outs["odd"] = sds((groups // 2, 2, per, piece, f), BF)
        outs["even_dn"] = outs["odd_dn"] = sds((groups // 2, per, f, piece), BF)
        scratch.update(
            dg=pltpu.VMEM((2, n, 8, t), F32),
            dg_relay=pltpu.VMEM((n, 8, t), F32),
            act=pltpu.VMEM((3, per, rows, f), BF),
            gu_buf=pltpu.VMEM((2, 2, 2, piece, f), BF),
            dn_buf=pltpu.VMEM((2, 2, f, piece), BF),
            gu_sem=dma((2, 2)),
            dn_sem=dma((2, 2)),
        )
    if mode == "both":
        outs["part0"] = outs["part1"] = sds((n, t, d), BF)
        scratch.update(pos=pltpu.VMEM((count, 8, t), jnp.int32), gate=pltpu.VMEM((count, 8, t), F32))
    names = tuple(ins) + tuple(outs) + tuple(scratch)
    results = pl.pallas_call(
        functools.partial(moe_kernel, layer, mode, n, e_pad, cap, names),
        out_shape=tuple(outs.values()),
        in_specs=[vm if name in on_chip else hbm for name in ins],
        out_specs=tuple(vm if name in on_chip else hbm for name in outs),
        scratch_shapes=list(scratch.values()),
        compiler_params=pltpu.CompilerParams(collective_id=cid, has_side_effects=True, vmem_limit_bytes=VMEM_LIMIT),
    )(*ins.values())
    return types.SimpleNamespace(**dict(zip(outs, results)))


def top_bit(q):
    return q.bit_length() - 1


def finish_kernel(
    n, dd0, dd1, egu0, ogu0, ed0, od0, egu1, ogu1, ed1, od1,
    dense_out, gate_out, up_out, down_out,
    core_gu, core_dn, hop_gu, hop_dn, core_dd, hop_y, hop_z, hop_x, dd_buf, gu_buf, dn_buf, gu_f32, dn_f32,
    s_core_gu, r_core_gu, s_core_dn, r_core_dn, s_hop_gu, r_hop_gu, s_hop_dn, r_hop_dn,
    s_core_dd, r_core_dd, s_y, r_y, s_z, r_z, s_x, r_x, l_dd, l_gu, l_dn, o_gu, o_dn,
):
    s, g, z = lax.axis_index("section"), lax.axis_index("group"), lax.axis_index("expert")
    pairs, cgu = core_gu.shape[:2]
    cdn = core_dn.shape[1]
    levels = top_bit(pairs)
    units = pairs * n
    remote = functools.partial(pltpu.make_async_remote_copy, device_id_type=MESH)
    twin = {"group": lax.bitwise_xor(g, 1)}
    other = {"section": 1 - s}

    def across(k):
        return {"group": lax.bitwise_xor(g, 2 << k)}

    barrier = pltpu.get_barrier_semaphore()
    peers = [twin, other] + [across(k) for k in range(levels)] + [{"expert": lax.rem(z + k, n)} for k in range(1, n)]
    for peer in peers:
        pl.semaphore_signal(barrier, inc=1, device_id=peer, device_id_type=MESH)
    pl.semaphore_wait(barrier, len(peers))

    def by_section(action):
        @pl.when(s == 0)
        def _():
            action(dd0, dd1, egu0, ogu0, ed0, od0)

        @pl.when(s != 0)
        def _():
            action(dd1, dd0, egu1, ogu1, ed1, od1)

    def unit(i):
        return pairs - 1 - i // n, lax.rem(z + 1 + lax.rem(i, n), n)

    def shard(i, core):
        q, place = unit(i)
        return (lax.bitwise_xor(g // 2, q) * 2 + core) * n + place

    core = lax.rem(g, 2)

    def core_dd_copy(kind, i, source):
        return remote(
            src_ref=source.at[shard(i, 1 - core)],
            dst_ref=core_dd.at[kind, i],
            send_sem=s_core_dd.at[kind, i],
            recv_sem=r_core_dd.at[kind, i],
            device_id=twin,
        )

    def core_chunk(source, dest, ssem, rsem, q, c):
        return remote(
            src_ref=source.at[q, c], dst_ref=dest.at[q, c], send_sem=ssem.at[q, c], recv_sem=rsem.at[q, c], device_id=twin
        )

    def core_gu_copy(source, q, c):
        return core_chunk(source, core_gu, s_core_gu, r_core_gu, q, c)

    def core_dn_copy(source, q, c):
        return core_chunk(source, core_dn, s_core_dn, r_core_dn, q, c)

    def send_all(own, away, egu, ogu, ed, od):
        @pl.loop(0, units)
        def _(i):
            core_dd_copy(0, i, away).start()

            @pl.when(i < cgu)
            def _():
                core_gu_copy(ogu, pairs - 1, i).start()

            @pl.when(i < cdn)
            def _():
                core_dn_copy(od, pairs - 1, i).start()

        for i in range(units, max(cgu, cdn)):
            if i < cgu:
                core_gu_copy(ogu, pairs - 1, i).start()
            if i < cdn:
                core_dn_copy(od, pairs - 1, i).start()

        @pl.loop(0, units)
        def _(i):
            core_dd_copy(1, i, own).start()

        for q in reversed(range(pairs - 1)):

            @pl.loop(0, cgu)
            def _(c):
                core_gu_copy(ogu, q, c).start()

            @pl.loop(0, cdn)
            def _(c):
                core_dn_copy(od, q, c).start()

    by_section(send_all)

    def load(buf, sem, slot, source):
        return pltpu.make_async_copy(source, buf.at[slot], sem.at[slot])

    def dd_load(i, slot, source):
        return load(dd_buf, l_dd, slot, source.at[shard(i, core)])

    def hop(dest, ssem, rsem, source, k, q, c):
        return remote(
            src_ref=source.at[q, c],
            dst_ref=dest.at[k, q - (1 << k), c],
            send_sem=ssem.at[k, q - (1 << k), c],
            recv_sem=rsem.at[k, q - (1 << k), c],
            device_id=across(k),
        )

    def gu_hop(k, q, c):
        return hop(hop_gu, s_hop_gu, r_hop_gu, core_gu, k, q, c)

    def dn_hop(k, q, c):
        return hop(hop_dn, s_hop_dn, r_hop_dn, core_dn, k, q, c)

    def y_copy(i):
        return remote(src_ref=core_dd.at[0, i], dst_ref=hop_y.at[i], send_sem=s_y.at[i], recv_sem=r_y.at[i], device_id=other)

    def z_copy(q, k, i):
        return remote(
            src_ref=core_dd.at[1, i],
            dst_ref=hop_z.at[k - 1, q],
            send_sem=s_z.at[k - 1, q],
            recv_sem=r_z.at[k - 1, q],
            device_id={"expert": lax.rem(z + k, n)},
        )

    def x_copy(k, q, i):
        return remote(
            src_ref=core_dd.at[1, i],
            dst_ref=hop_x.at[k, q - (1 << k)],
            send_sem=s_x.at[k, q - (1 << k)],
            recv_sem=r_x.at[k, q - (1 << k)],
            device_id=across(k),
        )

    def chunk_start(i, slot, q, egu, ed):
        @pl.when(i < cgu)
        def _():
            load(gu_buf, l_gu, slot, egu.at[q, i]).start()

        @pl.when(i < cdn)
        def _():
            load(dn_buf, l_dn, slot, ed.at[q, i]).start()

    def expert_sum(hops, rsem, dest, core_r, buf, sem, slot, even, q, c, hop_copy):
        load(buf, sem, slot, even.at[q, c]).wait()
        core_r(q, c).wait_recv()
        total = buf[slot].astype(F32) + dest[q, c].astype(F32)
        for k in range(top_bit(q) + 1 if q else 0, levels):
            hop_copy(k, q + (1 << k), c).wait_recv()
            total = total + hops[k, q, c].astype(F32)
        return total

    def gu_sum(slot, q, c):
        return expert_sum(hop_gu, r_hop_gu, core_gu, functools.partial(core_gu_copy, ogu0), gu_buf, l_gu, slot, egu0, q, c, gu_hop)

    def dn_sum(slot, q, c):
        return expert_sum(hop_dn, r_hop_dn, core_dn, functools.partial(core_dn_copy, od0), dn_buf, l_dn, slot, ed0, q, c, dn_hop)

    def stepped(count, start, body):
        start(0, 0)

        def step(i, carry):
            @pl.when(i + 1 < count)
            def _():
                start(i + 1, lax.rem(i + 1, 2))

            body(i, lax.rem(i, 2))
            return carry

        lax.fori_loop(0, count, step, 0)

    for q in reversed(range(1, pairs)):
        dense_too = q == pairs - 1
        steps = max(units, cgu, cdn) if dense_too else max(cgu, cdn)

        def start(i, slot):
            def go(own, away, egu, ogu, ed, od):
                if dense_too:

                    @pl.when(i < units)
                    def _():
                        dd_load(i, slot, away).start()

                chunk_start(i, slot, q, egu, ed)

            by_section(go)

        def body(i, slot):
            if dense_too:

                @pl.when(i < units)
                def _():
                    dd_load(i, slot, dd0).wait()
                    core_dd_copy(0, i, dd0).wait_recv()
                    core_dd[0, i] = core_dd[0, i] + dd_buf[slot]
                    y_copy(i).start()

            @pl.when(i < cgu)
            def _():
                core_gu[q, i] = gu_sum(slot, q, i).astype(BF)
                gu_hop(top_bit(q), q, i).start()

            @pl.when(i < cdn)
            def _():
                core_dn[q, i] = dn_sum(slot, q, i).astype(BF)
                dn_hop(top_bit(q), q, i).start()

        stepped(steps, start, body)

    def gu_out_copy(c, slot, to=gate_out):
        return pltpu.make_async_copy(gu_f32.at[slot], to.at[lax.rem(c, cgu // 2)], o_gu.at[slot])

    def dn_out_copy(c, slot):
        return pltpu.make_async_copy(dn_f32.at[slot], down_out.at[c], o_dn.at[slot])

    def dense_sum(q):
        i = (pairs - 1 - q) * n + n - 1
        total = core_dd[1, i].astype(F32)
        for k in range(1, n):
            z_copy(q, k, i).wait_recv()
            total = total + hop_z[k - 1, q].astype(F32)
        for k in range(top_bit(q) + 1 if q else 0, levels):
            x_copy(k, q + (1 << k), i).wait_recv()
            total = total + hop_x[k, q].astype(F32)
        return i, total

    def pass_on(q):
        i, total = dense_sum(q)
        core_dd[1, i] = total.astype(BF)
        x_copy(top_bit(q), q, i).start()

    steps = max(units, cgu, cdn)

    def start(i, slot):
        def go(own, away, egu, ogu, ed, od):
            @pl.when(i < units)
            def _():
                dd_load(i, slot, own).start()

            chunk_start(i, slot, 0, egu, ed)

        by_section(go)

    def body(i, slot):
        @pl.when(i < units)
        def _():
            dd_load(i, slot, dd0).wait()
            core_dd_copy(1, i, dd0).wait_recv()
            y_copy(i).wait_recv()
            core_dd[1, i] = (core_dd[1, i].astype(F32) + dd_buf[slot].astype(F32) + hop_y[i].astype(F32)).astype(BF)
            q, _ = unit(i)
            k = lax.rem(i, n) + 1

            @pl.when(k < n)
            def _():
                z_copy(q, k, i).start()

        for q in range(1, pairs):

            @pl.when(i == (pairs - q) * n + min(2, n - 1))
            def _():
                pass_on(q)

        @pl.when(i < cgu)
        def _():
            @pl.when(i >= 2)
            def _():
                gu_out_copy(i - 2, slot).wait()

            gu_f32[slot] = gu_sum(slot, 0, i)

            @pl.when(i < cgu // 2)
            def _():
                gu_out_copy(i, slot).start()

            @pl.when(i >= cgu // 2)
            def _():
                gu_out_copy(i, slot, up_out).start()

        @pl.when(i < cdn)
        def _():
            @pl.when(i >= 2)
            def _():
                dn_out_copy(i - 2, slot).wait()

            dn_f32[slot] = dn_sum(slot, 0, i)
            dn_out_copy(i, slot).start()

    stepped(steps, start, body)
    _, total = dense_sum(0)
    dense_out[...] = total
    for c in (cgu - 2, cgu - 1):
        gu_out_copy(c, c % 2).wait()
    for c in (cdn - 2, cdn - 1):
        dn_out_copy(c, c % 2).wait()

    @pl.loop(0, units)
    def _(i):
        core_dd_copy(0, i, dd0).wait_send()
        core_dd_copy(1, i, dd0).wait_send()
        y_copy(i).wait_send()
        q, _ = unit(i)
        k = lax.rem(i, n) + 1

        @pl.when(k < n)
        def _():
            z_copy(q, k, i).wait_send()

    for q in range(pairs):
        if q:
            x_copy(top_bit(q), q, (pairs - 1 - q) * n + n - 1).wait_send()

        @pl.loop(0, cgu)
        def _(c):
            core_gu_copy(ogu0, q, c).wait_send()
            if q:
                gu_hop(top_bit(q), q, c).wait_send()

        @pl.loop(0, cdn)
        def _(c):
            core_dn_copy(od0, q, c).wait_send()
            if q:
                dn_hop(top_bit(q), q, c).wait_send()


def finish(cid, dd0, dd1, experts0, experts1):
    n, groups = lax.axis_size("expert"), lax.axis_size("group")
    pairs, levels = groups // 2, top_bit(groups // 2)
    width = dd0.shape[1]
    rows = dd0.shape[0] // (groups * n)
    dd0, dd1 = (v.reshape(groups * n, rows, width) for v in (dd0, dd1))

    def chunked(arrays):
        gu_even, gu_odd, dn_even, dn_odd = arrays
        flat = (pairs, -1) + gu_even.shape[3:]
        return gu_even.reshape(flat), gu_odd.reshape(flat), dn_even, dn_odd

    experts0, experts1 = chunked(experts0), chunked(experts1)
    gu, dn = experts0[0].shape[1:], experts0[2].shape[1:]
    units = pairs * n
    dma = pltpu.SemaphoreType.DMA
    sds = jax.ShapeDtypeStruct
    half = max(1, pairs // 2)

    def both(shape):
        return [dma(shape), dma(shape)]

    return pl.pallas_call(
        functools.partial(finish_kernel, n),
        out_shape=(sds((rows, width), F32), sds((gu[0] // 2,) + gu[1:], F32), sds((gu[0] // 2,) + gu[1:], F32), sds(dn, F32)),
        in_specs=[any_spec()] * 10,
        out_specs=(pl.BlockSpec(memory_space=pltpu.VMEM), any_spec(), any_spec(), any_spec()),
        scratch_shapes=[
            pltpu.VMEM((pairs,) + gu, BF),
            pltpu.VMEM((pairs,) + dn, BF),
            pltpu.VMEM((levels, half) + gu, BF),
            pltpu.VMEM((levels, half) + dn, BF),
            pltpu.VMEM((2, units, rows, width), BF),
            pltpu.VMEM((units, rows, width), BF),
            pltpu.VMEM((n - 1, pairs, rows, width), BF),
            pltpu.VMEM((levels, half, rows, width), BF),
            pltpu.VMEM((2, rows, width), BF),
            pltpu.VMEM((2,) + gu[1:], BF),
            pltpu.VMEM((2,) + dn[1:], BF),
            pltpu.VMEM((2,) + gu[1:], F32),
            pltpu.VMEM((2,) + dn[1:], F32),
        ]
        + both((pairs, gu[0]))
        + both((pairs, dn[0]))
        + both((levels, half, gu[0]))
        + both((levels, half, dn[0]))
        + both((2, units))
        + both((units,))
        + both((n - 1, pairs))
        + both((levels, half))
        + [dma((2,))] * 5,
        compiler_params=pltpu.CompilerParams(collective_id=cid, has_side_effects=True, vmem_limit_bytes=VMEM_LIMIT),
    )(dd0, dd1, *experts0, *experts1)


def low_bit(q):
    return top_bit(q & -q)


def open_kernel(
    n, groups, pieces, w_ref, cot_ref, rt_ref, w_out, gy_out, rt_out, rt_side,
    s_right, r_right, s_left, r_left, s_group, r_group, s_y, r_y, s_cross, r_cross, s_rt, r_rt, s_side, r_side, local_sem,
):
    s, g, z = lax.axis_index("section"), lax.axis_index("group"), lax.axis_index("expert")
    remote = functools.partial(pltpu.make_async_remote_copy, device_id_type=MESH)
    rows = w_ref.shape[0] // pieces
    bits = top_bit(groups)
    other = {"section": 1 - s}
    barrier = pltpu.get_barrier_semaphore()
    peers = [other] + [{"group": lax.bitwise_xor(g, 1 << b)} for b in range(bits)] + [{"expert": lax.rem(z + k, n)} for k in range(1, n)]
    for peer in peers:
        pl.semaphore_signal(barrier, inc=1, device_id=peer, device_id_type=MESH)
    pl.semaphore_wait(barrier, len(peers))
    sent = []

    def launch(cond, make):
        sent.append((cond, make))
        if cond is None:
            make().start()
        else:

            @pl.when(cond)
            def _():
                make().start()

    def part(q, zz, c):
        return w_out.at[lax.bitwise_xor(g, q) * n + zz, pl.ds(c * rows, rows)] if c < pieces else gy_out.at[s, zz]

    def chain(to, zz, t, c, ssem, rsem):
        return remote(src_ref=part(0, zz, c), dst_ref=part(0, zz, c), send_sem=ssem.at[t, c], recv_sem=rsem.at[t, c], device_id={"expert": to})

    def right(t, c):
        return chain(z + 1, z - t, t, c, s_right, r_right)

    def left(t, c):
        return chain(z - 1, z + t, t, c, s_left, r_left)

    def over(q, b, zz, c):
        at = q | (1 << b)
        return remote(
            src_ref=part(q, zz, c), dst_ref=part(q, zz, c), send_sem=s_group.at[at, zz, c], recv_sem=r_group.at[at, zz, c],
            device_id={"group": lax.bitwise_xor(g, 1 << b)},
        )

    def hop(c):
        at = pl.ds(c * rows, rows)
        return remote(
            src_ref=w_ref.at[at], dst_ref=w_out.at[g * n + z, at], send_sem=s_y.at[c], recv_sem=r_y.at[c], device_id=other
        )

    def cross(zz):
        return remote(src_ref=gy_out.at[0, zz], dst_ref=gy_out.at[0, zz], send_sem=s_cross.at[zz], recv_sem=r_cross.at[zz], device_id=other)

    def route(m, k):
        return remote(
            src_ref=rt_ref.at[m], dst_ref=rt_out.at[m, z], send_sem=s_rt.at[m, k], recv_sem=r_rt.at[m, k],
            device_id={"expert": lax.rem(z + k, n)},
        )

    def side():
        return remote(src_ref=rt_ref.at[1 - s], dst_ref=rt_side, send_sem=s_side, recv_sem=r_side, device_id=other)

    launch(s == 0, functools.partial(hop, 0))
    launch(None, side)
    own = [pltpu.make_async_copy(cot_ref, gy_out.at[s, z], local_sem.at[0])]
    own += [pltpu.make_async_copy(rt_ref.at[m], rt_out.at[m, z], local_sem.at[1 + m]) for m in range(2)]

    def keep():
        return pltpu.make_async_copy(w_ref, w_out.at[g * n + z], local_sem.at[3])

    for copy in own:
        copy.start()

    @pl.when(s == 0)
    def _():
        keep().start()
        keep().wait()

    def spread_out(cond, zz, c):
        if c < pieces:
            for b in reversed(range(bits)):
                launch(cond, functools.partial(over, 0, b, zz, c))
        else:
            launch((s == 0) if cond is None else ((s == 0) & cond), functools.partial(cross, zz))

    def pass_along(t, c):
        if t == 0:
            if c < pieces:

                @pl.when(s != 0)
                def _():
                    hop(c).wait_recv()
            else:
                own[0].wait()
            launch(z < n - 1, functools.partial(right, t, c))
            launch(z > 0, functools.partial(left, t, c))
            spread_out(None, z, c)
            if c + 1 < pieces:

                @pl.when(s == 0)
                def _():
                    hop(c).wait_send()
                    hop(c + 1).start()
        else:
            from_left, from_right = z >= t, z + t < n

            @pl.when(from_left)
            def _():
                right(t - 1, c).wait_recv()

            launch(from_left & (z < n - 1), functools.partial(right, t, c))
            spread_out(from_left, z - t, c)

            @pl.when(from_right)
            def _():
                left(t - 1, c).wait_recv()

            launch(from_right & (z > 0), functools.partial(left, t, c))
            spread_out(from_right, z + t, c)

    def forward(q, k):
        zz = lax.rem(z + k, n)
        for c in range(pieces):
            over(q & (q - 1), low_bit(q), zz, c).wait_recv()
            for b in reversed(range(low_bit(q))):
                launch(None, functools.partial(over, q, b, zz, c))

    for t in range(n):
        for c in range(pieces):
            pass_along(t, c)
        if t == 0:
            for m in range(2):
                for k in range(1, n):
                    launch(None, functools.partial(route, m, k))
    pending = [(q, k) for q in sorted(range(1, groups), key=lambda q: -low_bit(q)) for k in range(n)]
    for t in range(n):
        pass_along(t, pieces)
        forward(*pending.pop(0))
    for q, k in pending:
        forward(q, k)

    @pl.when(s != 0)
    def _():
        for zz in range(n):
            cross(zz).wait_recv()

    side().wait_recv()
    for m in range(2):
        own[1 + m].wait()
        for k in range(1, n):
            route(m, k).wait_recv()
    @pl.when(s == 0)
    def _():
        if pieces > 1:
            hop(pieces - 1).wait_send()

    for cond, make in sent[(1 if pieces > 1 else 0) :]:
        if cond is None:
            make().wait_send()
        else:

            @pl.when(cond)
            def _(make=make):
                make().wait_send()


def open_up(cid, packed, cot, rt):
    n, groups = lax.axis_size("expert"), lax.axis_size("group")
    sh = packed.shape[0]
    pieces = 3 if sh % 48 == 0 else 1
    dma = pltpu.SemaphoreType.DMA
    sds = jax.ShapeDtypeStruct

    def both(shape):
        return [dma(shape), dma(shape)]

    w, gy, rt_all, rt_side = pl.pallas_call(
        functools.partial(open_kernel, n, groups, pieces),
        out_shape=(sds((groups * n,) + packed.shape, BF), sds((2, n) + cot.shape, BF), sds((2, n) + rt.shape[1:], rt.dtype), sds(rt.shape[1:], rt.dtype)),
        in_specs=vmem(3),
        out_specs=(any_spec(), any_spec(), any_spec(), any_spec()),
        scratch_shapes=both((n, pieces + 1)) + both((n, pieces + 1)) + both((groups, n, pieces)) + both((pieces,)) + both((n,)) + both((2, n)) + [dma, dma] + [dma((4,))],
        compiler_params=pltpu.CompilerParams(collective_id=cid, has_side_effects=True),
    )(packed, cot, rt)
    return w.reshape(groups * n * sh, -1), gy, rt_all, rt_side


def swap_sections(value):
    return lax.ppermute(value, "section", [(0, 1), (1, 0)])


def rope_tables(t):
    half = HEAD_SIZE // 2
    frequency = THETA ** (-jnp.arange(half, dtype=F32) * 2.0 / HEAD_SIZE)
    angles = jnp.arange(t, dtype=F32)[:, None] * frequency[None, :]
    reps = LANES // half
    return jnp.tile(jnp.cos(angles), (1, reps)), jnp.tile(jnp.sin(angles), (1, reps))


def local(
    inputs, cotangent, segment_ids, live_first, routes, gain_attn, gain_moe,
    w_query, key_weight, value_weight, w_out, w_router, w_gate, w_up, w_down,
):
    s = lax.axis_index("section")
    n = lax.axis_size("expert")
    groups = lax.axis_size("group")
    t, d = inputs.shape[2:]
    top = routes.shape[-1]
    per = w_gate.shape[1]
    experts = per * n
    e_pad = -(-experts // 16) * 16
    cap = t * top * 5 // (4 * experts)
    wg, wu, wd = w_gate[0], w_up[0], w_down[0]
    at_zero = s == 0

    shard = w_query.shape[1]
    aux = jnp.concatenate(
        [
            w_router[0],
            jnp.zeros((shard, GAIN_MOE_ROW - experts), BF),
            gain_moe[0][:, None],
            gain_attn[0][:, None],
        ],
        axis=1,
    )
    packed = jnp.concatenate([w_query[0], key_weight[0], value_weight[0], w_out[0].T, aux], axis=1)
    other = lax.ppermute(packed, "section", [(1, 0)])
    second_shard = jnp.where(at_zero, other, packed)

    x0 = lax.dynamic_index_in_dim(inputs[:, 0], s, 0, keepdims=False)
    cot = lax.dynamic_index_in_dim(cotangent[:, 0], s, 0, keepdims=False)
    seg = lax.dynamic_index_in_dim(segment_ids[:, 0], s, 0, keepdims=False)
    live = lax.dynamic_index_in_dim(live_first[:, 0], s, 0, keepdims=False)
    meta = jnp.stack([seg, jnp.repeat(live, BLK)], axis=1)
    meta = jnp.pad(meta, ((0, 0), (0, LANES - 2)))
    segr = jnp.broadcast_to(seg[None, :], (8, t))
    cos, sin = rope_tables(t)

    rt = jnp.swapaxes(routes[0, :, 0], 1, 2)
    rt_mine = lax.dynamic_index_in_dim(rt, s, 0, keepdims=False)

    def flat(z):
        return z.reshape((2 * n,) + z.shape[2:])

    def paired(z):
        return z.reshape((2, n) + z.shape[1:])

    first_weights, gy1, rt_all, rt_theirs = open_up(1, packed, cot, rt)
    rt_tokens = (jnp.where(at_zero, rt_mine, rt_theirs), jnp.where(at_zero, rt_theirs, rt_mine))
    gy1, rt_all = flat(gy1), flat(rt_all)

    qkv0, p0, o0, h0, b0, wrt0 = attn_fwd(x0, first_weights, cos, sin, meta, segr)
    second_shard, b0 = lax.optimization_barrier((second_shard, b0))
    second_weights = lax.all_gather(second_shard, ("group", "expert"), axis=0, tiled=True)
    m0 = moe(0, "fwd", 2, e_pad, cap, b0, wg, wu, wd, rt=rt_all, wrt=wrt0)
    x1 = (h0 + jnp.sum(m0.back.astype(F32), axis=0)).astype(BF)

    qkv1, p1, o1, h1, b1, wrt1 = attn_fwd(x1, second_weights, cos, sin, meta, segr)
    m1 = moe(1, "both", 3, e_pad, cap, b1, wg, wu, wd, rt=rt_all, wrt=wrt1, gy=gy1)

    crossed = lax.ppermute(m1.part0, "section", [(1, 0)])

    def gates_back(dg):
        dg = dg[:, :per].reshape(experts, t)
        return jnp.pad(dg, ((0, e_pad - experts), (0, 0)))

    dx1, dd1 = attn_bwd(cot, h1, x1, second_weights, qkv1, p1, o1, b1, wrt1, m1.back, gates_back(m1.dgate), rt_tokens[1], cos, sin)
    gy0 = dx1.astype(BF)

    n0 = moe(0, "bwd", 4, e_pad, cap, gy0, wg, wu, wd, pos=m0.pos, gate=m0.gate, gp=m0.gp, up=m0.up, blocks=flat(m0.blocks))
    dback0, crossed, straight = lax.optimization_barrier((n0.back, crossed, m1.part1))
    back1 = lax.all_to_all(jnp.where(at_zero, crossed, straight), "expert", split_axis=0, concat_axis=0, tiled=True)
    y1 = (h1 + jnp.sum(back1.astype(F32), axis=0)).astype(BF)
    dx0, dd0 = attn_bwd(gy0, h0, x0, first_weights, qkv0, p0, o0, b0, wrt0, dback0, gates_back(n0.dgate), rt_tokens[0], cos, sin)

    dense, gate_grad, up_grad, down = finish(5, dd0, dd1, (n0.even, n0.odd, n0.even_dn, n0.odd_dn), (m1.even, m1.odd, m1.even_dn, m1.odd_dn))

    kept_out = jnp.where(at_zero, x1, y1)
    swapped_out = swap_sections(jnp.where(at_zero, y1, x1))
    layer_out = jnp.where(at_zero, jnp.stack([kept_out, swapped_out]), jnp.stack([swapped_out, kept_out]))
    kept_in = jnp.where(at_zero, dx0, dx1)
    swapped_in = swap_sections(jnp.where(at_zero, dx1, dx0))
    input_grad = jnp.where(at_zero, jnp.stack([kept_in, swapped_in]), jnp.stack([swapped_in, kept_in]))

    return (
        layer_out[None, :, None],
        input_grad[None, :, None],
        dense[:, QKV + QW + GAIN_ATTN_ROW][None],
        dense[:, QKV + QW + GAIN_MOE_ROW][None],
        dense[None, :, 0:QW],
        dense[None, :, QW : QW + KW],
        dense[None, :, QW + KW : QKV],
        dense[:, QKV : QKV + QW].T[None],
        dense[None, :, QKV + QW : QKV + QW + experts],
        gate_grad[None],
        up_grad[None],
        down[None],
    )


def solution(mesh):
    return jax.shard_map(
        local,
        mesh=mesh,
        in_specs=(
            P(None, ("group", "expert"), None, None),
            P(None, ("group", "expert"), None, None),
            P(None, ("group", "expert"), None),
            P(None, ("group", "expert"), None),
            P("section", None, ("group", "expert"), None, None),
            P("section", ("group", "expert")),
            P("section", ("group", "expert")),
            P("section", ("group", "expert"), None),
            P("section", ("group", "expert"), None),
            P("section", ("group", "expert"), None),
            P("section", None, ("group", "expert")),
            P("section", ("group", "expert"), None),
            P("section", "expert", None, None),
            P("section", "expert", None, None),
            P("section", "expert", None, None),
        ),
        out_specs=(
            P("section", None, ("group", "expert"), None, None),
            P("section", None, ("group", "expert"), None, None),
            P("section", ("group", "expert")),
            P("section", ("group", "expert")),
            P("section", ("group", "expert"), None),
            P("section", ("group", "expert"), None),
            P("section", ("group", "expert"), None),
            P("section", None, ("group", "expert")),
            P("section", ("group", "expert"), None),
            P("section", "expert", "group", None),
            P("section", "expert", "group", None),
            P("section", "expert", None, "group"),
        ),
        check_vma=False,
    )
```

```python
import functools
import types

import jax
import jax.numpy as jnp
from jax import lax
from jax.experimental import pallas as pl
from jax.experimental.pallas import tpu as pltpu
from jax.sharding import PartitionSpec as P

QUERY_HEADS = 24
KEY_VALUE_HEADS = 8
HEAD_SIZE = 64
BLK = 64
EPS = 1e-06
THETA = 10000.0
NEG_FILL = -1e30
BF = jnp.bfloat16
F32 = jnp.float32
MESH = pl.DeviceIdType.MESH
LANES = 128
TILE = 512
QW = QUERY_HEADS * HEAD_SIZE
KW = KEY_VALUE_HEADS * HEAD_SIZE
QKV = QW + 2 * KW
GAIN_MOE_ROW = 126
GAIN_ATTN_ROW = 127
VMEM_LIMIT = 60 * 1024 * 1024
HEAD_PAIRS = KEY_VALUE_HEADS // 2
TILES_PER_PAIR = QUERY_HEADS // KEY_VALUE_HEADS


def dot(a, b, ca=1, cb=0):
    return lax.dot_general(a, b, (((ca,), (cb,)), ((), ())), preferred_element_type=F32)


def iota(shape, axis):
    return lax.broadcasted_iota(jnp.int32, shape, axis)


def rope(z, cos, sin, direction):
    width = z.shape[1]
    half = HEAD_SIZE // 2
    first = iota(z.shape, 1) % HEAD_SIZE < half
    partner = jnp.where(first, pltpu.roll(z, width - half, 1), pltpu.roll(z, half, 1))
    signed = jnp.where(first, -direction, direction) * partner
    reps = width // LANES
    return z * jnp.concatenate([cos] * reps, axis=1) + signed * jnp.concatenate([sin] * reps, axis=1)


def lane_masks(t):
    low = iota((t, LANES), 1) < HEAD_SIZE
    return low, jnp.logical_not(low)


def swapped(z):
    return pltpu.roll(z.astype(F32), HEAD_SIZE, 1).astype(BF)


def head_plan():
    return [(r, half, (2 * r + half) // TILES_PER_PAIR != half) for r in range(TILES_PER_PAIR) for half in range(2)]


def pick(z, half, masks):
    return jnp.where(masks[half], z, jnp.zeros_like(z))


def weight_pieces(d, order):
    aux = [(pl.ds(0, d), pl.ds(QKV + QW, LANES))]
    qkv = [(pl.ds(0, d), pl.ds(n * TILE, TILE)) for n in range(QKV // TILE)]
    out = [(pl.ds(n * TILE, TILE), pl.ds(QKV, QW)) for n in range(d // TILE)]
    down = [(pl.ds(0, d), pl.ds(QKV + n * TILE, TILE)) for n in range(QW // TILE)]
    rows = [(pl.ds(n * TILE, TILE), pl.ds(0, QKV)) for n in range(d // TILE)]
    return aux + qkv + out if order == "forward" else down + rows


def arriving(w_hbm, w_ref, sem, order):
    copies = [
        pltpu.make_async_copy(w_hbm.at[rows, cols], w_ref.at[rows, cols], sem.at[i])
        for i, (rows, cols) in enumerate(weight_pieces(w_ref.shape[0], order))
    ]
    for c in copies:
        c.start()
    return copies


def attn_fwd_kernel(
    below_ref, back_ref, w_hbm, cos_ref, sin_ref, meta_ref, segr_ref,
    qkv_ref, p_ref, o_ref, h_ref, b_ref, wrt_ref, x_ref, w_ref, w_sem,
):
    t, d = x_ref.shape
    pieces = arriving(w_hbm, w_ref, w_sem, "forward")
    entering = below_ref[...].astype(F32)
    for z in range(back_ref.shape[0]):
        entering = entering + back_ref[z].astype(F32)
    x_ref[...] = entering.astype(BF)
    pieces.pop(0).wait()
    aux = jnp.transpose(w_ref[:, QKV + QW :].astype(F32))
    wrt_ref[...] = aux.astype(BF)
    gain_attn = aux[GAIN_ATTN_ROW : GAIN_ATTN_ROW + 1]
    gain_moe = aux[GAIN_MOE_ROW : GAIN_MOE_ROW + 1]
    x = x_ref[...].astype(F32)
    r1 = lax.rsqrt(jnp.mean(x * x, axis=1, keepdims=True) + EPS)
    a = (x * r1 * gain_attn).astype(BF)
    cos, sin = cos_ref[...], sin_ref[...]
    for n in range(QKV // TILE):
        cols = slice(n * TILE, (n + 1) * TILE)
        pieces.pop(0).wait()
        y = dot(a, w_ref[:, cols])
        if n * TILE < QW + KW:
            y = rope(y, cos, sin, 1.0)
        qkv_ref[:, cols] = y.astype(BF)
    i, j = iota((t, t), 0), iota((t, t), 1)
    allowed = (j <= i) & (meta_ref[:, 0:1] == segr_ref[0:1, :]) & (j // BLK >= meta_ref[:, 1:2])
    masks = lane_masks(t)

    def pair(m, carry):
        def lanes(base):
            return pl.ds(pl.multiple_of(base, LANES), LANES)

        kp = qkv_ref[:, lanes(QW + m * LANES)]
        vp = qkv_ref[:, lanes(QW + KW + m * LANES)]
        ks, vs = swapped(kp), swapped(vp)
        parts = {}
        for r, half, swap in head_plan():
            q = pick(qkv_ref[:, lanes((m * TILES_PER_PAIR + r) * LANES)], half, masks)
            s = dot(q, ks if swap else kp, 1, 1) * HEAD_SIZE ** (-0.5)
            s = jnp.where(allowed, s, NEG_FILL)
            e = jnp.exp(s - jnp.max(s, axis=1, keepdims=True))
            p = e * (1.0 / jnp.sum(e, axis=1, keepdims=True))
            p_ref[m * 2 * TILES_PER_PAIR + 2 * r + half] = p
            part = dot(p.astype(BF), pick(vs if swap else vp, half, masks))
            parts[half] = part
            if half == 1:
                o_ref[:, lanes((m * TILES_PER_PAIR + r) * LANES)] = (parts[0] + parts[1]).astype(BF)
        return carry

    lax.fori_loop(0, HEAD_PAIRS, pair, 0)
    o = o_ref[...]
    for n in range(d // TILE):
        rows = slice(n * TILE, (n + 1) * TILE)
        pieces.pop(0).wait()
        h_ref[:, rows] = x_ref[:, rows].astype(F32) + dot(o, w_ref[rows, QKV : QKV + QW], 1, 1)
    h = h_ref[...]
    r2 = lax.rsqrt(jnp.mean(h * h, axis=1, keepdims=True) + EPS)
    b_ref[...] = (h * r2 * gain_moe).astype(BF)


def vmem(n):
    return [pl.BlockSpec(memory_space=pltpu.VMEM)] * n


def attn_fwd(below, back, w, cos, sin, meta, segr):
    t, d = below.shape
    sds = jax.ShapeDtypeStruct
    return pl.pallas_call(
        attn_fwd_kernel,
        out_shape=(
            sds((t, QKV), BF),
            sds((QUERY_HEADS, t, t), F32),
            sds((t, QW), BF),
            sds((t, d), F32),
            sds((t, d), BF),
            sds((LANES, d), BF),
            sds((t, d), BF),
        ),
        in_specs=vmem(2) + [any_spec()] + vmem(4),
        out_specs=tuple(vmem(7)),
        scratch_shapes=[pltpu.VMEM(w.shape, BF), pltpu.SemaphoreType.DMA((1 + QKV // TILE + d // TILE,))],
        compiler_params=pltpu.CompilerParams(vmem_limit_bytes=VMEM_LIMIT),
        cost_estimate=pl.CostEstimate(flops=2 * t * d * 4096, bytes_accessed=w.size * 2, transcendentals=QUERY_HEADS * t * t),
    )(below, back, w, cos, sin, meta, segr)


def gates_of(rt, wrt, b, e_pad):
    t = rt.shape[1]
    experts = iota((e_pad, t), 0)
    chosen = experts == rt[0:1]
    for k in range(1, rt.shape[0]):
        chosen = chosen | (experts == rt[k : k + 1])
    logits = jnp.where(chosen, dot(wrt[0:e_pad], b, 1, 1), NEG_FILL)
    e = jnp.where(chosen, jnp.exp(logits - jnp.max(logits, axis=0, keepdims=True)), 0.0)
    return e / jnp.sum(e, axis=0, keepdims=True)


def attn_bwd_kernel(
    now, e_pad, gy_ref, h_ref, x_ref, w_hbm, qkv_ref, p_ref, o_ref, b_ref, wrt_ref, back_ref, dg_ref, rt_ref, cos_ref, sin_ref,
    dx_ref, dxb_ref, *rest,
):
    t, d = x_ref.shape
    if now:
        dd_hbm, do_ref, dqkv_ref, dh_ref, w_ref, w_sem, lt_ref, dd_ref, dd_sem = rest
    else:
        dqkv_ref, at_ref, dht_ref, daux_ref, do_ref, dh_ref, w_ref, w_sem = rest
    pieces = arriving(w_hbm, w_ref, w_sem, "backward")
    leaving = []

    def leave(first, width):
        cols = pl.ds(first, width)
        leaving.append(pltpu.make_async_copy(dd_ref.at[:, cols], dd_hbm.at[:, cols], dd_sem.at[len(leaving)]))
        leaving[-1].start()

    gain_attn = wrt_ref[GAIN_ATTN_ROW - 7 :, :].astype(F32)[7:8]
    gain_moe = wrt_ref[GAIN_ATTN_ROW - 7 :, :].astype(F32)[6:7]
    b = b_ref[...]
    gates = gates_of(rt_ref[...], wrt_ref, b, e_pad)
    dg = dg_ref[...]
    dl = (gates * (dg - jnp.sum(gates * dg, axis=0, keepdims=True)))
    dlb = dl.astype(BF)
    db = dot(dlb, wrt_ref[0:e_pad, :], 0, 0)
    for z in range(back_ref.shape[0]):
        db = db + back_ref[z].astype(F32)
    h = h_ref[...]
    r2 = lax.rsqrt(jnp.mean(h * h, axis=1, keepdims=True) + EPS)
    grad_moe = jnp.sum(db * h * r2, axis=0, keepdims=True)
    dn = db * gain_moe
    dh = gy_ref[...].astype(F32) + r2 * dn - h * (r2 * r2 * r2) * jnp.mean(dn * h, axis=1, keepdims=True)
    dh_ref[...] = dh
    dhb = dh.astype(BF)
    for n in range(QW // TILE):
        cols = slice(n * TILE, (n + 1) * TILE)
        pieces.pop(0).wait()
        do_ref[:, cols] = dot(dhb, w_ref[:, QKV + n * TILE : QKV + (n + 1) * TILE]).astype(BF)
    masks = lane_masks(t)
    cos, sin = cos_ref[...], sin_ref[...]

    def pair(m, carry):
        def lanes(base):
            return pl.ds(pl.multiple_of(base, LANES), LANES)

        kp = qkv_ref[:, lanes(QW + m * LANES)]
        vp = qkv_ref[:, lanes(QW + KW + m * LANES)]
        ks, vs = swapped(kp), swapped(vp)
        zero = jnp.zeros((t, LANES), F32)
        dk = {False: zero, True: zero}
        dv = {False: zero, True: zero}
        dq = zero
        for r, half, swap in head_plan():
            tile = lanes((m * TILES_PER_PAIR + r) * LANES)
            q = pick(qkv_ref[:, tile], half, masks)
            do = pick(do_ref[:, tile], half, masks)
            p = p_ref[m * 2 * TILES_PER_PAIR + 2 * r + half]
            dp = dot(do, vs if swap else vp, 1, 1)
            dv[swap] = dv[swap] + dot(p.astype(BF), do, 0, 0)
            dt = p * (dp - jnp.sum(p * dp, axis=1, keepdims=True)) * HEAD_SIZE ** (-0.5)
            dt = dt.astype(BF)
            dk[swap] = dk[swap] + dot(dt, q, 0, 0)
            part = dot(dt, pick(ks if swap else kp, half, masks))
            dq = part if half == 0 else dq + part
            if half == 1:
                dqkv_ref[:, tile] = rope(dq, cos, sin, -1.0).astype(BF)
        dk_all = dk[False] + pltpu.roll(dk[True], HEAD_SIZE, 1)
        dv_all = dv[False] + pltpu.roll(dv[True], HEAD_SIZE, 1)
        dqkv_ref[:, lanes(QW + m * LANES)] = rope(dk_all, cos, sin, -1.0).astype(BF)
        dqkv_ref[:, lanes(QW + KW + m * LANES)] = dv_all.astype(BF)
        return carry

    lax.fori_loop(0, HEAD_PAIRS, pair, 0)
    x = x_ref[...].astype(F32)
    r1 = lax.rsqrt(jnp.mean(x * x, axis=1, keepdims=True) + EPS)
    dqkv = dqkv_ref[...]
    for n in range(d // TILE):
        rows = slice(n * TILE, (n + 1) * TILE)
        pieces.pop(0).wait()
        dx_ref[:, rows] = dot(dqkv, w_ref[rows, 0:QKV], 1, 1)
    da = dx_ref[...]
    grad_attn = jnp.sum(da * x * r1, axis=0, keepdims=True)
    dag = da * gain_attn
    dx = dh_ref[...] + r1 * dag - x * (r1 * r1 * r1) * jnp.mean(dag * x, axis=1, keepdims=True)
    dx_ref[...] = dx
    dxb_ref[...] = dx.astype(BF)
    row = iota((LANES, d), 0)
    grads = jnp.where(row == GAIN_MOE_ROW, grad_moe, jnp.where(row == GAIN_ATTN_ROW, grad_attn, 0.0))
    dl_full = jnp.concatenate([dl, jnp.zeros((LANES - e_pad, t), F32)], axis=0)
    dl_rows = jnp.transpose(dl_full).astype(BF)
    bt = jnp.transpose(b_ref[...].astype(F32)).astype(BF)
    daux = (dot(bt, dl_rows) + jnp.transpose(grads)).astype(BF)
    if not now:
        at_ref[...] = jnp.transpose(x * r1 * gain_attn).astype(BF)
        dht_ref[...] = jnp.transpose(dh_ref[...]).astype(BF)
        daux_ref[...] = daux
        return
    lt_ref[...] = jnp.transpose(x * r1 * gain_attn).astype(BF)
    for n in range(QKV // TILE):
        cols = slice(n * TILE, (n + 1) * TILE)
        dd_ref[:, cols] = dot(lt_ref[...], dqkv_ref[:, cols]).astype(BF)
        leave(n * TILE, TILE)
    lt_ref[...] = jnp.transpose(dh_ref[...]).astype(BF)
    for n in range(QW // TILE):
        cols = slice(n * TILE, (n + 1) * TILE)
        dd_ref[:, QKV + n * TILE : QKV + (n + 1) * TILE] = dot(lt_ref[...], o_ref[:, cols]).astype(BF)
        leave(QKV + n * TILE, TILE)
    dd_ref[:, QKV + QW :] = daux
    leave(QKV + QW, LANES)
    for c in leaving:
        c.wait()


def attn_bwd(now, gy, h, x, w, qkv, p, o, b, wrt, back, dg, rt, cos, sin):
    t, d = x.shape
    sds = jax.ShapeDtypeStruct
    dma = pltpu.SemaphoreType.DMA
    outs = [sds((t, d), F32), sds((t, d), BF)]
    scratch = [pltpu.VMEM((t, QW), BF)]
    if now:
        outs.append(sds(w.shape, BF))
        scratch.append(pltpu.VMEM((t, QKV), BF))
    else:
        outs += [sds((t, QKV), BF), sds((d, t), BF), sds((d, t), BF), sds((d, LANES), BF)]
    scratch += [pltpu.VMEM((t, d), F32), pltpu.VMEM(w.shape, BF), dma((QW // TILE + d // TILE,))]
    if now:
        scratch += [pltpu.VMEM((d, t), BF), pltpu.VMEM(w.shape, BF), dma((1 + QKV // TILE + QW // TILE,))]
    return pl.pallas_call(
        functools.partial(attn_bwd_kernel, now, dg.shape[0]),
        out_shape=tuple(outs),
        in_specs=vmem(3) + [any_spec()] + vmem(10),
        out_specs=tuple(vmem(2) + [any_spec()] if now else vmem(6)),
        scratch_shapes=scratch,
        compiler_params=pltpu.CompilerParams(vmem_limit_bytes=VMEM_LIMIT),
        cost_estimate=pl.CostEstimate(flops=4 * t * d * 4096, bytes_accessed=w.size * 4, transcendentals=0),
    )(gy, h, x, w, qkv, p, o, b, wrt, back, dg, rt, cos, sin)


def one_hot(pos_row, cap):
    return jnp.where(iota((cap, pos_row.shape[1]), 0) == pos_row, 1.0, 0.0)


def all_hots(pos, per, cap):
    return jnp.concatenate([one_hot(pos[j : j + 1], cap) for j in range(per)], axis=0)


def all_hots_back(pos, per, cap):
    width = per * cap
    expert = jnp.where(iota((8, width), 1) // cap == iota((8, width), 0), 1.0, 0.0).astype(BF)
    wide = dot(pos.astype(F32).astype(BF), expert, 0, 0)
    slot = (iota((1, width), 1) % cap).astype(F32)
    return jnp.where(wide == slot, 1.0, 0.0).astype(BF)


def slots_of(rt, first, per):
    t = rt.shape[1]
    experts = iota((16, t), 0)
    mine = jnp.where(experts < per, experts + first, -1)
    chosen = mine == rt[0:1]
    for k in range(1, rt.shape[0]):
        chosen = chosen | (mine == rt[k : k + 1])
    earlier = jnp.where(iota((t, t), 0) < iota((t, t), 1), 1.0, 0.0).astype(BF)
    before = dot(jnp.where(chosen, 1.0, 0.0).astype(BF), earlier)
    return jnp.where(chosen, before.astype(jnp.int32), -1)[0:8]


def streamed(count, copies, body, primed=False):
    if not primed:
        for c in copies(0, 0):
            c.start()

    def step(b, carry):
        slot = lax.rem(b, 2)

        @pl.when(b + 1 < count)
        def _():
            for c in copies(b + 1, lax.rem(b + 1, 2)):
                c.start()

        for c in copies(b, slot):
            c.wait()
        body(b, slot)
        return carry

    lax.fori_loop(0, count, step, 0)


def combine(base, count, per, cap, pos_ref, rows_ref, out_hbm, obuf, osem):
    def copy(b, slot):
        return pltpu.make_async_copy(obuf.at[slot], out_hbm.at[b], osem.at[slot])

    def step(b, carry):
        slot = lax.rem(b, 2)

        @pl.when(b >= 2)
        def _():
            copy(b - 2, slot).wait()

        back = all_hots_back(pos_ref[base + b], per, cap)
        at = pl.ds(pl.multiple_of((base + b) * cap, cap), cap)
        rows = jnp.concatenate([rows_ref[j, at, :] for j in range(per)], axis=0)
        obuf[slot] = dot(back, rows).astype(BF)
        copy(b, slot).start()
        return carry

    lax.fori_loop(0, count, step, 0)
    copy(count - 2, (count - 2) % 2).wait()
    copy(count - 1, (count - 1) % 2).wait()


def chunk_gates(c, j, chunk, cap, pos_ref, gate_ref):
    hots, gates = [], []
    for bb in range(chunk // cap):
        b = c * (chunk // cap) + bb
        hot = one_hot(pos_ref[b, pl.ds(j, 1), :], cap)
        hots.append(hot)
        gates.append(jnp.sum(hot * gate_ref[b, pl.ds(j, 1), :], axis=1, keepdims=True))
    return hots, jnp.concatenate(gates, axis=0)


def any_spec():
    return pl.BlockSpec(memory_space=pl.ANY)


def put_rows(hots, block, b, per, cap, dest):
    at = pl.ds(pl.multiple_of(b * cap, cap), cap)
    rows = dot(hots, block).astype(BF)
    for k in range(per):
        dest[k, at, :] = rows[k * cap : (k + 1) * cap]


def gather_from(count, per, cap, pos, source, dest, buf, sem):
    def body(b, slot):
        put_rows(all_hots(pos[b], per, cap).astype(BF), buf[slot], b, per, cap, dest)

    streamed(count, lambda b, slot: [pltpu.make_async_copy(source.at[b], buf.at[slot], sem.at[slot])], body)


def weight_grads(r, per):
    parts, piece = r.even.shape[0], r.even.shape[3]
    g = lax.axis_index("group")
    parity, place = lax.rem(g, 2), g // 2

    def outgoing(j, at, slot):
        return [
            pltpu.make_async_copy(r.gu_buf.at[slot, 0], r.even.at[at, :, j], r.gu_sem.at[slot, 0]),
            pltpu.make_async_copy(r.gu_buf.at[slot, 1], r.odd.at[at, :, j], r.gu_sem.at[slot, 1]),
            pltpu.make_async_copy(r.dn_buf.at[slot, 0], r.even_dn.at[at, j], r.dn_sem.at[slot, 0]),
            pltpu.make_async_copy(r.dn_buf.at[slot, 1], r.odd_dn.at[at, j], r.dn_sem.at[slot, 1]),
        ]

    def finished(slot):
        for c in outgoing(0, 0, slot):
            c.wait()

    def body(j, carry):
        for q in range(parts):
            slot = q % 2
            if q >= 2:
                finished(slot)
            else:

                @pl.when(j > 0)
                def _():
                    finished(slot)

            cols = slice(2 * q * piece, 2 * (q + 1) * piece)
            for m in range(2):
                full = dot(r.x_scr[j, :, cols], r.act[m, j], 0, 0).astype(BF)
                r.gu_buf[slot, parity, m] = full[:piece]
                r.gu_buf[slot, 1 - parity, m] = full[piece:]
            full = dot(r.act[2, j], r.y_scr[j, :, cols], 0, 0).astype(BF)
            r.dn_buf[slot, parity] = full[:, :piece]
            r.dn_buf[slot, 1 - parity] = full[:, piece:]
            for c in outgoing(j, lax.bitwise_xor(place, q), slot):
                c.start()
        return carry

    lax.fori_loop(0, per, body, 0)
    for slot in range(2):
        finished(slot)


def meet(n, bits):
    s, g, z = lax.axis_index("section"), lax.axis_index("group"), lax.axis_index("expert")
    barrier = pltpu.get_barrier_semaphore()
    peers = [{"section": 1 - s}] + [{"expert": lax.rem(z + k, n)} for k in range(1, n)]
    peers += [{"group": lax.bitwise_xor(g, 1 << b)} for b in range(bits)]
    for peer in peers:
        pl.semaphore_signal(barrier, inc=1, device_id=peer, device_id_type=MESH)
    pl.semaphore_wait(barrier, len(peers))


def moe_kernel(layer, mode, n, e_pad, cap, names, *refs):
    r = types.SimpleNamespace(**dict(zip(names, refs)))
    forward, backward = mode != "bwd", mode != "fwd"
    s, z = lax.axis_index("section"), lax.axis_index("expert")
    here = s == layer
    count = 2 * n
    per, rows, d = r.y_scr.shape
    first = z * per
    chunk = n * cap
    remote = functools.partial(pltpu.make_async_remote_copy, device_id_type=MESH)
    other = {"section": 1 - s}
    g = lax.axis_index("group")
    riding = forward and not backward
    groups = r.dense_out.shape[0] // n if riding else 1
    bits = top_bit(groups)
    meet(n, bits)
    r.blk[s, z] = r.own[...]

    def over(q, b, zz):
        at = q | (1 << b)
        shard = r.dense_out.at[lax.bitwise_xor(g, q) * n + zz]
        return remote(
            src_ref=shard, dst_ref=shard, send_sem=r.s_over.at[at, zz], recv_sem=r.r_over.at[at, zz],
            device_id={"group": lax.bitwise_xor(g, 1 << b)},
        )

    def ride():
        for b in reversed(range(bits)):
            for zz in range(n):
                over(0, b, zz).start()

    def ride_on():
        for q in sorted(range(1, groups), key=lambda q: -low_bit(q)):
            for zz in range(n):
                over(q & (q - 1), low_bit(q), zz).wait_recv()
                for b in reversed(range(low_bit(q))):
                    over(q, b, zz).start()

    if riding:
        ride()

    def half(i):
        section = jnp.where(i < per, layer, 1 - layer)
        return lax.rem(i, per), section, pl.ds(pl.multiple_of(section * chunk, chunk), chunk)

    def weights(i, slot):
        j, _, at = half(i)
        both = [
            pltpu.make_async_copy(r.wg.at[j], r.wg_buf.at[slot], r.w_sem.at[slot, 0]),
            pltpu.make_async_copy(r.wu.at[j], r.wu_buf.at[slot], r.w_sem.at[slot, 1]),
            pltpu.make_async_copy(r.wd.at[j], r.wd_buf.at[slot], r.w_sem.at[slot, 2]),
        ]
        if mode == "bwd":
            both.append(pltpu.make_async_copy(r.gp.at[j, at], r.gp_buf.at[slot], r.gp_sem.at[slot, 0]))
            both.append(pltpu.make_async_copy(r.up.at[j, at], r.gp_buf.at[2 + slot], r.gp_sem.at[slot, 1]))
        return both

    def chain(to, zz, t, ssem, rsem):
        return remote(
            src_ref=r.blk.at[s, zz], dst_ref=r.blk.at[s, zz], send_sem=ssem.at[t], recv_sem=rsem.at[t], device_id={"expert": to}
        )

    def right(t):
        return chain(z + 1, z - t, t, r.s_right, r.r_right)

    def left(t):
        return chain(z - 1, z + t, t, r.s_left, r.r_left)

    def cross(zz):
        return remote(
            src_ref=r.blk.at[s, zz], dst_ref=r.blk.at[s, zz], send_sem=r.s_cross.at[zz], recv_sem=r.r_cross.at[zz], device_id=other
        )

    def prepare(section, zz):
        b = section * n + zz
        block = r.blk[section, zz]
        if forward:
            rt = r.rt[b]
            pos = slots_of(rt, first, per)
            r.pos[b] = pos
            r.gates[...] = gates_of(rt, r.wrt, block, e_pad)
            r.gate[b] = jnp.concatenate(
                [r.gates[pl.ds(first + k, 1), :] for k in range(per)] + [jnp.zeros((8 - per, rt.shape[1]), F32)], axis=0
            )
            put_rows(all_hots(pos, per, cap).astype(BF), block, b, per, cap, r.x_scr)
        else:
            put_rows(all_hots(r.pos[b], per, cap).astype(BF), block, b, per, cap, r.y_scr)

    @pl.when(here)
    def _():
        for c in weights(0, 0):
            c.start()

    def prepare_at(section, t):
        def candidate(m, carry):
            zz = jnp.where(m == 0, z - t, z + t)

            @pl.when((zz >= 0) & (zz < n) & ((m == 0) | (t > 0)))
            def _():
                prepare(section, zz)

            return carry

        lax.fori_loop(0, 2, candidate, 0)

    def dense_tiles():
        tiles = []
        for first_row in range(0, d, rows):
            for left, right, col, width in ((r.at, r.dqkv, 0, QW), (r.at, r.dqkv, QW, 2 * KW), (r.dht, r.o, QKV, QW)):
                source = right if left is r.dht else right.at[:, pl.ds(col, width)]
                tiles.append((left.at[pl.ds(first_row, rows)], source, first_row, col, width))
        return tiles

    def dense_copy(i, tile):
        _, _, row, col, width = tile
        return pltpu.make_async_copy(
            r.x_scr.at[i % per, :, pl.ds(0, width)], r.dd.at[pl.ds(row, rows), pl.ds(col, width)], r.dd_sem.at[i]
        )

    def aux_copy():
        return pltpu.make_async_copy(r.daux, r.dd.at[:, pl.ds(QKV + QW, LANES)], r.daux_sem)

    def dense_start(step):
        if step == 0:
            aux_copy().start()
        tiles = dense_tiles()
        share = len(tiles) // 3
        for i, tile in list(enumerate(tiles))[step * share : (step + 1) * share]:
            if i >= per:
                dense_copy(i - per, tiles[i - per]).wait()
            left, right, _, _, width = tile
            r.x_scr[i % per, :, 0:width] = dot(left[...], right[...]).astype(BF)
            dense_copy(i, tile).start()

    def dense_wait():
        aux_copy().wait()
        tiles = dense_tiles()
        for i in range(max(0, len(tiles) - per), len(tiles)):
            dense_copy(i, tiles[i]).wait()

    @pl.loop(0, n)
    def _(t):
        from_left = z >= t
        from_right = z + t < n

        @pl.when(from_left & (t > 0))
        def _():
            right(t - 1).wait_recv()

        @pl.when(from_left & (z < n - 1))
        def _():
            right(t).start()

        @pl.when(from_left & jnp.logical_not(here))
        def _():
            cross(z - t).start()

        @pl.when(from_right & (t > 0))
        def _():
            left(t - 1).wait_recv()

        @pl.when(from_right & (z > 0))
        def _():
            left(t).start()

        @pl.when(from_right & (t > 0) & jnp.logical_not(here))
        def _():
            cross(z + t).start()

        if mode == "bwd":

            for step in range(3):

                @pl.when(t == step)
                def _(step=step):
                    dense_start(step)

        @pl.when(here)
        def _():
            if mode == "both":

                @pl.when(t == 0)
                def _():
                    @pl.loop(0, count)
                    def _(b):
                        r.pos[b] = slots_of(r.rt[b], first, per)

                    gather_from(count, per, cap, r.pos, r.gy, r.y_scr, r.row_buf, r.row_sem)

            prepare_at(layer, t)

    def late_blocks():
        @pl.loop(0, n)
        def _(t):
            @pl.when(z >= t)
            def _():
                cross(z - t).wait_recv()

            @pl.when((t > 0) & (z + t < n))
            def _():
                cross(z + t).wait_recv()

            prepare_at(1 - layer, t)

    def over_part(zz):
        return remote(
            src_ref=r.part.at[zz], dst_ref=r.part_out.at[zz], send_sem=r.s_part.at[zz], recv_sem=r.r_part.at[zz], device_id=other
        )

    if mode == "bwd":
        dense_wait()

        @pl.when(jnp.logical_not(here))
        def _():
            for zz in range(n):
                over_part(zz).start()

    srcs = (r.pbuf, r.dg) if backward else (r.pbuf,)
    outs = (r.back, r.dgate) if backward else (r.back,)
    relays = (r.relay, r.dg_relay) if backward else (r.relay,)
    arrays = range(len(srcs))

    def hop(a, to):
        return remote(
            src_ref=srcs[a].at[1 - layer, to],
            dst_ref=relays[a].at[to],
            send_sem=r.s_hop.at[a, to],
            recv_sem=r.r_hop.at[a, to],
            device_id=other,
        )

    def give(a, source, k):
        return remote(
            src_ref=source,
            dst_ref=outs[a].at[z],
            send_sem=r.s_give.at[a, k],
            recv_sem=r.r_give.at[a, k],
            device_id={"expert": lax.rem(z + k, n)},
        )

    def keep(a, source):
        return pltpu.make_async_copy(source, outs[a].at[z], r.keep_sem.at[a])

    def saved(i, slot):
        j, _, at = half(i)
        return [
            pltpu.make_async_copy(r.gp_buf.at[slot], r.gp.at[j, at], r.gp_sem.at[slot, 0]),
            pltpu.make_async_copy(r.gp_buf.at[2 + slot], r.up.at[j, at], r.gp_sem.at[slot, 1]),
        ]

    def expert(i, slot):
        j, section, at = half(i)

        @pl.when(i == per)
        def _():
            late_blocks()

        if mode == "fwd":

            @pl.when(i >= 2)
            def _():
                for c in saved(i - 2, slot):
                    c.wait()

        if forward:
            x = r.x_scr[j, at, :]
            gp = dot(x, r.wg_buf[slot])
            up = dot(x, r.wu_buf[slot])
        else:
            gp, up = r.gp_buf[slot].astype(F32), r.gp_buf[2 + slot].astype(F32)
        sg = 1.0 / (1.0 + jnp.exp(-gp))
        silu = gp * sg
        hid = silu * up
        hots, gate = chunk_gates(section, j, chunk, cap, r.pos, r.gate)
        if not backward:
            r.gp_buf[slot] = gp.astype(BF)
            r.gp_buf[2 + slot] = up.astype(BF)
            r.y_scr[j, at, :] = (dot(hid.astype(BF), r.wd_buf[slot]) * gate).astype(BF)
            for c in saved(i, slot):
                c.start()
            return
        raw = dot(r.y_scr[j, at, :], r.wd_buf[slot], 1, 1)
        dgate = jnp.sum(hid.astype(BF).astype(F32) * raw, axis=1, keepdims=True)
        for bb in range(n):
            r.dg[section, bb, pl.ds(j, 1), :] = jnp.sum(hots[bb] * dgate[bb * cap : (bb + 1) * cap], axis=0, keepdims=True)
        dh = raw * gate
        dgp = (dh * up * sg * (1.0 + gp * (1.0 - sg))).astype(BF)
        dup = (dh * silu).astype(BF)
        r.act[0, j, at, :] = dgp
        r.act[1, j, at, :] = dup
        r.act[2, j, at, :] = (hid * gate).astype(BF)
        r.y_scr[j, at, :] = (dot(dgp, r.wg_buf[slot], 1, 1) + dot(dup, r.wu_buf[slot], 1, 1)).astype(BF)

    def summed(b, source):
        at = pl.ds(pl.multiple_of(b * cap, cap), cap)
        stacked = jnp.concatenate([source[j, at, :] for j in range(per)], axis=0)
        return dot(all_hots_back(r.pos[b], per, cap), stacked).astype(BF)

    @pl.when(here)
    def _():
        if backward:
            r.dg[...] = jnp.zeros_like(r.dg)
        if mode == "fwd":
            keep_blocks = pltpu.make_async_copy(r.blk, r.blocks, r.row_sem.at[0])
        streamed(2 * per, weights, expert, primed=True)
        if mode == "fwd":
            keep_blocks.start()

        def emit(i, carry):
            to = lax.rem(z + i + 1, n)
            section = jnp.where(i < n, 1 - layer, layer)
            r.pbuf[section, to] = summed(section * n + to, r.y_scr)

            @pl.when(i < n)
            def _():
                for a in arrays:
                    hop(a, to).start()

            @pl.when((i >= n) & (to != z))
            def _():
                for a in arrays:
                    give(a, srcs[a].at[layer, to], i + 1 - n).start()

            return carry

        lax.fori_loop(0, 2 * n, emit, 0)
        for a in arrays:
            keep(a, srcs[a].at[layer, z]).start()
        if mode == "fwd":
            for i in (2 * per - 2, 2 * per - 1):
                for c in saved(i, i % 2):
                    c.wait()
            keep_blocks.wait()
        if mode == "bwd":

            @pl.loop(0, count)
            def _(b):
                put_rows(all_hots(r.pos[b], per, cap).astype(BF), r.blk[b // n, lax.rem(b, n)], b, per, cap, r.y_scr)

            gather_from(count, per, cap, r.pos, r.blocks, r.x_scr, r.row_buf, r.row_sem)
        if mode == "both":
            gather_from(count, per, cap, r.pos, r.gy, r.y_scr, r.row_buf, r.row_sem)
        if backward:
            weight_grads(r, per)
        if mode == "both":
            def output(j, slot):
                @pl.loop(0, 2)
                def _(c):
                    at = pl.ds(pl.multiple_of(c * chunk, chunk), chunk)
                    r.x_scr[j, at, :] = dot(r.act[2, j, at, :], r.wd_buf[slot]).astype(BF)

            streamed(per, lambda j, slot: weights(j, slot)[2:], output)
            combine(0, n, per, cap, r.pos, r.x_scr, r.part0, r.row_buf, r.row_sem)
            combine(n, n, per, cap, r.pos, r.x_scr, r.part1, r.row_buf, r.row_sem)
        for to in range(n):
            for a in arrays:
                hop(a, to).wait_send()

    @pl.when(jnp.logical_not(here))
    def _():
        @pl.loop(1, n + 1)
        def _(k):
            to = lax.rem(lax.rem(k, n) + z, n)
            for a in arrays:
                hop(a, to).wait_recv()

            @pl.when(k < n)
            def _():
                for a in arrays:
                    give(a, relays[a].at[to], k).start()

        for a in arrays:
            keep(a, relays[a].at[z]).start()
        for zz in range(n):
            cross(zz).wait_send()

    if mode == "bwd":

        @pl.when(here)
        def _():
            for zz in range(n):
                over_part(zz).wait_recv()

        @pl.when(jnp.logical_not(here))
        def _():
            for zz in range(n):
                over_part(zz).wait_send()

    if riding:
        ride_on()
        for q in range(1, groups):
            for zz in range(n):
                over(q & (q - 1), low_bit(q), zz).wait_send()
    for a in arrays:
        keep(a, relays[a].at[z]).wait()
        for k in range(1, n):
            give(a, relays[a].at[lax.rem(z + k, n)], k).wait()
    for t in range(n):

        @pl.when((z >= t) & (z < n - 1))
        def _():
            right(t).wait_send()

        @pl.when((z + t < n) & (z > 0))
        def _():
            left(t).wait_send()


def moe(layer, mode, cid, e_pad, cap, own, wg, wu, wd, **given):
    n, groups = lax.axis_size("expert"), lax.axis_size("group")
    count = 2 * n
    t, d = own.shape
    per, _, f = wg.shape
    rows = count * cap
    piece = d // groups
    sds = jax.ShapeDtypeStruct
    dma = pltpu.SemaphoreType.DMA
    vm, hbm = pl.BlockSpec(memory_space=pltpu.VMEM), any_spec()
    on_chip = ("own", "rt", "wrt", "pos", "gate", "dqkv", "at", "dht", "daux", "o")
    ins = dict(own=own, wg=wg, wu=wu, wd=wd, **given)
    outs = dict(back=sds((n, t, d), BF))
    scratch = dict(
        blk=pltpu.VMEM((2, n, t, d), BF),
        y_scr=pltpu.VMEM((per, rows, d), BF),
        wg_buf=pltpu.VMEM((2, d, f), BF),
        wu_buf=pltpu.VMEM((2, d, f), BF),
        wd_buf=pltpu.VMEM((2, f, d), BF),
        pbuf=pltpu.VMEM((2, n, t, d), BF),
        relay=pltpu.VMEM((n, t, d), BF),
        x_scr=pltpu.VMEM((per, rows, d), BF),
        row_buf=pltpu.VMEM((2, t, d), BF),
        row_sem=dma((2,)),
        w_sem=dma((2, 3)),
        keep_sem=dma((2,)),
    )
    for name in ("right", "left", "cross"):
        scratch["s_" + name] = dma((n,))
        scratch["r_" + name] = dma((n,))
    for name in ("hop", "give"):
        scratch["s_" + name] = dma((2, n))
        scratch["r_" + name] = dma((2, n))
    if mode != "both":
        scratch["gp_buf"] = pltpu.VMEM((4, n * cap, f), BF)
        scratch["gp_sem"] = dma((2, 2))
    if mode != "bwd":
        scratch["gates"] = pltpu.VMEM((e_pad, t), F32)
    if mode == "fwd":
        del scratch["row_buf"]
        outs.update(pos=sds((count, 8, t), jnp.int32), gate=sds((count, 8, t), F32))
        outs.update(gp=sds((per, rows, f), BF), up=sds((per, rows, f), BF), blocks=sds((2, n, t, d), BF))
        outs["dense_out"] = sds(given["dense"].shape, BF)
        scratch.update(s_over=dma((groups, n)), r_over=dma((groups, n)))
    else:
        outs["dgate"] = sds((n, 8, t), F32)
        outs["even"] = outs["odd"] = sds((groups // 2, 2, per, piece, f), BF)
        outs["even_dn"] = outs["odd_dn"] = sds((groups // 2, per, f, piece), BF)
        scratch.update(
            dg=pltpu.VMEM((2, n, 8, t), F32),
            dg_relay=pltpu.VMEM((n, 8, t), F32),
            act=pltpu.VMEM((3, per, rows, f), BF),
            gu_buf=pltpu.VMEM((2, 2, 2, piece, f), BF),
            dn_buf=pltpu.VMEM((2, 2, f, piece), BF),
            gu_sem=dma((2, 2)),
            dn_sem=dma((2, 2)),
        )
    if mode == "bwd":
        outs["dd"] = sds((d, QKV + QW + LANES), BF)
        outs["part_out"] = sds((n, t, d), BF)
        scratch.update(s_part=dma((n,)), r_part=dma((n,)))
        scratch.update(dd_sem=dma((3 * d // rows,)), daux_sem=dma)
    if mode == "both":
        outs["part0"] = outs["part1"] = sds((n, t, d), BF)
        scratch.update(pos=pltpu.VMEM((count, 8, t), jnp.int32), gate=pltpu.VMEM((count, 8, t), F32))
    names = tuple(ins) + tuple(outs) + tuple(scratch)
    results = pl.pallas_call(
        functools.partial(moe_kernel, layer, mode, n, e_pad, cap, names),
        out_shape=tuple(outs.values()),
        in_specs=[vm if name in on_chip else hbm for name in ins],
        out_specs=tuple(vm if name in on_chip else hbm for name in outs),
        scratch_shapes=list(scratch.values()),
        input_output_aliases={list(ins).index("dense"): list(outs).index("dense_out")} if mode == "fwd" else {},
        compiler_params=pltpu.CompilerParams(collective_id=cid, has_side_effects=True, vmem_limit_bytes=VMEM_LIMIT),
    )(*ins.values())
    return types.SimpleNamespace(**dict(zip(outs, results)))


def top_bit(q):
    return q.bit_length() - 1


def finish_kernel(
    n, dd0, dd1, egu0, ogu0, ed0, od0, egu1, ogu1, ed1, od1,
    dense_out, gate_out, up_out, down_out,
    core_gu, core_dn, hop_gu, hop_dn, core_dd, hop_y, hop_z, hop_x, dd_buf, gu_buf, dn_buf, gu_f32, dn_f32,
    s_core_gu, r_core_gu, s_core_dn, r_core_dn, s_hop_gu, r_hop_gu, s_hop_dn, r_hop_dn,
    s_core_dd, r_core_dd, s_y, r_y, s_z, r_z, s_x, r_x, l_dd, l_gu, l_dn, o_gu, o_dn,
):
    s, g, z = lax.axis_index("section"), lax.axis_index("group"), lax.axis_index("expert")
    pairs, cgu = core_gu.shape[:2]
    cdn = core_dn.shape[1]
    levels = top_bit(pairs)
    units = pairs * n
    remote = functools.partial(pltpu.make_async_remote_copy, device_id_type=MESH)
    twin = {"group": lax.bitwise_xor(g, 1)}
    other = {"section": 1 - s}

    def across(k):
        return {"group": lax.bitwise_xor(g, 2 << k)}

    barrier = pltpu.get_barrier_semaphore()
    peers = [twin, other] + [across(k) for k in range(levels)] + [{"expert": lax.rem(z + k, n)} for k in range(1, n)]
    for peer in peers:
        pl.semaphore_signal(barrier, inc=1, device_id=peer, device_id_type=MESH)
    pl.semaphore_wait(barrier, len(peers))

    def by_section(action):
        @pl.when(s == 0)
        def _():
            action(dd0, dd1, egu0, ogu0, ed0, od0)

        @pl.when(s != 0)
        def _():
            action(dd1, dd0, egu1, ogu1, ed1, od1)

    def unit(i):
        return pairs - 1 - i // n, lax.rem(z + 1 + lax.rem(i, n), n)

    def shard(i, core):
        q, place = unit(i)
        return (lax.bitwise_xor(g // 2, q) * 2 + core) * n + place

    core = lax.rem(g, 2)

    def core_dd_copy(kind, i, source):
        return remote(
            src_ref=source.at[shard(i, 1 - core)],
            dst_ref=core_dd.at[kind, i],
            send_sem=s_core_dd.at[kind, i],
            recv_sem=r_core_dd.at[kind, i],
            device_id=twin,
        )

    def core_chunk(source, dest, ssem, rsem, q, c):
        return remote(
            src_ref=source.at[q, c], dst_ref=dest.at[q, c], send_sem=ssem.at[q, c], recv_sem=rsem.at[q, c], device_id=twin
        )

    def core_gu_copy(source, q, c):
        return core_chunk(source, core_gu, s_core_gu, r_core_gu, q, c)

    def core_dn_copy(source, q, c):
        return core_chunk(source, core_dn, s_core_dn, r_core_dn, q, c)

    def send_all(own, away, egu, ogu, ed, od):
        @pl.loop(0, units)
        def _(i):
            core_dd_copy(0, i, away).start()

            @pl.when(i < cgu)
            def _():
                core_gu_copy(ogu, pairs - 1, i).start()

            @pl.when(i < cdn)
            def _():
                core_dn_copy(od, pairs - 1, i).start()

        for i in range(units, max(cgu, cdn)):
            if i < cgu:
                core_gu_copy(ogu, pairs - 1, i).start()
            if i < cdn:
                core_dn_copy(od, pairs - 1, i).start()

        @pl.loop(0, units)
        def _(i):
            core_dd_copy(1, i, own).start()

        for q in reversed(range(pairs - 1)):

            @pl.loop(0, cgu)
            def _(c):
                core_gu_copy(ogu, q, c).start()

            @pl.loop(0, cdn)
            def _(c):
                core_dn_copy(od, q, c).start()

    by_section(send_all)

    def load(buf, sem, slot, source):
        return pltpu.make_async_copy(source, buf.at[slot], sem.at[slot])

    def dd_load(i, slot, source):
        return load(dd_buf, l_dd, slot, source.at[shard(i, core)])

    def hop(dest, ssem, rsem, source, k, q, c):
        return remote(
            src_ref=source.at[q, c],
            dst_ref=dest.at[k, q - (1 << k), c],
            send_sem=ssem.at[k, q - (1 << k), c],
            recv_sem=rsem.at[k, q - (1 << k), c],
            device_id=across(k),
        )

    def gu_hop(k, q, c):
        return hop(hop_gu, s_hop_gu, r_hop_gu, core_gu, k, q, c)

    def dn_hop(k, q, c):
        return hop(hop_dn, s_hop_dn, r_hop_dn, core_dn, k, q, c)

    def y_copy(i):
        return remote(src_ref=core_dd.at[0, i], dst_ref=hop_y.at[i], send_sem=s_y.at[i], recv_sem=r_y.at[i], device_id=other)

    def z_copy(q, k, i):
        return remote(
            src_ref=core_dd.at[1, i],
            dst_ref=hop_z.at[k - 1, q],
            send_sem=s_z.at[k - 1, q],
            recv_sem=r_z.at[k - 1, q],
            device_id={"expert": lax.rem(z + k, n)},
        )

    def x_copy(k, q, i):
        return remote(
            src_ref=core_dd.at[1, i],
            dst_ref=hop_x.at[k, q - (1 << k)],
            send_sem=s_x.at[k, q - (1 << k)],
            recv_sem=r_x.at[k, q - (1 << k)],
            device_id=across(k),
        )

    def chunk_start(i, slot, q, egu, ed):
        @pl.when(i < cgu)
        def _():
            load(gu_buf, l_gu, slot, egu.at[q, i]).start()

        @pl.when(i < cdn)
        def _():
            load(dn_buf, l_dn, slot, ed.at[q, i]).start()

    def expert_sum(hops, rsem, dest, core_r, buf, sem, slot, even, q, c, hop_copy):
        load(buf, sem, slot, even.at[q, c]).wait()
        core_r(q, c).wait_recv()
        total = buf[slot].astype(F32) + dest[q, c].astype(F32)
        for k in range(top_bit(q) + 1 if q else 0, levels):
            hop_copy(k, q + (1 << k), c).wait_recv()
            total = total + hops[k, q, c].astype(F32)
        return total

    def gu_sum(slot, q, c):
        return expert_sum(hop_gu, r_hop_gu, core_gu, functools.partial(core_gu_copy, ogu0), gu_buf, l_gu, slot, egu0, q, c, gu_hop)

    def dn_sum(slot, q, c):
        return expert_sum(hop_dn, r_hop_dn, core_dn, functools.partial(core_dn_copy, od0), dn_buf, l_dn, slot, ed0, q, c, dn_hop)

    def stepped(count, start, body):
        start(0, 0)

        def step(i, carry):
            @pl.when(i + 1 < count)
            def _():
                start(i + 1, lax.rem(i + 1, 2))

            body(i, lax.rem(i, 2))
            return carry

        lax.fori_loop(0, count, step, 0)

    for q in reversed(range(1, pairs)):
        dense_too = q == pairs - 1
        steps = max(units, cgu, cdn) if dense_too else max(cgu, cdn)

        def start(i, slot):
            def go(own, away, egu, ogu, ed, od):
                if dense_too:

                    @pl.when(i < units)
                    def _():
                        dd_load(i, slot, away).start()

                chunk_start(i, slot, q, egu, ed)

            by_section(go)

        def body(i, slot):
            if dense_too:

                @pl.when(i < units)
                def _():
                    dd_load(i, slot, dd0).wait()
                    core_dd_copy(0, i, dd0).wait_recv()
                    core_dd[0, i] = core_dd[0, i] + dd_buf[slot]
                    y_copy(i).start()

            @pl.when(i < cgu)
            def _():
                core_gu[q, i] = gu_sum(slot, q, i).astype(BF)
                gu_hop(top_bit(q), q, i).start()

            @pl.when(i < cdn)
            def _():
                core_dn[q, i] = dn_sum(slot, q, i).astype(BF)
                dn_hop(top_bit(q), q, i).start()

        stepped(steps, start, body)

    def gu_out_copy(c, slot, to=gate_out):
        return pltpu.make_async_copy(gu_f32.at[slot], to.at[lax.rem(c, cgu // 2)], o_gu.at[slot])

    def dn_out_copy(c, slot):
        return pltpu.make_async_copy(dn_f32.at[slot], down_out.at[c], o_dn.at[slot])

    def dense_sum(q):
        i = (pairs - 1 - q) * n + n - 1
        total = core_dd[1, i].astype(F32)
        for k in range(1, n):
            z_copy(q, k, i).wait_recv()
            total = total + hop_z[k - 1, q].astype(F32)
        for k in range(top_bit(q) + 1 if q else 0, levels):
            x_copy(k, q + (1 << k), i).wait_recv()
            total = total + hop_x[k, q].astype(F32)
        return i, total

    def pass_on(q):
        i, total = dense_sum(q)
        core_dd[1, i] = total.astype(BF)
        x_copy(top_bit(q), q, i).start()

    steps = max(units, cgu, cdn)

    def start(i, slot):
        def go(own, away, egu, ogu, ed, od):
            @pl.when(i < units)
            def _():
                dd_load(i, slot, own).start()

            chunk_start(i, slot, 0, egu, ed)

        by_section(go)

    def body(i, slot):
        @pl.when(i < units)
        def _():
            dd_load(i, slot, dd0).wait()
            core_dd_copy(1, i, dd0).wait_recv()
            y_copy(i).wait_recv()
            core_dd[1, i] = (core_dd[1, i].astype(F32) + dd_buf[slot].astype(F32) + hop_y[i].astype(F32)).astype(BF)
            q, _ = unit(i)
            k = lax.rem(i, n) + 1

            @pl.when(k < n)
            def _():
                z_copy(q, k, i).start()

        for q in range(1, pairs):

            @pl.when(i == (pairs - q) * n + min(2, n - 1))
            def _():
                pass_on(q)

        @pl.when(i < cgu)
        def _():
            @pl.when(i >= 2)
            def _():
                gu_out_copy(i - 2, slot).wait()

            gu_f32[slot] = gu_sum(slot, 0, i)

            @pl.when(i < cgu // 2)
            def _():
                gu_out_copy(i, slot).start()

            @pl.when(i >= cgu // 2)
            def _():
                gu_out_copy(i, slot, up_out).start()

        @pl.when(i < cdn)
        def _():
            @pl.when(i >= 2)
            def _():
                dn_out_copy(i - 2, slot).wait()

            dn_f32[slot] = dn_sum(slot, 0, i)
            dn_out_copy(i, slot).start()

    stepped(steps, start, body)
    _, total = dense_sum(0)
    dense_out[...] = total
    for c in (cgu - 2, cgu - 1):
        gu_out_copy(c, c % 2).wait()
    for c in (cdn - 2, cdn - 1):
        dn_out_copy(c, c % 2).wait()

    @pl.loop(0, units)
    def _(i):
        core_dd_copy(0, i, dd0).wait_send()
        core_dd_copy(1, i, dd0).wait_send()
        y_copy(i).wait_send()
        q, _ = unit(i)
        k = lax.rem(i, n) + 1

        @pl.when(k < n)
        def _():
            z_copy(q, k, i).wait_send()

    for q in range(pairs):
        if q:
            x_copy(top_bit(q), q, (pairs - 1 - q) * n + n - 1).wait_send()

        @pl.loop(0, cgu)
        def _(c):
            core_gu_copy(ogu0, q, c).wait_send()
            if q:
                gu_hop(top_bit(q), q, c).wait_send()

        @pl.loop(0, cdn)
        def _(c):
            core_dn_copy(od0, q, c).wait_send()
            if q:
                dn_hop(top_bit(q), q, c).wait_send()


def finish(cid, dd0, dd1, experts0, experts1):
    n, groups = lax.axis_size("expert"), lax.axis_size("group")
    pairs, levels = groups // 2, top_bit(groups // 2)
    width = dd0.shape[1]
    rows = dd0.shape[0] // (groups * n)
    dd0, dd1 = (v.reshape(groups * n, rows, width) for v in (dd0, dd1))

    def chunked(arrays):
        gu_even, gu_odd, dn_even, dn_odd = arrays
        flat = (pairs, -1) + gu_even.shape[3:]
        return gu_even.reshape(flat), gu_odd.reshape(flat), dn_even, dn_odd

    experts0, experts1 = chunked(experts0), chunked(experts1)
    gu, dn = experts0[0].shape[1:], experts0[2].shape[1:]
    units = pairs * n
    dma = pltpu.SemaphoreType.DMA
    sds = jax.ShapeDtypeStruct
    half = max(1, pairs // 2)

    def both(shape):
        return [dma(shape), dma(shape)]

    return pl.pallas_call(
        functools.partial(finish_kernel, n),
        out_shape=(sds((rows, width), F32), sds((gu[0] // 2,) + gu[1:], F32), sds((gu[0] // 2,) + gu[1:], F32), sds(dn, F32)),
        in_specs=[any_spec()] * 10,
        out_specs=(pl.BlockSpec(memory_space=pltpu.VMEM), any_spec(), any_spec(), any_spec()),
        scratch_shapes=[
            pltpu.VMEM((pairs,) + gu, BF),
            pltpu.VMEM((pairs,) + dn, BF),
            pltpu.VMEM((levels, half) + gu, BF),
            pltpu.VMEM((levels, half) + dn, BF),
            pltpu.VMEM((2, units, rows, width), BF),
            pltpu.VMEM((units, rows, width), BF),
            pltpu.VMEM((n - 1, pairs, rows, width), BF),
            pltpu.VMEM((levels, half, rows, width), BF),
            pltpu.VMEM((2, rows, width), BF),
            pltpu.VMEM((2,) + gu[1:], BF),
            pltpu.VMEM((2,) + dn[1:], BF),
            pltpu.VMEM((2,) + gu[1:], F32),
            pltpu.VMEM((2,) + dn[1:], F32),
        ]
        + both((pairs, gu[0]))
        + both((pairs, dn[0]))
        + both((levels, half, gu[0]))
        + both((levels, half, dn[0]))
        + both((2, units))
        + both((units,))
        + both((n - 1, pairs))
        + both((levels, half))
        + [dma((2,))] * 5,
        compiler_params=pltpu.CompilerParams(collective_id=cid, has_side_effects=True, vmem_limit_bytes=VMEM_LIMIT),
    )(dd0, dd1, *experts0, *experts1)


def low_bit(q):
    return top_bit(q & -q)


def open_kernel(
    n, groups, pieces, w_ref, cot_ref, rt_ref, w0_out, w1_out, gy_out, rt_out, rt_side,
    s_right, r_right, s_left, r_left, s_group, r_group, s_y, r_y, s_cross, r_cross, s_rt, r_rt, s_side, r_side, local_sem,
):
    s, g, z = lax.axis_index("section"), lax.axis_index("group"), lax.axis_index("expert")
    remote = functools.partial(pltpu.make_async_remote_copy, device_id_type=MESH)
    rows = w_ref.shape[0] // pieces
    bits = top_bit(groups)
    other = {"section": 1 - s}
    barrier = pltpu.get_barrier_semaphore()
    peers = [other] + [{"group": lax.bitwise_xor(g, 1 << b)} for b in range(bits)] + [{"expert": lax.rem(z + k, n)} for k in range(1, n)]
    for peer in peers:
        pl.semaphore_signal(barrier, inc=1, device_id=peer, device_id_type=MESH)
    pl.semaphore_wait(barrier, len(peers))
    sent = []

    def launch(cond, make):
        sent.append((cond, make))
        if cond is None:
            make().start()
        else:

            @pl.when(cond)
            def _():
                make().start()

    def part(q, zz, c):
        if c == 2 * pieces:
            return gy_out.at[s, zz]
        return (w0_out, w1_out)[c // pieces].at[lax.bitwise_xor(g, q) * n + zz, pl.ds(c % pieces * rows, rows)]

    def chain(to, zz, t, c, ssem, rsem):
        return remote(src_ref=part(0, zz, c), dst_ref=part(0, zz, c), send_sem=ssem.at[t, c], recv_sem=rsem.at[t, c], device_id={"expert": to})

    def right(t, c):
        return chain(z + 1, z - t, t, c, s_right, r_right)

    def left(t, c):
        return chain(z - 1, z + t, t, c, s_left, r_left)

    def over(q, b, zz, c):
        at = q | (1 << b)
        return remote(
            src_ref=part(q, zz, c), dst_ref=part(q, zz, c), send_sem=s_group.at[at, zz, c], recv_sem=r_group.at[at, zz, c],
            device_id={"group": lax.bitwise_xor(g, 1 << b)},
        )

    def hop(c, to=w0_out):
        at = pl.ds(c * rows, rows)
        return remote(src_ref=w_ref.at[at], dst_ref=to.at[g * n + z, at], send_sem=s_y.at[c], recv_sem=r_y.at[c], device_id=other)

    def by_layer(action):
        for layer, to in enumerate((w0_out, w1_out)):

            @pl.when(s == layer)
            def _(to=to):
                action(to)

    def cross(zz):
        return remote(src_ref=gy_out.at[0, zz], dst_ref=gy_out.at[0, zz], send_sem=s_cross.at[zz], recv_sem=r_cross.at[zz], device_id=other)

    def route(m, k):
        return remote(
            src_ref=rt_ref.at[m], dst_ref=rt_out.at[m, z], send_sem=s_rt.at[m, k], recv_sem=r_rt.at[m, k],
            device_id={"expert": lax.rem(z + k, n)},
        )

    def side():
        return remote(src_ref=rt_ref.at[1 - s], dst_ref=rt_side, send_sem=s_side, recv_sem=r_side, device_id=other)

    by_layer(lambda to: hop(0, to).start())
    launch(None, side)
    own = [pltpu.make_async_copy(cot_ref, gy_out.at[s, z], local_sem.at[0])]
    own += [pltpu.make_async_copy(rt_ref.at[m], rt_out.at[m, z], local_sem.at[1 + m]) for m in range(2)]

    def keep(to=w0_out):
        return pltpu.make_async_copy(w_ref, to.at[g * n + z], local_sem.at[3])

    for copy in own:
        copy.start()

    by_layer(lambda to: keep(to).start())
    keep().wait()

    def spread_out(cond, zz, c):
        if c < pieces:
            for b in reversed(range(bits)):
                launch(cond, functools.partial(over, 0, b, zz, c))
        elif c == 2 * pieces:
            launch((s == 0) if cond is None else ((s == 0) & cond), functools.partial(cross, zz))

    def pass_along(t, c):
        if t == 0:
            if c < 2 * pieces:

                @pl.when(s != c // pieces)
                def _():
                    hop(c % pieces).wait_recv()
            else:
                own[0].wait()
            launch(z < n - 1, functools.partial(right, t, c))
            launch(z > 0, functools.partial(left, t, c))
            spread_out(None, z, c)
            if c + 1 < pieces:
                hop(c).wait_send()
                by_layer(lambda to: hop(c + 1, to).start())
        else:
            from_left, from_right = z >= t, z + t < n

            @pl.when(from_left)
            def _():
                right(t - 1, c).wait_recv()

            launch(from_left & (z < n - 1), functools.partial(right, t, c))
            spread_out(from_left, z - t, c)

            @pl.when(from_right)
            def _():
                left(t - 1, c).wait_recv()

            launch(from_right & (z > 0), functools.partial(left, t, c))
            spread_out(from_right, z + t, c)

    def forward(q, k):
        zz = lax.rem(z + k, n)
        for c in range(pieces):
            over(q & (q - 1), low_bit(q), zz, c).wait_recv()
            for b in reversed(range(low_bit(q))):
                launch(None, functools.partial(over, q, b, zz, c))

    for t in range(n):
        for c in range(pieces):
            pass_along(t, c)
        if t == 0:
            for m in range(2):
                for k in range(1, n):
                    launch(None, functools.partial(route, m, k))
    pending = [(q, k) for q in sorted(range(1, groups), key=lambda q: -low_bit(q)) for k in range(n)]
    for t in range(n):
        pass_along(t, 2 * pieces)
        forward(*pending.pop(0))
    for t in range(n):
        for c in range(pieces, 2 * pieces):
            pass_along(t, c)
    for q, k in pending:
        forward(q, k)

    @pl.when(s != 0)
    def _():
        for zz in range(n):
            cross(zz).wait_recv()

    side().wait_recv()
    for m in range(2):
        own[1 + m].wait()
        for k in range(1, n):
            route(m, k).wait_recv()
    hop(pieces - 1).wait_send()
    for cond, make in sent:
        if cond is None:
            make().wait_send()
        else:

            @pl.when(cond)
            def _(make=make):
                make().wait_send()


def open_up(cid, packed, cot, rt):
    n, groups = lax.axis_size("expert"), lax.axis_size("group")
    sh = packed.shape[0]
    pieces = 3 if sh % 48 == 0 else 1
    dma = pltpu.SemaphoreType.DMA
    sds = jax.ShapeDtypeStruct

    def both(shape):
        return [dma(shape), dma(shape)]

    w0, w1, gy, rt_all, rt_side = pl.pallas_call(
        functools.partial(open_kernel, n, groups, pieces),
        out_shape=(sds((groups * n,) + packed.shape, BF),) * 2 + (sds((2, n) + cot.shape, BF), sds((2, n) + rt.shape[1:], rt.dtype), sds(rt.shape[1:], rt.dtype)),
        in_specs=vmem(3),
        out_specs=tuple([any_spec()] * 5),
        scratch_shapes=both((n, 2 * pieces + 1)) + both((n, 2 * pieces + 1)) + both((groups, n, pieces)) + both((pieces,)) + both((n,)) + both((2, n)) + [dma, dma] + [dma((4,))],
        compiler_params=pltpu.CompilerParams(collective_id=cid, has_side_effects=True),
    )(packed, cot, rt)
    return w0.reshape(groups * n * sh, -1), w1, gy, rt_all, rt_side


def swap_sections(value):
    return lax.ppermute(value, "section", [(0, 1), (1, 0)])


def rope_tables(t):
    half = HEAD_SIZE // 2
    frequency = THETA ** (-jnp.arange(half, dtype=F32) * 2.0 / HEAD_SIZE)
    angles = jnp.arange(t, dtype=F32)[:, None] * frequency[None, :]
    reps = LANES // half
    return jnp.tile(jnp.cos(angles), (1, reps)), jnp.tile(jnp.sin(angles), (1, reps))


def local(
    inputs, cotangent, segment_ids, live_first, routes, gain_attn, gain_moe,
    w_query, key_weight, value_weight, w_out, w_router, w_gate, w_up, w_down,
):
    s = lax.axis_index("section")
    n = lax.axis_size("expert")
    groups = lax.axis_size("group")
    t, d = inputs.shape[2:]
    top = routes.shape[-1]
    per = w_gate.shape[1]
    experts = per * n
    e_pad = -(-experts // 16) * 16
    cap = t * top * 5 // (4 * experts)
    wg, wu, wd = w_gate[0], w_up[0], w_down[0]
    at_zero = s == 0

    shard = w_query.shape[1]
    aux = jnp.concatenate(
        [
            w_router[0],
            jnp.zeros((shard, GAIN_MOE_ROW - experts), BF),
            gain_moe[0][:, None],
            gain_attn[0][:, None],
        ],
        axis=1,
    )
    packed = jnp.concatenate([w_query[0], key_weight[0], value_weight[0], w_out[0].T, aux], axis=1)
    x0 = lax.dynamic_index_in_dim(inputs[:, 0], s, 0, keepdims=False)
    cot = lax.dynamic_index_in_dim(cotangent[:, 0], s, 0, keepdims=False)
    seg = lax.dynamic_index_in_dim(segment_ids[:, 0], s, 0, keepdims=False)
    live = lax.dynamic_index_in_dim(live_first[:, 0], s, 0, keepdims=False)
    meta = jnp.stack([seg, jnp.repeat(live, BLK)], axis=1)
    meta = jnp.pad(meta, ((0, 0), (0, LANES - 2)))
    segr = jnp.broadcast_to(seg[None, :], (8, t))
    cos, sin = rope_tables(t)

    rt = jnp.swapaxes(routes[0, :, 0], 1, 2)
    rt_mine = lax.dynamic_index_in_dim(rt, s, 0, keepdims=False)

    def flat(z):
        return z.reshape((2 * n,) + z.shape[2:])

    def paired(z):
        return z.reshape((2, n) + z.shape[1:])

    first_weights, second_weights, gy1, rt_all, rt_theirs = open_up(1, packed, cot, rt)
    rt_tokens = (jnp.where(at_zero, rt_mine, rt_theirs), jnp.where(at_zero, rt_theirs, rt_mine))
    gy1, rt_all = flat(gy1), flat(rt_all)

    none = jnp.zeros((1, t, d), BF)
    qkv0, p0, o0, h0, b0, wrt0, x0 = attn_fwd(x0, none, first_weights, cos, sin, meta, segr)
    m0 = moe(0, "fwd", 2, e_pad, cap, b0, wg, wu, wd, rt=rt_all, wrt=wrt0, dense=second_weights)
    second_weights = m0.dense_out.reshape(first_weights.shape)

    qkv1, p1, o1, h1, b1, wrt1, x1 = attn_fwd(h0, m0.back, second_weights, cos, sin, meta, segr)
    m1 = moe(1, "both", 3, e_pad, cap, b1, wg, wu, wd, rt=rt_all, wrt=wrt1, gy=gy1)

    def gates_back(dg):
        dg = dg[:, :per].reshape(experts, t)
        return jnp.pad(dg, ((0, e_pad - experts), (0, 0)))

    dx1, gy0, dqkv1, at1, dht1, daux1 = attn_bwd(False, cot, h1, x1, second_weights, qkv1, p1, o1, b1, wrt1, m1.back, gates_back(m1.dgate), rt_tokens[1], cos, sin)

    n0 = moe(0, "bwd", 4, e_pad, cap, gy0, wg, wu, wd, pos=m0.pos, gate=m0.gate, gp=m0.gp, up=m0.up, blocks=flat(m0.blocks),
             dqkv=dqkv1, at=at1, dht=dht1, daux=daux1, o=o1, part=m1.part0)
    dd1 = n0.dd
    dback0 = n0.back
    back1 = lax.all_to_all(jnp.where(at_zero, n0.part_out, m1.part1), "expert", split_axis=0, concat_axis=0, tiled=True)
    y1 = (h1 + jnp.sum(back1.astype(F32), axis=0)).astype(BF)
    dx0, _, dd0 = attn_bwd(True, gy0, h0, x0, first_weights, qkv0, p0, o0, b0, wrt0, dback0, gates_back(n0.dgate), rt_tokens[0], cos, sin)

    dense, gate_grad, up_grad, down = finish(5, dd0, dd1, (n0.even, n0.odd, n0.even_dn, n0.odd_dn), (m1.even, m1.odd, m1.even_dn, m1.odd_dn))

    kept_out = jnp.where(at_zero, x1, y1)
    swapped_out = swap_sections(jnp.where(at_zero, y1, x1))
    layer_out = jnp.where(at_zero, jnp.stack([kept_out, swapped_out]), jnp.stack([swapped_out, kept_out]))
    kept_in = jnp.where(at_zero, dx0, dx1)
    swapped_in = swap_sections(jnp.where(at_zero, dx1, dx0))
    input_grad = jnp.where(at_zero, jnp.stack([kept_in, swapped_in]), jnp.stack([swapped_in, kept_in]))

    return (
        layer_out[None, :, None],
        input_grad[None, :, None],
        dense[:, QKV + QW + GAIN_ATTN_ROW][None],
        dense[:, QKV + QW + GAIN_MOE_ROW][None],
        dense[None, :, 0:QW],
        dense[None, :, QW : QW + KW],
        dense[None, :, QW + KW : QKV],
        dense[:, QKV : QKV + QW].T[None],
        dense[None, :, QKV + QW : QKV + QW + experts],
        gate_grad[None],
        up_grad[None],
        down[None],
    )


def solution(mesh):
    return jax.shard_map(
        local,
        mesh=mesh,
        in_specs=(
            P(None, ("group", "expert"), None, None),
            P(None, ("group", "expert"), None, None),
            P(None, ("group", "expert"), None),
            P(None, ("group", "expert"), None),
            P("section", None, ("group", "expert"), None, None),
            P("section", ("group", "expert")),
            P("section", ("group", "expert")),
            P("section", ("group", "expert"), None),
            P("section", ("group", "expert"), None),
            P("section", ("group", "expert"), None),
            P("section", None, ("group", "expert")),
            P("section", ("group", "expert"), None),
            P("section", "expert", None, None),
            P("section", "expert", None, None),
            P("section", "expert", None, None),
        ),
        out_specs=(
            P("section", None, ("group", "expert"), None, None),
            P("section", None, ("group", "expert"), None, None),
            P("section", ("group", "expert")),
            P("section", ("group", "expert")),
            P("section", ("group", "expert"), None),
            P("section", ("group", "expert"), None),
            P("section", ("group", "expert"), None),
            P("section", None, ("group", "expert")),
            P("section", ("group", "expert"), None),
            P("section", "expert", "group", None),
            P("section", "expert", "group", None),
            P("section", "expert", None, "group"),
        ),
        check_vma=False,
    )
```

```python
import functools
import types

import jax
import jax.numpy as jnp
import numpy as np
from jax import lax
from jax.experimental import pallas as pl
from jax.experimental.pallas import tpu as pltpu
from jax.sharding import PartitionSpec as P

QUERY_HEADS = 24
KEY_VALUE_HEADS = 8
HEAD_SIZE = 64
BLK = 64
EPS = 1e-06
THETA = 10000.0
NEG_FILL = -1e30
BF = jnp.bfloat16
F32 = jnp.float32
MESH = pl.DeviceIdType.MESH
LANES = 128
TILE = 512
QW = QUERY_HEADS * HEAD_SIZE
KW = KEY_VALUE_HEADS * HEAD_SIZE
QKV = QW + 2 * KW
GAIN_MOE_ROW = 126
GAIN_ATTN_ROW = 127
VMEM_LIMIT = 60 * 1024 * 1024
HEAD_PAIRS = KEY_VALUE_HEADS // 2
TILES_PER_PAIR = QUERY_HEADS // KEY_VALUE_HEADS


def dot(a, b, ca=1, cb=0):
    return lax.dot_general(a, b, (((ca,), (cb,)), ((), ())), preferred_element_type=F32)


def iota(shape, axis):
    return lax.broadcasted_iota(jnp.int32, shape, axis)


def rope(z, cos, sin, direction):
    width = z.shape[1]
    half = HEAD_SIZE // 2
    first = iota(z.shape, 1) % HEAD_SIZE < half
    partner = jnp.where(first, pltpu.roll(z, width - half, 1), pltpu.roll(z, half, 1))
    signed = jnp.where(first, -direction, direction) * partner
    reps = width // LANES
    return z * jnp.concatenate([cos] * reps, axis=1) + signed * jnp.concatenate([sin] * reps, axis=1)


def lane_masks(t):
    low = iota((t, LANES), 1) < HEAD_SIZE
    return low, jnp.logical_not(low)


def swapped(z):
    return pltpu.roll(z.astype(F32), HEAD_SIZE, 1).astype(BF)


def head_plan():
    return [(r, half, (2 * r + half) // TILES_PER_PAIR != half) for r in range(TILES_PER_PAIR) for half in range(2)]


def pick(z, half, masks):
    return jnp.where(masks[half], z, jnp.zeros_like(z))


def weight_pieces(d, order):
    aux = [(pl.ds(0, d), pl.ds(QKV + QW, LANES))]
    qkv = [(pl.ds(0, d), pl.ds(n * TILE, TILE)) for n in range(QKV // TILE)]
    out = [(pl.ds(n * TILE, TILE), pl.ds(QKV, QW)) for n in range(d // TILE)]
    down = [(pl.ds(0, d), pl.ds(QKV + n * TILE, TILE)) for n in range(QW // TILE)]
    rows = [(pl.ds(n * TILE, TILE), pl.ds(0, QKV)) for n in range(d // TILE)]
    return aux + qkv + out if order == "forward" else down + rows


def arriving(w_hbm, w_ref, sem, order):
    copies = [
        pltpu.make_async_copy(w_hbm.at[rows, cols], w_ref.at[rows, cols], sem.at[i])
        for i, (rows, cols) in enumerate(weight_pieces(w_ref.shape[0], order))
    ]
    for c in copies:
        c.start()
    return copies


def attn_fwd_kernel(
    below_ref, back_ref, w_hbm, cos_ref, sin_ref, seg_ref, live_ref,
    qkv_ref, p_ref, o_ref, h_ref, b_ref, wrt_ref, x_ref, w_ref, w_sem,
):
    t, d = x_ref.shape
    pieces = arriving(w_hbm, w_ref, w_sem, "forward")
    mine = lax.axis_index("section")
    entering = (below_ref[mine] if len(below_ref.shape) == 3 else below_ref[...]).astype(F32)
    for z in range(back_ref.shape[0]):
        entering = entering + back_ref[z].astype(F32)
    x_ref[...] = entering.astype(BF)
    pieces.pop(0).wait()
    aux = jnp.transpose(w_ref[:, QKV + QW :].astype(F32))
    wrt_ref[...] = aux.astype(BF)
    gain_attn = aux[GAIN_ATTN_ROW : GAIN_ATTN_ROW + 1]
    gain_moe = aux[GAIN_MOE_ROW : GAIN_MOE_ROW + 1]
    x = x_ref[...].astype(F32)
    r1 = lax.rsqrt(jnp.mean(x * x, axis=1, keepdims=True) + EPS)
    a = (x * r1 * gain_attn).astype(BF)
    cos, sin = cos_ref[...], sin_ref[...]
    for n in range(QKV // TILE):
        cols = slice(n * TILE, (n + 1) * TILE)
        pieces.pop(0).wait()
        y = dot(a, w_ref[:, cols])
        if n * TILE < QW + KW:
            y = rope(y, cos, sin, 1.0)
        qkv_ref[:, cols] = y.astype(BF)
    i, j = iota((t, t), 0), iota((t, t), 1)
    segments = jnp.broadcast_to(seg_ref[pl.ds(mine, 1), :].astype(F32), (t, t))
    first_block = jnp.zeros((t, t), jnp.int32)
    for block in range(t // BLK):
        first_block = jnp.where(i // BLK == block, live_ref[mine, block], first_block)
    allowed = (j <= i) & (jnp.transpose(segments) == segments) & (j // BLK >= first_block)
    masks = lane_masks(t)

    def pair(m, carry):
        def lanes(base):
            return pl.ds(pl.multiple_of(base, LANES), LANES)

        kp = qkv_ref[:, lanes(QW + m * LANES)]
        vp = qkv_ref[:, lanes(QW + KW + m * LANES)]
        ks, vs = swapped(kp), swapped(vp)
        parts = {}
        for r, half, swap in head_plan():
            q = pick(qkv_ref[:, lanes((m * TILES_PER_PAIR + r) * LANES)], half, masks)
            s = dot(q, ks if swap else kp, 1, 1) * HEAD_SIZE ** (-0.5)
            s = jnp.where(allowed, s, NEG_FILL)
            e = jnp.exp(s - jnp.max(s, axis=1, keepdims=True))
            p = e * (1.0 / jnp.sum(e, axis=1, keepdims=True))
            p_ref[m * 2 * TILES_PER_PAIR + 2 * r + half] = p
            part = dot(p.astype(BF), pick(vs if swap else vp, half, masks))
            parts[half] = part
            if half == 1:
                o_ref[:, lanes((m * TILES_PER_PAIR + r) * LANES)] = (parts[0] + parts[1]).astype(BF)
        return carry

    lax.fori_loop(0, HEAD_PAIRS, pair, 0)
    o = o_ref[...]
    for n in range(d // TILE):
        rows = slice(n * TILE, (n + 1) * TILE)
        pieces.pop(0).wait()
        h_ref[:, rows] = x_ref[:, rows].astype(F32) + dot(o, w_ref[rows, QKV : QKV + QW], 1, 1)
    h = h_ref[...]
    r2 = lax.rsqrt(jnp.mean(h * h, axis=1, keepdims=True) + EPS)
    b_ref[...] = (h * r2 * gain_moe).astype(BF)


def vmem(n):
    return [pl.BlockSpec(memory_space=pltpu.VMEM)] * n


def attn_fwd(below, back, w, cos, sin, seg, live):
    t, d = below.shape[-2:]
    sds = jax.ShapeDtypeStruct
    return pl.pallas_call(
        attn_fwd_kernel,
        out_shape=(
            sds((t, QKV), BF),
            sds((QUERY_HEADS, t, t), F32),
            sds((t, QW), BF),
            sds((t, d), F32),
            sds((t, d), BF),
            sds((LANES, d), BF),
            sds((t, d), BF),
        ),
        in_specs=vmem(2) + [any_spec()] + vmem(3) + [pl.BlockSpec(memory_space=pltpu.SMEM)],
        out_specs=tuple(vmem(7)),
        scratch_shapes=[pltpu.VMEM(w.shape, BF), pltpu.SemaphoreType.DMA((1 + QKV // TILE + d // TILE,))],
        compiler_params=pltpu.CompilerParams(vmem_limit_bytes=VMEM_LIMIT),
        cost_estimate=pl.CostEstimate(flops=2 * t * d * 4096, bytes_accessed=w.size * 2, transcendentals=QUERY_HEADS * t * t),
    )(below, back, w, cos, sin, seg, live)


def gates_of(rt, wrt, b, e_pad):
    t = rt.shape[1]
    experts = iota((e_pad, t), 0)
    chosen = experts == rt[0:1]
    for k in range(1, rt.shape[0]):
        chosen = chosen | (experts == rt[k : k + 1])
    logits = jnp.where(chosen, dot(wrt[0:e_pad], b, 1, 1), NEG_FILL)
    e = jnp.where(chosen, jnp.exp(logits - jnp.max(logits, axis=0, keepdims=True)), 0.0)
    return e / jnp.sum(e, axis=0, keepdims=True)


def attn_bwd_kernel(
    now, e_pad, gy_ref, h_ref, x_ref, w_hbm, qkv_ref, p_ref, o_ref, b_ref, wrt_ref, back_ref, dg_ref, rt_ref, cos_ref, sin_ref,
    dx_ref, dxb_ref, *rest,
):
    t, d = x_ref.shape
    if now:
        dd_hbm, do_ref, dqkv_ref, dh_ref, w_ref, w_sem, lt_ref, dd_ref, dd_sem = rest
    else:
        dqkv_ref, at_ref, dht_ref, daux_ref, do_ref, dh_ref, w_ref, w_sem = rest
    pieces = arriving(w_hbm, w_ref, w_sem, "backward")
    leaving = []

    def leave(first, width):
        cols = pl.ds(first, width)
        leaving.append(pltpu.make_async_copy(dd_ref.at[:, cols], dd_hbm.at[:, cols], dd_sem.at[len(leaving)]))
        leaving[-1].start()

    gain_attn = wrt_ref[GAIN_ATTN_ROW - 7 :, :].astype(F32)[7:8]
    gain_moe = wrt_ref[GAIN_ATTN_ROW - 7 :, :].astype(F32)[6:7]
    b = b_ref[...]
    gates = gates_of(rt_ref[...], wrt_ref, b, e_pad)
    dg = dg_ref[...]
    dl = (gates * (dg - jnp.sum(gates * dg, axis=0, keepdims=True)))
    dlb = dl.astype(BF)
    db = dot(dlb, wrt_ref[0:e_pad, :], 0, 0)
    for z in range(back_ref.shape[0]):
        db = db + back_ref[z].astype(F32)
    h = h_ref[...]
    r2 = lax.rsqrt(jnp.mean(h * h, axis=1, keepdims=True) + EPS)
    grad_moe = jnp.sum(db * h * r2, axis=0, keepdims=True)
    dn = db * gain_moe
    gy = gy_ref[lax.axis_index("section")] if len(gy_ref.shape) == 3 else gy_ref[...]
    dh = gy.astype(F32) + r2 * dn - h * (r2 * r2 * r2) * jnp.mean(dn * h, axis=1, keepdims=True)
    dh_ref[...] = dh
    dhb = dh.astype(BF)
    for n in range(QW // TILE):
        cols = slice(n * TILE, (n + 1) * TILE)
        pieces.pop(0).wait()
        do_ref[:, cols] = dot(dhb, w_ref[:, QKV + n * TILE : QKV + (n + 1) * TILE]).astype(BF)
    masks = lane_masks(t)
    cos, sin = cos_ref[...], sin_ref[...]

    def pair(m, carry):
        def lanes(base):
            return pl.ds(pl.multiple_of(base, LANES), LANES)

        kp = qkv_ref[:, lanes(QW + m * LANES)]
        vp = qkv_ref[:, lanes(QW + KW + m * LANES)]
        ks, vs = swapped(kp), swapped(vp)
        zero = jnp.zeros((t, LANES), F32)
        dk = {False: zero, True: zero}
        dv = {False: zero, True: zero}
        dq = zero
        for r, half, swap in head_plan():
            tile = lanes((m * TILES_PER_PAIR + r) * LANES)
            q = pick(qkv_ref[:, tile], half, masks)
            do = pick(do_ref[:, tile], half, masks)
            p = p_ref[m * 2 * TILES_PER_PAIR + 2 * r + half]
            dp = dot(do, vs if swap else vp, 1, 1)
            dv[swap] = dv[swap] + dot(p.astype(BF), do, 0, 0)
            dt = p * (dp - jnp.sum(p * dp, axis=1, keepdims=True)) * HEAD_SIZE ** (-0.5)
            dt = dt.astype(BF)
            dk[swap] = dk[swap] + dot(dt, q, 0, 0)
            part = dot(dt, pick(ks if swap else kp, half, masks))
            dq = part if half == 0 else dq + part
            if half == 1:
                dqkv_ref[:, tile] = rope(dq, cos, sin, -1.0).astype(BF)
        dk_all = dk[False] + pltpu.roll(dk[True], HEAD_SIZE, 1)
        dv_all = dv[False] + pltpu.roll(dv[True], HEAD_SIZE, 1)
        dqkv_ref[:, lanes(QW + m * LANES)] = rope(dk_all, cos, sin, -1.0).astype(BF)
        dqkv_ref[:, lanes(QW + KW + m * LANES)] = dv_all.astype(BF)
        return carry

    lax.fori_loop(0, HEAD_PAIRS, pair, 0)
    x = x_ref[...].astype(F32)
    r1 = lax.rsqrt(jnp.mean(x * x, axis=1, keepdims=True) + EPS)
    dqkv = dqkv_ref[...]
    for n in range(d // TILE):
        rows = slice(n * TILE, (n + 1) * TILE)
        pieces.pop(0).wait()
        dx_ref[:, rows] = dot(dqkv, w_ref[rows, 0:QKV], 1, 1)
    da = dx_ref[...]
    grad_attn = jnp.sum(da * x * r1, axis=0, keepdims=True)
    dag = da * gain_attn
    dx = dh_ref[...] + r1 * dag - x * (r1 * r1 * r1) * jnp.mean(dag * x, axis=1, keepdims=True)
    dx_ref[...] = dx
    dxb_ref[...] = dx.astype(BF)
    row = iota((LANES, d), 0)
    grads = jnp.where(row == GAIN_MOE_ROW, grad_moe, jnp.where(row == GAIN_ATTN_ROW, grad_attn, 0.0))
    dl_full = jnp.concatenate([dl, jnp.zeros((LANES - e_pad, t), F32)], axis=0)
    dl_rows = jnp.transpose(dl_full).astype(BF)
    bt = jnp.transpose(b_ref[...].astype(F32)).astype(BF)
    daux = (dot(bt, dl_rows) + jnp.transpose(grads)).astype(BF)
    if not now:
        at_ref[...] = jnp.transpose(x * r1 * gain_attn).astype(BF)
        dht_ref[...] = jnp.transpose(dh_ref[...]).astype(BF)
        daux_ref[...] = daux
        return
    lt_ref[...] = jnp.transpose(x * r1 * gain_attn).astype(BF)
    for n in range(QKV // TILE):
        cols = slice(n * TILE, (n + 1) * TILE)
        dd_ref[:, cols] = dot(lt_ref[...], dqkv_ref[:, cols]).astype(BF)
        leave(n * TILE, TILE)
    lt_ref[...] = jnp.transpose(dh_ref[...]).astype(BF)
    for n in range(QW // TILE):
        cols = slice(n * TILE, (n + 1) * TILE)
        dd_ref[:, QKV + n * TILE : QKV + (n + 1) * TILE] = dot(lt_ref[...], o_ref[:, cols]).astype(BF)
        leave(QKV + n * TILE, TILE)
    dd_ref[:, QKV + QW :] = daux
    leave(QKV + QW, LANES)
    for c in leaving:
        c.wait()


def attn_bwd(now, gy, h, x, w, qkv, p, o, b, wrt, back, dg, rt, cos, sin):
    t, d = x.shape
    sds = jax.ShapeDtypeStruct
    dma = pltpu.SemaphoreType.DMA
    outs = [sds((t, d), F32), sds((t, d), BF)]
    scratch = [pltpu.VMEM((t, QW), BF)]
    if now:
        outs.append(sds(w.shape, BF))
        scratch.append(pltpu.VMEM((t, QKV), BF))
    else:
        outs += [sds((t, QKV), BF), sds((d, t), BF), sds((d, t), BF), sds((d, LANES), BF)]
    scratch += [pltpu.VMEM((t, d), F32), pltpu.VMEM(w.shape, BF), dma((QW // TILE + d // TILE,))]
    if now:
        scratch += [pltpu.VMEM((d, t), BF), pltpu.VMEM(w.shape, BF), dma((1 + QKV // TILE + QW // TILE,))]
    return pl.pallas_call(
        functools.partial(attn_bwd_kernel, now, dg.shape[0]),
        out_shape=tuple(outs),
        in_specs=vmem(3) + [any_spec()] + vmem(10),
        out_specs=tuple(vmem(2) + [any_spec()] if now else vmem(6)),
        scratch_shapes=scratch,
        compiler_params=pltpu.CompilerParams(vmem_limit_bytes=VMEM_LIMIT),
        cost_estimate=pl.CostEstimate(flops=4 * t * d * 4096, bytes_accessed=w.size * 4, transcendentals=0),
    )(gy, h, x, w, qkv, p, o, b, wrt, back, dg, rt, cos, sin)


def one_hot(pos_row, cap):
    return jnp.where(iota((cap, pos_row.shape[1]), 0) == pos_row, 1.0, 0.0)


def all_hots(pos, per, cap):
    return jnp.concatenate([one_hot(pos[j : j + 1], cap) for j in range(per)], axis=0)


def all_hots_back(pos, per, cap):
    width = per * cap
    expert = jnp.where(iota((8, width), 1) // cap == iota((8, width), 0), 1.0, 0.0).astype(BF)
    wide = dot(pos.astype(F32).astype(BF), expert, 0, 0)
    slot = (iota((1, width), 1) % cap).astype(F32)
    return jnp.where(wide == slot, 1.0, 0.0).astype(BF)


def slots_of(rt, first, per):
    t = rt.shape[1]
    experts = iota((16, t), 0)
    mine = jnp.where(experts < per, experts + first, -1)
    chosen = mine == rt[0:1]
    for k in range(1, rt.shape[0]):
        chosen = chosen | (mine == rt[k : k + 1])
    earlier = jnp.where(iota((t, t), 0) < iota((t, t), 1), 1.0, 0.0).astype(BF)
    before = dot(jnp.where(chosen, 1.0, 0.0).astype(BF), earlier)
    return jnp.where(chosen, before.astype(jnp.int32), -1)[0:8]


def streamed(count, copies, body, primed=False):
    if not primed:
        for c in copies(0, 0):
            c.start()

    def step(b, carry):
        slot = lax.rem(b, 2)

        @pl.when(b + 1 < count)
        def _():
            for c in copies(b + 1, lax.rem(b + 1, 2)):
                c.start()

        for c in copies(b, slot):
            c.wait()
        body(b, slot)
        return carry

    lax.fori_loop(0, count, step, 0)


def combine(base, count, per, cap, pos_ref, rows_ref, out_hbm, obuf, osem):
    def copy(b, slot):
        return pltpu.make_async_copy(obuf.at[slot], out_hbm.at[b], osem.at[slot])

    def step(b, carry):
        slot = lax.rem(b, 2)

        @pl.when(b >= 2)
        def _():
            copy(b - 2, slot).wait()

        back = all_hots_back(pos_ref[base + b], per, cap)
        at = pl.ds(pl.multiple_of((base + b) * cap, cap), cap)
        rows = jnp.concatenate([rows_ref[j, at, :] for j in range(per)], axis=0)
        obuf[slot] = dot(back, rows).astype(BF)
        copy(b, slot).start()
        return carry

    lax.fori_loop(0, count, step, 0)
    copy(count - 2, (count - 2) % 2).wait()
    copy(count - 1, (count - 1) % 2).wait()


def chunk_gates(c, j, chunk, cap, pos_ref, gate_ref):
    hots, gates = [], []
    for bb in range(chunk // cap):
        b = c * (chunk // cap) + bb
        hot = one_hot(pos_ref[b, pl.ds(j, 1), :], cap)
        hots.append(hot)
        gates.append(jnp.sum(hot * gate_ref[b, pl.ds(j, 1), :], axis=1, keepdims=True))
    return hots, jnp.concatenate(gates, axis=0)


def any_spec():
    return pl.BlockSpec(memory_space=pl.ANY)


def put_rows(hots, block, b, per, cap, dest):
    at = pl.ds(pl.multiple_of(b * cap, cap), cap)
    rows = dot(hots, block).astype(BF)
    for k in range(per):
        dest[k, at, :] = rows[k * cap : (k + 1) * cap]


def gather_from(count, per, cap, pos, source, dest, buf, sem):
    def body(b, slot):
        put_rows(all_hots(pos[b], per, cap).astype(BF), buf[slot], b, per, cap, dest)

    streamed(count, lambda b, slot: [pltpu.make_async_copy(source.at[b], buf.at[slot], sem.at[slot])], body)


def weight_grads(r, per):
    parts, piece = r.even.shape[0], r.even.shape[3]
    g = lax.axis_index("group")
    parity, place = lax.rem(g, 2), g // 2

    def outgoing(j, at, slot):
        return [
            pltpu.make_async_copy(r.gu_buf.at[slot, 0], r.even.at[at, :, j], r.gu_sem.at[slot, 0]),
            pltpu.make_async_copy(r.gu_buf.at[slot, 1], r.odd.at[at, :, j], r.gu_sem.at[slot, 1]),
            pltpu.make_async_copy(r.dn_buf.at[slot, 0], r.even_dn.at[at, j], r.dn_sem.at[slot, 0]),
            pltpu.make_async_copy(r.dn_buf.at[slot, 1], r.odd_dn.at[at, j], r.dn_sem.at[slot, 1]),
        ]

    def finished(slot):
        for c in outgoing(0, 0, slot):
            c.wait()

    def body(j, carry):
        for q in range(parts):
            slot = q % 2
            if q >= 2:
                finished(slot)
            else:

                @pl.when(j > 0)
                def _():
                    finished(slot)

            cols = slice(2 * q * piece, 2 * (q + 1) * piece)
            for m in range(2):
                full = dot(r.x_scr[j, :, cols], r.act[m, j], 0, 0).astype(BF)
                r.gu_buf[slot, parity, m] = full[:piece]
                r.gu_buf[slot, 1 - parity, m] = full[piece:]
            full = dot(r.act[2, j], r.y_scr[j, :, cols], 0, 0).astype(BF)
            r.dn_buf[slot, parity] = full[:, :piece]
            r.dn_buf[slot, 1 - parity] = full[:, piece:]
            for c in outgoing(j, lax.bitwise_xor(place, q), slot):
                c.start()
        return carry

    lax.fori_loop(0, per, body, 0)
    for slot in range(2):
        finished(slot)


def meet(n, bits):
    s, g, z = lax.axis_index("section"), lax.axis_index("group"), lax.axis_index("expert")
    barrier = pltpu.get_barrier_semaphore()
    peers = [{"section": 1 - s}] + [{"expert": lax.rem(z + k, n)} for k in range(1, n)]
    peers += [{"group": lax.bitwise_xor(g, 1 << b)} for b in range(bits)]
    for peer in peers:
        pl.semaphore_signal(barrier, inc=1, device_id=peer, device_id_type=MESH)
    pl.semaphore_wait(barrier, len(peers))


def moe_kernel(layer, mode, n, e_pad, cap, names, *refs):
    r = types.SimpleNamespace(**dict(zip(names, refs)))
    forward, backward = mode != "bwd", mode != "fwd"
    s, z = lax.axis_index("section"), lax.axis_index("expert")
    here = s == layer
    count = 2 * n
    per, rows, d = r.y_scr.shape
    first = z * per
    chunk = n * cap
    remote = functools.partial(pltpu.make_async_remote_copy, device_id_type=MESH)
    other = {"section": 1 - s}
    g = lax.axis_index("group")
    riding = forward and not backward
    groups = r.dense_out.shape[0] // n if riding else 1
    bits = top_bit(groups)
    meet(n, bits)
    r.blk[s, z] = r.own[...]

    def over(q, b, zz):
        at = q | (1 << b)
        shard = r.dense_out.at[lax.bitwise_xor(g, q) * n + zz]
        return remote(
            src_ref=shard, dst_ref=shard, send_sem=r.s_over.at[at, zz], recv_sem=r.r_over.at[at, zz],
            device_id={"group": lax.bitwise_xor(g, 1 << b)},
        )

    def ride():
        for b in reversed(range(bits)):
            for zz in range(n):
                over(0, b, zz).start()

    def ride_on():
        for q in sorted(range(1, groups), key=lambda q: -low_bit(q)):
            for zz in range(n):
                over(q & (q - 1), low_bit(q), zz).wait_recv()
                for b in reversed(range(low_bit(q))):
                    over(q, b, zz).start()

    if riding:
        ride()

    def half(i):
        section = jnp.where(i < per, layer, 1 - layer)
        return lax.rem(i, per), section, pl.ds(pl.multiple_of(section * chunk, chunk), chunk)

    def weights(i, slot):
        j, _, at = half(i)
        both = [
            pltpu.make_async_copy(r.wg.at[j], r.wg_buf.at[slot], r.w_sem.at[slot, 0]),
            pltpu.make_async_copy(r.wu.at[j], r.wu_buf.at[slot], r.w_sem.at[slot, 1]),
            pltpu.make_async_copy(r.wd.at[j], r.wd_buf.at[slot], r.w_sem.at[slot, 2]),
        ]
        if mode == "bwd":
            both.append(pltpu.make_async_copy(r.gp.at[j, at], r.gp_buf.at[slot], r.gp_sem.at[slot, 0]))
            both.append(pltpu.make_async_copy(r.up.at[j, at], r.gp_buf.at[2 + slot], r.gp_sem.at[slot, 1]))
        return both

    def chain(to, zz, t, ssem, rsem):
        return remote(
            src_ref=r.blk.at[s, zz], dst_ref=r.blk.at[s, zz], send_sem=ssem.at[t], recv_sem=rsem.at[t], device_id={"expert": to}
        )

    def right(t):
        return chain(z + 1, z - t, t, r.s_right, r.r_right)

    def left(t):
        return chain(z - 1, z + t, t, r.s_left, r.r_left)

    def cross(zz):
        return remote(
            src_ref=r.blk.at[s, zz], dst_ref=r.blk.at[s, zz], send_sem=r.s_cross.at[zz], recv_sem=r.r_cross.at[zz], device_id=other
        )

    def prepare(section, zz):
        b = section * n + zz
        block = r.blk[section, zz]
        if forward:
            rt = r.rt[b]
            pos = slots_of(rt, first, per)
            r.pos[b] = pos
            r.gates[...] = gates_of(rt, r.wrt, block, e_pad)
            r.gate[b] = jnp.concatenate(
                [r.gates[pl.ds(first + k, 1), :] for k in range(per)] + [jnp.zeros((8 - per, rt.shape[1]), F32)], axis=0
            )
            put_rows(all_hots(pos, per, cap).astype(BF), block, b, per, cap, r.x_scr)
        else:
            put_rows(all_hots(r.pos[b], per, cap).astype(BF), block, b, per, cap, r.y_scr)

    @pl.when(here)
    def _():
        for c in weights(0, 0):
            c.start()

    def prepare_at(section, t):
        def candidate(m, carry):
            zz = jnp.where(m == 0, z - t, z + t)

            @pl.when((zz >= 0) & (zz < n) & ((m == 0) | (t > 0)))
            def _():
                prepare(section, zz)

            return carry

        lax.fori_loop(0, 2, candidate, 0)

    def dense_tiles():
        tiles = []
        for first_row in range(0, d, rows):
            for left, right, col, width in ((r.at, r.dqkv, 0, QW), (r.at, r.dqkv, QW, 2 * KW), (r.dht, r.o, QKV, QW)):
                source = right if left is r.dht else right.at[:, pl.ds(col, width)]
                tiles.append((left.at[pl.ds(first_row, rows)], source, first_row, col, width))
        return tiles

    def dense_copy(i, tile):
        _, _, row, col, width = tile
        return pltpu.make_async_copy(
            r.x_scr.at[i % per, :, pl.ds(0, width)], r.dd.at[pl.ds(row, rows), pl.ds(col, width)], r.dd_sem.at[i]
        )

    def aux_copy():
        return pltpu.make_async_copy(r.daux, r.dd.at[:, pl.ds(QKV + QW, LANES)], r.daux_sem)

    def dense_start(step):
        if step == 0:
            aux_copy().start()
        tiles = dense_tiles()
        share = len(tiles) // 3
        for i, tile in list(enumerate(tiles))[step * share : (step + 1) * share]:
            if i >= per:
                dense_copy(i - per, tiles[i - per]).wait()
            left, right, _, _, width = tile
            r.x_scr[i % per, :, 0:width] = dot(left[...], right[...]).astype(BF)
            dense_copy(i, tile).start()

    def dense_wait():
        aux_copy().wait()
        tiles = dense_tiles()
        for i in range(max(0, len(tiles) - per), len(tiles)):
            dense_copy(i, tiles[i]).wait()

    @pl.loop(0, n)
    def _(t):
        from_left = z >= t
        from_right = z + t < n

        @pl.when(from_left & (t > 0))
        def _():
            right(t - 1).wait_recv()

        @pl.when(from_left & (z < n - 1))
        def _():
            right(t).start()

        @pl.when(from_left & jnp.logical_not(here))
        def _():
            cross(z - t).start()

        @pl.when(from_right & (t > 0))
        def _():
            left(t - 1).wait_recv()

        @pl.when(from_right & (z > 0))
        def _():
            left(t).start()

        @pl.when(from_right & (t > 0) & jnp.logical_not(here))
        def _():
            cross(z + t).start()

        if mode == "bwd":

            for step in range(3):

                @pl.when(t == step)
                def _(step=step):
                    dense_start(step)

        @pl.when(here)
        def _():
            if mode == "both":

                @pl.when(t == 0)
                def _():
                    @pl.loop(0, count)
                    def _(b):
                        r.pos[b] = slots_of(r.rt[b], first, per)

                    gather_from(count, per, cap, r.pos, r.gy, r.y_scr, r.row_buf, r.row_sem)

            prepare_at(layer, t)

    def late_blocks():
        @pl.loop(0, n)
        def _(t):
            @pl.when(z >= t)
            def _():
                cross(z - t).wait_recv()

            @pl.when((t > 0) & (z + t < n))
            def _():
                cross(z + t).wait_recv()

            prepare_at(1 - layer, t)

    def over_part(zz):
        return remote(
            src_ref=r.part.at[zz], dst_ref=r.part_out.at[zz], send_sem=r.s_part.at[zz], recv_sem=r.r_part.at[zz], device_id=other
        )

    if mode == "bwd":
        dense_wait()

        @pl.when(jnp.logical_not(here))
        def _():
            for zz in range(n):
                over_part(zz).start()

    srcs = (r.pbuf, r.dg) if backward else (r.pbuf,)
    outs = (r.back, r.dgate) if backward else (r.back,)
    relays = (r.relay, r.dg_relay) if backward else (r.relay,)
    arrays = range(len(srcs))

    def hop(a, to):
        return remote(
            src_ref=srcs[a].at[1 - layer, to],
            dst_ref=relays[a].at[to],
            send_sem=r.s_hop.at[a, to],
            recv_sem=r.r_hop.at[a, to],
            device_id=other,
        )

    def give(a, source, k):
        return remote(
            src_ref=source,
            dst_ref=outs[a].at[z],
            send_sem=r.s_give.at[a, k],
            recv_sem=r.r_give.at[a, k],
            device_id={"expert": lax.rem(z + k, n)},
        )

    def keep(a, source):
        return pltpu.make_async_copy(source, outs[a].at[z], r.keep_sem.at[a])

    def saved(i, slot):
        j, _, at = half(i)
        return [
            pltpu.make_async_copy(r.gp_buf.at[slot], r.gp.at[j, at], r.gp_sem.at[slot, 0]),
            pltpu.make_async_copy(r.gp_buf.at[2 + slot], r.up.at[j, at], r.gp_sem.at[slot, 1]),
        ]

    def expert(i, slot):
        j, section, at = half(i)

        @pl.when(i == per)
        def _():
            late_blocks()

        if mode == "fwd":

            @pl.when(i >= 2)
            def _():
                for c in saved(i - 2, slot):
                    c.wait()

        if forward:
            x = r.x_scr[j, at, :]
            gp = dot(x, r.wg_buf[slot])
            up = dot(x, r.wu_buf[slot])
        else:
            gp, up = r.gp_buf[slot].astype(F32), r.gp_buf[2 + slot].astype(F32)
        sg = 1.0 / (1.0 + jnp.exp(-gp))
        silu = gp * sg
        hid = silu * up
        hots, gate = chunk_gates(section, j, chunk, cap, r.pos, r.gate)
        if not backward:
            r.gp_buf[slot] = gp.astype(BF)
            r.gp_buf[2 + slot] = up.astype(BF)
            r.y_scr[j, at, :] = (dot(hid.astype(BF), r.wd_buf[slot]) * gate).astype(BF)
            for c in saved(i, slot):
                c.start()
            return
        raw = dot(r.y_scr[j, at, :], r.wd_buf[slot], 1, 1)
        dgate = jnp.sum(hid.astype(BF).astype(F32) * raw, axis=1, keepdims=True)
        for bb in range(n):
            r.dg[section, bb, pl.ds(j, 1), :] = jnp.sum(hots[bb] * dgate[bb * cap : (bb + 1) * cap], axis=0, keepdims=True)
        dh = raw * gate
        dgp = (dh * up * sg * (1.0 + gp * (1.0 - sg))).astype(BF)
        dup = (dh * silu).astype(BF)
        r.act[0, j, at, :] = dgp
        r.act[1, j, at, :] = dup
        r.act[2, j, at, :] = (hid * gate).astype(BF)
        r.y_scr[j, at, :] = (dot(dgp, r.wg_buf[slot], 1, 1) + dot(dup, r.wu_buf[slot], 1, 1)).astype(BF)

    def summed(b, source):
        at = pl.ds(pl.multiple_of(b * cap, cap), cap)
        stacked = jnp.concatenate([source[j, at, :] for j in range(per)], axis=0)
        return dot(all_hots_back(r.pos[b], per, cap), stacked).astype(BF)

    @pl.when(here)
    def _():
        if backward:
            r.dg[...] = jnp.zeros_like(r.dg)
        if mode == "fwd":
            keep_blocks = pltpu.make_async_copy(r.blk, r.blocks, r.row_sem.at[0])
        streamed(2 * per, weights, expert, primed=True)
        if mode == "fwd":
            keep_blocks.start()

        def emit(i, carry):
            to = lax.rem(z + i + 1, n)
            section = jnp.where(i < n, 1 - layer, layer)
            r.pbuf[section, to] = summed(section * n + to, r.y_scr)

            @pl.when(i < n)
            def _():
                for a in arrays:
                    hop(a, to).start()

            @pl.when((i >= n) & (to != z))
            def _():
                for a in arrays:
                    give(a, srcs[a].at[layer, to], i + 1 - n).start()

            return carry

        lax.fori_loop(0, 2 * n, emit, 0)
        for a in arrays:
            keep(a, srcs[a].at[layer, z]).start()
        if mode == "fwd":
            for i in (2 * per - 2, 2 * per - 1):
                for c in saved(i, i % 2):
                    c.wait()
            keep_blocks.wait()
        if mode == "bwd":

            @pl.loop(0, count)
            def _(b):
                put_rows(all_hots(r.pos[b], per, cap).astype(BF), r.blk[b // n, lax.rem(b, n)], b, per, cap, r.y_scr)

            gather_from(count, per, cap, r.pos, r.blocks, r.x_scr, r.row_buf, r.row_sem)
        if mode == "both":
            gather_from(count, per, cap, r.pos, r.gy, r.y_scr, r.row_buf, r.row_sem)
        if backward:
            weight_grads(r, per)
        if mode == "both":
            def output(j, slot):
                @pl.loop(0, 2)
                def _(c):
                    at = pl.ds(pl.multiple_of(c * chunk, chunk), chunk)
                    r.x_scr[j, at, :] = dot(r.act[2, j, at, :], r.wd_buf[slot]).astype(BF)

            streamed(per, lambda j, slot: weights(j, slot)[2:], output)
            combine(0, n, per, cap, r.pos, r.x_scr, r.part0, r.row_buf, r.row_sem)
            combine(n, n, per, cap, r.pos, r.x_scr, r.part1, r.row_buf, r.row_sem)
        for to in range(n):
            for a in arrays:
                hop(a, to).wait_send()

    @pl.when(jnp.logical_not(here))
    def _():
        @pl.loop(1, n + 1)
        def _(k):
            to = lax.rem(lax.rem(k, n) + z, n)
            for a in arrays:
                hop(a, to).wait_recv()

            @pl.when(k < n)
            def _():
                for a in arrays:
                    give(a, relays[a].at[to], k).start()

        for a in arrays:
            keep(a, relays[a].at[z]).start()
        for zz in range(n):
            cross(zz).wait_send()

    if mode == "bwd":

        @pl.when(here)
        def _():
            for zz in range(n):
                over_part(zz).wait_recv()

        @pl.when(jnp.logical_not(here))
        def _():
            for zz in range(n):
                over_part(zz).wait_send()

    if riding:
        ride_on()
        for q in range(1, groups):
            for zz in range(n):
                over(q & (q - 1), low_bit(q), zz).wait_send()
    for a in arrays:
        keep(a, relays[a].at[z]).wait()
        for k in range(1, n):
            give(a, relays[a].at[lax.rem(z + k, n)], k).wait()
    for t in range(n):

        @pl.when((z >= t) & (z < n - 1))
        def _():
            right(t).wait_send()

        @pl.when((z + t < n) & (z > 0))
        def _():
            left(t).wait_send()


def moe(layer, mode, cid, e_pad, cap, own, wg, wu, wd, **given):
    n, groups = lax.axis_size("expert"), lax.axis_size("group")
    count = 2 * n
    t, d = own.shape
    per, _, f = wg.shape
    rows = count * cap
    piece = d // groups
    sds = jax.ShapeDtypeStruct
    dma = pltpu.SemaphoreType.DMA
    vm, hbm = pl.BlockSpec(memory_space=pltpu.VMEM), any_spec()
    on_chip = ("own", "rt", "wrt", "pos", "gate", "dqkv", "at", "dht", "daux", "o")
    ins = dict(own=own, wg=wg, wu=wu, wd=wd, **given)
    outs = dict(back=sds((n, t, d), BF))
    scratch = dict(
        blk=pltpu.VMEM((2, n, t, d), BF),
        y_scr=pltpu.VMEM((per, rows, d), BF),
        wg_buf=pltpu.VMEM((2, d, f), BF),
        wu_buf=pltpu.VMEM((2, d, f), BF),
        wd_buf=pltpu.VMEM((2, f, d), BF),
        pbuf=pltpu.VMEM((2, n, t, d), BF),
        relay=pltpu.VMEM((n, t, d), BF),
        x_scr=pltpu.VMEM((per, rows, d), BF),
        row_buf=pltpu.VMEM((2, t, d), BF),
        row_sem=dma((2,)),
        w_sem=dma((2, 3)),
        keep_sem=dma((2,)),
    )
    for name in ("right", "left", "cross"):
        scratch["s_" + name] = dma((n,))
        scratch["r_" + name] = dma((n,))
    for name in ("hop", "give"):
        scratch["s_" + name] = dma((2, n))
        scratch["r_" + name] = dma((2, n))
    if mode != "both":
        scratch["gp_buf"] = pltpu.VMEM((4, n * cap, f), BF)
        scratch["gp_sem"] = dma((2, 2))
    if mode != "bwd":
        scratch["gates"] = pltpu.VMEM((e_pad, t), F32)
    if mode == "fwd":
        del scratch["row_buf"]
        outs.update(pos=sds((count, 8, t), jnp.int32), gate=sds((count, 8, t), F32))
        outs.update(gp=sds((per, rows, f), BF), up=sds((per, rows, f), BF), blocks=sds((2, n, t, d), BF))
        outs["dense_out"] = sds(given["dense"].shape, BF)
        scratch.update(s_over=dma((groups, n)), r_over=dma((groups, n)))
    else:
        outs["dgate"] = sds((n, 8, t), F32)
        outs["even"] = outs["odd"] = sds((groups // 2, 2, per, piece, f), BF)
        outs["even_dn"] = outs["odd_dn"] = sds((groups // 2, per, f, piece), BF)
        scratch.update(
            dg=pltpu.VMEM((2, n, 8, t), F32),
            dg_relay=pltpu.VMEM((n, 8, t), F32),
            act=pltpu.VMEM((3, per, rows, f), BF),
            gu_buf=pltpu.VMEM((2, 2, 2, piece, f), BF),
            dn_buf=pltpu.VMEM((2, 2, f, piece), BF),
            gu_sem=dma((2, 2)),
            dn_sem=dma((2, 2)),
        )
    if mode == "bwd":
        outs["dd"] = sds((d, QKV + QW + LANES), BF)
        outs["part_out"] = sds((n, t, d), BF)
        scratch.update(s_part=dma((n,)), r_part=dma((n,)))
        scratch.update(dd_sem=dma((3 * d // rows,)), daux_sem=dma)
    if mode == "both":
        outs["part0"] = outs["part1"] = sds((n, t, d), BF)
        scratch.update(pos=pltpu.VMEM((count, 8, t), jnp.int32), gate=pltpu.VMEM((count, 8, t), F32))
    names = tuple(ins) + tuple(outs) + tuple(scratch)
    results = pl.pallas_call(
        functools.partial(moe_kernel, layer, mode, n, e_pad, cap, names),
        out_shape=tuple(outs.values()),
        in_specs=[vm if name in on_chip else hbm for name in ins],
        out_specs=tuple(vm if name in on_chip else hbm for name in outs),
        scratch_shapes=list(scratch.values()),
        input_output_aliases={list(ins).index("dense"): list(outs).index("dense_out")} if mode == "fwd" else {},
        compiler_params=pltpu.CompilerParams(collective_id=cid, has_side_effects=True, vmem_limit_bytes=VMEM_LIMIT),
    )(*ins.values())
    return types.SimpleNamespace(**dict(zip(outs, results)))


def top_bit(q):
    return q.bit_length() - 1


def finish_kernel(
    n, dd0, dd1, dx0, dx1, egu0, ogu0, ed0, od0, egu1, ogu1, ed1, od1,
    dense_out, dx_out, gate_out, up_out, down_out,
    core_gu, core_dn, hop_gu, hop_dn, core_dd, hop_y, hop_z, hop_x, dd_buf, gu_buf, dn_buf, gu_res, dn_res,
    s_core_gu, r_core_gu, s_core_dn, r_core_dn, s_hop_gu, r_hop_gu, s_hop_dn, r_hop_dn,
    s_core_dd, r_core_dd, s_y, r_y, s_z, r_z, s_x, r_x, l_dd, l_gu, l_dn, o_gu, o_dn, s_dx, r_dx,
):
    s, g, z = lax.axis_index("section"), lax.axis_index("group"), lax.axis_index("expert")
    pairs, cgu = core_gu.shape[:2]
    cdn = core_dn.shape[1]
    levels = top_bit(pairs)
    units = pairs * n
    remote = functools.partial(pltpu.make_async_remote_copy, device_id_type=MESH)
    twin = {"group": lax.bitwise_xor(g, 1)}
    other = {"section": 1 - s}

    def across(k):
        return {"group": lax.bitwise_xor(g, 2 << k)}

    barrier = pltpu.get_barrier_semaphore()
    peers = [twin, other] + [across(k) for k in range(levels)] + [{"expert": lax.rem(z + k, n)} for k in range(1, n)]
    for peer in peers:
        pl.semaphore_signal(barrier, inc=1, device_id=peer, device_id_type=MESH)
    pl.semaphore_wait(barrier, len(peers))

    def by_section(action):
        @pl.when(s == 0)
        def _():
            action(dd0, dd1, egu0, ogu0, ed0, od0)

        @pl.when(s != 0)
        def _():
            action(dd1, dd0, egu1, ogu1, ed1, od1)

    def unit(i):
        return pairs - 1 - i // n, lax.rem(z + 1 + lax.rem(i, n), n)

    def shard(i, core):
        q, place = unit(i)
        return (lax.bitwise_xor(g // 2, q) * 2 + core) * n + place

    core = lax.rem(g, 2)

    def core_dd_copy(kind, i, source):
        return remote(
            src_ref=source.at[shard(i, 1 - core)],
            dst_ref=core_dd.at[kind, i],
            send_sem=s_core_dd.at[kind, i],
            recv_sem=r_core_dd.at[kind, i],
            device_id=twin,
        )

    def core_chunk(source, dest, ssem, rsem, q, c):
        return remote(
            src_ref=source.at[q, c], dst_ref=dest.at[q, c], send_sem=ssem.at[q, c], recv_sem=rsem.at[q, c], device_id=twin
        )

    def core_gu_copy(source, q, c):
        return core_chunk(source, core_gu, s_core_gu, r_core_gu, q, c)

    def core_dn_copy(source, q, c):
        return core_chunk(source, core_dn, s_core_dn, r_core_dn, q, c)

    def send_all(own, away, egu, ogu, ed, od):
        @pl.loop(0, units)
        def _(i):
            core_dd_copy(0, i, away).start()

            @pl.when(i < cgu)
            def _():
                core_gu_copy(ogu, pairs - 1, i).start()

            @pl.when(i < cdn)
            def _():
                core_dn_copy(od, pairs - 1, i).start()

        for i in range(units, max(cgu, cdn)):
            if i < cgu:
                core_gu_copy(ogu, pairs - 1, i).start()
            if i < cdn:
                core_dn_copy(od, pairs - 1, i).start()

        @pl.loop(0, units)
        def _(i):
            core_dd_copy(1, i, own).start()

        for q in reversed(range(pairs - 1)):

            @pl.loop(0, cgu)
            def _(c):
                core_gu_copy(ogu, q, c).start()

            @pl.loop(0, cdn)
            def _(c):
                core_dn_copy(od, q, c).start()

    by_section(send_all)

    def dx_copy(source):
        return remote(src_ref=source, dst_ref=dx_out, send_sem=s_dx, recv_sem=r_dx, device_id=other)

    def load(buf, sem, slot, source):
        return pltpu.make_async_copy(source, buf.at[slot], sem.at[slot])

    def dd_load(i, slot, source):
        return load(dd_buf, l_dd, slot, source.at[shard(i, core)])

    def hop(dest, ssem, rsem, source, k, q, c):
        return remote(
            src_ref=source.at[q, c],
            dst_ref=dest.at[k, q - (1 << k), c],
            send_sem=ssem.at[k, q - (1 << k), c],
            recv_sem=rsem.at[k, q - (1 << k), c],
            device_id=across(k),
        )

    def gu_hop(k, q, c):
        return hop(hop_gu, s_hop_gu, r_hop_gu, core_gu, k, q, c)

    def dn_hop(k, q, c):
        return hop(hop_dn, s_hop_dn, r_hop_dn, core_dn, k, q, c)

    def y_copy(i):
        return remote(src_ref=core_dd.at[0, i], dst_ref=hop_y.at[i], send_sem=s_y.at[i], recv_sem=r_y.at[i], device_id=other)

    def z_copy(q, k, i):
        return remote(
            src_ref=core_dd.at[1, i],
            dst_ref=hop_z.at[k - 1, q],
            send_sem=s_z.at[k - 1, q],
            recv_sem=r_z.at[k - 1, q],
            device_id={"expert": lax.rem(z + k, n)},
        )

    def x_copy(k, q, i):
        return remote(
            src_ref=core_dd.at[1, i],
            dst_ref=hop_x.at[k, q - (1 << k)],
            send_sem=s_x.at[k, q - (1 << k)],
            recv_sem=r_x.at[k, q - (1 << k)],
            device_id=across(k),
        )

    def chunk_start(i, slot, q, egu, ed):
        @pl.when(i < cgu)
        def _():
            load(gu_buf, l_gu, slot, egu.at[q, i]).start()

        @pl.when(i < cdn)
        def _():
            load(dn_buf, l_dn, slot, ed.at[q, i]).start()

    def expert_sum(hops, rsem, dest, core_r, buf, sem, slot, even, q, c, hop_copy):
        load(buf, sem, slot, even.at[q, c]).wait()
        core_r(q, c).wait_recv()
        total = buf[slot].astype(F32) + dest[q, c].astype(F32)
        for k in range(top_bit(q) + 1 if q else 0, levels):
            hop_copy(k, q + (1 << k), c).wait_recv()
            total = total + hops[k, q, c].astype(F32)
        return total

    def gu_sum(slot, q, c):
        return expert_sum(hop_gu, r_hop_gu, core_gu, functools.partial(core_gu_copy, ogu0), gu_buf, l_gu, slot, egu0, q, c, gu_hop)

    def dn_sum(slot, q, c):
        return expert_sum(hop_dn, r_hop_dn, core_dn, functools.partial(core_dn_copy, od0), dn_buf, l_dn, slot, ed0, q, c, dn_hop)

    def stepped(count, start, body):
        start(0, 0)

        def step(i, carry):
            @pl.when(i + 1 < count)
            def _():
                start(i + 1, lax.rem(i + 1, 2))

            body(i, lax.rem(i, 2))
            return carry

        lax.fori_loop(0, count, step, 0)

    for q in reversed(range(1, pairs)):
        dense_too = q == pairs - 1
        steps = max(units, cgu, cdn) if dense_too else max(cgu, cdn)

        def start(i, slot):
            def go(own, away, egu, ogu, ed, od):
                if dense_too:

                    @pl.when(i < units)
                    def _():
                        dd_load(i, slot, away).start()

                chunk_start(i, slot, q, egu, ed)

            by_section(go)

        def body(i, slot):
            if dense_too:

                @pl.when(i < units)
                def _():
                    dd_load(i, slot, dd0).wait()
                    core_dd_copy(0, i, dd0).wait_recv()
                    core_dd[0, i] = core_dd[0, i] + dd_buf[slot]
                    y_copy(i).start()

            @pl.when(i < cgu)
            def _():
                core_gu[q, i] = gu_sum(slot, q, i).astype(BF)
                gu_hop(top_bit(q), q, i).start()

            @pl.when(i < cdn)
            def _():
                core_dn[q, i] = dn_sum(slot, q, i).astype(BF)
                dn_hop(top_bit(q), q, i).start()

        stepped(steps, start, body)

    @pl.when(s == 0)
    def _():
        dx_copy(dx1).start()

    @pl.when(s != 0)
    def _():
        dx_copy(dx0).start()

    def gu_out_copy(c, slot, to=gate_out):
        return pltpu.make_async_copy(gu_res.at[slot], to.at[lax.rem(c, cgu // 2)], o_gu.at[slot])

    def dn_out_copy(c, slot):
        return pltpu.make_async_copy(dn_res.at[slot], down_out.at[c], o_dn.at[slot])

    def dense_sum(q):
        i = (pairs - 1 - q) * n + n - 1
        total = core_dd[1, i].astype(F32)
        for k in range(1, n):
            z_copy(q, k, i).wait_recv()
            total = total + hop_z[k - 1, q].astype(F32)
        for k in range(top_bit(q) + 1 if q else 0, levels):
            x_copy(k, q + (1 << k), i).wait_recv()
            total = total + hop_x[k, q].astype(F32)
        return i, total

    def pass_on(q):
        i, total = dense_sum(q)
        core_dd[1, i] = total.astype(BF)
        x_copy(top_bit(q), q, i).start()

    def core_sent():
        @pl.loop(0, units)
        def _(i):
            core_dd_copy(0, i, dd0).wait_send()
            core_dd_copy(1, i, dd0).wait_send()

        for q in range(pairs):

            @pl.loop(0, cgu)
            def _(c):
                core_gu_copy(ogu0, q, c).wait_send()

            @pl.loop(0, cdn)
            def _(c):
                core_dn_copy(od0, q, c).wait_send()

    steps = max(units, cgu, cdn)

    def start(i, slot):
        def go(own, away, egu, ogu, ed, od):
            @pl.when(i < units)
            def _():
                dd_load(i, slot, own).start()

            chunk_start(i, slot, 0, egu, ed)

        by_section(go)

    def body(i, slot):
        @pl.when(i < units)
        def _():
            dd_load(i, slot, dd0).wait()
            core_dd_copy(1, i, dd0).wait_recv()
            y_copy(i).wait_recv()
            core_dd[1, i] = (core_dd[1, i].astype(F32) + dd_buf[slot].astype(F32) + hop_y[i].astype(F32)).astype(BF)
            q, _ = unit(i)
            k = lax.rem(i, n) + 1

            @pl.when(k < n)
            def _():
                z_copy(q, k, i).start()

        for q in range(1, pairs):

            @pl.when(i == (pairs - q) * n + min(2, n - 1))
            def _():
                pass_on(q)

        @pl.when(i == units - 2)
        def _():
            core_sent()

        @pl.when(i < cgu)
        def _():
            @pl.when(i >= 2)
            def _():
                gu_out_copy(i - 2, slot).wait()

            gu_res[slot] = gu_sum(slot, 0, i).astype(BF)

            @pl.when(i < cgu // 2)
            def _():
                gu_out_copy(i, slot).start()

            @pl.when(i >= cgu // 2)
            def _():
                gu_out_copy(i, slot, up_out).start()

        @pl.when(i < cdn)
        def _():
            @pl.when(i >= 2)
            def _():
                dn_out_copy(i - 2, slot).wait()

            dn_res[slot] = dn_sum(slot, 0, i).astype(BF)
            dn_out_copy(i, slot).start()

    stepped(steps, start, body)
    _, total = dense_sum(0)
    dense_out[...] = total
    for c in (cgu - 2, cgu - 1):
        gu_out_copy(c, c % 2).wait()
    for c in (cdn - 2, cdn - 1):
        dn_out_copy(c, c % 2).wait()

    dx_copy(dx0).wait()

    @pl.loop(0, units)
    def _(i):
        y_copy(i).wait_send()
        q, _ = unit(i)
        k = lax.rem(i, n) + 1

        @pl.when(k < n)
        def _():
            z_copy(q, k, i).wait_send()

    for q in range(1, pairs):
        x_copy(top_bit(q), q, (pairs - 1 - q) * n + n - 1).wait_send()

        @pl.loop(0, cgu)
        def _(c):
            gu_hop(top_bit(q), q, c).wait_send()

        @pl.loop(0, cdn)
        def _(c):
            dn_hop(top_bit(q), q, c).wait_send()


def finish(cid, dd0, dd1, dx0, dx1, experts0, experts1):
    n, groups = lax.axis_size("expert"), lax.axis_size("group")
    pairs, levels = groups // 2, top_bit(groups // 2)
    width = dd0.shape[1]
    rows = dd0.shape[0] // (groups * n)
    dd0, dd1 = (v.reshape(groups * n, rows, width) for v in (dd0, dd1))

    def chunked(arrays):
        gu_even, gu_odd, dn_even, dn_odd = arrays
        flat = (pairs, -1) + gu_even.shape[3:]
        return gu_even.reshape(flat), gu_odd.reshape(flat), dn_even, dn_odd

    experts0, experts1 = chunked(experts0), chunked(experts1)
    gu, dn = experts0[0].shape[1:], experts0[2].shape[1:]
    units = pairs * n
    dma = pltpu.SemaphoreType.DMA
    sds = jax.ShapeDtypeStruct
    half = max(1, pairs // 2)

    def both(shape):
        return [dma(shape), dma(shape)]

    return pl.pallas_call(
        functools.partial(finish_kernel, n),
        out_shape=(
            sds((rows, width), F32),
            sds(dx0.shape, F32),
            sds((gu[0] // 2,) + gu[1:], BF),
            sds((gu[0] // 2,) + gu[1:], BF),
            sds(dn, BF),
        ),
        in_specs=[any_spec()] * 12,
        out_specs=tuple(vmem(1) + [any_spec()] * 4),
        scratch_shapes=[
            pltpu.VMEM((pairs,) + gu, BF),
            pltpu.VMEM((pairs,) + dn, BF),
            pltpu.VMEM((levels, half) + gu, BF),
            pltpu.VMEM((levels, half) + dn, BF),
            pltpu.VMEM((2, units, rows, width), BF),
            pltpu.VMEM((units, rows, width), BF),
            pltpu.VMEM((n - 1, pairs, rows, width), BF),
            pltpu.VMEM((levels, half, rows, width), BF),
            pltpu.VMEM((2, rows, width), BF),
            pltpu.VMEM((2,) + gu[1:], BF),
            pltpu.VMEM((2,) + dn[1:], BF),
            pltpu.VMEM((2,) + gu[1:], BF),
            pltpu.VMEM((2,) + dn[1:], BF),
        ]
        + both((pairs, gu[0]))
        + both((pairs, dn[0]))
        + both((levels, half, gu[0]))
        + both((levels, half, dn[0]))
        + both((2, units))
        + both((units,))
        + both((n - 1, pairs))
        + both((levels, half))
        + [dma((2,))] * 5
        + [dma, dma],
        compiler_params=pltpu.CompilerParams(collective_id=cid, has_side_effects=True, vmem_limit_bytes=VMEM_LIMIT),
    )(dd0, dd1, dx0, dx1, *experts0, *experts1)


def last_kernel(
    experts, dense_ref, dx0_ref, dx1_ref, got_ref, gate_ref, up_ref, down_ref,
    gate_out, up_out, down_out, q_out, k_out, v_out, o_out, router_out, attn_out, moe_out, dx_out,
):
    gate_out[...] = gate_ref[...].astype(F32)
    up_out[...] = up_ref[...].astype(F32)
    down_out[...] = down_ref[...].astype(F32)

    @pl.when(pl.program_id(0) == 0)
    def _():
        s = lax.axis_index("section")
        q_out[...] = dense_ref[:, 0:QW]
        k_out[...] = dense_ref[:, QW : QW + KW]
        v_out[...] = dense_ref[:, QW + KW : QKV]
        o_out[...] = jnp.transpose(dense_ref[:, QKV : QKV + QW])
        aux = dense_ref[:, QKV + QW :]
        router_out[...] = aux[:, 0:experts]
        aux_rows = jnp.transpose(aux)
        moe_out[...] = aux_rows[GAIN_MOE_ROW : GAIN_MOE_ROW + 1]
        attn_out[...] = aux_rows[GAIN_ATTN_ROW : GAIN_ATTN_ROW + 1]
        dx_out[s] = jnp.where(s == 0, dx0_ref[...], dx1_ref[...])
        dx_out[1 - s] = got_ref[...]


def last(experts, dense, dx0, dx1, got, gate, up, down):
    sh = dense.shape[0]
    t, d = dx0.shape
    per, piece, f = gate.shape
    sds = jax.ShapeDtypeStruct

    def whole(shape):
        return pl.BlockSpec(shape, lambda j: (0,) * len(shape))

    wide = pl.BlockSpec((1, piece, f), lambda j: (j, 0, 0))
    tall = pl.BlockSpec((1, f, piece), lambda j: (j, 0, 0))
    small = [(sh, QW), (sh, KW), (sh, KW), (QW, sh), (sh, experts), (1, sh), (1, sh), (2, t, d)]
    return pl.pallas_call(
        functools.partial(last_kernel, experts),
        grid=(per,),
        out_shape=tuple(sds(v.shape, F32) for v in (gate, up, down)) + tuple(sds(shape, F32) for shape in small),
        in_specs=[whole(v.shape) for v in (dense, dx0, dx1, got)] + [wide, wide, tall],
        out_specs=tuple([wide, wide, tall] + [whole(shape) for shape in small]),
        compiler_params=pltpu.CompilerParams(vmem_limit_bytes=VMEM_LIMIT),
    )(dense, dx0, dx1, got, gate, up, down)


def low_bit(q):
    return top_bit(q & -q)


def open_kernel(
    n, groups, pieces, w_ref, cot_ref, rt_ref, w0_out, w1_out, gy_out, rt_out, rt_side,
    s_right, r_right, s_left, r_left, s_group, r_group, s_y, r_y, s_cross, r_cross, s_rt, r_rt, s_side, r_side, local_sem,
):
    s, g, z = lax.axis_index("section"), lax.axis_index("group"), lax.axis_index("expert")
    remote = functools.partial(pltpu.make_async_remote_copy, device_id_type=MESH)
    rows = w_ref.shape[0] // pieces
    bits = top_bit(groups)
    other = {"section": 1 - s}
    barrier = pltpu.get_barrier_semaphore()
    peers = [other] + [{"group": lax.bitwise_xor(g, 1 << b)} for b in range(bits)] + [{"expert": lax.rem(z + k, n)} for k in range(1, n)]
    for peer in peers:
        pl.semaphore_signal(barrier, inc=1, device_id=peer, device_id_type=MESH)
    pl.semaphore_wait(barrier, len(peers))
    sent = []

    def launch(cond, make):
        sent.append((cond, make))
        if cond is None:
            make().start()
        else:

            @pl.when(cond)
            def _():
                make().start()

    def part(q, zz, c):
        if c == 2 * pieces:
            return gy_out.at[s, zz]
        return (w0_out, w1_out)[c // pieces].at[lax.bitwise_xor(g, q) * n + zz, pl.ds(c % pieces * rows, rows)]

    def chain(to, zz, t, c, ssem, rsem):
        return remote(src_ref=part(0, zz, c), dst_ref=part(0, zz, c), send_sem=ssem.at[t, c], recv_sem=rsem.at[t, c], device_id={"expert": to})

    def right(t, c):
        return chain(z + 1, z - t, t, c, s_right, r_right)

    def left(t, c):
        return chain(z - 1, z + t, t, c, s_left, r_left)

    def over(q, b, zz, c):
        at = q | (1 << b)
        return remote(
            src_ref=part(q, zz, c), dst_ref=part(q, zz, c), send_sem=s_group.at[at, zz, c], recv_sem=r_group.at[at, zz, c],
            device_id={"group": lax.bitwise_xor(g, 1 << b)},
        )

    def hop(c, to=w0_out):
        at = pl.ds(c * rows, rows)
        return remote(src_ref=w_ref.at[at], dst_ref=to.at[g * n + z, at], send_sem=s_y.at[c], recv_sem=r_y.at[c], device_id=other)

    def by_layer(action):
        for layer, to in enumerate((w0_out, w1_out)):

            @pl.when(s == layer)
            def _(to=to):
                action(to)

    def cross(zz):
        return remote(src_ref=gy_out.at[0, zz], dst_ref=gy_out.at[0, zz], send_sem=s_cross.at[zz], recv_sem=r_cross.at[zz], device_id=other)

    def route(m, k):
        return remote(
            src_ref=rt_ref.at[m], dst_ref=rt_out.at[m, z], send_sem=s_rt.at[m, k], recv_sem=r_rt.at[m, k],
            device_id={"expert": lax.rem(z + k, n)},
        )

    def side():
        return remote(src_ref=rt_ref.at[1 - s], dst_ref=rt_side, send_sem=s_side, recv_sem=r_side, device_id=other)

    by_layer(lambda to: hop(0, to).start())
    launch(None, side)
    own = [pltpu.make_async_copy(cot_ref.at[s], gy_out.at[s, z], local_sem.at[0])]
    own += [pltpu.make_async_copy(rt_ref.at[m], rt_out.at[m, z], local_sem.at[1 + m]) for m in range(2)]

    def keep(to=w0_out):
        return pltpu.make_async_copy(w_ref, to.at[g * n + z], local_sem.at[3])

    for copy in own:
        copy.start()

    by_layer(lambda to: keep(to).start())
    keep().wait()

    def spread_out(cond, zz, c):
        if c < pieces:
            for b in reversed(range(bits)):
                launch(cond, functools.partial(over, 0, b, zz, c))
        elif c == 2 * pieces:
            launch((s == 0) if cond is None else ((s == 0) & cond), functools.partial(cross, zz))

    def pass_along(t, c):
        if t == 0:
            if c < 2 * pieces:

                @pl.when(s != c // pieces)
                def _():
                    hop(c % pieces).wait_recv()
            else:
                own[0].wait()
            launch(z < n - 1, functools.partial(right, t, c))
            launch(z > 0, functools.partial(left, t, c))
            spread_out(None, z, c)
            if c + 1 < pieces:
                hop(c).wait_send()
                by_layer(lambda to: hop(c + 1, to).start())
        else:
            from_left, from_right = z >= t, z + t < n

            @pl.when(from_left)
            def _():
                right(t - 1, c).wait_recv()

            launch(from_left & (z < n - 1), functools.partial(right, t, c))
            spread_out(from_left, z - t, c)

            @pl.when(from_right)
            def _():
                left(t - 1, c).wait_recv()

            launch(from_right & (z > 0), functools.partial(left, t, c))
            spread_out(from_right, z + t, c)

    def forward(q, k):
        zz = lax.rem(z + k, n)
        for c in range(pieces):
            over(q & (q - 1), low_bit(q), zz, c).wait_recv()
            for b in reversed(range(low_bit(q))):
                launch(None, functools.partial(over, q, b, zz, c))

    for t in range(n):
        for c in range(pieces):
            pass_along(t, c)
        if t == 0:
            for m in range(2):
                for k in range(1, n):
                    launch(None, functools.partial(route, m, k))
    pending = [(q, k) for q in sorted(range(1, groups), key=lambda q: -low_bit(q)) for k in range(n)]
    for t in range(n):
        pass_along(t, 2 * pieces)
        forward(*pending.pop(0))
    for t in range(n):
        for c in range(pieces, 2 * pieces):
            pass_along(t, c)
    for q, k in pending:
        forward(q, k)

    @pl.when(s != 0)
    def _():
        for zz in range(n):
            cross(zz).wait_recv()

    side().wait_recv()
    for m in range(2):
        own[1 + m].wait()
        for k in range(1, n):
            route(m, k).wait_recv()
    hop(pieces - 1).wait_send()
    for cond, make in sent:
        if cond is None:
            make().wait_send()
        else:

            @pl.when(cond)
            def _(make=make):
                make().wait_send()


def open_up(cid, packed, cot, rt):
    n, groups = lax.axis_size("expert"), lax.axis_size("group")
    sh = packed.shape[0]
    pieces = 3 if sh % 48 == 0 else 1
    dma = pltpu.SemaphoreType.DMA
    sds = jax.ShapeDtypeStruct

    def both(shape):
        return [dma(shape), dma(shape)]

    w0, w1, gy, rt_all, rt_side = pl.pallas_call(
        functools.partial(open_kernel, n, groups, pieces),
        out_shape=(sds((groups * n,) + packed.shape, BF),) * 2 + (sds((2, n) + cot.shape[1:], BF), sds((2, n) + rt.shape[1:], rt.dtype), sds(rt.shape[1:], rt.dtype)),
        in_specs=vmem(3),
        out_specs=tuple([any_spec()] * 5),
        scratch_shapes=both((n, 2 * pieces + 1)) + both((n, 2 * pieces + 1)) + both((groups, n, pieces)) + both((pieces,)) + both((n,)) + both((2, n)) + [dma, dma] + [dma((4,))],
        compiler_params=pltpu.CompilerParams(collective_id=cid, has_side_effects=True),
    )(packed, cot, rt)
    return w0.reshape(groups * n * sh, -1), w1, gy, rt_all, rt_side


def swap_sections(value):
    return lax.ppermute(value, "section", [(0, 1), (1, 0)])


def rope_tables(t):
    half = HEAD_SIZE // 2
    frequency = THETA ** (-np.arange(half) * 2.0 / HEAD_SIZE)
    angles = np.arange(t)[:, None] * frequency[None, :]
    reps = LANES // half
    return (jnp.asarray(np.tile(f(angles), (1, reps)).astype(np.float32)) for f in (np.cos, np.sin))


def local(
    inputs, cotangent, segment_ids, live_first, routes, gain_attn, gain_moe,
    w_query, key_weight, value_weight, w_out, w_router, w_gate, w_up, w_down,
):
    s = lax.axis_index("section")
    n = lax.axis_size("expert")
    groups = lax.axis_size("group")
    t, d = inputs.shape[2:]
    top = routes.shape[-1]
    per = w_gate.shape[1]
    experts = per * n
    e_pad = -(-experts // 16) * 16
    cap = t * top * 5 // (4 * experts)
    wg, wu, wd = w_gate[0], w_up[0], w_down[0]
    at_zero = s == 0

    shard = w_query.shape[1]
    aux = jnp.concatenate(
        [
            w_router[0],
            jnp.zeros((shard, GAIN_MOE_ROW - experts), BF),
            gain_moe[0][:, None],
            gain_attn[0][:, None],
        ],
        axis=1,
    )
    packed = jnp.concatenate([w_query[0], key_weight[0], value_weight[0], w_out[0].T, aux], axis=1)
    seg, live, cot = segment_ids[:, 0], live_first[:, 0], cotangent[:, 0]
    cos, sin = rope_tables(t)

    rt = jnp.swapaxes(routes[0, :, 0], 1, 2)
    rt_mine = lax.dynamic_index_in_dim(rt, s, 0, keepdims=False)

    def flat(z):
        return z.reshape((2 * n,) + z.shape[2:])

    def paired(z):
        return z.reshape((2, n) + z.shape[1:])

    first_weights, second_weights, gy1, rt_all, rt_theirs = open_up(1, packed, cot, rt)
    rt_tokens = (jnp.where(at_zero, rt_mine, rt_theirs), jnp.where(at_zero, rt_theirs, rt_mine))
    gy1, rt_all = flat(gy1), flat(rt_all)

    none = jnp.zeros((1, t, d), BF)
    qkv0, p0, o0, h0, b0, wrt0, x0 = attn_fwd(inputs[:, 0], none, first_weights, cos, sin, seg, live)
    m0 = moe(0, "fwd", 2, e_pad, cap, b0, wg, wu, wd, rt=rt_all, wrt=wrt0, dense=second_weights)
    second_weights = m0.dense_out.reshape(first_weights.shape)

    qkv1, p1, o1, h1, b1, wrt1, x1 = attn_fwd(h0, m0.back, second_weights, cos, sin, seg, live)
    m1 = moe(1, "both", 3, e_pad, cap, b1, wg, wu, wd, rt=rt_all, wrt=wrt1, gy=gy1)

    def gates_back(dg):
        dg = dg[:, :per].reshape(experts, t)
        return jnp.pad(dg, ((0, e_pad - experts), (0, 0)))

    dx1, gy0, dqkv1, at1, dht1, daux1 = attn_bwd(False, cot, h1, x1, second_weights, qkv1, p1, o1, b1, wrt1, m1.back, gates_back(m1.dgate), rt_tokens[1], cos, sin)

    n0 = moe(0, "bwd", 4, e_pad, cap, gy0, wg, wu, wd, pos=m0.pos, gate=m0.gate, gp=m0.gp, up=m0.up, blocks=flat(m0.blocks),
             dqkv=dqkv1, at=at1, dht=dht1, daux=daux1, o=o1, part=m1.part0)
    dd1 = n0.dd
    dback0 = n0.back
    back1 = lax.all_to_all(jnp.where(at_zero, n0.part_out, m1.part1), "expert", split_axis=0, concat_axis=0, tiled=True)
    dx0, _, dd0 = attn_bwd(True, gy0, h0, x0, first_weights, qkv0, p0, o0, b0, wrt0, dback0, gates_back(n0.dgate), rt_tokens[0], cos, sin)

    dense, got, *sums = finish(5, dd0, dd1, dx0, dx1, (n0.even, n0.odd, n0.even_dn, n0.odd_dn), (m1.even, m1.odd, m1.even_dn, m1.odd_dn))
    dense, late = lax.optimization_barrier((dense, h1))
    y1 = (late + jnp.sum(back1.astype(F32), axis=0)).astype(BF)

    kept_out = jnp.where(at_zero, x1, y1)
    swapped_out = swap_sections(jnp.where(at_zero, y1, x1))
    layer_out = jnp.where(at_zero, jnp.stack([kept_out, swapped_out]), jnp.stack([swapped_out, kept_out]))
    gate_grad, up_grad, down_grad, *dense_grads, router_grad, attn_grad, moe_grad, input_grad = last(
        experts, dense, dx0, dx1, got, *sums
    )
    return (
        layer_out[None, :, None],
        input_grad[None, :, None],
        attn_grad,
        moe_grad,
        *(v[None] for v in dense_grads),
        router_grad[None],
        gate_grad[None],
        up_grad[None],
        down_grad[None],
    )


def solution(mesh):
    return jax.shard_map(
        local,
        mesh=mesh,
        in_specs=(
            P(None, ("group", "expert"), None, None),
            P(None, ("group", "expert"), None, None),
            P(None, ("group", "expert"), None),
            P(None, ("group", "expert"), None),
            P("section", None, ("group", "expert"), None, None),
            P("section", ("group", "expert")),
            P("section", ("group", "expert")),
            P("section", ("group", "expert"), None),
            P("section", ("group", "expert"), None),
            P("section", ("group", "expert"), None),
            P("section", None, ("group", "expert")),
            P("section", ("group", "expert"), None),
            P("section", "expert", None, None),
            P("section", "expert", None, None),
            P("section", "expert", None, None),
        ),
        out_specs=(
            P("section", None, ("group", "expert"), None, None),
            P("section", None, ("group", "expert"), None, None),
            P("section", ("group", "expert")),
            P("section", ("group", "expert")),
            P("section", ("group", "expert"), None),
            P("section", ("group", "expert"), None),
            P("section", ("group", "expert"), None),
            P("section", None, ("group", "expert")),
            P("section", ("group", "expert"), None),
            P("section", "expert", "group", None),
            P("section", "expert", "group", None),
            P("section", "expert", None, "group"),
        ),
        check_vma=False,
    )
```

```python
import functools
import types

import jax
import jax.numpy as jnp
import numpy as np
from jax import lax
from jax.experimental import pallas as pl
from jax.experimental.pallas import tpu as pltpu
from jax.sharding import PartitionSpec as P

QUERY_HEADS = 24
KEY_VALUE_HEADS = 8
HEAD_SIZE = 64
BLK = 64
EPS = 1e-06
THETA = 10000.0
NEG_FILL = -1e30
BF = jnp.bfloat16
F32 = jnp.float32
MESH = pl.DeviceIdType.MESH
LANES = 128
TILE = 512
QW = QUERY_HEADS * HEAD_SIZE
KW = KEY_VALUE_HEADS * HEAD_SIZE
QKV = QW + 2 * KW
GAIN_MOE_ROW = 126
GAIN_ATTN_ROW = 127
VMEM_LIMIT = 60 * 1024 * 1024
HEAD_PAIRS = KEY_VALUE_HEADS // 2
TILES_PER_PAIR = QUERY_HEADS // KEY_VALUE_HEADS


def dot(a, b, ca=1, cb=0):
    return lax.dot_general(a, b, (((ca,), (cb,)), ((), ())), preferred_element_type=F32)


def iota(shape, axis):
    return lax.broadcasted_iota(jnp.int32, shape, axis)


def rope(z, cos, sin, direction):
    width = z.shape[1]
    half = HEAD_SIZE // 2
    first = iota(z.shape, 1) % HEAD_SIZE < half
    partner = jnp.where(first, pltpu.roll(z, width - half, 1), pltpu.roll(z, half, 1))
    signed = jnp.where(first, -direction, direction) * partner
    reps = width // LANES
    return z * jnp.concatenate([cos] * reps, axis=1) + signed * jnp.concatenate([sin] * reps, axis=1)


def lane_masks(t):
    low = iota((t, LANES), 1) < HEAD_SIZE
    return low, jnp.logical_not(low)


def swapped(z):
    return pltpu.roll(z.astype(F32), HEAD_SIZE, 1).astype(BF)


def head_plan():
    return [(r, half, (2 * r + half) // TILES_PER_PAIR != half) for r in range(TILES_PER_PAIR) for half in range(2)]


def pick(z, half, masks):
    return jnp.where(masks[half], z, jnp.zeros_like(z))


def weight_pieces(d, order):
    aux = [(pl.ds(0, d), pl.ds(QKV + QW, LANES))]
    qkv = [(pl.ds(0, d), pl.ds(n * TILE, TILE)) for n in range(QKV // TILE)]
    out = [(pl.ds(n * TILE, TILE), pl.ds(QKV, QW)) for n in range(d // TILE)]
    down = [(pl.ds(0, d), pl.ds(QKV + n * TILE, TILE)) for n in range(QW // TILE)]
    rows = [(pl.ds(n * TILE, TILE), pl.ds(0, QKV)) for n in range(d // TILE)]
    return aux + qkv + out if order == "forward" else down + rows


def arriving(w_hbm, w_ref, sem, order):
    copies = [
        pltpu.make_async_copy(w_hbm.at[rows, cols], w_ref.at[rows, cols], sem.at[i])
        for i, (rows, cols) in enumerate(weight_pieces(w_ref.shape[0], order))
    ]
    for c in copies:
        c.start()
    return copies


def attn_fwd_kernel(
    blocks, below_ref, *refs,
):
    back_ref = refs[0] if blocks else None
    (
        w_hbm, cos_ref, sin_ref, seg_ref, live_ref,
        qkv_ref, p_ref, o_ref, h_ref, b_ref, wrt_ref, x_ref, w_ref, w_sem,
    ) = refs[1 if blocks else 0 :]
    t, d = x_ref.shape
    pieces = arriving(w_hbm, w_ref, w_sem, "forward")
    mine = lax.axis_index("section")
    entering = (below_ref[mine] if len(below_ref.shape) == 3 else below_ref[...]).astype(F32)
    for z in range(blocks):
        entering = entering + back_ref[z].astype(F32)
    x_ref[...] = entering.astype(BF)
    pieces.pop(0).wait()
    aux = jnp.transpose(w_ref[:, QKV + QW :].astype(F32))
    wrt_ref[...] = aux.astype(BF)
    gain_attn = aux[GAIN_ATTN_ROW : GAIN_ATTN_ROW + 1]
    gain_moe = aux[GAIN_MOE_ROW : GAIN_MOE_ROW + 1]
    x = x_ref[...].astype(F32)
    r1 = lax.rsqrt(jnp.mean(x * x, axis=1, keepdims=True) + EPS)
    a = (x * r1 * gain_attn).astype(BF)
    cos, sin = cos_ref[...], sin_ref[...]
    for n in range(QKV // TILE):
        cols = slice(n * TILE, (n + 1) * TILE)
        pieces.pop(0).wait()
        y = dot(a, w_ref[:, cols])
        if n * TILE < QW + KW:
            y = rope(y, cos, sin, 1.0)
        qkv_ref[:, cols] = y.astype(BF)
    i, j = iota((t, t), 0), iota((t, t), 1)
    segments = jnp.broadcast_to(seg_ref[pl.ds(mine, 1), :].astype(F32), (t, t))
    first_block = jnp.zeros((t, t), jnp.int32)
    for block in range(t // BLK):
        first_block = jnp.where(i // BLK == block, live_ref[mine, block], first_block)
    allowed = (j <= i) & (jnp.transpose(segments) == segments) & (j // BLK >= first_block)
    masks = lane_masks(t)

    def pair(m, carry):
        def lanes(base):
            return pl.ds(pl.multiple_of(base, LANES), LANES)

        kp = qkv_ref[:, lanes(QW + m * LANES)]
        vp = qkv_ref[:, lanes(QW + KW + m * LANES)]
        ks, vs = swapped(kp), swapped(vp)
        plan = head_plan()
        scores = []
        for r, half, swap in plan:
            q = pick(qkv_ref[:, lanes((m * TILES_PER_PAIR + r) * LANES)], half, masks)
            s = dot(q, ks if swap else kp, 1, 1) * HEAD_SIZE ** (-0.5)
            scores.append(jnp.where(allowed, s, NEG_FILL))
        tops = [jnp.max(s, axis=1, keepdims=True) for s in scores]
        exps = [jnp.exp(s - top) for s, top in zip(scores, tops)]
        sums = [1.0 / jnp.sum(e, axis=1, keepdims=True) for e in exps]
        probs = [e * u for e, u in zip(exps, sums)]
        for (r, half, swap), p in zip(plan, probs):
            p_ref[m * 2 * TILES_PER_PAIR + 2 * r + half] = p
        parts = [dot(p.astype(BF), pick(vs if swap else vp, half, masks)) for (r, half, swap), p in zip(plan, probs)]
        for r in range(TILES_PER_PAIR):
            o_ref[:, lanes((m * TILES_PER_PAIR + r) * LANES)] = (parts[2 * r] + parts[2 * r + 1]).astype(BF)
        return carry

    lax.fori_loop(0, HEAD_PAIRS, pair, 0)
    o = o_ref[...]
    for n in range(d // TILE):
        rows = slice(n * TILE, (n + 1) * TILE)
        pieces.pop(0).wait()
        h_ref[:, rows] = x_ref[:, rows].astype(F32) + dot(o, w_ref[rows, QKV : QKV + QW], 1, 1)
    h = h_ref[...]
    r2 = lax.rsqrt(jnp.mean(h * h, axis=1, keepdims=True) + EPS)
    b_ref[...] = (h * r2 * gain_moe).astype(BF)


def vmem(n):
    return [pl.BlockSpec(memory_space=pltpu.VMEM)] * n


def attn_fwd(below, back, w, cos, sin, seg, live):
    t, d = below.shape[-2:]
    sds = jax.ShapeDtypeStruct
    return pl.pallas_call(
        functools.partial(attn_fwd_kernel, len(back)),
        out_shape=(
            sds((t, QKV), BF),
            sds((QUERY_HEADS, t, t), F32),
            sds((t, QW), BF),
            sds((t, d), F32),
            sds((t, d), BF),
            sds((LANES, d), BF),
            sds((t, d), BF),
        ),
        in_specs=vmem(2 if len(back) else 1) + [any_spec()] + vmem(3) + [pl.BlockSpec(memory_space=pltpu.SMEM)],
        out_specs=tuple(vmem(7)),
        scratch_shapes=[pltpu.VMEM(w.shape, BF), pltpu.SemaphoreType.DMA((1 + QKV // TILE + d // TILE,))],
        compiler_params=pltpu.CompilerParams(vmem_limit_bytes=VMEM_LIMIT),
        cost_estimate=pl.CostEstimate(flops=2 * t * d * 4096, bytes_accessed=w.size * 2, transcendentals=QUERY_HEADS * t * t),
    )(below, *((back,) if len(back) else ()), w, cos, sin, seg, live)


def gates_of(rt, wrt, b, e_pad):
    t = rt.shape[1]
    experts = iota((e_pad, t), 0)
    chosen = experts == rt[0:1]
    for k in range(1, rt.shape[0]):
        chosen = chosen | (experts == rt[k : k + 1])
    logits = jnp.where(chosen, dot(wrt[0:e_pad], b, 1, 1), NEG_FILL)
    e = jnp.where(chosen, jnp.exp(logits - jnp.max(logits, axis=0, keepdims=True)), 0.0)
    return e / jnp.sum(e, axis=0, keepdims=True)


def attn_bwd_kernel(
    layer, now, e_pad, e_real, gy_ref, h_ref, x_ref, w_hbm, qkv_ref, p_ref, o_ref, b_ref, wrt_ref, back_ref, dg_ref, rt_ref, side_ref, cos_ref, sin_ref,
    dx_ref, dxb_ref, *rest,
):
    t, d = x_ref.shape
    if now:
        dd_hbm, do_ref, dqkv_ref, dh_ref, w_ref, w_sem, lt_ref, dd_ref, dd_sem = rest
    else:
        dqkv_ref, at_ref, dht_ref, daux_ref, do_ref, dh_ref, w_ref, w_sem = rest
    pieces = arriving(w_hbm, w_ref, w_sem, "backward")
    leaving = []

    def leave(first, width):
        cols = pl.ds(first, width)
        leaving.append(pltpu.make_async_copy(dd_ref.at[:, cols], dd_hbm.at[:, cols], dd_sem.at[len(leaving)]))
        leaving[-1].start()

    gain_attn = wrt_ref[GAIN_ATTN_ROW - 7 :, :].astype(F32)[7:8]
    gain_moe = wrt_ref[GAIN_ATTN_ROW - 7 :, :].astype(F32)[6:7]
    b = b_ref[...]
    mine = lax.axis_index("section")
    gates = gates_of(jnp.where(mine == layer, rt_ref[mine], side_ref[...]), wrt_ref, b, e_pad)
    per = e_real // dg_ref.shape[0]
    dg = [dg_ref[z][0:per] for z in range(dg_ref.shape[0])]
    if e_pad > e_real:
        dg.append(jnp.zeros((e_pad - e_real, t), F32))
    dg = jnp.concatenate(dg, axis=0)
    dl = (gates * (dg - jnp.sum(gates * dg, axis=0, keepdims=True)))
    dlb = dl.astype(BF)
    db = dot(dlb, wrt_ref[0:e_pad, :], 0, 0)
    for z in range(back_ref.shape[0]):
        db = db + back_ref[z].astype(F32)
    h = h_ref[...]
    r2 = lax.rsqrt(jnp.mean(h * h, axis=1, keepdims=True) + EPS)
    grad_moe = jnp.sum(db * h * r2, axis=0, keepdims=True)
    dn = db * gain_moe
    gy = gy_ref[lax.axis_index("section")] if len(gy_ref.shape) == 3 else gy_ref[...]
    dh = gy.astype(F32) + r2 * dn - h * (r2 * r2 * r2) * jnp.mean(dn * h, axis=1, keepdims=True)
    dh_ref[...] = dh
    dhb = dh.astype(BF)
    for n in range(QW // TILE):
        cols = slice(n * TILE, (n + 1) * TILE)
        pieces.pop(0).wait()
        do_ref[:, cols] = dot(dhb, w_ref[:, QKV + n * TILE : QKV + (n + 1) * TILE]).astype(BF)
    masks = lane_masks(t)
    cos, sin = cos_ref[...], sin_ref[...]

    def pair(m, carry):
        def lanes(base):
            return pl.ds(pl.multiple_of(base, LANES), LANES)

        kp = qkv_ref[:, lanes(QW + m * LANES)]
        vp = qkv_ref[:, lanes(QW + KW + m * LANES)]
        ks, vs = swapped(kp), swapped(vp)
        plan = head_plan()
        tiles = [lanes((m * TILES_PER_PAIR + r) * LANES) for r in range(TILES_PER_PAIR)]
        qs = [pick(qkv_ref[:, tiles[r]], half, masks) for r, half, _ in plan]
        dos = [pick(do_ref[:, tiles[r]], half, masks) for r, half, _ in plan]
        ps = [p_ref[m * 2 * TILES_PER_PAIR + 2 * r + half] for r, half, _ in plan]
        dps = [dot(do, vs if swap else vp, 1, 1) for do, (_, _, swap) in zip(dos, plan)]
        dvs = [dot(p.astype(BF), do, 0, 0) for p, do in zip(ps, dos)]
        sums = [jnp.sum(p * dp, axis=1, keepdims=True) for p, dp in zip(ps, dps)]
        dts = [(p * (dp - total) * HEAD_SIZE ** (-0.5)).astype(BF) for p, dp, total in zip(ps, dps, sums)]
        dks = [dot(dt, q, 0, 0) for dt, q in zip(dts, qs)]
        dqs = [dot(dt, pick(ks if swap else kp, half, masks)) for dt, (_, half, swap) in zip(dts, plan)]
        for r in range(TILES_PER_PAIR):
            dqkv_ref[:, tiles[r]] = rope(dqs[2 * r] + dqs[2 * r + 1], cos, sin, -1.0).astype(BF)
        dk, dv = (
            {way: functools.reduce(jnp.add, [v for v, (_, _, swap) in zip(vals, plan) if swap == way]) for way in (False, True)}
            for vals in (dks, dvs)
        )
        dk_all = dk[False] + pltpu.roll(dk[True], HEAD_SIZE, 1)
        dv_all = dv[False] + pltpu.roll(dv[True], HEAD_SIZE, 1)
        dqkv_ref[:, lanes(QW + m * LANES)] = rope(dk_all, cos, sin, -1.0).astype(BF)
        dqkv_ref[:, lanes(QW + KW + m * LANES)] = dv_all.astype(BF)
        return carry

    lax.fori_loop(0, HEAD_PAIRS, pair, 0)
    x = x_ref[...].astype(F32)
    r1 = lax.rsqrt(jnp.mean(x * x, axis=1, keepdims=True) + EPS)
    dqkv = dqkv_ref[...]
    for n in range(d // TILE):
        rows = slice(n * TILE, (n + 1) * TILE)
        pieces.pop(0).wait()
        dx_ref[:, rows] = dot(dqkv, w_ref[rows, 0:QKV], 1, 1)
    da = dx_ref[...]
    grad_attn = jnp.sum(da * x * r1, axis=0, keepdims=True)
    dag = da * gain_attn
    dx = dh_ref[...] + r1 * dag - x * (r1 * r1 * r1) * jnp.mean(dag * x, axis=1, keepdims=True)
    dx_ref[...] = dx
    dxb_ref[...] = dx.astype(BF)
    row = iota((LANES, d), 0)
    grads = jnp.where(row == GAIN_MOE_ROW, grad_moe, jnp.where(row == GAIN_ATTN_ROW, grad_attn, 0.0))
    dl_full = jnp.concatenate([dl, jnp.zeros((LANES - e_pad, t), F32)], axis=0)
    dl_rows = jnp.transpose(dl_full).astype(BF)
    bt = jnp.transpose(b_ref[...].astype(F32)).astype(BF)
    daux = (dot(bt, dl_rows) + jnp.transpose(grads)).astype(BF)
    if not now:
        at_ref[...] = jnp.transpose(x * r1 * gain_attn).astype(BF)
        dht_ref[...] = jnp.transpose(dh_ref[...]).astype(BF)
        daux_ref[...] = daux
        return
    lt_ref[...] = jnp.transpose(x * r1 * gain_attn).astype(BF)
    for n in range(QKV // TILE):
        cols = slice(n * TILE, (n + 1) * TILE)
        dd_ref[:, cols] = dot(lt_ref[...], dqkv_ref[:, cols]).astype(BF)
        leave(n * TILE, TILE)
    lt_ref[...] = jnp.transpose(dh_ref[...]).astype(BF)
    for n in range(QW // TILE):
        cols = slice(n * TILE, (n + 1) * TILE)
        dd_ref[:, QKV + n * TILE : QKV + (n + 1) * TILE] = dot(lt_ref[...], o_ref[:, cols]).astype(BF)
        leave(QKV + n * TILE, TILE)
    dd_ref[:, QKV + QW :] = daux
    leave(QKV + QW, LANES)
    for c in leaving:
        c.wait()


def attn_bwd(layer, now, experts, gy, h, x, w, qkv, p, o, b, wrt, back, dg, rt, side, cos, sin):
    t, d = x.shape
    sds = jax.ShapeDtypeStruct
    dma = pltpu.SemaphoreType.DMA
    outs = [sds((t, d), F32), sds((t, d), BF)]
    scratch = [pltpu.VMEM((t, QW), BF)]
    if now:
        outs.append(sds(w.shape, BF))
        scratch.append(pltpu.VMEM((t, QKV), BF))
    else:
        outs += [sds((t, QKV), BF), sds((d, t), BF), sds((d, t), BF), sds((d, LANES), BF)]
    scratch += [pltpu.VMEM((t, d), F32), pltpu.VMEM(w.shape, BF), dma((QW // TILE + d // TILE,))]
    if now:
        scratch += [pltpu.VMEM((d, t), BF), pltpu.VMEM(w.shape, BF), dma((1 + QKV // TILE + QW // TILE,))]
    return pl.pallas_call(
        functools.partial(attn_bwd_kernel, layer, now, -(-experts // 16) * 16, experts),
        out_shape=tuple(outs),
        in_specs=vmem(3) + [any_spec()] + vmem(11),
        out_specs=tuple(vmem(2) + [any_spec()] if now else vmem(6)),
        scratch_shapes=scratch,
        compiler_params=pltpu.CompilerParams(vmem_limit_bytes=VMEM_LIMIT),
        cost_estimate=pl.CostEstimate(flops=4 * t * d * 4096, bytes_accessed=w.size * 4, transcendentals=0),
    )(gy, h, x, w, qkv, p, o, b, wrt, back, dg, rt, side, cos, sin)


def one_hot(pos_row, cap):
    return jnp.where(iota((cap, pos_row.shape[1]), 0) == pos_row, 1.0, 0.0)


def all_hots(pos, per, cap):
    return jnp.concatenate([one_hot(pos[j : j + 1], cap) for j in range(per)], axis=0)


def all_hots_back(pos, per, cap):
    width = per * cap
    expert = jnp.where(iota((8, width), 1) // cap == iota((8, width), 0), 1.0, 0.0).astype(BF)
    wide = dot(pos.astype(F32).astype(BF), expert, 0, 0)
    slot = (iota((1, width), 1) % cap).astype(F32)
    return jnp.where(wide == slot, 1.0, 0.0).astype(BF)


def slots_of(rt, first, per):
    t = rt.shape[1]
    experts = iota((16, t), 0)
    mine = jnp.where(experts < per, experts + first, -1)
    chosen = mine == rt[0:1]
    for k in range(1, rt.shape[0]):
        chosen = chosen | (mine == rt[k : k + 1])
    earlier = jnp.where(iota((t, t), 0) < iota((t, t), 1), 1.0, 0.0).astype(BF)
    before = dot(jnp.where(chosen, 1.0, 0.0).astype(BF), earlier)
    return jnp.where(chosen, before.astype(jnp.int32), -1)[0:8]


def streamed(count, copies, body, primed=False):
    if not primed:
        for c in copies(0, 0):
            c.start()

    def step(b, carry):
        slot = lax.rem(b, 2)

        @pl.when(b + 1 < count)
        def _():
            for c in copies(b + 1, lax.rem(b + 1, 2)):
                c.start()

        for c in copies(b, slot):
            c.wait()
        body(b, slot)
        return carry

    lax.fori_loop(0, count, step, 0)


def combine(base, count, per, cap, pos_ref, rows_ref, out_hbm, obuf, osem):
    def copy(b, slot):
        return pltpu.make_async_copy(obuf.at[slot], out_hbm.at[b], osem.at[slot])

    def step(b, carry):
        slot = lax.rem(b, 2)

        @pl.when(b >= 2)
        def _():
            copy(b - 2, slot).wait()

        back = all_hots_back(pos_ref[base + b], per, cap)
        at = pl.ds(pl.multiple_of((base + b) * cap, cap), cap)
        rows = jnp.concatenate([rows_ref[j, at, :] for j in range(per)], axis=0)
        obuf[slot] = dot(back, rows).astype(BF)
        copy(b, slot).start()
        return carry

    lax.fori_loop(0, count, step, 0)
    copy(count - 2, (count - 2) % 2).wait()
    copy(count - 1, (count - 1) % 2).wait()


def chunk_gates(c, j, chunk, cap, pos_ref, gate_ref):
    hots, gates = [], []
    for bb in range(chunk // cap):
        b = c * (chunk // cap) + bb
        hot = one_hot(pos_ref[b, pl.ds(j, 1), :], cap)
        hots.append(hot)
        gates.append(jnp.sum(hot * gate_ref[b, pl.ds(j, 1), :], axis=1, keepdims=True))
    return hots, jnp.concatenate(gates, axis=0)


def any_spec():
    return pl.BlockSpec(memory_space=pl.ANY)


def put_rows(hots, block, b, per, cap, dest):
    at = pl.ds(pl.multiple_of(b * cap, cap), cap)
    rows = dot(hots, block).astype(BF)
    for k in range(per):
        dest[k, at, :] = rows[k * cap : (k + 1) * cap]


def gather_from(count, per, cap, pos, source, dest, buf, sem):
    def body(b, slot):
        put_rows(all_hots(pos[b], per, cap).astype(BF), buf[slot], b, per, cap, dest)

    streamed(count, lambda b, slot: [pltpu.make_async_copy(source.at[b], buf.at[slot], sem.at[slot])], body)


def weight_grads(r, per):
    parts, piece = r.even.shape[0], r.even.shape[3]
    g = lax.axis_index("group")
    parity, place = lax.rem(g, 2), g // 2

    def outgoing(j, at, slot):
        return [
            pltpu.make_async_copy(r.gu_buf.at[slot, 0], r.even.at[at, :, j], r.gu_sem.at[slot, 0]),
            pltpu.make_async_copy(r.gu_buf.at[slot, 1], r.odd.at[at, :, j], r.gu_sem.at[slot, 1]),
            pltpu.make_async_copy(r.dn_buf.at[slot, 0], r.even_dn.at[at, j], r.dn_sem.at[slot, 0]),
            pltpu.make_async_copy(r.dn_buf.at[slot, 1], r.odd_dn.at[at, j], r.dn_sem.at[slot, 1]),
        ]

    def finished(slot):
        for c in outgoing(0, 0, slot):
            c.wait()

    def body(j, carry):
        for q in range(parts):
            slot = q % 2
            if q >= 2:
                finished(slot)
            else:

                @pl.when(j > 0)
                def _():
                    finished(slot)

            cols = slice(2 * q * piece, 2 * (q + 1) * piece)
            for m in range(2):
                full = dot(r.x_scr[j, :, cols], r.act[m, j], 0, 0).astype(BF)
                r.gu_buf[slot, parity, m] = full[:piece]
                r.gu_buf[slot, 1 - parity, m] = full[piece:]
            full = dot(r.act[2, j], r.y_scr[j, :, cols], 0, 0).astype(BF)
            r.dn_buf[slot, parity] = full[:, :piece]
            r.dn_buf[slot, 1 - parity] = full[:, piece:]
            for c in outgoing(j, lax.bitwise_xor(place, q), slot):
                c.start()
        return carry

    lax.fori_loop(0, per, body, 0)
    for slot in range(2):
        finished(slot)


def meet(n, bits):
    s, g, z = lax.axis_index("section"), lax.axis_index("group"), lax.axis_index("expert")
    barrier = pltpu.get_barrier_semaphore()
    peers = [{"section": 1 - s}] + [{"expert": lax.rem(z + k, n)} for k in range(1, n)]
    peers += [{"group": lax.bitwise_xor(g, 1 << b)} for b in range(bits)]
    for peer in peers:
        pl.semaphore_signal(barrier, inc=1, device_id=peer, device_id_type=MESH)
    pl.semaphore_wait(barrier, len(peers))


def moe_kernel(layer, mode, n, e_pad, cap, names, *refs):
    r = types.SimpleNamespace(**dict(zip(names, refs)))
    forward, backward = mode != "bwd", mode != "fwd"
    s, z = lax.axis_index("section"), lax.axis_index("expert")
    here = s == layer
    count = 2 * n
    per, rows, d = r.y_scr.shape
    first = z * per
    chunk = n * cap
    remote = functools.partial(pltpu.make_async_remote_copy, device_id_type=MESH)
    other = {"section": 1 - s}
    g = lax.axis_index("group")
    riding = forward and not backward
    groups = r.dense_out.shape[0] // n if riding else 1
    bits = top_bit(groups)
    meet(n, bits)
    r.blk[s, z] = r.own[...]

    def over(q, b, zz):
        at = q | (1 << b)
        shard = r.dense_out.at[lax.bitwise_xor(g, q) * n + zz]
        return remote(
            src_ref=shard, dst_ref=shard, send_sem=r.s_over.at[at, zz], recv_sem=r.r_over.at[at, zz],
            device_id={"group": lax.bitwise_xor(g, 1 << b)},
        )

    def ride(bs):
        for b in bs:
            for zz in range(n):
                over(0, b, zz).start()

    def ride_on():
        for q in sorted(range(1, groups), key=lambda q: -low_bit(q)):
            for zz in range(n):
                over(q & (q - 1), low_bit(q), zz).wait_recv()
                for b in reversed(range(low_bit(q))):
                    over(q, b, zz).start()

    if riding:
        ride(reversed(range(1, bits)))

    def half(i):
        section = jnp.where(i < per, layer, 1 - layer)
        return lax.rem(i, per), section, pl.ds(pl.multiple_of(section * chunk, chunk), chunk)

    def weights(i, slot):
        j, _, at = half(i)
        both = [
            pltpu.make_async_copy(r.wg.at[j], r.wg_buf.at[slot], r.w_sem.at[slot, 0]),
            pltpu.make_async_copy(r.wu.at[j], r.wu_buf.at[slot], r.w_sem.at[slot, 1]),
            pltpu.make_async_copy(r.wd.at[j], r.wd_buf.at[slot], r.w_sem.at[slot, 2]),
        ]
        if mode == "bwd":
            both.append(pltpu.make_async_copy(r.gp.at[j, at], r.gp_buf.at[slot], r.gp_sem.at[slot, 0]))
            both.append(pltpu.make_async_copy(r.up.at[j, at], r.gp_buf.at[2 + slot], r.gp_sem.at[slot, 1]))
        return both

    def chain(to, zz, t, ssem, rsem):
        return remote(
            src_ref=r.blk.at[s, zz], dst_ref=r.blk.at[s, zz], send_sem=ssem.at[t], recv_sem=rsem.at[t], device_id={"expert": to}
        )

    def right(t):
        return chain(z + 1, z - t, t, r.s_right, r.r_right)

    def left(t):
        return chain(z - 1, z + t, t, r.s_left, r.r_left)

    def cross(zz):
        return remote(
            src_ref=r.blk.at[s, zz], dst_ref=r.blk.at[s, zz], send_sem=r.s_cross.at[zz], recv_sem=r.r_cross.at[zz], device_id=other
        )

    def prepare(section, zz):
        b = section * n + zz
        block = r.blk[section, zz]
        if forward:
            rt = r.rt[b]
            pos = slots_of(rt, first, per)
            r.pos[b] = pos
            r.gates[...] = gates_of(rt, r.wrt, block, e_pad)
            r.gate[b] = jnp.concatenate(
                [r.gates[pl.ds(first + k, 1), :] for k in range(per)] + [jnp.zeros((8 - per, rt.shape[1]), F32)], axis=0
            )
            put_rows(all_hots(pos, per, cap).astype(BF), block, b, per, cap, r.x_scr)
        else:
            put_rows(all_hots(r.pos[b], per, cap).astype(BF), block, b, per, cap, r.y_scr)

    @pl.when(here)
    def _():
        for c in weights(0, 0):
            c.start()

    def prepare_at(section, t):
        def candidate(m, carry):
            zz = jnp.where(m == 0, z - t, z + t)

            @pl.when((zz >= 0) & (zz < n) & ((m == 0) | (t > 0)))
            def _():
                prepare(section, zz)

            return carry

        lax.fori_loop(0, 2, candidate, 0)

    def dense_tiles():
        tiles = []
        for first_row in range(0, d, rows):
            for left, right, col, width in ((r.at, r.dqkv, 0, QW), (r.at, r.dqkv, QW, 2 * KW), (r.dht, r.o, QKV, QW)):
                source = right if left is r.dht else right.at[:, pl.ds(col, width)]
                tiles.append((left.at[pl.ds(first_row, rows)], source, first_row, col, width))
        return tiles

    def dense_copy(i, tile):
        _, _, row, col, width = tile
        return pltpu.make_async_copy(
            r.x_scr.at[i % per, :, pl.ds(0, width)], r.dd.at[pl.ds(row, rows), pl.ds(col, width)], r.dd_sem.at[i]
        )

    def aux_copy():
        return pltpu.make_async_copy(r.daux, r.dd.at[:, pl.ds(QKV + QW, LANES)], r.daux_sem)

    def dense_start(step):
        if step == 0:
            aux_copy().start()
        tiles = dense_tiles()
        share = len(tiles) // 3
        for i, tile in list(enumerate(tiles))[step * share : (step + 1) * share]:
            if i >= per:
                dense_copy(i - per, tiles[i - per]).wait()
            left, right, _, _, width = tile
            r.x_scr[i % per, :, 0:width] = dot(left[...], right[...]).astype(BF)
            dense_copy(i, tile).start()

    def dense_wait():
        aux_copy().wait()
        tiles = dense_tiles()
        for i in range(max(0, len(tiles) - per), len(tiles)):
            dense_copy(i, tiles[i]).wait()

    @pl.loop(0, n)
    def _(t):
        from_left = z >= t
        from_right = z + t < n

        @pl.when(from_left & (t > 0))
        def _():
            right(t - 1).wait_recv()

        @pl.when(from_left & (z < n - 1))
        def _():
            right(t).start()

        @pl.when(from_left & jnp.logical_not(here))
        def _():
            cross(z - t).start()

        @pl.when(from_right & (t > 0))
        def _():
            left(t - 1).wait_recv()

        @pl.when(from_right & (z > 0))
        def _():
            left(t).start()

        @pl.when(from_right & (t > 0) & jnp.logical_not(here))
        def _():
            cross(z + t).start()

        if mode == "bwd":

            for step in range(3):

                @pl.when(t == step)
                def _(step=step):
                    dense_start(step)

        @pl.when(here)
        def _():
            if mode == "both":

                @pl.when(t == 0)
                def _():
                    @pl.loop(0, count)
                    def _(b):
                        r.pos[b] = slots_of(r.rt[b], first, per)

                    gather_from(count, per, cap, r.pos, r.gy, r.y_scr, r.row_buf, r.row_sem)

            prepare_at(layer, t)

    def late_blocks():
        @pl.loop(0, n)
        def _(t):
            @pl.when(z >= t)
            def _():
                cross(z - t).wait_recv()

            @pl.when((t > 0) & (z + t < n))
            def _():
                cross(z + t).wait_recv()

            prepare_at(1 - layer, t)

    if riding:
        ride((0,))

    def over_part(zz):
        return remote(
            src_ref=r.part.at[zz], dst_ref=r.part_out.at[zz], send_sem=r.s_part.at[zz], recv_sem=r.r_part.at[zz], device_id=other
        )

    if mode == "bwd":
        dense_wait()

        @pl.when(jnp.logical_not(here))
        def _():
            for zz in range(n):
                over_part(zz).start()

    srcs = (r.pbuf, r.dg) if backward else (r.pbuf,)
    outs = (r.back, r.dgate) if backward else (r.back,)
    relays = (r.relay, r.dg_relay) if backward else (r.relay,)
    arrays = range(len(srcs))

    def hop(a, to):
        return remote(
            src_ref=srcs[a].at[1 - layer, to],
            dst_ref=relays[a].at[to],
            send_sem=r.s_hop.at[a, to],
            recv_sem=r.r_hop.at[a, to],
            device_id=other,
        )

    def give(a, source, k):
        return remote(
            src_ref=source,
            dst_ref=outs[a].at[z],
            send_sem=r.s_give.at[a, k],
            recv_sem=r.r_give.at[a, k],
            device_id={"expert": lax.rem(z + k, n)},
        )

    def keep(a, source):
        return pltpu.make_async_copy(source, outs[a].at[z], r.keep_sem.at[a])

    def saved(i, slot):
        j, _, at = half(i)
        return [
            pltpu.make_async_copy(r.gp_buf.at[slot], r.gp.at[j, at], r.gp_sem.at[slot, 0]),
            pltpu.make_async_copy(r.gp_buf.at[2 + slot], r.up.at[j, at], r.gp_sem.at[slot, 1]),
        ]

    def expert(i, slot):
        j, section, at = half(i)

        @pl.when(i == per)
        def _():
            late_blocks()

        if mode == "fwd":

            @pl.when(i >= 2)
            def _():
                for c in saved(i - 2, slot):
                    c.wait()

        if forward:
            x = r.x_scr[j, at, :]
            gp = dot(x, r.wg_buf[slot])
            up = dot(x, r.wu_buf[slot])
        else:
            gp, up = r.gp_buf[slot].astype(F32), r.gp_buf[2 + slot].astype(F32)
        sg = 1.0 / (1.0 + jnp.exp(-gp))
        silu = gp * sg
        hid = silu * up
        hots, gate = chunk_gates(section, j, chunk, cap, r.pos, r.gate)
        if not backward:
            r.gp_buf[slot] = gp.astype(BF)
            r.gp_buf[2 + slot] = up.astype(BF)
            r.y_scr[j, at, :] = (dot(hid.astype(BF), r.wd_buf[slot]) * gate).astype(BF)
            for c in saved(i, slot):
                c.start()
            return
        raw = dot(r.y_scr[j, at, :], r.wd_buf[slot], 1, 1)
        dgate = jnp.sum(hid.astype(BF).astype(F32) * raw, axis=1, keepdims=True)
        for bb in range(n):
            r.dg[section, bb, pl.ds(j, 1), :] = jnp.sum(hots[bb] * dgate[bb * cap : (bb + 1) * cap], axis=0, keepdims=True)
        dh = raw * gate
        dgp = (dh * up * sg * (1.0 + gp * (1.0 - sg))).astype(BF)
        dup = (dh * silu).astype(BF)
        r.act[0, j, at, :] = dgp
        r.act[1, j, at, :] = dup
        r.act[2, j, at, :] = (hid * gate).astype(BF)
        r.y_scr[j, at, :] = (dot(dgp, r.wg_buf[slot], 1, 1) + dot(dup, r.wu_buf[slot], 1, 1)).astype(BF)

    def summed(b, source):
        at = pl.ds(pl.multiple_of(b * cap, cap), cap)
        stacked = jnp.concatenate([source[j, at, :] for j in range(per)], axis=0)
        return dot(all_hots_back(r.pos[b], per, cap), stacked).astype(BF)

    @pl.when(here)
    def _():
        if backward:
            r.dg[...] = jnp.zeros_like(r.dg)
        if mode == "fwd":
            keep_blocks = pltpu.make_async_copy(r.blk, r.blocks, r.row_sem.at[0])
        streamed(2 * per, weights, expert, primed=True)
        if mode == "fwd":
            keep_blocks.start()

        def emit(i, carry):
            to = lax.rem(z + i + 1, n)
            section = jnp.where(i < n, 1 - layer, layer)
            r.pbuf[section, to] = summed(section * n + to, r.y_scr)

            @pl.when(i < n)
            def _():
                for a in arrays:
                    hop(a, to).start()

            @pl.when((i >= n) & (to != z))
            def _():
                for a in arrays:
                    give(a, srcs[a].at[layer, to], i + 1 - n).start()

            return carry

        lax.fori_loop(0, 2 * n, emit, 0)
        for a in arrays:
            keep(a, srcs[a].at[layer, z]).start()
        if mode == "fwd":
            for i in (2 * per - 2, 2 * per - 1):
                for c in saved(i, i % 2):
                    c.wait()
            keep_blocks.wait()
        if mode == "bwd":

            @pl.loop(0, count)
            def _(b):
                put_rows(all_hots(r.pos[b], per, cap).astype(BF), r.blk[b // n, lax.rem(b, n)], b, per, cap, r.y_scr)

            gather_from(count, per, cap, r.pos, r.blocks, r.x_scr, r.row_buf, r.row_sem)
        if mode == "both":
            gather_from(count, per, cap, r.pos, r.gy, r.y_scr, r.row_buf, r.row_sem)
        if backward:
            weight_grads(r, per)
        if mode == "both":
            def output(j, slot):
                @pl.loop(0, 2)
                def _(c):
                    at = pl.ds(pl.multiple_of(c * chunk, chunk), chunk)
                    r.x_scr[j, at, :] = dot(r.act[2, j, at, :], r.wd_buf[slot]).astype(BF)

            streamed(per, lambda j, slot: weights(j, slot)[2:], output)
            combine(0, n, per, cap, r.pos, r.x_scr, r.part0, r.row_buf, r.row_sem)
            combine(n, n, per, cap, r.pos, r.x_scr, r.part1, r.row_buf, r.row_sem)
        for to in range(n):
            for a in arrays:
                hop(a, to).wait_send()

    @pl.when(jnp.logical_not(here))
    def _():
        @pl.loop(1, n + 1)
        def _(k):
            to = lax.rem(lax.rem(k, n) + z, n)
            for a in arrays:
                hop(a, to).wait_recv()

            @pl.when(k < n)
            def _():
                for a in arrays:
                    give(a, relays[a].at[to], k).start()

        for a in arrays:
            keep(a, relays[a].at[z]).start()
        for zz in range(n):
            cross(zz).wait_send()

    if mode == "bwd":

        @pl.when(here)
        def _():
            for zz in range(n):
                over_part(zz).wait_recv()

        @pl.when(jnp.logical_not(here))
        def _():
            for zz in range(n):
                over_part(zz).wait_send()

    if riding:
        ride_on()
        for q in range(1, groups):
            for zz in range(n):
                over(q & (q - 1), low_bit(q), zz).wait_send()
    for a in arrays:
        keep(a, relays[a].at[z]).wait()
        for k in range(1, n):
            give(a, relays[a].at[lax.rem(z + k, n)], k).wait()
    for t in range(n):

        @pl.when((z >= t) & (z < n - 1))
        def _():
            right(t).wait_send()

        @pl.when((z + t < n) & (z > 0))
        def _():
            left(t).wait_send()


def moe(layer, mode, cid, e_pad, cap, own, wg, wu, wd, **given):
    n, groups = lax.axis_size("expert"), lax.axis_size("group")
    count = 2 * n
    t, d = own.shape
    per, _, f = wg.shape
    rows = count * cap
    piece = d // groups
    sds = jax.ShapeDtypeStruct
    dma = pltpu.SemaphoreType.DMA
    vm, hbm = pl.BlockSpec(memory_space=pltpu.VMEM), any_spec()
    on_chip = ("own", "rt", "wrt", "pos", "gate", "dqkv", "at", "dht", "daux", "o")
    ins = dict(own=own, wg=wg, wu=wu, wd=wd, **given)
    outs = dict(back=sds((n, t, d), BF))
    scratch = dict(
        blk=pltpu.VMEM((2, n, t, d), BF),
        y_scr=pltpu.VMEM((per, rows, d), BF),
        wg_buf=pltpu.VMEM((2, d, f), BF),
        wu_buf=pltpu.VMEM((2, d, f), BF),
        wd_buf=pltpu.VMEM((2, f, d), BF),
        pbuf=pltpu.VMEM((2, n, t, d), BF),
        relay=pltpu.VMEM((n, t, d), BF),
        x_scr=pltpu.VMEM((per, rows, d), BF),
        row_buf=pltpu.VMEM((2, t, d), BF),
        row_sem=dma((2,)),
        w_sem=dma((2, 3)),
        keep_sem=dma((2,)),
    )
    for name in ("right", "left", "cross"):
        scratch["s_" + name] = dma((n,))
        scratch["r_" + name] = dma((n,))
    for name in ("hop", "give"):
        scratch["s_" + name] = dma((2, n))
        scratch["r_" + name] = dma((2, n))
    if mode != "both":
        scratch["gp_buf"] = pltpu.VMEM((4, n * cap, f), BF)
        scratch["gp_sem"] = dma((2, 2))
    if mode != "bwd":
        scratch["gates"] = pltpu.VMEM((e_pad, t), F32)
    if mode == "fwd":
        del scratch["row_buf"]
        outs.update(pos=sds((count, 8, t), jnp.int32), gate=sds((count, 8, t), F32))
        outs.update(gp=sds((per, rows, f), BF), up=sds((per, rows, f), BF), blocks=sds((2, n, t, d), BF))
        outs["dense_out"] = sds(given["dense"].shape, BF)
        scratch.update(s_over=dma((groups, n)), r_over=dma((groups, n)))
    else:
        outs["dgate"] = sds((n, 8, t), F32)
        outs["even"] = outs["odd"] = sds((groups // 2, 2, per, piece, f), BF)
        outs["even_dn"] = outs["odd_dn"] = sds((groups // 2, per, f, piece), BF)
        scratch.update(
            dg=pltpu.VMEM((2, n, 8, t), F32),
            dg_relay=pltpu.VMEM((n, 8, t), F32),
            act=pltpu.VMEM((3, per, rows, f), BF),
            gu_buf=pltpu.VMEM((2, 2, 2, piece, f), BF),
            dn_buf=pltpu.VMEM((2, 2, f, piece), BF),
            gu_sem=dma((2, 2)),
            dn_sem=dma((2, 2)),
        )
    if mode == "bwd":
        outs["dd"] = sds((d, QKV + QW + LANES), BF)
        outs["part_out"] = sds((n, t, d), BF)
        scratch.update(s_part=dma((n,)), r_part=dma((n,)))
        scratch.update(dd_sem=dma((3 * d // rows,)), daux_sem=dma)
    if mode == "both":
        outs["part0"] = outs["part1"] = sds((n, t, d), BF)
        scratch.update(pos=pltpu.VMEM((count, 8, t), jnp.int32), gate=pltpu.VMEM((count, 8, t), F32))
    names = tuple(ins) + tuple(outs) + tuple(scratch)
    results = pl.pallas_call(
        functools.partial(moe_kernel, layer, mode, n, e_pad, cap, names),
        out_shape=tuple(outs.values()),
        in_specs=[vm if name in on_chip else hbm for name in ins],
        out_specs=tuple(vm if name in on_chip else hbm for name in outs),
        scratch_shapes=list(scratch.values()),
        input_output_aliases={list(ins).index("dense"): list(outs).index("dense_out")} if mode == "fwd" else {},
        compiler_params=pltpu.CompilerParams(collective_id=cid, has_side_effects=True, vmem_limit_bytes=VMEM_LIMIT),
    )(*ins.values())
    return types.SimpleNamespace(**dict(zip(outs, results)))


def top_bit(q):
    return q.bit_length() - 1


def finish_kernel(
    n, dd0, dd1, dx0, dx1, egu0, ogu0, ed0, od0, egu1, ogu1, ed1, od1,
    dense_out, dx_out, gate_out, up_out, down_out,
    core_gu, core_dn, hop_gu, hop_dn, core_dd, hop_y, hop_z, hop_x, dd_buf, gu_buf, dn_buf, gu_res, dn_res,
    s_core_gu, r_core_gu, s_core_dn, r_core_dn, s_hop_gu, r_hop_gu, s_hop_dn, r_hop_dn,
    s_core_dd, r_core_dd, s_y, r_y, s_z, r_z, s_x, r_x, l_dd, l_gu, l_dn, o_gu, o_dn, s_dx, r_dx,
):
    s, g, z = lax.axis_index("section"), lax.axis_index("group"), lax.axis_index("expert")
    pairs, cgu = core_gu.shape[:2]
    cdn = core_dn.shape[1]
    levels = top_bit(pairs)
    units = pairs * n
    remote = functools.partial(pltpu.make_async_remote_copy, device_id_type=MESH)
    twin = {"group": lax.bitwise_xor(g, 1)}
    other = {"section": 1 - s}

    def across(k):
        return {"group": lax.bitwise_xor(g, 2 << k)}

    barrier = pltpu.get_barrier_semaphore()
    peers = [twin, other] + [across(k) for k in range(levels)] + [{"expert": lax.rem(z + k, n)} for k in range(1, n)]
    for peer in peers:
        pl.semaphore_signal(barrier, inc=1, device_id=peer, device_id_type=MESH)
    pl.semaphore_wait(barrier, len(peers))

    def by_section(action):
        @pl.when(s == 0)
        def _():
            action(dd0, dd1, egu0, ogu0, ed0, od0)

        @pl.when(s != 0)
        def _():
            action(dd1, dd0, egu1, ogu1, ed1, od1)

    def unit(i):
        return pairs - 1 - i // n, lax.rem(z + 1 + lax.rem(i, n), n)

    def shard(i, core):
        q, place = unit(i)
        return (lax.bitwise_xor(g // 2, q) * 2 + core) * n + place

    core = lax.rem(g, 2)

    def core_dd_copy(kind, i, source):
        return remote(
            src_ref=source.at[shard(i, 1 - core)],
            dst_ref=core_dd.at[kind, i],
            send_sem=s_core_dd.at[kind, i],
            recv_sem=r_core_dd.at[kind, i],
            device_id=twin,
        )

    def core_chunk(source, dest, ssem, rsem, q, c):
        return remote(
            src_ref=source.at[q, c], dst_ref=dest.at[q, c], send_sem=ssem.at[q, c], recv_sem=rsem.at[q, c], device_id=twin
        )

    def core_gu_copy(source, q, c):
        return core_chunk(source, core_gu, s_core_gu, r_core_gu, q, c)

    def core_dn_copy(source, q, c):
        return core_chunk(source, core_dn, s_core_dn, r_core_dn, q, c)

    def send_all(own, away, egu, ogu, ed, od):
        @pl.loop(0, units)
        def _(i):
            core_dd_copy(0, i, away).start()

            @pl.when(i < cgu)
            def _():
                core_gu_copy(ogu, pairs - 1, i).start()

            @pl.when(i < cdn)
            def _():
                core_dn_copy(od, pairs - 1, i).start()

        for i in range(units, max(cgu, cdn)):
            if i < cgu:
                core_gu_copy(ogu, pairs - 1, i).start()
            if i < cdn:
                core_dn_copy(od, pairs - 1, i).start()

        @pl.loop(0, units)
        def _(i):
            core_dd_copy(1, i, own).start()

        for q in reversed(range(pairs - 1)):

            @pl.loop(0, cgu)
            def _(c):
                core_gu_copy(ogu, q, c).start()

            @pl.loop(0, cdn)
            def _(c):
                core_dn_copy(od, q, c).start()

    by_section(send_all)

    def dx_copy(source):
        return remote(src_ref=source, dst_ref=dx_out, send_sem=s_dx, recv_sem=r_dx, device_id=other)

    def load(buf, sem, slot, source):
        return pltpu.make_async_copy(source, buf.at[slot], sem.at[slot])

    def dd_load(i, slot, source):
        return load(dd_buf, l_dd, slot, source.at[shard(i, core)])

    def hop(dest, ssem, rsem, source, k, q, c):
        return remote(
            src_ref=source.at[q, c],
            dst_ref=dest.at[k, q - (1 << k), c],
            send_sem=ssem.at[k, q - (1 << k), c],
            recv_sem=rsem.at[k, q - (1 << k), c],
            device_id=across(k),
        )

    def gu_hop(k, q, c):
        return hop(hop_gu, s_hop_gu, r_hop_gu, core_gu, k, q, c)

    def dn_hop(k, q, c):
        return hop(hop_dn, s_hop_dn, r_hop_dn, core_dn, k, q, c)

    def y_copy(i):
        return remote(src_ref=core_dd.at[0, i], dst_ref=hop_y.at[i], send_sem=s_y.at[i], recv_sem=r_y.at[i], device_id=other)

    def z_copy(q, k, i):
        return remote(
            src_ref=core_dd.at[1, i],
            dst_ref=hop_z.at[k - 1, q],
            send_sem=s_z.at[k - 1, q],
            recv_sem=r_z.at[k - 1, q],
            device_id={"expert": lax.rem(z + k, n)},
        )

    def x_copy(k, q, i):
        return remote(
            src_ref=core_dd.at[1, i],
            dst_ref=hop_x.at[k, q - (1 << k)],
            send_sem=s_x.at[k, q - (1 << k)],
            recv_sem=r_x.at[k, q - (1 << k)],
            device_id=across(k),
        )

    def chunk_start(i, slot, q, egu, ed):
        @pl.when(i < cgu)
        def _():
            load(gu_buf, l_gu, slot, egu.at[q, i]).start()

        @pl.when(i < cdn)
        def _():
            load(dn_buf, l_dn, slot, ed.at[q, i]).start()

    def expert_sum(hops, rsem, dest, core_r, buf, sem, slot, even, q, c, hop_copy):
        load(buf, sem, slot, even.at[q, c]).wait()
        core_r(q, c).wait_recv()
        total = buf[slot].astype(F32) + dest[q, c].astype(F32)
        for k in range(top_bit(q) + 1 if q else 0, levels):
            hop_copy(k, q + (1 << k), c).wait_recv()
            total = total + hops[k, q, c].astype(F32)
        return total

    def gu_sum(slot, q, c):
        return expert_sum(hop_gu, r_hop_gu, core_gu, functools.partial(core_gu_copy, ogu0), gu_buf, l_gu, slot, egu0, q, c, gu_hop)

    def dn_sum(slot, q, c):
        return expert_sum(hop_dn, r_hop_dn, core_dn, functools.partial(core_dn_copy, od0), dn_buf, l_dn, slot, ed0, q, c, dn_hop)

    def stepped(count, start, body):
        start(0, 0)

        def step(i, carry):
            @pl.when(i + 1 < count)
            def _():
                start(i + 1, lax.rem(i + 1, 2))

            body(i, lax.rem(i, 2))
            return carry

        lax.fori_loop(0, count, step, 0)

    for q in reversed(range(1, pairs)):
        dense_too = q == pairs - 1
        steps = max(units, cgu, cdn) if dense_too else max(cgu, cdn)

        def start(i, slot):
            def go(own, away, egu, ogu, ed, od):
                if dense_too:

                    @pl.when(i < units)
                    def _():
                        dd_load(i, slot, away).start()

                chunk_start(i, slot, q, egu, ed)

            by_section(go)

        def body(i, slot):
            if dense_too:

                @pl.when(i < units)
                def _():
                    dd_load(i, slot, dd0).wait()
                    core_dd_copy(0, i, dd0).wait_recv()
                    core_dd[0, i] = core_dd[0, i] + dd_buf[slot]
                    y_copy(i).start()

            @pl.when(i < cgu)
            def _():
                core_gu[q, i] = gu_sum(slot, q, i).astype(BF)
                gu_hop(top_bit(q), q, i).start()

            @pl.when(i < cdn)
            def _():
                core_dn[q, i] = dn_sum(slot, q, i).astype(BF)
                dn_hop(top_bit(q), q, i).start()

        stepped(steps, start, body)

    @pl.when(s == 0)
    def _():
        dx_copy(dx1).start()

    @pl.when(s != 0)
    def _():
        dx_copy(dx0).start()

    def gu_out_copy(c, slot, to=gate_out):
        return pltpu.make_async_copy(gu_res.at[slot], to.at[lax.rem(c, cgu // 2)], o_gu.at[slot])

    def dn_out_copy(c, slot):
        return pltpu.make_async_copy(dn_res.at[slot], down_out.at[c], o_dn.at[slot])

    def dense_sum(q):
        i = (pairs - 1 - q) * n + n - 1
        total = core_dd[1, i].astype(F32)
        for k in range(1, n):
            z_copy(q, k, i).wait_recv()
            total = total + hop_z[k - 1, q].astype(F32)
        for k in range(top_bit(q) + 1 if q else 0, levels):
            x_copy(k, q + (1 << k), i).wait_recv()
            total = total + hop_x[k, q].astype(F32)
        return i, total

    def pass_on(q):
        i, total = dense_sum(q)
        core_dd[1, i] = total.astype(BF)
        x_copy(top_bit(q), q, i).start()

    def core_sent():
        @pl.loop(0, units)
        def _(i):
            core_dd_copy(0, i, dd0).wait_send()
            core_dd_copy(1, i, dd0).wait_send()

        for q in range(pairs):

            @pl.loop(0, cgu)
            def _(c):
                core_gu_copy(ogu0, q, c).wait_send()

            @pl.loop(0, cdn)
            def _(c):
                core_dn_copy(od0, q, c).wait_send()

    steps = max(units, cgu, cdn)

    def start(i, slot):
        def go(own, away, egu, ogu, ed, od):
            @pl.when(i < units)
            def _():
                dd_load(i, slot, own).start()

            chunk_start(i, slot, 0, egu, ed)

        by_section(go)

    def body(i, slot):
        @pl.when(i < units)
        def _():
            dd_load(i, slot, dd0).wait()
            core_dd_copy(1, i, dd0).wait_recv()
            y_copy(i).wait_recv()
            core_dd[1, i] = (core_dd[1, i].astype(F32) + dd_buf[slot].astype(F32) + hop_y[i].astype(F32)).astype(BF)
            q, _ = unit(i)
            k = lax.rem(i, n) + 1

            @pl.when(k < n)
            def _():
                z_copy(q, k, i).start()

        for q in range(1, pairs):

            @pl.when(i == (pairs - q) * n + min(2, n - 1))
            def _():
                pass_on(q)

        @pl.when(i == units - 2)
        def _():
            core_sent()

        @pl.when(i < cgu)
        def _():
            @pl.when(i >= 2)
            def _():
                gu_out_copy(i - 2, slot).wait()

            gu_res[slot] = gu_sum(slot, 0, i).astype(BF)

            @pl.when(i < cgu // 2)
            def _():
                gu_out_copy(i, slot).start()

            @pl.when(i >= cgu // 2)
            def _():
                gu_out_copy(i, slot, up_out).start()

        @pl.when(i < cdn)
        def _():
            @pl.when(i >= 2)
            def _():
                dn_out_copy(i - 2, slot).wait()

            dn_res[slot] = dn_sum(slot, 0, i).astype(BF)
            dn_out_copy(i, slot).start()

    stepped(steps, start, body)
    _, total = dense_sum(0)
    dense_out[...] = total
    for c in (cgu - 2, cgu - 1):
        gu_out_copy(c, c % 2).wait()
    for c in (cdn - 2, cdn - 1):
        dn_out_copy(c, c % 2).wait()

    dx_copy(dx0).wait()

    @pl.loop(0, units)
    def _(i):
        y_copy(i).wait_send()
        q, _ = unit(i)
        k = lax.rem(i, n) + 1

        @pl.when(k < n)
        def _():
            z_copy(q, k, i).wait_send()

    for q in range(1, pairs):
        x_copy(top_bit(q), q, (pairs - 1 - q) * n + n - 1).wait_send()

        @pl.loop(0, cgu)
        def _(c):
            gu_hop(top_bit(q), q, c).wait_send()

        @pl.loop(0, cdn)
        def _(c):
            dn_hop(top_bit(q), q, c).wait_send()


def finish(cid, dd0, dd1, dx0, dx1, experts0, experts1):
    n, groups = lax.axis_size("expert"), lax.axis_size("group")
    pairs, levels = groups // 2, top_bit(groups // 2)
    width = dd0.shape[1]
    rows = dd0.shape[0] // (groups * n)
    dd0, dd1 = (v.reshape(groups * n, rows, width) for v in (dd0, dd1))

    def chunked(arrays):
        gu_even, gu_odd, dn_even, dn_odd = arrays
        flat = (pairs, -1) + gu_even.shape[3:]
        return gu_even.reshape(flat), gu_odd.reshape(flat), dn_even, dn_odd

    experts0, experts1 = chunked(experts0), chunked(experts1)
    gu, dn = experts0[0].shape[1:], experts0[2].shape[1:]
    units = pairs * n
    dma = pltpu.SemaphoreType.DMA
    sds = jax.ShapeDtypeStruct
    half = max(1, pairs // 2)

    def both(shape):
        return [dma(shape), dma(shape)]

    return pl.pallas_call(
        functools.partial(finish_kernel, n),
        out_shape=(
            sds((rows, width), F32),
            sds(dx0.shape, dx0.dtype),
            sds((gu[0] // 2,) + gu[1:], BF),
            sds((gu[0] // 2,) + gu[1:], BF),
            sds(dn, BF),
        ),
        in_specs=[any_spec()] * 12,
        out_specs=tuple(vmem(1) + [any_spec()] * 4),
        scratch_shapes=[
            pltpu.VMEM((pairs,) + gu, BF),
            pltpu.VMEM((pairs,) + dn, BF),
            pltpu.VMEM((levels, half) + gu, BF),
            pltpu.VMEM((levels, half) + dn, BF),
            pltpu.VMEM((2, units, rows, width), BF),
            pltpu.VMEM((units, rows, width), BF),
            pltpu.VMEM((n - 1, pairs, rows, width), BF),
            pltpu.VMEM((levels, half, rows, width), BF),
            pltpu.VMEM((2, rows, width), BF),
            pltpu.VMEM((2,) + gu[1:], BF),
            pltpu.VMEM((2,) + dn[1:], BF),
            pltpu.VMEM((2,) + gu[1:], BF),
            pltpu.VMEM((2,) + dn[1:], BF),
        ]
        + both((pairs, gu[0]))
        + both((pairs, dn[0]))
        + both((levels, half, gu[0]))
        + both((levels, half, dn[0]))
        + both((2, units))
        + both((units,))
        + both((n - 1, pairs))
        + both((levels, half))
        + [dma((2,))] * 5
        + [dma, dma],
        compiler_params=pltpu.CompilerParams(collective_id=cid, has_side_effects=True, vmem_limit_bytes=VMEM_LIMIT),
    )(dd0, dd1, dx0, dx1, *experts0, *experts1)


def last_kernel(
    experts, dense_ref, dx0_ref, dx1_ref, got_ref, gate_ref, up_ref, down_ref,
    gate_out, up_out, down_out, q_out, k_out, v_out, o_out, router_out, attn_out, moe_out, dx_out,
):
    gate_out[...] = gate_ref[...].astype(F32)
    up_out[...] = up_ref[...].astype(F32)
    down_out[...] = down_ref[...].astype(F32)

    @pl.when(pl.program_id(0) == 0)
    def _():
        s = lax.axis_index("section")
        q_out[...] = dense_ref[:, 0:QW]
        k_out[...] = dense_ref[:, QW : QW + KW]
        v_out[...] = dense_ref[:, QW + KW : QKV]
        o_out[...] = dense_ref[:, QKV : QKV + QW]
        aux_rows = jnp.transpose(dense_ref[:, QKV + QW :])
        router_out[...] = aux_rows[0:experts]
        moe_out[...] = aux_rows[GAIN_MOE_ROW : GAIN_MOE_ROW + 1]
        attn_out[...] = aux_rows[GAIN_ATTN_ROW : GAIN_ATTN_ROW + 1]
        dx_out[s] = jnp.where(s == 0, dx0_ref[...], dx1_ref[...])
        dx_out[1 - s] = got_ref[...].astype(F32)


def last(experts, dense, dx0, dx1, got, gate, up, down):
    sh = dense.shape[0]
    t, d = dx0.shape
    per, piece, f = gate.shape
    sds = jax.ShapeDtypeStruct

    def whole(shape):
        return pl.BlockSpec(shape, lambda j: (0,) * len(shape))

    wide = pl.BlockSpec((1, piece, f), lambda j: (j, 0, 0))
    tall = pl.BlockSpec((1, f, piece), lambda j: (j, 0, 0))
    small = [(sh, QW), (sh, KW), (sh, KW), (sh, QW), (experts, sh), (1, sh), (1, sh), (2, t, d)]
    return pl.pallas_call(
        functools.partial(last_kernel, experts),
        grid=(per,),
        out_shape=tuple(sds(v.shape, F32) for v in (gate, up, down)) + tuple(sds(shape, F32) for shape in small),
        in_specs=[whole(v.shape) for v in (dense, dx0, dx1, got)] + [wide, wide, tall],
        out_specs=tuple([wide, wide, tall] + [whole(shape) for shape in small]),
        compiler_params=pltpu.CompilerParams(vmem_limit_bytes=VMEM_LIMIT),
    )(dense, dx0, dx1, got, gate, up, down)


def low_bit(q):
    return top_bit(q & -q)


def open_kernel(
    n, groups, pieces, wq_ref, wk_ref, wv_ref, wo_ref, wr_ref, ga_ref, gm_ref, cot_ref, rt_ref, w0_out, w1_out, gy_out, rt_out, rt_side,
    w_ref, s_right, r_right, s_left, r_left, s_group, r_group, s_y, r_y, s_cross, r_cross, s_rt, r_rt, s_side, r_side, local_sem,
):
    s, g, z = lax.axis_index("section"), lax.axis_index("group"), lax.axis_index("expert")
    remote = functools.partial(pltpu.make_async_remote_copy, device_id_type=MESH)
    rows = w_ref.shape[0] // pieces
    bits = top_bit(groups)
    other = {"section": 1 - s}
    w_ref[:, 0:QW] = wq_ref[...]
    w_ref[:, QW : QW + KW] = wk_ref[...]
    w_ref[:, QW + KW : QKV] = wv_ref[...]
    w_ref[:, QKV : QKV + QW] = wo_ref[...]
    experts, sh = wr_ref.shape
    gap = jnp.zeros((GAIN_MOE_ROW - experts, sh), F32)
    aux = jnp.concatenate([wr_ref[...].astype(F32), gap, gm_ref[...].astype(F32), ga_ref[...].astype(F32)], axis=0)
    w_ref[:, QKV + QW :] = jnp.transpose(aux).astype(BF)
    barrier = pltpu.get_barrier_semaphore()
    peers = [other] + [{"group": lax.bitwise_xor(g, 1 << b)} for b in range(bits)] + [{"expert": lax.rem(z + k, n)} for k in range(1, n)]
    for peer in peers:
        pl.semaphore_signal(barrier, inc=1, device_id=peer, device_id_type=MESH)
    pl.semaphore_wait(barrier, len(peers))
    sent = []

    def launch(cond, make):
        sent.append((cond, make))
        if cond is None:
            make().start()
        else:

            @pl.when(cond)
            def _():
                make().start()

    def part(q, zz, c):
        if c == 2 * pieces:
            return gy_out.at[s, zz]
        return (w0_out, w1_out)[c // pieces].at[lax.bitwise_xor(g, q) * n + zz, pl.ds(c % pieces * rows, rows)]

    def chain(to, zz, t, c, ssem, rsem):
        return remote(src_ref=part(0, zz, c), dst_ref=part(0, zz, c), send_sem=ssem.at[t, c], recv_sem=rsem.at[t, c], device_id={"expert": to})

    def right(t, c):
        return chain(z + 1, z - t, t, c, s_right, r_right)

    def left(t, c):
        return chain(z - 1, z + t, t, c, s_left, r_left)

    def over(q, b, zz, c):
        at = q | (1 << b)
        return remote(
            src_ref=part(q, zz, c), dst_ref=part(q, zz, c), send_sem=s_group.at[at, zz, c], recv_sem=r_group.at[at, zz, c],
            device_id={"group": lax.bitwise_xor(g, 1 << b)},
        )

    def hop(c, to=w0_out):
        at = pl.ds(c * rows, rows)
        return remote(src_ref=w_ref.at[at], dst_ref=to.at[g * n + z, at], send_sem=s_y.at[c], recv_sem=r_y.at[c], device_id=other)

    def by_layer(action):
        for layer, to in enumerate((w0_out, w1_out)):

            @pl.when(s == layer)
            def _(to=to):
                action(to)

    def cross(zz):
        return remote(src_ref=gy_out.at[0, zz], dst_ref=gy_out.at[0, zz], send_sem=s_cross.at[zz], recv_sem=r_cross.at[zz], device_id=other)

    def route(m, k):
        return remote(
            src_ref=rt_ref.at[m], dst_ref=rt_out.at[m, z], send_sem=s_rt.at[m, k], recv_sem=r_rt.at[m, k],
            device_id={"expert": lax.rem(z + k, n)},
        )

    def side():
        return remote(src_ref=rt_ref.at[1 - s], dst_ref=rt_side, send_sem=s_side, recv_sem=r_side, device_id=other)

    by_layer(lambda to: hop(0, to).start())
    launch(None, side)
    own = [pltpu.make_async_copy(cot_ref.at[s], gy_out.at[s, z], local_sem.at[0])]
    own += [pltpu.make_async_copy(rt_ref.at[m], rt_out.at[m, z], local_sem.at[1 + m]) for m in range(2)]

    def keep(to=w0_out):
        return pltpu.make_async_copy(w_ref, to.at[g * n + z], local_sem.at[3])

    for copy in own:
        copy.start()

    by_layer(lambda to: keep(to).start())
    keep().wait()

    def spread_out(cond, zz, c):
        if c < pieces:
            for b in reversed(range(bits)):
                launch(cond, functools.partial(over, 0, b, zz, c))
        elif c == 2 * pieces:
            launch((s == 0) if cond is None else ((s == 0) & cond), functools.partial(cross, zz))

    def pass_along(t, c):
        if t == 0:
            if c < 2 * pieces:

                @pl.when(s != c // pieces)
                def _():
                    hop(c % pieces).wait_recv()
            else:
                own[0].wait()
            launch(z < n - 1, functools.partial(right, t, c))
            launch(z > 0, functools.partial(left, t, c))
            spread_out(None, z, c)
            if c + 1 < pieces:
                hop(c).wait_send()
                by_layer(lambda to: hop(c + 1, to).start())
        else:
            from_left, from_right = z >= t, z + t < n

            @pl.when(from_left)
            def _():
                right(t - 1, c).wait_recv()

            launch(from_left & (z < n - 1), functools.partial(right, t, c))
            spread_out(from_left, z - t, c)

            @pl.when(from_right)
            def _():
                left(t - 1, c).wait_recv()

            launch(from_right & (z > 0), functools.partial(left, t, c))
            spread_out(from_right, z + t, c)

    def forward(q, k):
        zz = lax.rem(z + k, n)
        for c in range(pieces):
            over(q & (q - 1), low_bit(q), zz, c).wait_recv()
            for b in reversed(range(low_bit(q))):
                launch(None, functools.partial(over, q, b, zz, c))

    for t in range(n):
        for c in range(pieces):
            pass_along(t, c)
        if t == 0:
            for m in range(2):
                for k in range(1, n):
                    launch(None, functools.partial(route, m, k))
    pending = [(q, k) for q in sorted(range(1, groups), key=lambda q: -low_bit(q)) for k in range(n)]
    for t in range(n):
        pass_along(t, 2 * pieces)
        forward(*pending.pop(0))
    for t in range(n):
        for c in range(pieces, 2 * pieces):
            pass_along(t, c)
    for q, k in pending:
        forward(q, k)

    @pl.when(s != 0)
    def _():
        for zz in range(n):
            cross(zz).wait_recv()

    side().wait_recv()
    for m in range(2):
        own[1 + m].wait()
        for k in range(1, n):
            route(m, k).wait_recv()
    hop(pieces - 1).wait_send()
    for cond, make in sent:
        if cond is None:
            make().wait_send()
        else:

            @pl.when(cond)
            def _(make=make):
                make().wait_send()


def open_up(cid, weights, cot, rt):
    n, groups = lax.axis_size("expert"), lax.axis_size("group")
    sh = weights[0].shape[0]
    packed = (sh, QKV + QW + LANES)
    pieces = 3 if sh % 48 == 0 else 1
    dma = pltpu.SemaphoreType.DMA
    sds = jax.ShapeDtypeStruct

    def both(shape):
        return [dma(shape), dma(shape)]

    w0, w1, gy, rt_all, rt_side = pl.pallas_call(
        functools.partial(open_kernel, n, groups, pieces),
        out_shape=(sds((groups * n,) + packed, BF),) * 2 + (sds((2, n) + cot.shape[1:], BF), sds((2, n) + rt.shape[1:], rt.dtype), sds(rt.shape[1:], rt.dtype)),
        in_specs=vmem(9),
        out_specs=tuple([any_spec()] * 5),
        scratch_shapes=[pltpu.VMEM(packed, BF)] + both((n, 2 * pieces + 1)) + both((n, 2 * pieces + 1)) + both((groups, n, pieces)) + both((pieces,)) + both((n,)) + both((2, n)) + [dma, dma] + [dma((4,))],
        compiler_params=pltpu.CompilerParams(collective_id=cid, has_side_effects=True),
    )(*weights, cot, rt)
    return w0.reshape(groups * n * sh, -1), w1, gy, rt_all, rt_side


def swap_sections(value):
    return lax.ppermute(value, "section", [(0, 1), (1, 0)])


def rope_tables(t):
    half = HEAD_SIZE // 2
    frequency = THETA ** (-np.arange(half) * 2.0 / HEAD_SIZE)
    angles = np.arange(t)[:, None] * frequency[None, :]
    reps = LANES // half
    return (jnp.asarray(np.tile(f(angles), (1, reps)).astype(np.float32)) for f in (np.cos, np.sin))


def local(
    inputs, cotangent, segment_ids, live_first, routes, gain_attn, gain_moe,
    w_query, key_weight, value_weight, w_out, w_router, w_gate, w_up, w_down,
):
    s = lax.axis_index("section")
    n = lax.axis_size("expert")
    groups = lax.axis_size("group")
    t, d = inputs.shape[2:]
    top = routes.shape[-1]
    per = w_gate.shape[1]
    experts = per * n
    e_pad = -(-experts // 16) * 16
    cap = t * top * 5 // (4 * experts)
    wg, wu, wd = w_gate[0], w_up[0], w_down[0]
    at_zero = s == 0

    dense_shards = (w_query[0], key_weight[0], value_weight[0], w_out[0].T, w_router[0].T, gain_attn, gain_moe)

    seg, live, cot = segment_ids[:, 0], live_first[:, 0], cotangent[:, 0]
    cos, sin = rope_tables(t)

    rt = jnp.swapaxes(routes[0, :, 0], 1, 2)

    def flat(z):
        return z.reshape((2 * n,) + z.shape[2:])

    def paired(z):
        return z.reshape((2, n) + z.shape[1:])

    first_weights, second_weights, gy1, rt_all, rt_theirs = open_up(1, dense_shards, cot, rt)
    gy1, rt_all = flat(gy1), flat(rt_all)

    qkv0, p0, o0, h0, b0, wrt0, x0 = attn_fwd(inputs[:, 0], (), first_weights, cos, sin, seg, live)
    m0 = moe(0, "fwd", 2, e_pad, cap, b0, wg, wu, wd, rt=rt_all, wrt=wrt0, dense=second_weights)
    second_weights = m0.dense_out.reshape(first_weights.shape)

    qkv1, p1, o1, h1, b1, wrt1, x1 = attn_fwd(h0, m0.back, second_weights, cos, sin, seg, live)
    m1 = moe(1, "both", 3, e_pad, cap, b1, wg, wu, wd, rt=rt_all, wrt=wrt1, gy=gy1)

    dx1, gy0, dqkv1, at1, dht1, daux1 = attn_bwd(1, False, experts, cot, h1, x1, second_weights, qkv1, p1, o1, b1, wrt1, m1.back, m1.dgate, rt, rt_theirs, cos, sin)

    n0 = moe(0, "bwd", 4, e_pad, cap, gy0, wg, wu, wd, pos=m0.pos, gate=m0.gate, gp=m0.gp, up=m0.up, blocks=flat(m0.blocks),
             dqkv=dqkv1, at=at1, dht=dht1, daux=daux1, o=o1, part=m1.part0)
    dd1 = n0.dd
    dback0 = n0.back
    back1 = lax.all_to_all(jnp.where(at_zero, n0.part_out, m1.part1), "expert", split_axis=0, concat_axis=0, tiled=True)
    dx0, low0, dd0 = attn_bwd(0, True, experts, gy0, h0, x0, first_weights, qkv0, p0, o0, b0, wrt0, dback0, n0.dgate, rt, rt_theirs, cos, sin)

    dense, got, *sums = finish(5, dd0, dd1, low0, gy0, (n0.even, n0.odd, n0.even_dn, n0.odd_dn), (m1.even, m1.odd, m1.even_dn, m1.odd_dn))
    dense, late = lax.optimization_barrier((dense, h1))
    y1 = (late + jnp.sum(back1.astype(F32), axis=0)).astype(BF)

    kept_out = jnp.where(at_zero, x1, y1)
    swapped_out = swap_sections(jnp.where(at_zero, y1, x1))
    layer_out = jnp.where(at_zero, jnp.stack([kept_out, swapped_out]), jnp.stack([swapped_out, kept_out]))
    gate_grad, up_grad, down_grad, *dense_grads, out_grad, router_grad, attn_grad, moe_grad, input_grad = last(
        experts, dense, dx0, dx1, got, *sums
    )
    return (
        layer_out[None, :, None],
        input_grad[None, :, None],
        attn_grad,
        moe_grad,
        *(v[None] for v in dense_grads),
        out_grad.T[None],
        router_grad.T[None],
        gate_grad[None],
        up_grad[None],
        down_grad[None],
    )


def solution(mesh):
    return jax.shard_map(
        local,
        mesh=mesh,
        in_specs=(
            P(None, ("group", "expert"), None, None),
            P(None, ("group", "expert"), None, None),
            P(None, ("group", "expert"), None),
            P(None, ("group", "expert"), None),
            P("section", None, ("group", "expert"), None, None),
            P("section", ("group", "expert")),
            P("section", ("group", "expert")),
            P("section", ("group", "expert"), None),
            P("section", ("group", "expert"), None),
            P("section", ("group", "expert"), None),
            P("section", None, ("group", "expert")),
            P("section", ("group", "expert"), None),
            P("section", "expert", None, None),
            P("section", "expert", None, None),
            P("section", "expert", None, None),
        ),
        out_specs=(
            P("section", None, ("group", "expert"), None, None),
            P("section", None, ("group", "expert"), None, None),
            P("section", ("group", "expert")),
            P("section", ("group", "expert")),
            P("section", ("group", "expert"), None),
            P("section", ("group", "expert"), None),
            P("section", ("group", "expert"), None),
            P("section", None, ("group", "expert")),
            P("section", ("group", "expert"), None),
            P("section", "expert", "group", None),
            P("section", "expert", "group", None),
            P("section", "expert", None, "group"),
        ),
        check_vma=False,
    )
```

```python
import functools
import types

import jax
import jax.numpy as jnp
import numpy as np
from jax import lax
from jax.experimental import pallas as pl
from jax.experimental.pallas import tpu as pltpu
from jax.sharding import PartitionSpec as P

QUERY_HEADS = 24
KEY_VALUE_HEADS = 8
HEAD_SIZE = 64
BLK = 64
EPS = 1e-06
THETA = 10000.0
NEG_FILL = -1e30
BF = jnp.bfloat16
F32 = jnp.float32
MESH = pl.DeviceIdType.MESH
LANES = 128
TILE = 512
QW = QUERY_HEADS * HEAD_SIZE
KW = KEY_VALUE_HEADS * HEAD_SIZE
QKV = QW + 2 * KW
GAIN_MOE_ROW = 126
GAIN_ATTN_ROW = 127
VMEM_LIMIT = 60 * 1024 * 1024
HEAD_PAIRS = KEY_VALUE_HEADS // 2
TILES_PER_PAIR = QUERY_HEADS // KEY_VALUE_HEADS


def dot(a, b, ca=1, cb=0):
    return lax.dot_general(a, b, (((ca,), (cb,)), ((), ())), preferred_element_type=F32)


def iota(shape, axis):
    return lax.broadcasted_iota(jnp.int32, shape, axis)


def rope(z, cos, sin, direction):
    width = z.shape[1]
    half = HEAD_SIZE // 2
    first = iota(z.shape, 1) % HEAD_SIZE < half
    partner = jnp.where(first, pltpu.roll(z, width - half, 1), pltpu.roll(z, half, 1))
    signed = jnp.where(first, -direction, direction) * partner
    reps = width // LANES
    return z * jnp.concatenate([cos] * reps, axis=1) + signed * jnp.concatenate([sin] * reps, axis=1)


def lane_masks(t):
    low = iota((t, LANES), 1) < HEAD_SIZE
    return low, jnp.logical_not(low)


def swapped(z):
    return pltpu.roll(z.astype(F32), HEAD_SIZE, 1).astype(BF)


def head_plan():
    return [(r, half, (2 * r + half) // TILES_PER_PAIR != half) for r in range(TILES_PER_PAIR) for half in range(2)]


def pick(z, half, masks):
    return jnp.where(masks[half], z, jnp.zeros_like(z))


def weight_pieces(d, order):
    aux = [(pl.ds(0, d), pl.ds(QKV + QW, LANES))]
    qkv = [(pl.ds(0, d), pl.ds(n * TILE, TILE)) for n in range(QKV // TILE)]
    out = [(pl.ds(n * TILE, TILE), pl.ds(QKV, QW)) for n in range(d // TILE)]
    down = [(pl.ds(0, d), pl.ds(QKV + n * TILE, TILE)) for n in range(QW // TILE)]
    rows = [(pl.ds(n * TILE, TILE), pl.ds(0, QKV)) for n in range(d // TILE)]
    return aux + qkv + out if order == "forward" else down + rows


def arriving(w_hbm, w_ref, sem, order):
    copies = [
        pltpu.make_async_copy(w_hbm.at[rows, cols], w_ref.at[rows, cols], sem.at[i])
        for i, (rows, cols) in enumerate(weight_pieces(w_ref.shape[0], order))
    ]
    for c in copies:
        c.start()
    return copies


def attn_fwd_kernel(
    blocks, below_ref, *refs,
):
    back_ref = refs[0] if blocks else None
    (
        w_hbm, cos_ref, sin_ref, seg_ref, live_ref,
        qkv_ref, p_ref, o_ref, h_ref, b_ref, wrt_ref, x_ref, w_ref, w_sem,
    ) = refs[1 if blocks else 0 :]
    t, d = x_ref.shape
    pieces = arriving(w_hbm, w_ref, w_sem, "forward")
    mine = lax.axis_index("section")
    entering = (below_ref[mine] if len(below_ref.shape) == 3 else below_ref[...]).astype(F32)
    for z in range(blocks):
        entering = entering + back_ref[z].astype(F32)
    x_ref[...] = entering.astype(BF)
    pieces.pop(0).wait()
    aux = jnp.transpose(w_ref[:, QKV + QW :].astype(F32))
    wrt_ref[...] = aux.astype(BF)
    gain_attn = aux[GAIN_ATTN_ROW : GAIN_ATTN_ROW + 1]
    gain_moe = aux[GAIN_MOE_ROW : GAIN_MOE_ROW + 1]
    x = x_ref[...].astype(F32)
    r1 = lax.rsqrt(jnp.mean(x * x, axis=1, keepdims=True) + EPS)
    a = (x * r1 * gain_attn).astype(BF)
    cos, sin = cos_ref[...], sin_ref[...]
    for n in range(QKV // TILE):
        cols = slice(n * TILE, (n + 1) * TILE)
        pieces.pop(0).wait()
        y = dot(a, w_ref[:, cols])
        if n * TILE < QW + KW:
            y = rope(y, cos, sin, 1.0)
        qkv_ref[:, cols] = y.astype(BF)
    i, j = iota((t, t), 0), iota((t, t), 1)
    segments = jnp.broadcast_to(seg_ref[pl.ds(mine, 1), :].astype(F32), (t, t))
    first_block = jnp.zeros((t, t), jnp.int32)
    for block in range(t // BLK):
        first_block = jnp.where(i // BLK == block, live_ref[mine, block], first_block)
    allowed = (j <= i) & (jnp.transpose(segments) == segments) & (j // BLK >= first_block)
    masks = lane_masks(t)

    def pair(m, carry):
        def lanes(base):
            return pl.ds(pl.multiple_of(base, LANES), LANES)

        kp = qkv_ref[:, lanes(QW + m * LANES)]
        vp = qkv_ref[:, lanes(QW + KW + m * LANES)]
        ks, vs = swapped(kp), swapped(vp)
        plan = head_plan()
        scores = []
        for r, half, swap in plan:
            q = pick(qkv_ref[:, lanes((m * TILES_PER_PAIR + r) * LANES)], half, masks)
            s = dot(q, ks if swap else kp, 1, 1) * HEAD_SIZE ** (-0.5)
            scores.append(jnp.where(allowed, s, NEG_FILL))
        tops = [jnp.max(s, axis=1, keepdims=True) for s in scores]
        exps = [jnp.exp(s - top) for s, top in zip(scores, tops)]
        sums = [1.0 / jnp.sum(e, axis=1, keepdims=True) for e in exps]
        probs = [e * u for e, u in zip(exps, sums)]
        for (r, half, swap), p in zip(plan, probs):
            p_ref[m * 2 * TILES_PER_PAIR + 2 * r + half] = p
        parts = [dot(p.astype(BF), pick(vs if swap else vp, half, masks)) for (r, half, swap), p in zip(plan, probs)]
        for r in range(TILES_PER_PAIR):
            o_ref[:, lanes((m * TILES_PER_PAIR + r) * LANES)] = (parts[2 * r] + parts[2 * r + 1]).astype(BF)
        return carry

    lax.fori_loop(0, HEAD_PAIRS, pair, 0, unroll=True)
    o = o_ref[...]
    for n in range(d // TILE):
        rows = slice(n * TILE, (n + 1) * TILE)
        pieces.pop(0).wait()
        h_ref[:, rows] = x_ref[:, rows].astype(F32) + dot(o, w_ref[rows, QKV : QKV + QW], 1, 1)
    h = h_ref[...]
    r2 = lax.rsqrt(jnp.mean(h * h, axis=1, keepdims=True) + EPS)
    b_ref[...] = (h * r2 * gain_moe).astype(BF)


def vmem(n):
    return [pl.BlockSpec(memory_space=pltpu.VMEM)] * n


def attn_fwd(below, back, w, cos, sin, seg, live):
    t, d = below.shape[-2:]
    sds = jax.ShapeDtypeStruct
    return pl.pallas_call(
        functools.partial(attn_fwd_kernel, len(back)),
        out_shape=(
            sds((t, QKV), BF),
            sds((QUERY_HEADS, t, t), F32),
            sds((t, QW), BF),
            sds((t, d), F32),
            sds((t, d), BF),
            sds((LANES, d), BF),
            sds((t, d), BF),
        ),
        in_specs=vmem(2 if len(back) else 1) + [any_spec()] + vmem(3) + [pl.BlockSpec(memory_space=pltpu.SMEM)],
        out_specs=tuple(vmem(7)),
        scratch_shapes=[pltpu.VMEM(w.shape, BF), pltpu.SemaphoreType.DMA((1 + QKV // TILE + d // TILE,))],
        compiler_params=pltpu.CompilerParams(vmem_limit_bytes=VMEM_LIMIT),
        cost_estimate=pl.CostEstimate(flops=2 * t * d * 4096, bytes_accessed=w.size * 2, transcendentals=QUERY_HEADS * t * t),
    )(below, *((back,) if len(back) else ()), w, cos, sin, seg, live)


def gates_of(rt, wrt, b, e_pad):
    t = rt.shape[1]
    experts = iota((e_pad, t), 0)
    chosen = experts == rt[0:1]
    for k in range(1, rt.shape[0]):
        chosen = chosen | (experts == rt[k : k + 1])
    logits = jnp.where(chosen, dot(wrt[0:e_pad], b, 1, 1), NEG_FILL)
    e = jnp.where(chosen, jnp.exp(logits - jnp.max(logits, axis=0, keepdims=True)), 0.0)
    return e / jnp.sum(e, axis=0, keepdims=True)


def attn_bwd_kernel(
    layer, now, e_pad, e_real, gy_ref, h_ref, x_ref, w_hbm, qkv_ref, p_ref, o_ref, b_ref, wrt_ref, back_ref, dg_ref, rt_ref, side_ref, cos_ref, sin_ref,
    dx_ref, dxb_ref, *rest,
):
    t, d = x_ref.shape
    if now:
        dd_hbm, do_ref, dqkv_ref, dh_ref, w_ref, w_sem, lt_ref, dd_ref, dd_sem = rest
    else:
        dqkv_ref, at_ref, dht_ref, daux_ref, do_ref, dh_ref, w_ref, w_sem = rest
    pieces = arriving(w_hbm, w_ref, w_sem, "backward")
    leaving = []

    def leave(first, width):
        cols = pl.ds(first, width)
        leaving.append(pltpu.make_async_copy(dd_ref.at[:, cols], dd_hbm.at[:, cols], dd_sem.at[len(leaving)]))
        leaving[-1].start()

    gain_attn = wrt_ref[GAIN_ATTN_ROW - 7 :, :].astype(F32)[7:8]
    gain_moe = wrt_ref[GAIN_ATTN_ROW - 7 :, :].astype(F32)[6:7]
    b = b_ref[...]
    mine = lax.axis_index("section")
    gates = gates_of(jnp.where(mine == layer, rt_ref[mine], side_ref[...]), wrt_ref, b, e_pad)
    per = e_real // dg_ref.shape[0]
    dg = [dg_ref[z][0:per] for z in range(dg_ref.shape[0])]
    if e_pad > e_real:
        dg.append(jnp.zeros((e_pad - e_real, t), F32))
    dg = jnp.concatenate(dg, axis=0)
    dl = (gates * (dg - jnp.sum(gates * dg, axis=0, keepdims=True)))
    dlb = dl.astype(BF)
    db = dot(dlb, wrt_ref[0:e_pad, :], 0, 0)
    for z in range(back_ref.shape[0]):
        db = db + back_ref[z].astype(F32)
    h = h_ref[...]
    r2 = lax.rsqrt(jnp.mean(h * h, axis=1, keepdims=True) + EPS)
    grad_moe = jnp.sum(db * h * r2, axis=0, keepdims=True)
    dn = db * gain_moe
    gy = gy_ref[lax.axis_index("section")] if len(gy_ref.shape) == 3 else gy_ref[...]
    dh = gy.astype(F32) + r2 * dn - h * (r2 * r2 * r2) * jnp.mean(dn * h, axis=1, keepdims=True)
    dh_ref[...] = dh
    dhb = dh.astype(BF)
    for n in range(QW // TILE):
        cols = slice(n * TILE, (n + 1) * TILE)
        pieces.pop(0).wait()
        do_ref[:, cols] = dot(dhb, w_ref[:, QKV + n * TILE : QKV + (n + 1) * TILE]).astype(BF)
    masks = lane_masks(t)
    cos, sin = cos_ref[...], sin_ref[...]

    def pair(m, carry):
        def lanes(base):
            return pl.ds(pl.multiple_of(base, LANES), LANES)

        kp = qkv_ref[:, lanes(QW + m * LANES)]
        vp = qkv_ref[:, lanes(QW + KW + m * LANES)]
        ks, vs = swapped(kp), swapped(vp)
        plan = head_plan()
        tiles = [lanes((m * TILES_PER_PAIR + r) * LANES) for r in range(TILES_PER_PAIR)]
        qs = [pick(qkv_ref[:, tiles[r]], half, masks) for r, half, _ in plan]
        dos = [pick(do_ref[:, tiles[r]], half, masks) for r, half, _ in plan]
        ps = [p_ref[m * 2 * TILES_PER_PAIR + 2 * r + half] for r, half, _ in plan]
        dps = [dot(do, vs if swap else vp, 1, 1) for do, (_, _, swap) in zip(dos, plan)]
        dvs = [dot(p.astype(BF), do, 0, 0) for p, do in zip(ps, dos)]
        sums = [jnp.sum(p * dp, axis=1, keepdims=True) for p, dp in zip(ps, dps)]
        dts = [(p * (dp - total) * HEAD_SIZE ** (-0.5)).astype(BF) for p, dp, total in zip(ps, dps, sums)]
        dks = [dot(dt, q, 0, 0) for dt, q in zip(dts, qs)]
        dqs = [dot(dt, pick(ks if swap else kp, half, masks)) for dt, (_, half, swap) in zip(dts, plan)]
        for r in range(TILES_PER_PAIR):
            dqkv_ref[:, tiles[r]] = rope(dqs[2 * r] + dqs[2 * r + 1], cos, sin, -1.0).astype(BF)
        dk, dv = (
            {way: functools.reduce(jnp.add, [v for v, (_, _, swap) in zip(vals, plan) if swap == way]) for way in (False, True)}
            for vals in (dks, dvs)
        )
        dk_all = dk[False] + pltpu.roll(dk[True], HEAD_SIZE, 1)
        dv_all = dv[False] + pltpu.roll(dv[True], HEAD_SIZE, 1)
        dqkv_ref[:, lanes(QW + m * LANES)] = rope(dk_all, cos, sin, -1.0).astype(BF)
        dqkv_ref[:, lanes(QW + KW + m * LANES)] = dv_all.astype(BF)
        return carry

    lax.fori_loop(0, HEAD_PAIRS, pair, 0, unroll=True)
    x = x_ref[...].astype(F32)
    r1 = lax.rsqrt(jnp.mean(x * x, axis=1, keepdims=True) + EPS)
    dqkv = dqkv_ref[...]
    for n in range(d // TILE):
        rows = slice(n * TILE, (n + 1) * TILE)
        pieces.pop(0).wait()
        dx_ref[:, rows] = dot(dqkv, w_ref[rows, 0:QKV], 1, 1)
    da = dx_ref[...]
    grad_attn = jnp.sum(da * x * r1, axis=0, keepdims=True)
    dag = da * gain_attn
    dx = dh_ref[...] + r1 * dag - x * (r1 * r1 * r1) * jnp.mean(dag * x, axis=1, keepdims=True)
    dx_ref[...] = dx
    dxb_ref[...] = dx.astype(BF)
    row = iota((LANES, d), 0)
    grads = jnp.where(row == GAIN_MOE_ROW, grad_moe, jnp.where(row == GAIN_ATTN_ROW, grad_attn, 0.0))
    dl_full = jnp.concatenate([dl, jnp.zeros((LANES - e_pad, t), F32)], axis=0)
    dl_rows = jnp.transpose(dl_full).astype(BF)
    bt = jnp.transpose(b_ref[...].astype(F32)).astype(BF)
    daux = (dot(bt, dl_rows) + jnp.transpose(grads)).astype(BF)
    if not now:
        at_ref[...] = jnp.transpose(x * r1 * gain_attn).astype(BF)
        dht_ref[...] = jnp.transpose(dh_ref[...]).astype(BF)
        daux_ref[...] = daux
        return
    lt_ref[...] = jnp.transpose(x * r1 * gain_attn).astype(BF)
    for n in range(QKV // TILE):
        cols = slice(n * TILE, (n + 1) * TILE)
        dd_ref[:, cols] = dot(lt_ref[...], dqkv_ref[:, cols]).astype(BF)
        leave(n * TILE, TILE)
    lt_ref[...] = jnp.transpose(dh_ref[...]).astype(BF)
    for n in range(QW // TILE):
        cols = slice(n * TILE, (n + 1) * TILE)
        dd_ref[:, QKV + n * TILE : QKV + (n + 1) * TILE] = dot(lt_ref[...], o_ref[:, cols]).astype(BF)
        leave(QKV + n * TILE, TILE)
    dd_ref[:, QKV + QW :] = daux
    leave(QKV + QW, LANES)
    for c in leaving:
        c.wait()


def attn_bwd(layer, now, experts, gy, h, x, w, qkv, p, o, b, wrt, back, dg, rt, side, cos, sin):
    t, d = x.shape
    sds = jax.ShapeDtypeStruct
    dma = pltpu.SemaphoreType.DMA
    outs = [sds((t, d), F32), sds((t, d), BF)]
    scratch = [pltpu.VMEM((t, QW), BF)]
    if now:
        outs.append(sds(w.shape, BF))
        scratch.append(pltpu.VMEM((t, QKV), BF))
    else:
        outs += [sds((t, QKV), BF), sds((d, t), BF), sds((d, t), BF), sds((d, LANES), BF)]
    scratch += [pltpu.VMEM((t, d), F32), pltpu.VMEM(w.shape, BF), dma((QW // TILE + d // TILE,))]
    if now:
        scratch += [pltpu.VMEM((d, t), BF), pltpu.VMEM(w.shape, BF), dma((1 + QKV // TILE + QW // TILE,))]
    return pl.pallas_call(
        functools.partial(attn_bwd_kernel, layer, now, -(-experts // 16) * 16, experts),
        out_shape=tuple(outs),
        in_specs=vmem(3) + [any_spec()] + vmem(11),
        out_specs=tuple(vmem(2) + [any_spec()] if now else vmem(6)),
        scratch_shapes=scratch,
        compiler_params=pltpu.CompilerParams(vmem_limit_bytes=VMEM_LIMIT),
        cost_estimate=pl.CostEstimate(flops=4 * t * d * 4096, bytes_accessed=w.size * 4, transcendentals=0),
    )(gy, h, x, w, qkv, p, o, b, wrt, back, dg, rt, side, cos, sin)


def one_hot(pos_row, cap):
    return jnp.where(iota((cap, pos_row.shape[1]), 0) == pos_row, 1.0, 0.0)


def all_hots(pos, per, cap):
    return jnp.concatenate([one_hot(pos[j : j + 1], cap) for j in range(per)], axis=0)


def all_hots_back(pos, per, cap):
    width = per * cap
    expert = jnp.where(iota((8, width), 1) // cap == iota((8, width), 0), 1.0, 0.0).astype(BF)
    wide = dot(pos.astype(F32).astype(BF), expert, 0, 0)
    slot = (iota((1, width), 1) % cap).astype(F32)
    return jnp.where(wide == slot, 1.0, 0.0).astype(BF)


def slots_of(rt, first, per):
    t = rt.shape[1]
    experts = iota((16, t), 0)
    mine = jnp.where(experts < per, experts + first, -1)
    chosen = mine == rt[0:1]
    for k in range(1, rt.shape[0]):
        chosen = chosen | (mine == rt[k : k + 1])
    earlier = jnp.where(iota((t, t), 0) < iota((t, t), 1), 1.0, 0.0).astype(BF)
    before = dot(jnp.where(chosen, 1.0, 0.0).astype(BF), earlier)
    return jnp.where(chosen, before.astype(jnp.int32), -1)[0:8]


def streamed(count, copies, body, primed=False):
    if not primed:
        for c in copies(0, 0):
            c.start()

    def step(b, carry):
        slot = lax.rem(b, 2)

        @pl.when(b + 1 < count)
        def _():
            for c in copies(b + 1, lax.rem(b + 1, 2)):
                c.start()

        for c in copies(b, slot):
            c.wait()
        body(b, slot)
        return carry

    lax.fori_loop(0, count, step, 0)


def combine(base, count, per, cap, pos_ref, rows_ref, out_hbm, obuf, osem):
    def copy(b, slot):
        return pltpu.make_async_copy(obuf.at[slot], out_hbm.at[b], osem.at[slot])

    def step(b, carry):
        slot = lax.rem(b, 2)

        @pl.when(b >= 2)
        def _():
            copy(b - 2, slot).wait()

        back = all_hots_back(pos_ref[base + b], per, cap)
        at = pl.ds(pl.multiple_of((base + b) * cap, cap), cap)
        rows = jnp.concatenate([rows_ref[j, at, :] for j in range(per)], axis=0)
        obuf[slot] = dot(back, rows).astype(BF)
        copy(b, slot).start()
        return carry

    lax.fori_loop(0, count, step, 0)
    copy(count - 2, (count - 2) % 2).wait()
    copy(count - 1, (count - 1) % 2).wait()


def chunk_gates(c, j, chunk, cap, pos_ref, gate_ref):
    hots, gates = [], []
    for bb in range(chunk // cap):
        b = c * (chunk // cap) + bb
        hot = one_hot(pos_ref[b, pl.ds(j, 1), :], cap)
        hots.append(hot)
        gates.append(jnp.sum(hot * gate_ref[b, pl.ds(j, 1), :], axis=1, keepdims=True))
    return hots, jnp.concatenate(gates, axis=0)


def any_spec():
    return pl.BlockSpec(memory_space=pl.ANY)


def put_rows(hots, block, b, per, cap, dest):
    at = pl.ds(pl.multiple_of(b * cap, cap), cap)
    rows = dot(hots, block).astype(BF)
    for k in range(per):
        dest[k, at, :] = rows[k * cap : (k + 1) * cap]


def gather_from(count, per, cap, pos, source, dest, buf, sem):
    def body(b, slot):
        put_rows(all_hots(pos[b], per, cap).astype(BF), buf[slot], b, per, cap, dest)

    streamed(count, lambda b, slot: [pltpu.make_async_copy(source.at[b], buf.at[slot], sem.at[slot])], body)


def weight_grads(r, per):
    parts, piece = r.even.shape[0], r.even.shape[3]
    g = lax.axis_index("group")
    parity, place = lax.rem(g, 2), g // 2

    def outgoing(j, at, slot):
        return [
            pltpu.make_async_copy(r.gu_buf.at[slot, 0], r.even.at[at, :, j], r.gu_sem.at[slot, 0]),
            pltpu.make_async_copy(r.gu_buf.at[slot, 1], r.odd.at[at, :, j], r.gu_sem.at[slot, 1]),
            pltpu.make_async_copy(r.dn_buf.at[slot, 0], r.even_dn.at[at, j], r.dn_sem.at[slot, 0]),
            pltpu.make_async_copy(r.dn_buf.at[slot, 1], r.odd_dn.at[at, j], r.dn_sem.at[slot, 1]),
        ]

    def finished(slot):
        for c in outgoing(0, 0, slot):
            c.wait()

    def body(j, carry):
        for q in range(parts):
            slot = q % 2
            if q >= 2:
                finished(slot)
            else:

                @pl.when(j > 0)
                def _():
                    finished(slot)

            cols = slice(2 * q * piece, 2 * (q + 1) * piece)
            for m in range(2):
                full = dot(r.x_scr[j, :, cols], r.act[m, j], 0, 0).astype(BF)
                r.gu_buf[slot, parity, m] = full[:piece]
                r.gu_buf[slot, 1 - parity, m] = full[piece:]
            full = dot(r.act[2, j], r.y_scr[j, :, cols], 0, 0).astype(BF)
            r.dn_buf[slot, parity] = full[:, :piece]
            r.dn_buf[slot, 1 - parity] = full[:, piece:]
            for c in outgoing(j, lax.bitwise_xor(place, q), slot):
                c.start()
        return carry

    lax.fori_loop(0, per, body, 0)
    for slot in range(2):
        finished(slot)


def meet(n, bits):
    s, g, z = lax.axis_index("section"), lax.axis_index("group"), lax.axis_index("expert")
    barrier = pltpu.get_barrier_semaphore()
    peers = [{"section": 1 - s}] + [{"expert": lax.rem(z + k, n)} for k in range(1, n)]
    peers += [{"group": lax.bitwise_xor(g, 1 << b)} for b in range(bits)]
    for peer in peers:
        pl.semaphore_signal(barrier, inc=1, device_id=peer, device_id_type=MESH)
    pl.semaphore_wait(barrier, len(peers))


def moe_kernel(layer, mode, n, e_pad, cap, names, *refs):
    r = types.SimpleNamespace(**dict(zip(names, refs)))
    forward, backward = mode != "bwd", mode != "fwd"
    s, z = lax.axis_index("section"), lax.axis_index("expert")
    here = s == layer
    count = 2 * n
    per, rows, d = r.y_scr.shape
    first = z * per
    chunk = n * cap
    remote = functools.partial(pltpu.make_async_remote_copy, device_id_type=MESH)
    other = {"section": 1 - s}
    g = lax.axis_index("group")
    riding = forward and not backward
    groups = r.dense_out.shape[0] // n if riding else 1
    bits = top_bit(groups)
    meet(n, bits)
    r.blk[s, z] = r.own[...]

    def over(q, b, zz):
        at = q | (1 << b)
        shard = r.dense_out.at[lax.bitwise_xor(g, q) * n + zz]
        return remote(
            src_ref=shard, dst_ref=shard, send_sem=r.s_over.at[at, zz], recv_sem=r.r_over.at[at, zz],
            device_id={"group": lax.bitwise_xor(g, 1 << b)},
        )

    def ride(bs):
        for b in bs:
            for zz in range(n):
                over(0, b, zz).start()

    def ride_on():
        for q in sorted(range(1, groups), key=lambda q: -low_bit(q)):
            for zz in range(n):
                over(q & (q - 1), low_bit(q), zz).wait_recv()
                for b in reversed(range(low_bit(q))):
                    over(q, b, zz).start()

    if riding:
        ride(reversed(range(1, bits)))

    def half(i):
        section = jnp.where(i < per, layer, 1 - layer)
        return lax.rem(i, per), section, pl.ds(pl.multiple_of(section * chunk, chunk), chunk)

    def weights(i, slot):
        j, _, at = half(i)
        both = [
            pltpu.make_async_copy(r.wg.at[j], r.wg_buf.at[slot], r.w_sem.at[slot, 0]),
            pltpu.make_async_copy(r.wu.at[j], r.wu_buf.at[slot], r.w_sem.at[slot, 1]),
            pltpu.make_async_copy(r.wd.at[j], r.wd_buf.at[slot], r.w_sem.at[slot, 2]),
        ]
        if mode == "bwd":
            both.append(pltpu.make_async_copy(r.gp.at[j, at], r.gp_buf.at[slot], r.gp_sem.at[slot, 0]))
            both.append(pltpu.make_async_copy(r.up.at[j, at], r.gp_buf.at[2 + slot], r.gp_sem.at[slot, 1]))
        return both

    def chain(to, zz, t, ssem, rsem):
        return remote(
            src_ref=r.blk.at[s, zz], dst_ref=r.blk.at[s, zz], send_sem=ssem.at[t], recv_sem=rsem.at[t], device_id={"expert": to}
        )

    def right(t):
        return chain(z + 1, z - t, t, r.s_right, r.r_right)

    def left(t):
        return chain(z - 1, z + t, t, r.s_left, r.r_left)

    def cross(zz):
        return remote(
            src_ref=r.blk.at[s, zz], dst_ref=r.blk.at[s, zz], send_sem=r.s_cross.at[zz], recv_sem=r.r_cross.at[zz], device_id=other
        )

    def prepare(section, zz):
        b = section * n + zz
        block = r.blk[section, zz]
        if forward:
            rt = r.rt[b]
            pos = slots_of(rt, first, per)
            r.pos[b] = pos
            r.gates[...] = gates_of(rt, r.wrt, block, e_pad)
            r.gate[b] = jnp.concatenate(
                [r.gates[pl.ds(first + k, 1), :] for k in range(per)] + [jnp.zeros((8 - per, rt.shape[1]), F32)], axis=0
            )
            put_rows(all_hots(pos, per, cap).astype(BF), block, b, per, cap, r.x_scr)
        else:
            put_rows(all_hots(r.pos[b], per, cap).astype(BF), block, b, per, cap, r.y_scr)

    @pl.when(here)
    def _():
        for c in weights(0, 0):
            c.start()

    def prepare_at(section, t):
        def candidate(m, carry):
            zz = jnp.where(m == 0, z - t, z + t)

            @pl.when((zz >= 0) & (zz < n) & ((m == 0) | (t > 0)))
            def _():
                prepare(section, zz)

            return carry

        lax.fori_loop(0, 2, candidate, 0)

    tiles = (("at", "dqkv", 0, QW), ("at", "dqkv", QW, 2 * KW), ("dht", "o", QKV, QW))

    def dense_copy(block, m):
        _, _, col, width = tiles[m]
        at = pl.ds(pl.multiple_of(block * rows, rows), rows)
        return pltpu.make_async_copy(
            r.x_scr.at[m, :, pl.ds(0, width)], r.dd.at[at, pl.ds(col, width)], r.dd_sem.at[m]
        )

    def aux_copy():
        return pltpu.make_async_copy(r.daux, r.dd.at[:, pl.ds(QKV + QW, LANES)], r.daux_sem)

    def dense_start(block):
        @pl.when(block == 0)
        def _():
            aux_copy().start()

        at = pl.ds(pl.multiple_of(block * rows, rows), rows)
        for m, (left, right, col, width) in enumerate(tiles):

            @pl.when(block > 0)
            def _():
                dense_copy(block - 1, m).wait()

            source = getattr(r, right)
            source = source[:, col : col + width] if right == "dqkv" else source[...]
            r.x_scr[m, :, 0:width] = dot(getattr(r, left)[at, :], source).astype(BF)
            dense_copy(block, m).start()

    def dense_wait():
        aux_copy().wait()
        for m in range(len(tiles)):
            dense_copy(d // rows - 1, m).wait()

    @pl.loop(0, n)
    def _(t):
        from_left = z >= t
        from_right = z + t < n

        @pl.when(from_left & (t > 0))
        def _():
            right(t - 1).wait_recv()

        @pl.when(from_left & (z < n - 1))
        def _():
            right(t).start()

        @pl.when(from_left & jnp.logical_not(here))
        def _():
            cross(z - t).start()

        @pl.when(from_right & (t > 0))
        def _():
            left(t - 1).wait_recv()

        @pl.when(from_right & (z > 0))
        def _():
            left(t).start()

        @pl.when(from_right & (t > 0) & jnp.logical_not(here))
        def _():
            cross(z + t).start()

        if mode == "bwd":

            @pl.when(t < d // rows)
            def _():
                dense_start(t)

        @pl.when(here)
        def _():
            if mode == "both":

                @pl.when(t == 0)
                def _():
                    @pl.loop(0, count)
                    def _(b):
                        r.pos[b] = slots_of(r.rt[b], first, per)

                    gather_from(count, per, cap, r.pos, r.gy, r.y_scr, r.row_buf, r.row_sem)

            prepare_at(layer, t)

            @pl.when(t == min(2, n - 1))
            def _():
                cross(z).wait_recv()
                prepare(1 - layer, z)

    def late_blocks():
        @pl.loop(1, n)
        def _(t):
            @pl.when(z >= t)
            def _():
                cross(z - t).wait_recv()

            @pl.when(z + t < n)
            def _():
                cross(z + t).wait_recv()

            prepare_at(1 - layer, t)

    if riding:
        ride((0,))

    def over_part(zz):
        return remote(
            src_ref=r.part.at[zz], dst_ref=r.part_out.at[zz], send_sem=r.s_part.at[zz], recv_sem=r.r_part.at[zz], device_id=other
        )

    if mode == "bwd":
        dense_wait()

        @pl.when(jnp.logical_not(here))
        def _():
            for zz in range(n):
                over_part(zz).start()
            pltpu.make_async_copy(r.part_own, r.pbuf.at[layer], r.part_sem.at[0]).start()

    def part_home():
        return pltpu.make_async_copy(r.pbuf.at[layer], r.part_out, r.part_sem.at[1])

    srcs = (r.pbuf, r.dg) if backward else (r.pbuf,)
    outs = (r.back, r.dgate) if backward else (r.back,)
    relays = (r.relay, r.dg_relay) if backward else (r.relay,)
    arrays = range(len(srcs))

    def hop(a, to):
        return remote(
            src_ref=srcs[a].at[1 - layer, to],
            dst_ref=relays[a].at[to],
            send_sem=r.s_hop.at[a, to],
            recv_sem=r.r_hop.at[a, to],
            device_id=other,
        )

    def give(a, source, k):
        return remote(
            src_ref=source,
            dst_ref=outs[a].at[z],
            send_sem=r.s_give.at[a, k],
            recv_sem=r.r_give.at[a, k],
            device_id={"expert": lax.rem(z + k, n)},
        )

    def keep(a, source):
        return pltpu.make_async_copy(source, outs[a].at[z], r.keep_sem.at[a])

    def saved(i, slot):
        j, _, at = half(i)
        return [
            pltpu.make_async_copy(r.gp_buf.at[slot], r.gp.at[j, at], r.gp_sem.at[slot, 0]),
            pltpu.make_async_copy(r.gp_buf.at[2 + slot], r.up.at[j, at], r.gp_sem.at[slot, 1]),
        ]

    def expert(i, slot):
        j, section, at = half(i)

        @pl.when(i == per)
        def _():
            late_blocks()

        if mode == "fwd":

            @pl.when(i >= 2)
            def _():
                for c in saved(i - 2, slot):
                    c.wait()

        if forward:
            x = r.x_scr[j, at, :]
            gp = dot(x, r.wg_buf[slot])
            up = dot(x, r.wu_buf[slot])
        else:
            gp, up = r.gp_buf[slot].astype(F32), r.gp_buf[2 + slot].astype(F32)
        sg = 1.0 / (1.0 + jnp.exp(-gp))
        silu = gp * sg
        hid = silu * up
        hots, gate = chunk_gates(section, j, chunk, cap, r.pos, r.gate)
        if not backward:
            r.gp_buf[slot] = gp.astype(BF)
            r.gp_buf[2 + slot] = up.astype(BF)
            r.y_scr[j, at, :] = (dot(hid.astype(BF), r.wd_buf[slot]) * gate).astype(BF)
            for c in saved(i, slot):
                c.start()
            return
        raw = dot(r.y_scr[j, at, :], r.wd_buf[slot], 1, 1)
        dgate = jnp.sum(hid.astype(BF).astype(F32) * raw, axis=1, keepdims=True)
        for bb in range(n):
            r.dg[section, bb, pl.ds(j, 1), :] = jnp.sum(hots[bb] * dgate[bb * cap : (bb + 1) * cap], axis=0, keepdims=True)
        dh = raw * gate
        dgp = (dh * up * sg * (1.0 + gp * (1.0 - sg))).astype(BF)
        dup = (dh * silu).astype(BF)
        r.act[0, j, at, :] = dgp
        r.act[1, j, at, :] = dup
        r.act[2, j, at, :] = (hid * gate).astype(BF)
        r.y_scr[j, at, :] = (dot(dgp, r.wg_buf[slot], 1, 1) + dot(dup, r.wu_buf[slot], 1, 1)).astype(BF)

    def summed(b, source):
        at = pl.ds(pl.multiple_of(b * cap, cap), cap)
        stacked = jnp.concatenate([source[j, at, :] for j in range(per)], axis=0)
        return dot(all_hots_back(r.pos[b], per, cap), stacked).astype(BF)

    @pl.when(here)
    def _():
        if backward:
            r.dg[...] = jnp.zeros_like(r.dg)
        if mode == "fwd":
            keep_blocks = pltpu.make_async_copy(r.blk, r.blocks, r.row_sem.at[0])
        streamed(2 * per, weights, expert, primed=True)
        if mode == "fwd":
            keep_blocks.start()

        def emit(i, carry):
            to = lax.rem(z + i + 1, n)
            section = jnp.where(i < n, 1 - layer, layer)
            r.pbuf[section, to] = summed(section * n + to, r.y_scr)

            @pl.when(i < n)
            def _():
                for a in arrays:
                    hop(a, to).start()

            @pl.when((i >= n) & (to != z))
            def _():
                for a in arrays:
                    give(a, srcs[a].at[layer, to], i + 1 - n).start()

            return carry

        lax.fori_loop(0, 2 * n, emit, 0)
        for a in arrays:
            keep(a, srcs[a].at[layer, z]).start()
        if mode == "fwd":
            for i in (2 * per - 2, 2 * per - 1):
                for c in saved(i, i % 2):
                    c.wait()
            keep_blocks.wait()
        if mode == "bwd":

            @pl.loop(0, count)
            def _(b):
                put_rows(all_hots(r.pos[b], per, cap).astype(BF), r.blk[b // n, lax.rem(b, n)], b, per, cap, r.y_scr)

            gather_from(count, per, cap, r.pos, r.blocks, r.x_scr, r.row_buf, r.row_sem)
        if mode == "both":
            gather_from(count, per, cap, r.pos, r.gy, r.y_scr, r.row_buf, r.row_sem)
        if backward:
            weight_grads(r, per)
        if mode == "both":
            def output(j, slot):
                @pl.loop(0, 2)
                def _(c):
                    at = pl.ds(pl.multiple_of(c * chunk, chunk), chunk)
                    r.x_scr[j, at, :] = dot(r.act[2, j, at, :], r.wd_buf[slot]).astype(BF)

            streamed(per, lambda j, slot: weights(j, slot)[2:], output)
            combine(0, n, per, cap, r.pos, r.x_scr, r.part0, r.row_buf, r.row_sem)
            combine(n, n, per, cap, r.pos, r.x_scr, r.part1, r.row_buf, r.row_sem)
        for to in range(n):
            for a in arrays:
                hop(a, to).wait_send()

    @pl.when(jnp.logical_not(here))
    def _():
        @pl.loop(1, n + 1)
        def _(k):
            to = lax.rem(lax.rem(k, n) + z, n)
            for a in arrays:
                hop(a, to).wait_recv()

            @pl.when(k < n)
            def _():
                for a in arrays:
                    give(a, relays[a].at[to], k).start()

        for a in arrays:
            keep(a, relays[a].at[z]).start()
        for zz in range(n):
            cross(zz).wait_send()

    if mode == "bwd":

        @pl.when(here)
        def _():
            for zz in range(n):
                over_part(zz).wait_recv()

        @pl.when(jnp.logical_not(here))
        def _():
            pltpu.make_async_copy(r.part_own, r.pbuf.at[layer], r.part_sem.at[0]).wait()
            part_home().start()
            part_home().wait()
            for zz in range(n):
                over_part(zz).wait_send()

    if riding:
        ride_on()
        for q in range(1, groups):
            for zz in range(n):
                over(q & (q - 1), low_bit(q), zz).wait_send()
    for a in arrays:
        keep(a, relays[a].at[z]).wait()
        for k in range(1, n):
            give(a, relays[a].at[lax.rem(z + k, n)], k).wait()
    for t in range(n):

        @pl.when((z >= t) & (z < n - 1))
        def _():
            right(t).wait_send()

        @pl.when((z + t < n) & (z > 0))
        def _():
            left(t).wait_send()


def moe(layer, mode, cid, e_pad, cap, own, wg, wu, wd, **given):
    n, groups = lax.axis_size("expert"), lax.axis_size("group")
    count = 2 * n
    t, d = own.shape
    per, _, f = wg.shape
    rows = count * cap
    piece = d // groups
    sds = jax.ShapeDtypeStruct
    dma = pltpu.SemaphoreType.DMA
    vm, hbm = pl.BlockSpec(memory_space=pltpu.VMEM), any_spec()
    on_chip = ("own", "rt", "wrt", "pos", "gate", "dqkv", "at", "dht", "daux", "o")
    ins = dict(own=own, wg=wg, wu=wu, wd=wd, **given)
    outs = dict(back=sds((n, t, d), BF))
    scratch = dict(
        blk=pltpu.VMEM((2, n, t, d), BF),
        y_scr=pltpu.VMEM((per, rows, d), BF),
        wg_buf=pltpu.VMEM((2, d, f), BF),
        wu_buf=pltpu.VMEM((2, d, f), BF),
        wd_buf=pltpu.VMEM((2, f, d), BF),
        pbuf=pltpu.VMEM((2, n, t, d), BF),
        relay=pltpu.VMEM((n, t, d), BF),
        x_scr=pltpu.VMEM((per, rows, d), BF),
        row_buf=pltpu.VMEM((2, t, d), BF),
        row_sem=dma((2,)),
        w_sem=dma((2, 3)),
        keep_sem=dma((2,)),
    )
    for name in ("right", "left", "cross"):
        scratch["s_" + name] = dma((n,))
        scratch["r_" + name] = dma((n,))
    for name in ("hop", "give"):
        scratch["s_" + name] = dma((2, n))
        scratch["r_" + name] = dma((2, n))
    if mode != "both":
        scratch["gp_buf"] = pltpu.VMEM((4, n * cap, f), BF)
        scratch["gp_sem"] = dma((2, 2))
    if mode != "bwd":
        scratch["gates"] = pltpu.VMEM((e_pad, t), F32)
    if mode == "fwd":
        del scratch["row_buf"]
        outs.update(pos=sds((count, 8, t), jnp.int32), gate=sds((count, 8, t), F32))
        outs.update(gp=sds((per, rows, f), BF), up=sds((per, rows, f), BF), blocks=sds((2, n, t, d), BF))
        outs["dense_out"] = sds(given["dense"].shape, BF)
        scratch.update(s_over=dma((groups, n)), r_over=dma((groups, n)))
    else:
        outs["dgate"] = sds((n, 8, t), F32)
        outs["even"] = outs["odd"] = sds((groups // 2, 2, per, piece, f), BF)
        outs["even_dn"] = outs["odd_dn"] = sds((groups // 2, per, f, piece), BF)
        scratch.update(
            dg=pltpu.VMEM((2, n, 8, t), F32),
            dg_relay=pltpu.VMEM((n, 8, t), F32),
            act=pltpu.VMEM((3, per, rows, f), BF),
            gu_buf=pltpu.VMEM((2, 2, 2, piece, f), BF),
            dn_buf=pltpu.VMEM((2, 2, f, piece), BF),
            gu_sem=dma((2, 2)),
            dn_sem=dma((2, 2)),
        )
    if mode == "bwd":
        outs["dd"] = sds((d, QKV + QW + LANES), BF)
        outs["part_out"] = sds((n, t, d), BF)
        scratch.update(s_part=dma((n,)), r_part=dma((n,)), part_sem=dma((2,)))
        scratch.update(dd_sem=dma((3,)), daux_sem=dma)
    if mode == "both":
        outs["part0"] = outs["part1"] = sds((n, t, d), BF)
        scratch.update(pos=pltpu.VMEM((count, 8, t), jnp.int32), gate=pltpu.VMEM((count, 8, t), F32))
    names = tuple(ins) + tuple(outs) + tuple(scratch)
    results = pl.pallas_call(
        functools.partial(moe_kernel, layer, mode, n, e_pad, cap, names),
        out_shape=tuple(outs.values()),
        in_specs=[vm if name in on_chip else hbm for name in ins],
        out_specs=tuple(vm if name in on_chip else hbm for name in outs),
        scratch_shapes=list(scratch.values()),
        input_output_aliases={list(ins).index("dense"): list(outs).index("dense_out")} if mode == "fwd" else {},
        compiler_params=pltpu.CompilerParams(collective_id=cid, has_side_effects=True, vmem_limit_bytes=VMEM_LIMIT),
    )(*ins.values())
    return types.SimpleNamespace(**dict(zip(outs, results)))


def top_bit(q):
    return q.bit_length() - 1


def finish_kernel(
    n, dd0, dd1, dx0, dx1, egu0, ogu0, ed0, od0, egu1, ogu1, ed1, od1,
    dense_out, dx_out, gate_out, up_out, down_out,
    core_gu, core_dn, hop_gu, hop_dn, core_dd, hop_y, hop_z, hop_x, dd_buf, gu_buf, dn_buf, gu_res, dn_res,
    s_core_gu, r_core_gu, s_core_dn, r_core_dn, s_hop_gu, r_hop_gu, s_hop_dn, r_hop_dn,
    s_core_dd, r_core_dd, s_y, r_y, s_z, r_z, s_x, r_x, l_dd, l_gu, l_dn, o_gu, o_dn, s_dx, r_dx,
):
    s, g, z = lax.axis_index("section"), lax.axis_index("group"), lax.axis_index("expert")
    pairs, cgu = core_gu.shape[:2]
    cdn = core_dn.shape[1]
    levels = top_bit(pairs)
    units = pairs * n
    remote = functools.partial(pltpu.make_async_remote_copy, device_id_type=MESH)
    twin = {"group": lax.bitwise_xor(g, 1)}
    other = {"section": 1 - s}

    def across(k):
        return {"group": lax.bitwise_xor(g, 2 << k)}

    barrier = pltpu.get_barrier_semaphore()
    peers = [twin, other] + [across(k) for k in range(levels)] + [{"expert": lax.rem(z + k, n)} for k in range(1, n)]
    for peer in peers:
        pl.semaphore_signal(barrier, inc=1, device_id=peer, device_id_type=MESH)
    pl.semaphore_wait(barrier, len(peers))

    def by_section(action):
        @pl.when(s == 0)
        def _():
            action(dd0, dd1, egu0, ogu0, ed0, od0)

        @pl.when(s != 0)
        def _():
            action(dd1, dd0, egu1, ogu1, ed1, od1)

    def unit(i):
        return pairs - 1 - i // n, lax.rem(z + 1 + lax.rem(i, n), n)

    def shard(i, core):
        q, place = unit(i)
        return (lax.bitwise_xor(g // 2, q) * 2 + core) * n + place

    core = lax.rem(g, 2)

    def core_dd_copy(kind, i, source):
        return remote(
            src_ref=source.at[shard(i, 1 - core)],
            dst_ref=core_dd.at[kind, i],
            send_sem=s_core_dd.at[kind, i],
            recv_sem=r_core_dd.at[kind, i],
            device_id=twin,
        )

    def core_chunk(source, dest, ssem, rsem, q, c):
        return remote(
            src_ref=source.at[q, c], dst_ref=dest.at[q, c], send_sem=ssem.at[q, c], recv_sem=rsem.at[q, c], device_id=twin
        )

    def core_gu_copy(source, q, c):
        return core_chunk(source, core_gu, s_core_gu, r_core_gu, q, c)

    def core_dn_copy(source, q, c):
        return core_chunk(source, core_dn, s_core_dn, r_core_dn, q, c)

    def send_first(own, away, egu, ogu, ed, od):
        @pl.loop(0, units)
        def _(i):
            core_dd_copy(0, i, away).start()

            @pl.when(i < cgu)
            def _():
                core_gu_copy(ogu, pairs - 1, i).start()

            @pl.when(i < cdn)
            def _():
                core_dn_copy(od, pairs - 1, i).start()

        for i in range(units, max(cgu, cdn)):
            if i < cgu:
                core_gu_copy(ogu, pairs - 1, i).start()
            if i < cdn:
                core_dn_copy(od, pairs - 1, i).start()

    def send_rest(own, away, egu, ogu, ed, od):
        @pl.loop(0, units)
        def _(i):
            core_dd_copy(1, i, own).start()

        for q in reversed(range(pairs - 1)):

            @pl.loop(0, cgu)
            def _(c):
                core_gu_copy(ogu, q, c).start()

            @pl.loop(0, cdn)
            def _(c):
                core_dn_copy(od, q, c).start()

    by_section(send_first)

    def dx_copy(source):
        return remote(src_ref=source, dst_ref=dx_out, send_sem=s_dx, recv_sem=r_dx, device_id=other)

    def load(buf, sem, slot, source):
        return pltpu.make_async_copy(source, buf.at[slot], sem.at[slot])

    def dd_load(i, slot, source):
        return load(dd_buf, l_dd, slot, source.at[shard(i, core)])

    def hop(dest, ssem, rsem, source, k, q, c):
        return remote(
            src_ref=source.at[q, c],
            dst_ref=dest.at[k, q - (1 << k), c],
            send_sem=ssem.at[k, q - (1 << k), c],
            recv_sem=rsem.at[k, q - (1 << k), c],
            device_id=across(k),
        )

    def gu_hop(k, q, c):
        return hop(hop_gu, s_hop_gu, r_hop_gu, core_gu, k, q, c)

    def dn_hop(k, q, c):
        return hop(hop_dn, s_hop_dn, r_hop_dn, core_dn, k, q, c)

    def y_copy(i):
        return remote(src_ref=core_dd.at[0, i], dst_ref=hop_y.at[i], send_sem=s_y.at[i], recv_sem=r_y.at[i], device_id=other)

    def z_copy(q, k, i):
        return remote(
            src_ref=core_dd.at[1, i],
            dst_ref=hop_z.at[k - 1, q],
            send_sem=s_z.at[k - 1, q],
            recv_sem=r_z.at[k - 1, q],
            device_id={"expert": lax.rem(z + k, n)},
        )

    def x_copy(k, q, i):
        return remote(
            src_ref=core_dd.at[1, i],
            dst_ref=hop_x.at[k, q - (1 << k)],
            send_sem=s_x.at[k, q - (1 << k)],
            recv_sem=r_x.at[k, q - (1 << k)],
            device_id=across(k),
        )

    def chunk_start(i, slot, q, egu, ed):
        @pl.when(i < cgu)
        def _():
            load(gu_buf, l_gu, slot, egu.at[q, i]).start()

        @pl.when(i < cdn)
        def _():
            load(dn_buf, l_dn, slot, ed.at[q, i]).start()

    def expert_sum(hops, rsem, dest, core_r, buf, sem, slot, even, q, c, hop_copy):
        load(buf, sem, slot, even.at[q, c]).wait()
        core_r(q, c).wait_recv()
        total = buf[slot].astype(F32) + dest[q, c].astype(F32)
        for k in range(top_bit(q) + 1 if q else 0, levels):
            hop_copy(k, q + (1 << k), c).wait_recv()
            total = total + hops[k, q, c].astype(F32)
        return total

    def gu_sum(slot, q, c):
        return expert_sum(hop_gu, r_hop_gu, core_gu, functools.partial(core_gu_copy, ogu0), gu_buf, l_gu, slot, egu0, q, c, gu_hop)

    def dn_sum(slot, q, c):
        return expert_sum(hop_dn, r_hop_dn, core_dn, functools.partial(core_dn_copy, od0), dn_buf, l_dn, slot, ed0, q, c, dn_hop)

    def stepped(count, start, body):
        start(0, 0)

        def step(i, carry):
            @pl.when(i + 1 < count)
            def _():
                start(i + 1, lax.rem(i + 1, 2))

            body(i, lax.rem(i, 2))
            return carry

        lax.fori_loop(0, count, step, 0)

    for q in reversed(range(1, pairs)):
        dense_too = q == pairs - 1
        if not dense_too and q == pairs - 2:
            by_section(send_rest)
        steps = max(units, cgu, cdn) if dense_too else max(cgu, cdn)

        def start(i, slot):
            def go(own, away, egu, ogu, ed, od):
                if dense_too:

                    @pl.when(i < units)
                    def _():
                        dd_load(i, slot, away).start()

                chunk_start(i, slot, q, egu, ed)

            by_section(go)

        def body(i, slot):
            if dense_too:

                @pl.when(i < units)
                def _():
                    dd_load(i, slot, dd0).wait()
                    core_dd_copy(0, i, dd0).wait_recv()
                    core_dd[0, i] = core_dd[0, i] + dd_buf[slot]
                    y_copy(i).start()

            @pl.when(i < cgu)
            def _():
                core_gu[q, i] = gu_sum(slot, q, i).astype(BF)
                gu_hop(top_bit(q), q, i).start()

            @pl.when(i < cdn)
            def _():
                core_dn[q, i] = dn_sum(slot, q, i).astype(BF)
                dn_hop(top_bit(q), q, i).start()

        stepped(steps, start, body)

    if pairs == 2:
        by_section(send_rest)

    @pl.when(s == 0)
    def _():
        dx_copy(dx1).start()

    @pl.when(s != 0)
    def _():
        dx_copy(dx0).start()

    def gu_out_copy(c, slot, to=gate_out):
        return pltpu.make_async_copy(gu_res.at[slot], to.at[lax.rem(c, cgu // 2)], o_gu.at[slot])

    def dn_out_copy(c, slot):
        return pltpu.make_async_copy(dn_res.at[slot], down_out.at[c], o_dn.at[slot])

    def dense_sum(q):
        i = (pairs - 1 - q) * n + n - 1
        total = core_dd[1, i].astype(F32)
        for k in range(1, n):
            z_copy(q, k, i).wait_recv()
            total = total + hop_z[k - 1, q].astype(F32)
        for k in range(top_bit(q) + 1 if q else 0, levels):
            x_copy(k, q + (1 << k), i).wait_recv()
            total = total + hop_x[k, q].astype(F32)
        return i, total

    def pass_on(q):
        i, total = dense_sum(q)
        core_dd[1, i] = total.astype(BF)
        x_copy(top_bit(q), q, i).start()

    def core_sent():
        @pl.loop(0, units)
        def _(i):
            core_dd_copy(0, i, dd0).wait_send()
            core_dd_copy(1, i, dd0).wait_send()

        for q in range(pairs):

            @pl.loop(0, cgu)
            def _(c):
                core_gu_copy(ogu0, q, c).wait_send()

            @pl.loop(0, cdn)
            def _(c):
                core_dn_copy(od0, q, c).wait_send()

    steps = max(units, cgu, cdn)

    def start(i, slot):
        def go(own, away, egu, ogu, ed, od):
            @pl.when(i < units)
            def _():
                dd_load(i, slot, own).start()

            chunk_start(i, slot, 0, egu, ed)

        by_section(go)

    def body(i, slot):
        @pl.when(i < units)
        def _():
            dd_load(i, slot, dd0).wait()
            core_dd_copy(1, i, dd0).wait_recv()
            y_copy(i).wait_recv()
            core_dd[1, i] = (core_dd[1, i].astype(F32) + dd_buf[slot].astype(F32) + hop_y[i].astype(F32)).astype(BF)
            q, _ = unit(i)
            k = lax.rem(i, n) + 1

            @pl.when(k < n)
            def _():
                z_copy(q, k, i).start()

        for q in range(1, pairs):

            @pl.when(i == (pairs - q) * n + min(2, n - 1))
            def _():
                pass_on(q)

        @pl.when(i == units - 2)
        def _():
            core_sent()

        @pl.when(i < cgu)
        def _():
            @pl.when(i >= 2)
            def _():
                gu_out_copy(i - 2, slot).wait()

            gu_res[slot] = gu_sum(slot, 0, i).astype(BF)

            @pl.when(i < cgu // 2)
            def _():
                gu_out_copy(i, slot).start()

            @pl.when(i >= cgu // 2)
            def _():
                gu_out_copy(i, slot, up_out).start()

        @pl.when(i < cdn)
        def _():
            @pl.when(i >= 2)
            def _():
                dn_out_copy(i - 2, slot).wait()

            dn_res[slot] = dn_sum(slot, 0, i).astype(BF)
            dn_out_copy(i, slot).start()

    stepped(steps, start, body)
    _, total = dense_sum(0)
    dense_out[...] = total
    for c in (cgu - 2, cgu - 1):
        gu_out_copy(c, c % 2).wait()
    for c in (cdn - 2, cdn - 1):
        dn_out_copy(c, c % 2).wait()

    dx_copy(dx0).wait()

    @pl.loop(0, units)
    def _(i):
        y_copy(i).wait_send()
        q, _ = unit(i)
        k = lax.rem(i, n) + 1

        @pl.when(k < n)
        def _():
            z_copy(q, k, i).wait_send()

    for q in range(1, pairs):
        x_copy(top_bit(q), q, (pairs - 1 - q) * n + n - 1).wait_send()

        @pl.loop(0, cgu)
        def _(c):
            gu_hop(top_bit(q), q, c).wait_send()

        @pl.loop(0, cdn)
        def _(c):
            dn_hop(top_bit(q), q, c).wait_send()


def finish(cid, dd0, dd1, dx0, dx1, experts0, experts1):
    n, groups = lax.axis_size("expert"), lax.axis_size("group")
    pairs, levels = groups // 2, top_bit(groups // 2)
    width = dd0.shape[1]
    rows = dd0.shape[0] // (groups * n)
    dd0, dd1 = (v.reshape(groups * n, rows, width) for v in (dd0, dd1))

    def chunked(arrays):
        gu_even, gu_odd, dn_even, dn_odd = arrays
        flat = (pairs, -1) + gu_even.shape[3:]
        return gu_even.reshape(flat), gu_odd.reshape(flat), dn_even, dn_odd

    experts0, experts1 = chunked(experts0), chunked(experts1)
    gu, dn = experts0[0].shape[1:], experts0[2].shape[1:]
    units = pairs * n
    dma = pltpu.SemaphoreType.DMA
    sds = jax.ShapeDtypeStruct
    half = max(1, pairs // 2)

    def both(shape):
        return [dma(shape), dma(shape)]

    return pl.pallas_call(
        functools.partial(finish_kernel, n),
        out_shape=(
            sds((rows, width), F32),
            sds(dx0.shape, dx0.dtype),
            sds((gu[0] // 2,) + gu[1:], BF),
            sds((gu[0] // 2,) + gu[1:], BF),
            sds(dn, BF),
        ),
        in_specs=[any_spec()] * 12,
        out_specs=tuple(vmem(1) + [any_spec()] * 4),
        scratch_shapes=[
            pltpu.VMEM((pairs,) + gu, BF),
            pltpu.VMEM((pairs,) + dn, BF),
            pltpu.VMEM((levels, half) + gu, BF),
            pltpu.VMEM((levels, half) + dn, BF),
            pltpu.VMEM((2, units, rows, width), BF),
            pltpu.VMEM((units, rows, width), BF),
            pltpu.VMEM((n - 1, pairs, rows, width), BF),
            pltpu.VMEM((levels, half, rows, width), BF),
            pltpu.VMEM((2, rows, width), BF),
            pltpu.VMEM((2,) + gu[1:], BF),
            pltpu.VMEM((2,) + dn[1:], BF),
            pltpu.VMEM((2,) + gu[1:], BF),
            pltpu.VMEM((2,) + dn[1:], BF),
        ]
        + both((pairs, gu[0]))
        + both((pairs, dn[0]))
        + both((levels, half, gu[0]))
        + both((levels, half, dn[0]))
        + both((2, units))
        + both((units,))
        + both((n - 1, pairs))
        + both((levels, half))
        + [dma((2,))] * 5
        + [dma, dma],
        compiler_params=pltpu.CompilerParams(collective_id=cid, has_side_effects=True, vmem_limit_bytes=VMEM_LIMIT),
    )(dd0, dd1, dx0, dx1, *experts0, *experts1)


def last_kernel(
    experts, dense_ref, dx0_ref, dx1_ref, got_ref, gate_ref, up_ref, down_ref,
    gate_out, up_out, down_out, q_out, k_out, v_out, o_out, router_out, attn_out, moe_out, dx_out,
):
    gate_out[...] = gate_ref[...].astype(F32)
    up_out[...] = up_ref[...].astype(F32)
    down_out[...] = down_ref[...].astype(F32)

    @pl.when(pl.program_id(0) == 0)
    def _():
        s = lax.axis_index("section")
        q_out[...] = dense_ref[:, 0:QW]
        k_out[...] = dense_ref[:, QW : QW + KW]
        v_out[...] = dense_ref[:, QW + KW : QKV]
        o_out[...] = dense_ref[:, QKV : QKV + QW]
        aux_rows = jnp.transpose(dense_ref[:, QKV + QW :])
        for e in range(experts):
            router_out[e] = aux_rows[e : e + 1]
        moe_out[...] = aux_rows[GAIN_MOE_ROW : GAIN_MOE_ROW + 1]
        attn_out[...] = aux_rows[GAIN_ATTN_ROW : GAIN_ATTN_ROW + 1]
        dx_out[s] = jnp.where(s == 0, dx0_ref[...], dx1_ref[...])
        dx_out[1 - s] = got_ref[...].astype(F32)


def last(experts, dense, dx0, dx1, got, gate, up, down):
    sh = dense.shape[0]
    t, d = dx0.shape
    per, piece, f = gate.shape
    sds = jax.ShapeDtypeStruct

    def whole(shape):
        return pl.BlockSpec(shape, lambda j: (0,) * len(shape))

    wide = pl.BlockSpec((1, piece, f), lambda j: (j, 0, 0))
    tall = pl.BlockSpec((1, f, piece), lambda j: (j, 0, 0))
    small = [(sh, QW), (sh, KW), (sh, KW), (sh, QW), (experts, 1, sh), (1, sh), (1, sh), (2, t, d)]
    return pl.pallas_call(
        functools.partial(last_kernel, experts),
        grid=(per,),
        out_shape=tuple(sds(v.shape, F32) for v in (gate, up, down)) + tuple(sds(shape, F32) for shape in small),
        in_specs=[whole(v.shape) for v in (dense, dx0, dx1, got)] + [wide, wide, tall],
        out_specs=tuple([wide, wide, tall] + [whole(shape) for shape in small]),
        compiler_params=pltpu.CompilerParams(vmem_limit_bytes=VMEM_LIMIT),
    )(dense, dx0, dx1, got, gate, up, down)


def low_bit(q):
    return top_bit(q & -q)


def open_kernel(
    n, groups, pieces, wq_ref, wk_ref, wv_ref, wo_ref, wr_ref, ga_ref, gm_ref, cot_ref, rt_ref, w0_out, w1_out, gy_out, rt_out, rt_side,
    w_ref, s_right, r_right, s_left, r_left, s_group, r_group, s_y, r_y, s_cross, r_cross, s_rt, r_rt, s_side, r_side, local_sem,
):
    s, g, z = lax.axis_index("section"), lax.axis_index("group"), lax.axis_index("expert")
    remote = functools.partial(pltpu.make_async_remote_copy, device_id_type=MESH)
    rows = w_ref.shape[0] // pieces
    bits = top_bit(groups)
    other = {"section": 1 - s}
    w_ref[:, 0:QW] = wq_ref[...]
    w_ref[:, QW : QW + KW] = wk_ref[...]
    w_ref[:, QW + KW : QKV] = wv_ref[...]
    w_ref[:, QKV : QKV + QW] = wo_ref[...]
    experts, sh = wr_ref.shape
    gap = jnp.zeros((GAIN_MOE_ROW - experts, sh), F32)
    aux = jnp.concatenate([wr_ref[...].astype(F32), gap, gm_ref[...].astype(F32), ga_ref[...].astype(F32)], axis=0)
    w_ref[:, QKV + QW :] = jnp.transpose(aux).astype(BF)
    barrier = pltpu.get_barrier_semaphore()
    peers = [other] + [{"group": lax.bitwise_xor(g, 1 << b)} for b in range(bits)] + [{"expert": lax.rem(z + k, n)} for k in range(1, n)]
    for peer in peers:
        pl.semaphore_signal(barrier, inc=1, device_id=peer, device_id_type=MESH)
    pl.semaphore_wait(barrier, len(peers))
    sent = []

    def launch(cond, make):
        sent.append((cond, make))
        if cond is None:
            make().start()
        else:

            @pl.when(cond)
            def _():
                make().start()

    def part(q, zz, c):
        if c == 2 * pieces:
            return gy_out.at[s, zz]
        return (w0_out, w1_out)[c // pieces].at[lax.bitwise_xor(g, q) * n + zz, pl.ds(c % pieces * rows, rows)]

    def chain(to, zz, t, c, ssem, rsem):
        return remote(src_ref=part(0, zz, c), dst_ref=part(0, zz, c), send_sem=ssem.at[t, c], recv_sem=rsem.at[t, c], device_id={"expert": to})

    def right(t, c):
        return chain(z + 1, z - t, t, c, s_right, r_right)

    def left(t, c):
        return chain(z - 1, z + t, t, c, s_left, r_left)

    def over(q, b, zz, c):
        at = q | (1 << b)
        return remote(
            src_ref=part(q, zz, c), dst_ref=part(q, zz, c), send_sem=s_group.at[at, zz, c], recv_sem=r_group.at[at, zz, c],
            device_id={"group": lax.bitwise_xor(g, 1 << b)},
        )

    def hop(c, to=w0_out):
        at = pl.ds(c * rows, rows)
        return remote(src_ref=w_ref.at[at], dst_ref=to.at[g * n + z, at], send_sem=s_y.at[c], recv_sem=r_y.at[c], device_id=other)

    def by_layer(action):
        for layer, to in enumerate((w0_out, w1_out)):

            @pl.when(s == layer)
            def _(to=to):
                action(to)

    def cross(zz):
        return remote(src_ref=gy_out.at[0, zz], dst_ref=gy_out.at[0, zz], send_sem=s_cross.at[zz], recv_sem=r_cross.at[zz], device_id=other)

    def route(m, k):
        return remote(
            src_ref=rt_ref.at[m], dst_ref=rt_out.at[m, z], send_sem=s_rt.at[m, k], recv_sem=r_rt.at[m, k],
            device_id={"expert": lax.rem(z + k, n)},
        )

    def side():
        return remote(src_ref=rt_ref.at[1 - s], dst_ref=rt_side, send_sem=s_side, recv_sem=r_side, device_id=other)

    by_layer(lambda to: hop(0, to).start())
    launch(None, side)
    own = [pltpu.make_async_copy(cot_ref.at[s], gy_out.at[s, z], local_sem.at[0])]
    own += [pltpu.make_async_copy(rt_ref.at[m], rt_out.at[m, z], local_sem.at[1 + m]) for m in range(2)]

    def keep(to=w0_out):
        return pltpu.make_async_copy(w_ref, to.at[g * n + z], local_sem.at[3])

    for copy in own:
        copy.start()

    by_layer(lambda to: keep(to).start())
    keep().wait()

    def spread_out(cond, zz, c):
        if c < pieces:
            for b in reversed(range(bits)):
                launch(cond, functools.partial(over, 0, b, zz, c))
        elif c == 2 * pieces:
            launch((s == 0) if cond is None else ((s == 0) & cond), functools.partial(cross, zz))

    def pass_along(t, c):
        if t == 0:
            if c < 2 * pieces:

                @pl.when(s != c // pieces)
                def _():
                    hop(c % pieces).wait_recv()
            else:
                own[0].wait()
            launch(z < n - 1, functools.partial(right, t, c))
            launch(z > 0, functools.partial(left, t, c))
            spread_out(None, z, c)
            if c + 1 < pieces:
                hop(c).wait_send()
                by_layer(lambda to: hop(c + 1, to).start())
        else:
            from_left, from_right = z >= t, z + t < n

            @pl.when(from_left)
            def _():
                right(t - 1, c).wait_recv()

            launch(from_left & (z < n - 1), functools.partial(right, t, c))
            spread_out(from_left, z - t, c)

            @pl.when(from_right)
            def _():
                left(t - 1, c).wait_recv()

            launch(from_right & (z > 0), functools.partial(left, t, c))
            spread_out(from_right, z + t, c)

    def forward(q, k):
        zz = lax.rem(z + k, n)
        for c in range(pieces):
            over(q & (q - 1), low_bit(q), zz, c).wait_recv()
            for b in reversed(range(low_bit(q))):
                launch(None, functools.partial(over, q, b, zz, c))

    for t in range(n):
        for c in range(pieces):
            pass_along(t, c)
        if t == 0:
            for m in range(2):
                for k in range(1, n):
                    launch(None, functools.partial(route, m, k))
    pending = [(q, k) for q in sorted(range(1, groups), key=lambda q: -low_bit(q)) for k in range(n)]
    for t in range(n):
        pass_along(t, 2 * pieces)
        forward(*pending.pop(0))
    for t in range(n):
        for c in range(pieces, 2 * pieces):
            pass_along(t, c)
    for q, k in pending:
        forward(q, k)

    @pl.when(s != 0)
    def _():
        for zz in range(n):
            cross(zz).wait_recv()

    side().wait_recv()
    for m in range(2):
        own[1 + m].wait()
        for k in range(1, n):
            route(m, k).wait_recv()
    hop(pieces - 1).wait_send()
    for cond, make in sent:
        if cond is None:
            make().wait_send()
        else:

            @pl.when(cond)
            def _(make=make):
                make().wait_send()


def open_up(cid, weights, cot, rt):
    n, groups = lax.axis_size("expert"), lax.axis_size("group")
    sh = weights[0].shape[0]
    packed = (sh, QKV + QW + LANES)
    pieces = 3 if sh % 48 == 0 else 1
    dma = pltpu.SemaphoreType.DMA
    sds = jax.ShapeDtypeStruct

    def both(shape):
        return [dma(shape), dma(shape)]

    w0, w1, gy, rt_all, rt_side = pl.pallas_call(
        functools.partial(open_kernel, n, groups, pieces),
        out_shape=(sds((groups * n,) + packed, BF),) * 2 + (sds((2, n) + cot.shape[1:], BF), sds((2, n) + rt.shape[1:], rt.dtype), sds(rt.shape[1:], rt.dtype)),
        in_specs=vmem(9),
        out_specs=tuple([any_spec()] * 5),
        scratch_shapes=[pltpu.VMEM(packed, BF)] + both((n, 2 * pieces + 1)) + both((n, 2 * pieces + 1)) + both((groups, n, pieces)) + both((pieces,)) + both((n,)) + both((2, n)) + [dma, dma] + [dma((4,))],
        compiler_params=pltpu.CompilerParams(collective_id=cid, has_side_effects=True),
    )(*weights, cot, rt)
    return w0.reshape(groups * n * sh, -1), w1, gy, rt_all, rt_side


def swap_sections(value):
    return lax.ppermute(value, "section", [(0, 1), (1, 0)])


def rope_tables(t):
    half = HEAD_SIZE // 2
    frequency = THETA ** (-np.arange(half) * 2.0 / HEAD_SIZE)
    angles = np.arange(t)[:, None] * frequency[None, :]
    reps = LANES // half
    return (jnp.asarray(np.tile(f(angles), (1, reps)).astype(np.float32)) for f in (np.cos, np.sin))


def local(
    inputs, cotangent, segment_ids, live_first, routes, gain_attn, gain_moe,
    w_query, key_weight, value_weight, w_out, w_router, w_gate, w_up, w_down,
):
    s = lax.axis_index("section")
    n = lax.axis_size("expert")
    groups = lax.axis_size("group")
    t, d = inputs.shape[2:]
    top = routes.shape[-1]
    per = w_gate.shape[1]
    experts = per * n
    e_pad = -(-experts // 16) * 16
    cap = t * top * 5 // (4 * experts)
    wg, wu, wd = w_gate[0], w_up[0], w_down[0]
    at_zero = s == 0

    dense_shards = (w_query[0], key_weight[0], value_weight[0], w_out[0].T, w_router[0].T, gain_attn, gain_moe)

    seg, live, cot = segment_ids[:, 0], live_first[:, 0], cotangent[:, 0]
    cos, sin = rope_tables(t)

    rt = jnp.swapaxes(routes[0, :, 0], 1, 2)

    def flat(z):
        return z.reshape((2 * n,) + z.shape[2:])

    def paired(z):
        return z.reshape((2, n) + z.shape[1:])

    first_weights, second_weights, gy1, rt_all, rt_theirs = open_up(1, dense_shards, cot, rt)
    gy1, rt_all = flat(gy1), flat(rt_all)

    qkv0, p0, o0, h0, b0, wrt0, x0 = attn_fwd(inputs[:, 0], (), first_weights, cos, sin, seg, live)
    m0 = moe(0, "fwd", 2, e_pad, cap, b0, wg, wu, wd, rt=rt_all, wrt=wrt0, dense=second_weights)
    second_weights = m0.dense_out.reshape(first_weights.shape)

    qkv1, p1, o1, h1, b1, wrt1, x1 = attn_fwd(h0, m0.back, second_weights, cos, sin, seg, live)
    m1 = moe(1, "both", 3, e_pad, cap, b1, wg, wu, wd, rt=rt_all, wrt=wrt1, gy=gy1)

    dx1, gy0, dqkv1, at1, dht1, daux1 = attn_bwd(1, False, experts, cot, h1, x1, second_weights, qkv1, p1, o1, b1, wrt1, m1.back, m1.dgate, rt, rt_theirs, cos, sin)

    n0 = moe(0, "bwd", 4, e_pad, cap, gy0, wg, wu, wd, pos=m0.pos, gate=m0.gate, gp=m0.gp, up=m0.up, blocks=flat(m0.blocks),
             dqkv=dqkv1, at=at1, dht=dht1, daux=daux1, o=o1, part=m1.part0, part_own=m1.part1)
    dd1 = n0.dd
    dback0 = n0.back
    back1 = lax.all_to_all(n0.part_out, "expert", split_axis=0, concat_axis=0, tiled=True)
    dx0, low0, dd0 = attn_bwd(0, True, experts, gy0, h0, x0, first_weights, qkv0, p0, o0, b0, wrt0, dback0, n0.dgate, rt, rt_theirs, cos, sin)

    dense, got, *sums = finish(5, dd0, dd1, low0, gy0, (n0.even, n0.odd, n0.even_dn, n0.odd_dn), (m1.even, m1.odd, m1.even_dn, m1.odd_dn))
    dense, late = lax.optimization_barrier((dense, h1))
    y1 = (late + jnp.sum(back1.astype(F32), axis=0)).astype(BF)

    kept_out = jnp.where(at_zero, x1, y1)
    swapped_out = swap_sections(jnp.where(at_zero, y1, x1))
    layer_out = jnp.where(at_zero, jnp.stack([kept_out, swapped_out]), jnp.stack([swapped_out, kept_out]))
    gate_grad, up_grad, down_grad, *dense_grads, out_grad, router_grad, attn_grad, moe_grad, input_grad = last(
        experts, dense, dx0, dx1, got, *sums
    )
    return (
        layer_out[None, :, None],
        input_grad[None, :, None],
        attn_grad,
        moe_grad,
        *(v[None] for v in dense_grads),
        out_grad.T[None],
        jnp.transpose(router_grad, (1, 2, 0)),
        gate_grad[None],
        up_grad[None],
        down_grad[None],
    )


def solution(mesh):
    return jax.shard_map(
        local,
        mesh=mesh,
        in_specs=(
            P(None, ("group", "expert"), None, None),
            P(None, ("group", "expert"), None, None),
            P(None, ("group", "expert"), None),
            P(None, ("group", "expert"), None),
            P("section", None, ("group", "expert"), None, None),
            P("section", ("group", "expert")),
            P("section", ("group", "expert")),
            P("section", ("group", "expert"), None),
            P("section", ("group", "expert"), None),
            P("section", ("group", "expert"), None),
            P("section", None, ("group", "expert")),
            P("section", ("group", "expert"), None),
            P("section", "expert", None, None),
            P("section", "expert", None, None),
            P("section", "expert", None, None),
        ),
        out_specs=(
            P("section", None, ("group", "expert"), None, None),
            P("section", None, ("group", "expert"), None, None),
            P("section", ("group", "expert")),
            P("section", ("group", "expert")),
            P("section", ("group", "expert"), None),
            P("section", ("group", "expert"), None),
            P("section", ("group", "expert"), None),
            P("section", None, ("group", "expert")),
            P("section", ("group", "expert"), None),
            P("section", "expert", "group", None),
            P("section", "expert", "group", None),
            P("section", "expert", None, "group"),
        ),
        check_vma=False,
    )
```

```python
import functools
import types

import jax
import jax.numpy as jnp
import numpy as np
from jax import lax
from jax.experimental import pallas as pl
from jax.experimental.pallas import tpu as pltpu
from jax.sharding import PartitionSpec as P

QUERY_HEADS = 24
KEY_VALUE_HEADS = 8
HEAD_SIZE = 64
BLK = 64
EPS = 1e-06
THETA = 10000.0
NEG_FILL = -1e30
BF = jnp.bfloat16
F32 = jnp.float32
MESH = pl.DeviceIdType.MESH
LANES = 128
TILE = 512
QW = QUERY_HEADS * HEAD_SIZE
KW = KEY_VALUE_HEADS * HEAD_SIZE
QKV = QW + 2 * KW
GAIN_MOE_ROW = 126
GAIN_ATTN_ROW = 127
VMEM_LIMIT = 60 * 1024 * 1024
HEAD_PAIRS = KEY_VALUE_HEADS // 2
TILES_PER_PAIR = QUERY_HEADS // KEY_VALUE_HEADS


def dot(a, b, ca=1, cb=0):
    return lax.dot_general(a, b, (((ca,), (cb,)), ((), ())), preferred_element_type=F32)


def iota(shape, axis):
    return lax.broadcasted_iota(jnp.int32, shape, axis)


def rope(z, cos, sin, direction):
    width = z.shape[1]
    half = HEAD_SIZE // 2
    first = iota(z.shape, 1) % HEAD_SIZE < half
    partner = jnp.where(first, pltpu.roll(z, width - half, 1), pltpu.roll(z, half, 1))
    signed = jnp.where(first, -direction, direction) * partner
    reps = width // LANES
    return z * jnp.concatenate([cos] * reps, axis=1) + signed * jnp.concatenate([sin] * reps, axis=1)


def lane_masks(t):
    low = iota((t, LANES), 1) < HEAD_SIZE
    return low, jnp.logical_not(low)


def swapped(z):
    return pltpu.roll(z.astype(F32), HEAD_SIZE, 1).astype(BF)


def head_plan():
    return [(r, half, (2 * r + half) // TILES_PER_PAIR != half) for r in range(TILES_PER_PAIR) for half in range(2)]


def pick(z, half, masks):
    return jnp.where(masks[half], z, jnp.zeros_like(z))


def weight_pieces(d, order):
    aux = [(pl.ds(0, d), pl.ds(QKV + QW, LANES))]
    qkv = [(pl.ds(0, d), pl.ds(n * TILE, TILE)) for n in range(QKV // TILE)]
    out = [(pl.ds(n * TILE, TILE), pl.ds(QKV, QW)) for n in range(d // TILE)]
    down = [(pl.ds(0, d), pl.ds(QKV + n * TILE, TILE)) for n in range(QW // TILE)]
    rows = [(pl.ds(n * TILE, TILE), pl.ds(0, QKV)) for n in range(d // TILE)]
    return aux + qkv + out if order == "forward" else down + rows


def arriving(w_hbm, w_ref, sem, order):
    copies = [
        pltpu.make_async_copy(w_hbm.at[rows, cols], w_ref.at[rows, cols], sem.at[i])
        for i, (rows, cols) in enumerate(weight_pieces(w_ref.shape[0], order))
    ]
    for c in copies:
        c.start()
    return copies


def attn_fwd_kernel(
    blocks, below_ref, *refs,
):
    back_ref = refs[0] if blocks else None
    (
        w_hbm, cos_ref, sin_ref, seg_ref, live_ref,
        qkv_ref, p_ref, o_ref, h_ref, b_ref, wrt_ref, x_ref, w_ref, w_sem,
    ) = refs[1 if blocks else 0 :]
    t, d = x_ref.shape
    pieces = arriving(w_hbm, w_ref, w_sem, "forward")
    mine = lax.axis_index("section")
    entering = (below_ref[mine] if len(below_ref.shape) == 3 else below_ref[...]).astype(F32)
    for z in range(blocks):
        entering = entering + back_ref[z].astype(F32)
    x_ref[...] = entering.astype(BF)
    pieces.pop(0).wait()
    aux = jnp.transpose(w_ref[:, QKV + QW :].astype(F32))
    wrt_ref[...] = aux.astype(BF)
    gain_attn = aux[GAIN_ATTN_ROW : GAIN_ATTN_ROW + 1]
    gain_moe = aux[GAIN_MOE_ROW : GAIN_MOE_ROW + 1]
    x = x_ref[...].astype(F32)
    r1 = lax.rsqrt(jnp.mean(x * x, axis=1, keepdims=True) + EPS)
    a = (x * r1 * gain_attn).astype(BF)
    cos, sin = cos_ref[...], sin_ref[...]
    for n in range(QKV // TILE):
        cols = slice(n * TILE, (n + 1) * TILE)
        pieces.pop(0).wait()
        y = dot(a, w_ref[:, cols])
        if n * TILE < QW + KW:
            y = rope(y, cos, sin, 1.0)
        qkv_ref[:, cols] = y.astype(BF)
    i, j = iota((t, t), 0), iota((t, t), 1)
    segments = jnp.broadcast_to(seg_ref[pl.ds(mine, 1), :].astype(F32), (t, t))
    first_block = jnp.zeros((t, t), jnp.int32)
    for block in range(t // BLK):
        first_block = jnp.where(i // BLK == block, live_ref[mine, block], first_block)
    allowed = (j <= i) & (jnp.transpose(segments) == segments) & (j // BLK >= first_block)
    masks = lane_masks(t)

    def pair(m, carry):
        def lanes(base):
            return pl.ds(pl.multiple_of(base, LANES), LANES)

        kp = qkv_ref[:, lanes(QW + m * LANES)]
        vp = qkv_ref[:, lanes(QW + KW + m * LANES)]
        ks, vs = swapped(kp), swapped(vp)
        plan = head_plan()
        scores = []
        for r, half, swap in plan:
            q = pick(qkv_ref[:, lanes((m * TILES_PER_PAIR + r) * LANES)], half, masks)
            s = dot(q, ks if swap else kp, 1, 1) * HEAD_SIZE ** (-0.5)
            scores.append(jnp.where(allowed, s, NEG_FILL))
        tops = [jnp.max(s, axis=1, keepdims=True) for s in scores]
        exps = [jnp.exp(s - top) for s, top in zip(scores, tops)]
        sums = [1.0 / jnp.sum(e, axis=1, keepdims=True) for e in exps]
        probs = [e * u for e, u in zip(exps, sums)]
        for (r, half, swap), p in zip(plan, probs):
            p_ref[m * 2 * TILES_PER_PAIR + 2 * r + half] = p
        parts = [dot(p.astype(BF), pick(vs if swap else vp, half, masks)) for (r, half, swap), p in zip(plan, probs)]
        for r in range(TILES_PER_PAIR):
            o_ref[:, lanes((m * TILES_PER_PAIR + r) * LANES)] = (parts[2 * r] + parts[2 * r + 1]).astype(BF)
        return carry

    lax.fori_loop(0, HEAD_PAIRS, pair, 0, unroll=True)
    o = o_ref[...]
    for n in range(d // TILE):
        rows = slice(n * TILE, (n + 1) * TILE)
        pieces.pop(0).wait()
        h_ref[:, rows] = x_ref[:, rows].astype(F32) + dot(o, w_ref[rows, QKV : QKV + QW], 1, 1)
    h = h_ref[...]
    r2 = lax.rsqrt(jnp.mean(h * h, axis=1, keepdims=True) + EPS)
    b_ref[...] = (h * r2 * gain_moe).astype(BF)


def vmem(n):
    return [pl.BlockSpec(memory_space=pltpu.VMEM)] * n


def attn_fwd(below, back, w, cos, sin, seg, live):
    t, d = below.shape[-2:]
    sds = jax.ShapeDtypeStruct
    return pl.pallas_call(
        functools.partial(attn_fwd_kernel, len(back)),
        out_shape=(
            sds((t, QKV), BF),
            sds((QUERY_HEADS, t, t), F32),
            sds((t, QW), BF),
            sds((t, d), F32),
            sds((t, d), BF),
            sds((LANES, d), BF),
            sds((t, d), BF),
        ),
        in_specs=vmem(2 if len(back) else 1) + [any_spec()] + vmem(3) + [pl.BlockSpec(memory_space=pltpu.SMEM)],
        out_specs=tuple(vmem(7)),
        scratch_shapes=[pltpu.VMEM(w.shape, BF), pltpu.SemaphoreType.DMA((1 + QKV // TILE + d // TILE,))],
        compiler_params=pltpu.CompilerParams(vmem_limit_bytes=VMEM_LIMIT),
        cost_estimate=pl.CostEstimate(flops=2 * t * d * 4096, bytes_accessed=w.size * 2, transcendentals=QUERY_HEADS * t * t),
    )(below, *((back,) if len(back) else ()), w, cos, sin, seg, live)


def gates_of(rt, wrt, b, e_pad):
    t = rt.shape[1]
    experts = iota((e_pad, t), 0)
    chosen = experts == rt[0:1]
    for k in range(1, rt.shape[0]):
        chosen = chosen | (experts == rt[k : k + 1])
    logits = jnp.where(chosen, dot(wrt[0:e_pad], b, 1, 1), NEG_FILL)
    e = jnp.where(chosen, jnp.exp(logits - jnp.max(logits, axis=0, keepdims=True)), 0.0)
    return e / jnp.sum(e, axis=0, keepdims=True)


def attn_bwd_kernel(
    layer, now, e_pad, e_real, gy_ref, h_ref, x_ref, w_hbm, qkv_ref, p_ref, o_ref, b_ref, wrt_ref, back_ref, dg_ref, rt_ref, side_ref, cos_ref, sin_ref,
    dx_ref, dxb_ref, *rest,
):
    t, d = x_ref.shape
    if now:
        dd_hbm, do_ref, dqkv_ref, dh_ref, w_ref, w_sem, lt_ref, dd_ref, dd_sem = rest
    else:
        dqkv_ref, at_ref, dht_ref, daux_ref, do_ref, dh_ref, w_ref, w_sem = rest
    pieces = arriving(w_hbm, w_ref, w_sem, "backward")
    last_tile = (QKV + QW) // TILE

    def leave(n, width):
        cols = pl.ds(pl.multiple_of(n * TILE, LANES), width)
        return pltpu.make_async_copy(dd_ref.at[:, cols], dd_hbm.at[:, cols], dd_sem.at[n])

    gain_attn = wrt_ref[GAIN_ATTN_ROW - 7 :, :].astype(F32)[7:8]
    gain_moe = wrt_ref[GAIN_ATTN_ROW - 7 :, :].astype(F32)[6:7]
    b = b_ref[...]
    mine = lax.axis_index("section")
    gates = gates_of(jnp.where(mine == layer, rt_ref[mine], side_ref[...]), wrt_ref, b, e_pad)
    per = e_real // dg_ref.shape[0]
    dg = [dg_ref[z][0:per] for z in range(dg_ref.shape[0])]
    if e_pad > e_real:
        dg.append(jnp.zeros((e_pad - e_real, t), F32))
    dg = jnp.concatenate(dg, axis=0)
    dl = (gates * (dg - jnp.sum(gates * dg, axis=0, keepdims=True)))
    dlb = dl.astype(BF)
    db = dot(dlb, wrt_ref[0:e_pad, :], 0, 0)
    for z in range(back_ref.shape[0]):
        db = db + back_ref[z].astype(F32)
    h = h_ref[...]
    r2 = lax.rsqrt(jnp.mean(h * h, axis=1, keepdims=True) + EPS)
    grad_moe = jnp.sum(db * h * r2, axis=0, keepdims=True)
    dn = db * gain_moe
    gy = gy_ref[lax.axis_index("section")] if len(gy_ref.shape) == 3 else gy_ref[...]
    dh = gy.astype(F32) + r2 * dn - h * (r2 * r2 * r2) * jnp.mean(dn * h, axis=1, keepdims=True)
    dh_ref[...] = dh
    dhb = dh.astype(BF)
    for n in range(QW // TILE):
        cols = slice(n * TILE, (n + 1) * TILE)
        pieces.pop(0).wait()
        do_ref[:, cols] = dot(dhb, w_ref[:, QKV + n * TILE : QKV + (n + 1) * TILE]).astype(BF)
    masks = lane_masks(t)
    cos, sin = cos_ref[...], sin_ref[...]

    def pair(m, carry):
        def lanes(base):
            return pl.ds(pl.multiple_of(base, LANES), LANES)

        kp = qkv_ref[:, lanes(QW + m * LANES)]
        vp = qkv_ref[:, lanes(QW + KW + m * LANES)]
        ks, vs = swapped(kp), swapped(vp)
        plan = head_plan()
        tiles = [lanes((m * TILES_PER_PAIR + r) * LANES) for r in range(TILES_PER_PAIR)]
        qs = [pick(qkv_ref[:, tiles[r]], half, masks) for r, half, _ in plan]
        dos = [pick(do_ref[:, tiles[r]], half, masks) for r, half, _ in plan]
        ps = [p_ref[m * 2 * TILES_PER_PAIR + 2 * r + half] for r, half, _ in plan]
        dps = [dot(do, vs if swap else vp, 1, 1) for do, (_, _, swap) in zip(dos, plan)]
        dvs = [dot(p.astype(BF), do, 0, 0) for p, do in zip(ps, dos)]
        sums = [jnp.sum(p * dp, axis=1, keepdims=True) for p, dp in zip(ps, dps)]
        dts = [(p * (dp - total) * HEAD_SIZE ** (-0.5)).astype(BF) for p, dp, total in zip(ps, dps, sums)]
        dks = [dot(dt, q, 0, 0) for dt, q in zip(dts, qs)]
        dqs = [dot(dt, pick(ks if swap else kp, half, masks)) for dt, (_, half, swap) in zip(dts, plan)]
        for r in range(TILES_PER_PAIR):
            dqkv_ref[:, tiles[r]] = rope(dqs[2 * r] + dqs[2 * r + 1], cos, sin, -1.0).astype(BF)
        dk, dv = (
            {way: functools.reduce(jnp.add, [v for v, (_, _, swap) in zip(vals, plan) if swap == way]) for way in (False, True)}
            for vals in (dks, dvs)
        )
        dk_all = dk[False] + pltpu.roll(dk[True], HEAD_SIZE, 1)
        dv_all = dv[False] + pltpu.roll(dv[True], HEAD_SIZE, 1)
        dqkv_ref[:, lanes(QW + m * LANES)] = rope(dk_all, cos, sin, -1.0).astype(BF)
        dqkv_ref[:, lanes(QW + KW + m * LANES)] = dv_all.astype(BF)
        return carry

    lax.fori_loop(0, HEAD_PAIRS, pair, 0, unroll=True)
    x = x_ref[...].astype(F32)
    r1 = lax.rsqrt(jnp.mean(x * x, axis=1, keepdims=True) + EPS)
    dqkv = dqkv_ref[...]
    for n in range(d // TILE):
        rows = slice(n * TILE, (n + 1) * TILE)
        pieces.pop(0).wait()
        dx_ref[:, rows] = dot(dqkv, w_ref[rows, 0:QKV], 1, 1)
    da = dx_ref[...]
    grad_attn = jnp.sum(da * x * r1, axis=0, keepdims=True)
    dag = da * gain_attn
    dx = dh_ref[...] + r1 * dag - x * (r1 * r1 * r1) * jnp.mean(dag * x, axis=1, keepdims=True)
    dx_ref[...] = dx
    dxb_ref[...] = dx.astype(BF)
    row = iota((LANES, d), 0)
    grads = jnp.where(row == GAIN_MOE_ROW, grad_moe, jnp.where(row == GAIN_ATTN_ROW, grad_attn, 0.0))
    dl_full = jnp.concatenate([dl, jnp.zeros((LANES - e_pad, t), F32)], axis=0)
    dl_rows = jnp.transpose(dl_full).astype(BF)
    bt = jnp.transpose(b_ref[...].astype(F32)).astype(BF)
    daux = (dot(bt, dl_rows) + jnp.transpose(grads)).astype(BF)
    if not now:
        at_ref[...] = jnp.transpose(x * r1 * gain_attn).astype(BF)
        dht_ref[...] = jnp.transpose(dh_ref[...]).astype(BF)
        daux_ref[...] = daux
        return
    lt_ref[...] = jnp.transpose(x * r1 * gain_attn).astype(BF)

    @pl.loop(0, QKV // TILE)
    def _(n):
        cols = pl.ds(pl.multiple_of(n * TILE, LANES), TILE)
        dd_ref[:, cols] = dot(lt_ref[...], dqkv_ref[:, cols]).astype(BF)
        leave(n, TILE).start()

    lt_ref[...] = jnp.transpose(dh_ref[...]).astype(BF)

    @pl.loop(0, QW // TILE)
    def _(n):
        cols = pl.ds(pl.multiple_of(n * TILE, LANES), TILE)
        dd_ref[:, pl.ds(pl.multiple_of(QKV + n * TILE, LANES), TILE)] = dot(lt_ref[...], o_ref[:, cols]).astype(BF)
        leave(QKV // TILE + n, TILE).start()

    dd_ref[:, QKV + QW :] = daux
    leave(last_tile, LANES).start()

    @pl.loop(0, last_tile)
    def _(n):
        leave(n, TILE).wait()

    leave(last_tile, LANES).wait()


def attn_bwd(layer, now, experts, gy, h, x, w, qkv, p, o, b, wrt, back, dg, rt, side, cos, sin):
    t, d = x.shape
    sds = jax.ShapeDtypeStruct
    dma = pltpu.SemaphoreType.DMA
    outs = [sds((t, d), F32), sds((t, d), BF)]
    scratch = [pltpu.VMEM((t, QW), BF)]
    if now:
        outs.append(sds(w.shape, BF))
        scratch.append(pltpu.VMEM((t, QKV), BF))
    else:
        outs += [sds((t, QKV), BF), sds((d, t), BF), sds((d, t), BF), sds((d, LANES), BF)]
    scratch += [pltpu.VMEM((t, d), F32), pltpu.VMEM(w.shape, BF), dma((QW // TILE + d // TILE,))]
    if now:
        scratch += [pltpu.VMEM((d, t), BF), pltpu.VMEM(w.shape, BF), dma((1 + QKV // TILE + QW // TILE,))]
    return pl.pallas_call(
        functools.partial(attn_bwd_kernel, layer, now, -(-experts // 16) * 16, experts),
        out_shape=tuple(outs),
        in_specs=vmem(3) + [any_spec()] + vmem(11),
        out_specs=tuple(vmem(2) + [any_spec()] if now else vmem(6)),
        scratch_shapes=scratch,
        compiler_params=pltpu.CompilerParams(vmem_limit_bytes=VMEM_LIMIT),
        cost_estimate=pl.CostEstimate(flops=4 * t * d * 4096, bytes_accessed=w.size * 4, transcendentals=0),
    )(gy, h, x, w, qkv, p, o, b, wrt, back, dg, rt, side, cos, sin)


def one_hot(pos_row, cap):
    return jnp.where(iota((cap, pos_row.shape[1]), 0) == pos_row, 1.0, 0.0)


def all_hots(pos, per, cap):
    return jnp.concatenate([one_hot(pos[j : j + 1], cap) for j in range(per)], axis=0)


def all_hots_back(pos, per, cap):
    width = per * cap
    expert = jnp.where(iota((8, width), 1) // cap == iota((8, width), 0), 1.0, 0.0).astype(BF)
    wide = dot(pos.astype(F32).astype(BF), expert, 0, 0)
    slot = (iota((1, width), 1) % cap).astype(F32)
    return jnp.where(wide == slot, 1.0, 0.0).astype(BF)


def slots_of(rt, first, per):
    t = rt.shape[1]
    experts = iota((16, t), 0)
    mine = jnp.where(experts < per, experts + first, -1)
    chosen = mine == rt[0:1]
    for k in range(1, rt.shape[0]):
        chosen = chosen | (mine == rt[k : k + 1])
    earlier = jnp.where(iota((t, t), 0) < iota((t, t), 1), 1.0, 0.0).astype(BF)
    before = dot(jnp.where(chosen, 1.0, 0.0).astype(BF), earlier)
    return jnp.where(chosen, before.astype(jnp.int32), -1)[0:8]


def streamed(count, copies, body, primed=False):
    if not primed:
        for c in copies(0, 0):
            c.start()

    def step(b, carry):
        slot = lax.rem(b, 2)

        @pl.when(b + 1 < count)
        def _():
            for c in copies(b + 1, lax.rem(b + 1, 2)):
                c.start()

        for c in copies(b, slot):
            c.wait()
        body(b, slot)
        return carry

    lax.fori_loop(0, count, step, 0)


def combine(base, count, per, cap, pos_ref, rows_ref, out_hbm, obuf, osem):
    def copy(b, slot):
        return pltpu.make_async_copy(obuf.at[slot], out_hbm.at[b], osem.at[slot])

    def step(b, carry):
        slot = lax.rem(b, 2)

        @pl.when(b >= 2)
        def _():
            copy(b - 2, slot).wait()

        back = all_hots_back(pos_ref[base + b], per, cap)
        at = pl.ds(pl.multiple_of((base + b) * cap, cap), cap)
        rows = jnp.concatenate([rows_ref[j, at, :] for j in range(per)], axis=0)
        obuf[slot] = dot(back, rows).astype(BF)
        copy(b, slot).start()
        return carry

    lax.fori_loop(0, count, step, 0)
    copy(count - 2, (count - 2) % 2).wait()
    copy(count - 1, (count - 1) % 2).wait()


def chunk_gates(c, j, chunk, cap, pos_ref, gate_ref):
    hots, gates = [], []
    for bb in range(chunk // cap):
        b = c * (chunk // cap) + bb
        hot = one_hot(pos_ref[b, pl.ds(j, 1), :], cap)
        hots.append(hot)
        gates.append(jnp.sum(hot * gate_ref[b, pl.ds(j, 1), :], axis=1, keepdims=True))
    return hots, jnp.concatenate(gates, axis=0)


def any_spec():
    return pl.BlockSpec(memory_space=pl.ANY)


def put_rows(hots, block, b, per, cap, dest):
    at = pl.ds(pl.multiple_of(b * cap, cap), cap)
    rows = dot(hots, block).astype(BF)
    for k in range(per):
        dest[k, at, :] = rows[k * cap : (k + 1) * cap]


def gather_from(count, per, cap, pos, source, dest, buf, sem):
    def body(b, slot):
        put_rows(all_hots(pos[b], per, cap).astype(BF), buf[slot], b, per, cap, dest)

    streamed(count, lambda b, slot: [pltpu.make_async_copy(source.at[b], buf.at[slot], sem.at[slot])], body)


def weight_grads(r, per):
    parts, piece = r.even.shape[0], r.even.shape[3]
    g = lax.axis_index("group")
    parity, place = lax.rem(g, 2), g // 2

    def outgoing(j, at, slot):
        return [
            pltpu.make_async_copy(r.gu_buf.at[slot, 0], r.even.at[at, :, j], r.gu_sem.at[slot, 0]),
            pltpu.make_async_copy(r.gu_buf.at[slot, 1], r.odd.at[at, :, j], r.gu_sem.at[slot, 1]),
            pltpu.make_async_copy(r.dn_buf.at[slot, 0], r.even_dn.at[at, j], r.dn_sem.at[slot, 0]),
            pltpu.make_async_copy(r.dn_buf.at[slot, 1], r.odd_dn.at[at, j], r.dn_sem.at[slot, 1]),
        ]

    def finished(slot):
        for c in outgoing(0, 0, slot):
            c.wait()

    def body(i, carry):
        j, q = i // parts, lax.rem(i, parts)
        slot = lax.rem(i, 2)

        @pl.when(i >= 2)
        def _():
            finished(slot)

        cols = pl.ds(pl.multiple_of(2 * q * piece, LANES), 2 * piece)
        for m in range(2):
            full = dot(r.x_scr[j, :, cols], r.act[m, j], 0, 0).astype(BF)
            r.gu_buf[slot, parity, m] = full[:piece]
            r.gu_buf[slot, 1 - parity, m] = full[piece:]
        full = dot(r.act[2, j], r.y_scr[j, :, cols], 0, 0).astype(BF)
        r.dn_buf[slot, parity] = full[:, :piece]
        r.dn_buf[slot, 1 - parity] = full[:, piece:]
        for c in outgoing(j, lax.bitwise_xor(place, q), slot):
            c.start()
        return carry

    lax.fori_loop(0, per * parts, body, 0)
    for slot in range(2):
        finished(slot)


def meet(n, bits):
    s, g, z = lax.axis_index("section"), lax.axis_index("group"), lax.axis_index("expert")
    barrier = pltpu.get_barrier_semaphore()
    peers = [{"section": 1 - s}] + [{"expert": lax.rem(z + k, n)} for k in range(1, n)]
    peers += [{"group": lax.bitwise_xor(g, 1 << b)} for b in range(bits)]
    for peer in peers:
        pl.semaphore_signal(barrier, inc=1, device_id=peer, device_id_type=MESH)
    pl.semaphore_wait(barrier, len(peers))


def moe_kernel(layer, mode, n, e_pad, cap, names, *refs):
    r = types.SimpleNamespace(**dict(zip(names, refs)))
    forward, backward = mode != "bwd", mode != "fwd"
    s, z = lax.axis_index("section"), lax.axis_index("expert")
    here = s == layer
    count = 2 * n
    per, rows, d = r.y_scr.shape
    first = z * per
    chunk = n * cap
    remote = functools.partial(pltpu.make_async_remote_copy, device_id_type=MESH)
    other = {"section": 1 - s}
    g = lax.axis_index("group")
    riding = forward and not backward
    groups = r.dense_out.shape[0] // n if riding else 1
    bits = top_bit(groups)
    meet(n, bits)
    r.blk[s, z] = r.own[...]

    def over(q, b, zz):
        at = q | (1 << b)
        shard = r.dense_out.at[lax.bitwise_xor(g, q) * n + zz]
        return remote(
            src_ref=shard, dst_ref=shard, send_sem=r.s_over.at[at, zz], recv_sem=r.r_over.at[at, zz],
            device_id={"group": lax.bitwise_xor(g, 1 << b)},
        )

    def ride(bs):
        for b in bs:
            for zz in range(n):
                over(0, b, zz).start()

    def ride_on():
        for q in sorted(range(1, groups), key=lambda q: -low_bit(q)):
            for zz in range(n):
                over(q & (q - 1), low_bit(q), zz).wait_recv()
                for b in reversed(range(low_bit(q))):
                    over(q, b, zz).start()

    if riding:
        ride(reversed(range(1, bits)))

    def half(i):
        section = jnp.where(i < per, layer, 1 - layer)
        return lax.rem(i, per), section, pl.ds(pl.multiple_of(section * chunk, chunk), chunk)

    def weights(i, slot):
        j, _, at = half(i)
        both = [
            pltpu.make_async_copy(r.wg.at[j], r.wg_buf.at[slot], r.w_sem.at[slot, 0]),
            pltpu.make_async_copy(r.wu.at[j], r.wu_buf.at[slot], r.w_sem.at[slot, 1]),
            pltpu.make_async_copy(r.wd.at[j], r.wd_buf.at[slot], r.w_sem.at[slot, 2]),
        ]
        if mode == "bwd":
            both.append(pltpu.make_async_copy(r.gp.at[j, at], r.gp_buf.at[slot], r.gp_sem.at[slot, 0]))
            both.append(pltpu.make_async_copy(r.up.at[j, at], r.gp_buf.at[2 + slot], r.gp_sem.at[slot, 1]))
        return both

    def chain(to, zz, t, ssem, rsem):
        return remote(
            src_ref=r.blk.at[s, zz], dst_ref=r.blk.at[s, zz], send_sem=ssem.at[t], recv_sem=rsem.at[t], device_id={"expert": to}
        )

    def right(t):
        return chain(z + 1, z - t, t, r.s_right, r.r_right)

    def left(t):
        return chain(z - 1, z + t, t, r.s_left, r.r_left)

    def cross(zz):
        return remote(
            src_ref=r.blk.at[s, zz], dst_ref=r.blk.at[s, zz], send_sem=r.s_cross.at[zz], recv_sem=r.r_cross.at[zz], device_id=other
        )

    def prepare(section, zz):
        b = section * n + zz
        block = r.blk[section, zz]
        if forward:
            rt = r.rt[b]
            pos = slots_of(rt, first, per)
            r.pos[b] = pos
            r.gates[...] = gates_of(rt, r.wrt, block, e_pad)
            r.gate[b] = jnp.concatenate(
                [r.gates[pl.ds(first + k, 1), :] for k in range(per)] + [jnp.zeros((8 - per, rt.shape[1]), F32)], axis=0
            )
            put_rows(all_hots(pos, per, cap).astype(BF), block, b, per, cap, r.x_scr)
        else:
            put_rows(all_hots(r.pos[b], per, cap).astype(BF), block, b, per, cap, r.y_scr)

    @pl.when(here)
    def _():
        for c in weights(0, 0):
            c.start()

    def prepare_at(section, t):
        def candidate(m, carry):
            zz = jnp.where(m == 0, z - t, z + t)

            @pl.when((zz >= 0) & (zz < n) & ((m == 0) | (t > 0)))
            def _():
                prepare(section, zz)

            return carry

        lax.fori_loop(0, 2, candidate, 0)

    tiles = (("at", "dqkv", 0, QW), ("at", "dqkv", QW, 2 * KW), ("dht", "o", QKV, QW))

    def dense_copy(block, m):
        _, _, col, width = tiles[m]
        at = pl.ds(pl.multiple_of(block * rows, rows), rows)
        return pltpu.make_async_copy(
            r.x_scr.at[m, :, pl.ds(0, width)], r.dd.at[at, pl.ds(col, width)], r.dd_sem.at[m]
        )

    def aux_copy():
        return pltpu.make_async_copy(r.daux, r.dd.at[:, pl.ds(QKV + QW, LANES)], r.daux_sem)

    def dense_start(block):
        @pl.when(block == 0)
        def _():
            aux_copy().start()

        at = pl.ds(pl.multiple_of(block * rows, rows), rows)
        for m, (left, right, col, width) in enumerate(tiles):

            @pl.when(block > 0)
            def _():
                dense_copy(block - 1, m).wait()

            source = getattr(r, right)
            source = source[:, col : col + width] if right == "dqkv" else source[...]
            r.x_scr[m, :, 0:width] = dot(getattr(r, left)[at, :], source).astype(BF)
            dense_copy(block, m).start()

    def dense_wait():
        aux_copy().wait()
        for m in range(len(tiles)):
            dense_copy(d // rows - 1, m).wait()

    @pl.loop(0, n)
    def _(t):
        from_left = z >= t
        from_right = z + t < n

        @pl.when(from_left & (t > 0))
        def _():
            right(t - 1).wait_recv()

        @pl.when(from_left & (z < n - 1))
        def _():
            right(t).start()

        @pl.when(from_left & jnp.logical_not(here))
        def _():
            cross(z - t).start()

        @pl.when(from_right & (t > 0))
        def _():
            left(t - 1).wait_recv()

        @pl.when(from_right & (z > 0))
        def _():
            left(t).start()

        @pl.when(from_right & (t > 0) & jnp.logical_not(here))
        def _():
            cross(z + t).start()

        if mode == "bwd":

            @pl.when(t < d // rows)
            def _():
                dense_start(t)

        @pl.when(here)
        def _():
            if mode == "both":

                @pl.when(t == 0)
                def _():
                    @pl.loop(0, count)
                    def _(b):
                        r.pos[b] = slots_of(r.rt[b], first, per)

                    gather_from(count, per, cap, r.pos, r.gy, r.y_scr, r.row_buf, r.row_sem)

            prepare_at(layer, t)

            @pl.when(t == min(2, n - 1))
            def _():
                cross(z).wait_recv()
                prepare(1 - layer, z)

    def late_blocks():
        @pl.loop(1, n)
        def _(t):
            @pl.when(z >= t)
            def _():
                cross(z - t).wait_recv()

            @pl.when(z + t < n)
            def _():
                cross(z + t).wait_recv()

            prepare_at(1 - layer, t)

    if riding:
        ride((0,))

    def over_part(zz):
        return remote(
            src_ref=r.part.at[zz], dst_ref=r.part_out.at[zz], send_sem=r.s_part.at[zz], recv_sem=r.r_part.at[zz], device_id=other
        )

    if mode == "bwd":
        dense_wait()

        @pl.when(jnp.logical_not(here))
        def _():
            for zz in range(n):
                over_part(zz).start()
            pltpu.make_async_copy(r.part_own, r.pbuf.at[layer], r.part_sem.at[0]).start()

    def part_home():
        return pltpu.make_async_copy(r.pbuf.at[layer], r.part_out, r.part_sem.at[1])

    srcs = (r.pbuf, r.dg) if backward else (r.pbuf,)
    outs = (r.back, r.dgate) if backward else (r.back,)
    relays = (r.relay, r.dg_relay) if backward else (r.relay,)
    arrays = range(len(srcs))

    def hop(a, to):
        return remote(
            src_ref=srcs[a].at[1 - layer, to],
            dst_ref=relays[a].at[to],
            send_sem=r.s_hop.at[a, to],
            recv_sem=r.r_hop.at[a, to],
            device_id=other,
        )

    def give(a, source, k):
        return remote(
            src_ref=source,
            dst_ref=outs[a].at[z],
            send_sem=r.s_give.at[a, k],
            recv_sem=r.r_give.at[a, k],
            device_id={"expert": lax.rem(z + k, n)},
        )

    def keep(a, source):
        return pltpu.make_async_copy(source, outs[a].at[z], r.keep_sem.at[a])

    def saved(i, slot):
        j, _, at = half(i)
        return [
            pltpu.make_async_copy(r.gp_buf.at[slot], r.gp.at[j, at], r.gp_sem.at[slot, 0]),
            pltpu.make_async_copy(r.gp_buf.at[2 + slot], r.up.at[j, at], r.gp_sem.at[slot, 1]),
        ]

    def expert(i, slot):
        j, section, at = half(i)

        @pl.when(i == per)
        def _():
            late_blocks()

        if mode == "fwd":

            @pl.when(i >= 2)
            def _():
                for c in saved(i - 2, slot):
                    c.wait()

        if forward:
            x = r.x_scr[j, at, :]
            gp = dot(x, r.wg_buf[slot])
            up = dot(x, r.wu_buf[slot])
        else:
            gp, up = r.gp_buf[slot].astype(F32), r.gp_buf[2 + slot].astype(F32)
        sg = 1.0 / (1.0 + jnp.exp(-gp))
        silu = gp * sg
        hid = silu * up
        hots, gate = chunk_gates(section, j, chunk, cap, r.pos, r.gate)
        if not backward:
            r.gp_buf[slot] = gp.astype(BF)
            r.gp_buf[2 + slot] = up.astype(BF)
            r.y_scr[j, at, :] = (dot(hid.astype(BF), r.wd_buf[slot]) * gate).astype(BF)
            for c in saved(i, slot):
                c.start()
            return
        raw = dot(r.y_scr[j, at, :], r.wd_buf[slot], 1, 1)
        dgate = jnp.sum(hid.astype(BF).astype(F32) * raw, axis=1, keepdims=True)
        for bb in range(n):
            r.dg[section, bb, pl.ds(j, 1), :] = jnp.sum(hots[bb] * dgate[bb * cap : (bb + 1) * cap], axis=0, keepdims=True)
        dh = raw * gate
        dgp = (dh * up * sg * (1.0 + gp * (1.0 - sg))).astype(BF)
        dup = (dh * silu).astype(BF)
        r.act[0, j, at, :] = dgp
        r.act[1, j, at, :] = dup
        r.act[2, j, at, :] = (hid * gate).astype(BF)
        r.y_scr[j, at, :] = (dot(dgp, r.wg_buf[slot], 1, 1) + dot(dup, r.wu_buf[slot], 1, 1)).astype(BF)

    def summed(b, source):
        at = pl.ds(pl.multiple_of(b * cap, cap), cap)
        stacked = jnp.concatenate([source[j, at, :] for j in range(per)], axis=0)
        return dot(all_hots_back(r.pos[b], per, cap), stacked).astype(BF)

    @pl.when(here)
    def _():
        if backward:
            r.dg[...] = jnp.zeros_like(r.dg)
        if mode == "fwd":
            keep_blocks = pltpu.make_async_copy(r.blk, r.blocks, r.row_sem.at[0])
        streamed(2 * per, weights, expert, primed=True)
        if mode == "fwd":
            keep_blocks.start()

        def emit(i, carry):
            to = lax.rem(z + i + 1, n)
            section = jnp.where(i < n, 1 - layer, layer)
            r.pbuf[section, to] = summed(section * n + to, r.y_scr)

            @pl.when(i < n)
            def _():
                for a in arrays:
                    hop(a, to).start()

            @pl.when((i >= n) & (to != z))
            def _():
                for a in arrays:
                    give(a, srcs[a].at[layer, to], i + 1 - n).start()

            return carry

        lax.fori_loop(0, 2 * n, emit, 0)
        for a in arrays:
            keep(a, srcs[a].at[layer, z]).start()
        if mode == "fwd":
            for i in (2 * per - 2, 2 * per - 1):
                for c in saved(i, i % 2):
                    c.wait()
            keep_blocks.wait()
        if mode == "bwd":

            @pl.loop(0, count)
            def _(b):
                put_rows(all_hots(r.pos[b], per, cap).astype(BF), r.blk[b // n, lax.rem(b, n)], b, per, cap, r.y_scr)

            gather_from(count, per, cap, r.pos, r.blocks, r.x_scr, r.row_buf, r.row_sem)
        if mode == "both":
            gather_from(count, per, cap, r.pos, r.gy, r.y_scr, r.row_buf, r.row_sem)
        if backward:
            weight_grads(r, per)
        if mode == "both":
            def output(j, slot):
                @pl.loop(0, 2)
                def _(c):
                    at = pl.ds(pl.multiple_of(c * chunk, chunk), chunk)
                    r.x_scr[j, at, :] = dot(r.act[2, j, at, :], r.wd_buf[slot]).astype(BF)

            streamed(per, lambda j, slot: weights(j, slot)[2:], output)
            combine(0, n, per, cap, r.pos, r.x_scr, r.part0, r.row_buf, r.row_sem)
            combine(n, n, per, cap, r.pos, r.x_scr, r.part1, r.row_buf, r.row_sem)
        for to in range(n):
            for a in arrays:
                hop(a, to).wait_send()

    @pl.when(jnp.logical_not(here))
    def _():
        @pl.loop(1, n + 1)
        def _(k):
            to = lax.rem(lax.rem(k, n) + z, n)
            for a in arrays:
                hop(a, to).wait_recv()

            @pl.when(k < n)
            def _():
                for a in arrays:
                    give(a, relays[a].at[to], k).start()

        for a in arrays:
            keep(a, relays[a].at[z]).start()
        for zz in range(n):
            cross(zz).wait_send()

    if mode == "bwd":

        @pl.when(here)
        def _():
            for zz in range(n):
                over_part(zz).wait_recv()

        @pl.when(jnp.logical_not(here))
        def _():
            pltpu.make_async_copy(r.part_own, r.pbuf.at[layer], r.part_sem.at[0]).wait()
            part_home().start()
            part_home().wait()
            for zz in range(n):
                over_part(zz).wait_send()

    if riding:
        ride_on()
        for q in range(1, groups):
            for zz in range(n):
                over(q & (q - 1), low_bit(q), zz).wait_send()
    for a in arrays:
        keep(a, relays[a].at[z]).wait()
        for k in range(1, n):
            give(a, relays[a].at[lax.rem(z + k, n)], k).wait()
    for t in range(n):

        @pl.when((z >= t) & (z < n - 1))
        def _():
            right(t).wait_send()

        @pl.when((z + t < n) & (z > 0))
        def _():
            left(t).wait_send()


def moe(layer, mode, cid, e_pad, cap, own, wg, wu, wd, **given):
    n, groups = lax.axis_size("expert"), lax.axis_size("group")
    count = 2 * n
    t, d = own.shape
    per, _, f = wg.shape
    rows = count * cap
    piece = d // groups
    sds = jax.ShapeDtypeStruct
    dma = pltpu.SemaphoreType.DMA
    vm, hbm = pl.BlockSpec(memory_space=pltpu.VMEM), any_spec()
    on_chip = ("own", "rt", "wrt", "pos", "gate", "dqkv", "at", "dht", "daux", "o")
    ins = dict(own=own, wg=wg, wu=wu, wd=wd, **given)
    outs = dict(back=sds((n, t, d), BF))
    scratch = dict(
        blk=pltpu.VMEM((2, n, t, d), BF),
        y_scr=pltpu.VMEM((per, rows, d), BF),
        wg_buf=pltpu.VMEM((2, d, f), BF),
        wu_buf=pltpu.VMEM((2, d, f), BF),
        wd_buf=pltpu.VMEM((2, f, d), BF),
        pbuf=pltpu.VMEM((2, n, t, d), BF),
        relay=pltpu.VMEM((n, t, d), BF),
        x_scr=pltpu.VMEM((per, rows, d), BF),
        row_buf=pltpu.VMEM((2, t, d), BF),
        row_sem=dma((2,)),
        w_sem=dma((2, 3)),
        keep_sem=dma((2,)),
    )
    for name in ("right", "left", "cross"):
        scratch["s_" + name] = dma((n,))
        scratch["r_" + name] = dma((n,))
    for name in ("hop", "give"):
        scratch["s_" + name] = dma((2, n))
        scratch["r_" + name] = dma((2, n))
    if mode != "both":
        scratch["gp_buf"] = pltpu.VMEM((4, n * cap, f), BF)
        scratch["gp_sem"] = dma((2, 2))
    if mode != "bwd":
        scratch["gates"] = pltpu.VMEM((e_pad, t), F32)
    if mode == "fwd":
        del scratch["row_buf"]
        outs.update(pos=sds((count, 8, t), jnp.int32), gate=sds((count, 8, t), F32))
        outs.update(gp=sds((per, rows, f), BF), up=sds((per, rows, f), BF), blocks=sds((2, n, t, d), BF))
        outs["dense_out"] = sds(given["dense"].shape, BF)
        scratch.update(s_over=dma((groups, n)), r_over=dma((groups, n)))
    else:
        outs["dgate"] = sds((n, 8, t), F32)
        outs["even"] = outs["odd"] = sds((groups // 2, 2, per, piece, f), BF)
        outs["even_dn"] = outs["odd_dn"] = sds((groups // 2, per, f, piece), BF)
        scratch.update(
            dg=pltpu.VMEM((2, n, 8, t), F32),
            dg_relay=pltpu.VMEM((n, 8, t), F32),
            act=pltpu.VMEM((3, per, rows, f), BF),
            gu_buf=pltpu.VMEM((2, 2, 2, piece, f), BF),
            dn_buf=pltpu.VMEM((2, 2, f, piece), BF),
            gu_sem=dma((2, 2)),
            dn_sem=dma((2, 2)),
        )
    if mode == "bwd":
        outs["dd"] = sds((d, QKV + QW + LANES), BF)
        outs["part_out"] = sds((n, t, d), BF)
        scratch.update(s_part=dma((n,)), r_part=dma((n,)), part_sem=dma((2,)))
        scratch.update(dd_sem=dma((3,)), daux_sem=dma)
    if mode == "both":
        outs["part0"] = outs["part1"] = sds((n, t, d), BF)
        scratch.update(pos=pltpu.VMEM((count, 8, t), jnp.int32), gate=pltpu.VMEM((count, 8, t), F32))
    names = tuple(ins) + tuple(outs) + tuple(scratch)
    results = pl.pallas_call(
        functools.partial(moe_kernel, layer, mode, n, e_pad, cap, names),
        out_shape=tuple(outs.values()),
        in_specs=[vm if name in on_chip else hbm for name in ins],
        out_specs=tuple(vm if name in on_chip else hbm for name in outs),
        scratch_shapes=list(scratch.values()),
        input_output_aliases={list(ins).index("dense"): list(outs).index("dense_out")} if mode == "fwd" else {},
        compiler_params=pltpu.CompilerParams(collective_id=cid, has_side_effects=True, vmem_limit_bytes=VMEM_LIMIT),
    )(*ins.values())
    return types.SimpleNamespace(**dict(zip(outs, results)))


def top_bit(q):
    return q.bit_length() - 1


def finish_kernel(
    n, dd0, dd1, dx0, dx1, egu0, ogu0, ed0, od0, egu1, ogu1, ed1, od1,
    dense_out, dx_out, gate_out, up_out, down_out,
    core_gu, core_dn, hop_gu, hop_dn, core_dd, hop_y, hop_z, hop_x, dd_buf, gu_buf, dn_buf, gu_res, dn_res,
    s_core_gu, r_core_gu, s_core_dn, r_core_dn, s_hop_gu, r_hop_gu, s_hop_dn, r_hop_dn,
    s_core_dd, r_core_dd, s_y, r_y, s_z, r_z, s_x, r_x, l_dd, l_gu, l_dn, o_gu, o_dn, s_dx, r_dx,
):
    s, g, z = lax.axis_index("section"), lax.axis_index("group"), lax.axis_index("expert")
    pairs, cgu = core_gu.shape[:2]
    cdn = core_dn.shape[1]
    levels = top_bit(pairs)
    units = pairs * n
    remote = functools.partial(pltpu.make_async_remote_copy, device_id_type=MESH)
    twin = {"group": lax.bitwise_xor(g, 1)}
    other = {"section": 1 - s}

    def across(k):
        return {"group": lax.bitwise_xor(g, 2 << k)}

    barrier = pltpu.get_barrier_semaphore()
    peers = [twin, other] + [across(k) for k in range(levels)] + [{"expert": lax.rem(z + k, n)} for k in range(1, n)]
    for peer in peers:
        pl.semaphore_signal(barrier, inc=1, device_id=peer, device_id_type=MESH)
    pl.semaphore_wait(barrier, len(peers))

    def by_section(action):
        @pl.when(s == 0)
        def _():
            action(dd0, dd1, egu0, ogu0, ed0, od0)

        @pl.when(s != 0)
        def _():
            action(dd1, dd0, egu1, ogu1, ed1, od1)

    def unit(i):
        return pairs - 1 - i // n, lax.rem(z + 1 + lax.rem(i, n), n)

    def shard(i, core):
        q, place = unit(i)
        return (lax.bitwise_xor(g // 2, q) * 2 + core) * n + place

    core = lax.rem(g, 2)

    def core_dd_copy(kind, i, source):
        return remote(
            src_ref=source.at[shard(i, 1 - core)],
            dst_ref=core_dd.at[kind, i],
            send_sem=s_core_dd.at[kind, i],
            recv_sem=r_core_dd.at[kind, i],
            device_id=twin,
        )

    def core_chunk(source, dest, ssem, rsem, q, c):
        return remote(
            src_ref=source.at[q, c], dst_ref=dest.at[q, c], send_sem=ssem.at[q, c], recv_sem=rsem.at[q, c], device_id=twin
        )

    def core_gu_copy(source, q, c):
        return core_chunk(source, core_gu, s_core_gu, r_core_gu, q, c)

    def core_dn_copy(source, q, c):
        return core_chunk(source, core_dn, s_core_dn, r_core_dn, q, c)

    def send_first(own, away, egu, ogu, ed, od):
        @pl.loop(0, units)
        def _(i):
            core_dd_copy(0, i, away).start()

            @pl.when(i < cgu)
            def _():
                core_gu_copy(ogu, pairs - 1, i).start()

            @pl.when(i < cdn)
            def _():
                core_dn_copy(od, pairs - 1, i).start()

        for i in range(units, max(cgu, cdn)):
            if i < cgu:
                core_gu_copy(ogu, pairs - 1, i).start()
            if i < cdn:
                core_dn_copy(od, pairs - 1, i).start()

    def send_rest(own, away, egu, ogu, ed, od):
        @pl.loop(0, units)
        def _(i):
            core_dd_copy(1, i, own).start()

        for q in reversed(range(pairs - 1)):

            @pl.loop(0, cgu)
            def _(c):
                core_gu_copy(ogu, q, c).start()

            @pl.loop(0, cdn)
            def _(c):
                core_dn_copy(od, q, c).start()

    by_section(send_first)

    def dx_copy(source):
        return remote(src_ref=source, dst_ref=dx_out, send_sem=s_dx, recv_sem=r_dx, device_id=other)

    def load(buf, sem, slot, source):
        return pltpu.make_async_copy(source, buf.at[slot], sem.at[slot])

    def dd_load(i, slot, source):
        return load(dd_buf, l_dd, slot, source.at[shard(i, core)])

    def hop(dest, ssem, rsem, source, k, q, c):
        return remote(
            src_ref=source.at[q, c],
            dst_ref=dest.at[k, q - (1 << k), c],
            send_sem=ssem.at[k, q - (1 << k), c],
            recv_sem=rsem.at[k, q - (1 << k), c],
            device_id=across(k),
        )

    def gu_hop(k, q, c):
        return hop(hop_gu, s_hop_gu, r_hop_gu, core_gu, k, q, c)

    def dn_hop(k, q, c):
        return hop(hop_dn, s_hop_dn, r_hop_dn, core_dn, k, q, c)

    def y_copy(i):
        return remote(src_ref=core_dd.at[0, i], dst_ref=hop_y.at[i], send_sem=s_y.at[i], recv_sem=r_y.at[i], device_id=other)

    def z_copy(q, k, i):
        return remote(
            src_ref=core_dd.at[1, i],
            dst_ref=hop_z.at[k - 1, q],
            send_sem=s_z.at[k - 1, q],
            recv_sem=r_z.at[k - 1, q],
            device_id={"expert": lax.rem(z + k, n)},
        )

    def x_copy(k, q, i):
        return remote(
            src_ref=core_dd.at[1, i],
            dst_ref=hop_x.at[k, q - (1 << k)],
            send_sem=s_x.at[k, q - (1 << k)],
            recv_sem=r_x.at[k, q - (1 << k)],
            device_id=across(k),
        )

    def chunk_start(i, slot, q, egu, ed):
        @pl.when(i < cgu)
        def _():
            load(gu_buf, l_gu, slot, egu.at[q, i]).start()

        @pl.when(i < cdn)
        def _():
            load(dn_buf, l_dn, slot, ed.at[q, i]).start()

    def expert_sum(hops, rsem, dest, core_r, buf, sem, slot, even, q, c, hop_copy):
        load(buf, sem, slot, even.at[q, c]).wait()
        core_r(q, c).wait_recv()
        total = buf[slot].astype(F32) + dest[q, c].astype(F32)
        for k in range(top_bit(q) + 1 if q else 0, levels):
            hop_copy(k, q + (1 << k), c).wait_recv()
            total = total + hops[k, q, c].astype(F32)
        return total

    def gu_sum(slot, q, c):
        return expert_sum(hop_gu, r_hop_gu, core_gu, functools.partial(core_gu_copy, ogu0), gu_buf, l_gu, slot, egu0, q, c, gu_hop)

    def dn_sum(slot, q, c):
        return expert_sum(hop_dn, r_hop_dn, core_dn, functools.partial(core_dn_copy, od0), dn_buf, l_dn, slot, ed0, q, c, dn_hop)

    def stepped(count, start, body):
        start(0, 0)

        def step(i, carry):
            @pl.when(i + 1 < count)
            def _():
                start(i + 1, lax.rem(i + 1, 2))

            body(i, lax.rem(i, 2))
            return carry

        lax.fori_loop(0, count, step, 0)

    for q in reversed(range(1, pairs)):
        dense_too = q == pairs - 1
        if not dense_too and q == pairs - 2:
            by_section(send_rest)
        steps = max(units, cgu, cdn) if dense_too else max(cgu, cdn)

        def start(i, slot):
            def go(own, away, egu, ogu, ed, od):
                if dense_too:

                    @pl.when(i < units)
                    def _():
                        dd_load(i, slot, away).start()

                chunk_start(i, slot, q, egu, ed)

            by_section(go)

        def body(i, slot):
            if dense_too:

                @pl.when(i < units)
                def _():
                    dd_load(i, slot, dd0).wait()
                    core_dd_copy(0, i, dd0).wait_recv()
                    core_dd[0, i] = core_dd[0, i] + dd_buf[slot]
                    y_copy(i).start()

            @pl.when(i < cgu)
            def _():
                core_gu[q, i] = gu_sum(slot, q, i).astype(BF)
                gu_hop(top_bit(q), q, i).start()

            @pl.when(i < cdn)
            def _():
                core_dn[q, i] = dn_sum(slot, q, i).astype(BF)
                dn_hop(top_bit(q), q, i).start()

        stepped(steps, start, body)

    if pairs == 2:
        by_section(send_rest)

    @pl.when(s == 0)
    def _():
        dx_copy(dx1).start()

    @pl.when(s != 0)
    def _():
        dx_copy(dx0).start()

    def gu_out_copy(c, slot, to=gate_out):
        return pltpu.make_async_copy(gu_res.at[slot], to.at[lax.rem(c, cgu // 2)], o_gu.at[slot])

    def dn_out_copy(c, slot):
        return pltpu.make_async_copy(dn_res.at[slot], down_out.at[c], o_dn.at[slot])

    def dense_sum(q):
        i = (pairs - 1 - q) * n + n - 1
        total = core_dd[1, i].astype(F32)
        for k in range(1, n):
            z_copy(q, k, i).wait_recv()
            total = total + hop_z[k - 1, q].astype(F32)
        for k in range(top_bit(q) + 1 if q else 0, levels):
            x_copy(k, q + (1 << k), i).wait_recv()
            total = total + hop_x[k, q].astype(F32)
        return i, total

    def pass_on(q):
        i, total = dense_sum(q)
        core_dd[1, i] = total.astype(BF)
        x_copy(top_bit(q), q, i).start()

    def core_sent():
        @pl.loop(0, units)
        def _(i):
            core_dd_copy(0, i, dd0).wait_send()
            core_dd_copy(1, i, dd0).wait_send()

        for q in range(pairs):

            @pl.loop(0, cgu)
            def _(c):
                core_gu_copy(ogu0, q, c).wait_send()

            @pl.loop(0, cdn)
            def _(c):
                core_dn_copy(od0, q, c).wait_send()

    steps = max(units, cgu, cdn)

    def start(i, slot):
        def go(own, away, egu, ogu, ed, od):
            @pl.when(i < units)
            def _():
                dd_load(i, slot, own).start()

            chunk_start(i, slot, 0, egu, ed)

        by_section(go)

    def body(i, slot):
        @pl.when(i < units)
        def _():
            dd_load(i, slot, dd0).wait()
            core_dd_copy(1, i, dd0).wait_recv()
            y_copy(i).wait_recv()
            core_dd[1, i] = (core_dd[1, i].astype(F32) + dd_buf[slot].astype(F32) + hop_y[i].astype(F32)).astype(BF)
            q, _ = unit(i)
            k = lax.rem(i, n) + 1

            @pl.when(k < n)
            def _():
                z_copy(q, k, i).start()

        for q in range(1, pairs):

            @pl.when(i == (pairs - q) * n + min(2, n - 1))
            def _():
                pass_on(q)

        @pl.when(i == units - 2)
        def _():
            core_sent()

        @pl.when(i < cgu)
        def _():
            @pl.when(i >= 2)
            def _():
                gu_out_copy(i - 2, slot).wait()

            gu_res[slot] = gu_sum(slot, 0, i).astype(BF)

            @pl.when(i < cgu // 2)
            def _():
                gu_out_copy(i, slot).start()

            @pl.when(i >= cgu // 2)
            def _():
                gu_out_copy(i, slot, up_out).start()

        @pl.when(i < cdn)
        def _():
            @pl.when(i >= 2)
            def _():
                dn_out_copy(i - 2, slot).wait()

            dn_res[slot] = dn_sum(slot, 0, i).astype(BF)
            dn_out_copy(i, slot).start()

    stepped(steps, start, body)
    _, total = dense_sum(0)
    dense_out[...] = total
    for c in (cgu - 2, cgu - 1):
        gu_out_copy(c, c % 2).wait()
    for c in (cdn - 2, cdn - 1):
        dn_out_copy(c, c % 2).wait()

    dx_copy(dx0).wait()

    @pl.loop(0, units)
    def _(i):
        y_copy(i).wait_send()
        q, _ = unit(i)
        k = lax.rem(i, n) + 1

        @pl.when(k < n)
        def _():
            z_copy(q, k, i).wait_send()

    for q in range(1, pairs):
        x_copy(top_bit(q), q, (pairs - 1 - q) * n + n - 1).wait_send()

        @pl.loop(0, cgu)
        def _(c):
            gu_hop(top_bit(q), q, c).wait_send()

        @pl.loop(0, cdn)
        def _(c):
            dn_hop(top_bit(q), q, c).wait_send()


def finish(cid, dd0, dd1, dx0, dx1, experts0, experts1):
    n, groups = lax.axis_size("expert"), lax.axis_size("group")
    pairs, levels = groups // 2, top_bit(groups // 2)
    width = dd0.shape[1]
    rows = dd0.shape[0] // (groups * n)
    dd0, dd1 = (v.reshape(groups * n, rows, width) for v in (dd0, dd1))

    def chunked(arrays):
        gu_even, gu_odd, dn_even, dn_odd = arrays
        flat = (pairs, -1) + gu_even.shape[3:]
        return gu_even.reshape(flat), gu_odd.reshape(flat), dn_even, dn_odd

    experts0, experts1 = chunked(experts0), chunked(experts1)
    gu, dn = experts0[0].shape[1:], experts0[2].shape[1:]
    units = pairs * n
    dma = pltpu.SemaphoreType.DMA
    sds = jax.ShapeDtypeStruct
    half = max(1, pairs // 2)

    def both(shape):
        return [dma(shape), dma(shape)]

    return pl.pallas_call(
        functools.partial(finish_kernel, n),
        out_shape=(
            sds((rows, width), F32),
            sds(dx0.shape, dx0.dtype),
            sds((gu[0] // 2,) + gu[1:], BF),
            sds((gu[0] // 2,) + gu[1:], BF),
            sds(dn, BF),
        ),
        in_specs=[any_spec()] * 12,
        out_specs=tuple(vmem(1) + [any_spec()] * 4),
        scratch_shapes=[
            pltpu.VMEM((pairs,) + gu, BF),
            pltpu.VMEM((pairs,) + dn, BF),
            pltpu.VMEM((levels, half) + gu, BF),
            pltpu.VMEM((levels, half) + dn, BF),
            pltpu.VMEM((2, units, rows, width), BF),
            pltpu.VMEM((units, rows, width), BF),
            pltpu.VMEM((n - 1, pairs, rows, width), BF),
            pltpu.VMEM((levels, half, rows, width), BF),
            pltpu.VMEM((2, rows, width), BF),
            pltpu.VMEM((2,) + gu[1:], BF),
            pltpu.VMEM((2,) + dn[1:], BF),
            pltpu.VMEM((2,) + gu[1:], BF),
            pltpu.VMEM((2,) + dn[1:], BF),
        ]
        + both((pairs, gu[0]))
        + both((pairs, dn[0]))
        + both((levels, half, gu[0]))
        + both((levels, half, dn[0]))
        + both((2, units))
        + both((units,))
        + both((n - 1, pairs))
        + both((levels, half))
        + [dma((2,))] * 5
        + [dma, dma],
        compiler_params=pltpu.CompilerParams(collective_id=cid, has_side_effects=True, vmem_limit_bytes=VMEM_LIMIT),
    )(dd0, dd1, dx0, dx1, *experts0, *experts1)


def last_kernel(
    experts, dense_ref, dx0_ref, dx1_ref, got_ref, gate_ref, up_ref, down_ref,
    gate_out, up_out, down_out, q_out, k_out, v_out, o_out, router_out, attn_out, moe_out, dx_out,
):
    gate_out[...] = gate_ref[...].astype(F32)
    up_out[...] = up_ref[...].astype(F32)
    down_out[...] = down_ref[...].astype(F32)

    @pl.when(pl.program_id(0) == 0)
    def _():
        s = lax.axis_index("section")
        q_out[...] = dense_ref[:, 0:QW]
        k_out[...] = dense_ref[:, QW : QW + KW]
        v_out[...] = dense_ref[:, QW + KW : QKV]
        o_out[...] = dense_ref[:, QKV : QKV + QW]
        aux_rows = jnp.transpose(dense_ref[:, QKV + QW :])
        for e in range(experts):
            router_out[e] = aux_rows[e : e + 1]
        moe_out[...] = aux_rows[GAIN_MOE_ROW : GAIN_MOE_ROW + 1]
        attn_out[...] = aux_rows[GAIN_ATTN_ROW : GAIN_ATTN_ROW + 1]
        dx_out[s] = jnp.where(s == 0, dx0_ref[...], dx1_ref[...])
        dx_out[1 - s] = got_ref[...].astype(F32)


def last(experts, dense, dx0, dx1, got, gate, up, down):
    sh = dense.shape[0]
    t, d = dx0.shape
    per, piece, f = gate.shape
    sds = jax.ShapeDtypeStruct

    def whole(shape):
        return pl.BlockSpec(shape, lambda j: (0,) * len(shape))

    wide = pl.BlockSpec((1, piece, f), lambda j: (j, 0, 0))
    tall = pl.BlockSpec((1, f, piece), lambda j: (j, 0, 0))
    small = [(sh, QW), (sh, KW), (sh, KW), (sh, QW), (experts, 1, sh), (1, sh), (1, sh), (2, t, d)]
    return pl.pallas_call(
        functools.partial(last_kernel, experts),
        grid=(per,),
        out_shape=tuple(sds(v.shape, F32) for v in (gate, up, down)) + tuple(sds(shape, F32) for shape in small),
        in_specs=[whole(v.shape) for v in (dense, dx0, dx1, got)] + [wide, wide, tall],
        out_specs=tuple([wide, wide, tall] + [whole(shape) for shape in small]),
        compiler_params=pltpu.CompilerParams(vmem_limit_bytes=VMEM_LIMIT),
    )(dense, dx0, dx1, got, gate, up, down)


def low_bit(q):
    return top_bit(q & -q)


def open_kernel(
    n, groups, pieces, wq_ref, wk_ref, wv_ref, wo_ref, wr_ref, ga_ref, gm_ref, cot_ref, rt_ref, w0_out, w1_out, gy_out, rt_out, rt_side,
    w_ref, s_right, r_right, s_left, r_left, s_group, r_group, s_y, r_y, s_cross, r_cross, s_rt, r_rt, s_side, r_side, local_sem,
):
    s, g, z = lax.axis_index("section"), lax.axis_index("group"), lax.axis_index("expert")
    remote = functools.partial(pltpu.make_async_remote_copy, device_id_type=MESH)
    rows = w_ref.shape[0] // pieces
    bits = top_bit(groups)
    other = {"section": 1 - s}
    w_ref[:, 0:QW] = wq_ref[...]
    w_ref[:, QW : QW + KW] = wk_ref[...]
    w_ref[:, QW + KW : QKV] = wv_ref[...]
    w_ref[:, QKV : QKV + QW] = wo_ref[...]
    experts, sh = wr_ref.shape
    gap = jnp.zeros((GAIN_MOE_ROW - experts, sh), F32)
    aux = jnp.concatenate([wr_ref[...].astype(F32), gap, gm_ref[...].astype(F32), ga_ref[...].astype(F32)], axis=0)
    w_ref[:, QKV + QW :] = jnp.transpose(aux).astype(BF)
    barrier = pltpu.get_barrier_semaphore()
    peers = [other] + [{"group": lax.bitwise_xor(g, 1 << b)} for b in range(bits)] + [{"expert": lax.rem(z + k, n)} for k in range(1, n)]
    for peer in peers:
        pl.semaphore_signal(barrier, inc=1, device_id=peer, device_id_type=MESH)
    pl.semaphore_wait(barrier, len(peers))
    sent = []

    def launch(cond, make):
        sent.append((cond, make))
        if cond is None:
            make().start()
        else:

            @pl.when(cond)
            def _():
                make().start()

    def part(q, zz, c):
        if c == 2 * pieces:
            return gy_out.at[s, zz]
        return (w0_out, w1_out)[c // pieces].at[lax.bitwise_xor(g, q) * n + zz, pl.ds(c % pieces * rows, rows)]

    def chain(to, zz, t, c, ssem, rsem):
        return remote(src_ref=part(0, zz, c), dst_ref=part(0, zz, c), send_sem=ssem.at[t, c], recv_sem=rsem.at[t, c], device_id={"expert": to})

    def right(t, c):
        return chain(z + 1, z - t, t, c, s_right, r_right)

    def left(t, c):
        return chain(z - 1, z + t, t, c, s_left, r_left)

    def over(q, b, zz, c):
        at = q | (1 << b)
        return remote(
            src_ref=part(q, zz, c), dst_ref=part(q, zz, c), send_sem=s_group.at[at, zz, c], recv_sem=r_group.at[at, zz, c],
            device_id={"group": lax.bitwise_xor(g, 1 << b)},
        )

    def hop(c, to=w0_out):
        at = pl.ds(c * rows, rows)
        return remote(src_ref=w_ref.at[at], dst_ref=to.at[g * n + z, at], send_sem=s_y.at[c], recv_sem=r_y.at[c], device_id=other)

    def by_layer(action):
        for layer, to in enumerate((w0_out, w1_out)):

            @pl.when(s == layer)
            def _(to=to):
                action(to)

    def cross(zz):
        return remote(src_ref=gy_out.at[0, zz], dst_ref=gy_out.at[0, zz], send_sem=s_cross.at[zz], recv_sem=r_cross.at[zz], device_id=other)

    def route(m, k):
        return remote(
            src_ref=rt_ref.at[m], dst_ref=rt_out.at[m, z], send_sem=s_rt.at[m, k], recv_sem=r_rt.at[m, k],
            device_id={"expert": lax.rem(z + k, n)},
        )

    def side():
        return remote(src_ref=rt_ref.at[1 - s], dst_ref=rt_side, send_sem=s_side, recv_sem=r_side, device_id=other)

    by_layer(lambda to: hop(0, to).start())
    launch(None, side)
    own = [pltpu.make_async_copy(cot_ref.at[s], gy_out.at[s, z], local_sem.at[0])]
    own += [pltpu.make_async_copy(rt_ref.at[m], rt_out.at[m, z], local_sem.at[1 + m]) for m in range(2)]

    def keep(to=w0_out):
        return pltpu.make_async_copy(w_ref, to.at[g * n + z], local_sem.at[3])

    for copy in own:
        copy.start()

    by_layer(lambda to: keep(to).start())
    keep().wait()

    def spread_out(cond, zz, c):
        if c < pieces:
            for b in reversed(range(bits)):
                launch(cond, functools.partial(over, 0, b, zz, c))
        elif c == 2 * pieces:
            launch((s == 0) if cond is None else ((s == 0) & cond), functools.partial(cross, zz))

    def pass_along(t, c):
        if t == 0:
            if c < 2 * pieces:

                @pl.when(s != c // pieces)
                def _():
                    hop(c % pieces).wait_recv()
            else:
                own[0].wait()
            launch(z < n - 1, functools.partial(right, t, c))
            launch(z > 0, functools.partial(left, t, c))
            spread_out(None, z, c)
            if c + 1 < pieces:
                hop(c).wait_send()
                by_layer(lambda to: hop(c + 1, to).start())
        else:
            from_left, from_right = z >= t, z + t < n

            @pl.when(from_left)
            def _():
                right(t - 1, c).wait_recv()

            launch(from_left & (z < n - 1), functools.partial(right, t, c))
            spread_out(from_left, z - t, c)

            @pl.when(from_right)
            def _():
                left(t - 1, c).wait_recv()

            launch(from_right & (z > 0), functools.partial(left, t, c))
            spread_out(from_right, z + t, c)

    def forward(q, k):
        zz = lax.rem(z + k, n)
        for c in range(pieces):
            over(q & (q - 1), low_bit(q), zz, c).wait_recv()
            for b in reversed(range(low_bit(q))):
                launch(None, functools.partial(over, q, b, zz, c))

    for t in range(n):
        for c in range(pieces):
            pass_along(t, c)
        if t == 0:
            for m in range(2):
                for k in range(1, n):
                    launch(None, functools.partial(route, m, k))
    pending = [(q, k) for q in sorted(range(1, groups), key=lambda q: -low_bit(q)) for k in range(n)]
    for t in range(n):
        pass_along(t, 2 * pieces)
        forward(*pending.pop(0))
    for t in range(n):
        for c in range(pieces, 2 * pieces):
            pass_along(t, c)
    for q, k in pending:
        forward(q, k)

    @pl.when(s != 0)
    def _():
        for zz in range(n):
            cross(zz).wait_recv()

    side().wait_recv()
    for m in range(2):
        own[1 + m].wait()
        for k in range(1, n):
            route(m, k).wait_recv()
    hop(pieces - 1).wait_send()
    for cond, make in sent:
        if cond is None:
            make().wait_send()
        else:

            @pl.when(cond)
            def _(make=make):
                make().wait_send()


def open_up(cid, weights, cot, rt):
    n, groups = lax.axis_size("expert"), lax.axis_size("group")
    sh = weights[0].shape[0]
    packed = (sh, QKV + QW + LANES)
    pieces = 3 if sh % 48 == 0 else 1
    dma = pltpu.SemaphoreType.DMA
    sds = jax.ShapeDtypeStruct

    def both(shape):
        return [dma(shape), dma(shape)]

    w0, w1, gy, rt_all, rt_side = pl.pallas_call(
        functools.partial(open_kernel, n, groups, pieces),
        out_shape=(sds((groups * n,) + packed, BF),) * 2 + (sds((2, n) + cot.shape[1:], BF), sds((2, n) + rt.shape[1:], rt.dtype), sds(rt.shape[1:], rt.dtype)),
        in_specs=vmem(9),
        out_specs=tuple([any_spec()] * 5),
        scratch_shapes=[pltpu.VMEM(packed, BF)] + both((n, 2 * pieces + 1)) + both((n, 2 * pieces + 1)) + both((groups, n, pieces)) + both((pieces,)) + both((n,)) + both((2, n)) + [dma, dma] + [dma((4,))],
        compiler_params=pltpu.CompilerParams(collective_id=cid, has_side_effects=True),
    )(*weights, cot, rt)
    return w0.reshape(groups * n * sh, -1), w1, gy, rt_all, rt_side


def swap_sections(value):
    return lax.ppermute(value, "section", [(0, 1), (1, 0)])


def rope_tables(t):
    half = HEAD_SIZE // 2
    frequency = THETA ** (-np.arange(half) * 2.0 / HEAD_SIZE)
    angles = np.arange(t)[:, None] * frequency[None, :]
    reps = LANES // half
    return (jnp.asarray(np.tile(f(angles), (1, reps)).astype(np.float32)) for f in (np.cos, np.sin))


def local(
    inputs, cotangent, segment_ids, live_first, routes, gain_attn, gain_moe,
    w_query, key_weight, value_weight, w_out, w_router, w_gate, w_up, w_down,
):
    s = lax.axis_index("section")
    n = lax.axis_size("expert")
    groups = lax.axis_size("group")
    t, d = inputs.shape[2:]
    top = routes.shape[-1]
    per = w_gate.shape[1]
    experts = per * n
    e_pad = -(-experts // 16) * 16
    cap = t * top * 5 // (4 * experts)
    wg, wu, wd = w_gate[0], w_up[0], w_down[0]
    at_zero = s == 0

    dense_shards = (w_query[0], key_weight[0], value_weight[0], w_out[0].T, w_router[0].T, gain_attn, gain_moe)

    seg, live, cot = segment_ids[:, 0], live_first[:, 0], cotangent[:, 0]
    cos, sin = rope_tables(t)

    rt = jnp.swapaxes(routes[0, :, 0], 1, 2)

    def flat(z):
        return z.reshape((2 * n,) + z.shape[2:])

    def paired(z):
        return z.reshape((2, n) + z.shape[1:])

    first_weights, second_weights, gy1, rt_all, rt_theirs = open_up(1, dense_shards, cot, rt)
    gy1, rt_all = flat(gy1), flat(rt_all)

    qkv0, p0, o0, h0, b0, wrt0, x0 = attn_fwd(inputs[:, 0], (), first_weights, cos, sin, seg, live)
    m0 = moe(0, "fwd", 2, e_pad, cap, b0, wg, wu, wd, rt=rt_all, wrt=wrt0, dense=second_weights)
    second_weights = m0.dense_out.reshape(first_weights.shape)

    qkv1, p1, o1, h1, b1, wrt1, x1 = attn_fwd(h0, m0.back, second_weights, cos, sin, seg, live)
    m1 = moe(1, "both", 3, e_pad, cap, b1, wg, wu, wd, rt=rt_all, wrt=wrt1, gy=gy1)

    dx1, gy0, dqkv1, at1, dht1, daux1 = attn_bwd(1, False, experts, cot, h1, x1, second_weights, qkv1, p1, o1, b1, wrt1, m1.back, m1.dgate, rt, rt_theirs, cos, sin)

    n0 = moe(0, "bwd", 4, e_pad, cap, gy0, wg, wu, wd, pos=m0.pos, gate=m0.gate, gp=m0.gp, up=m0.up, blocks=flat(m0.blocks),
             dqkv=dqkv1, at=at1, dht=dht1, daux=daux1, o=o1, part=m1.part0, part_own=m1.part1)
    dd1 = n0.dd
    dback0 = n0.back
    back1 = lax.all_to_all(n0.part_out, "expert", split_axis=0, concat_axis=0, tiled=True)
    dx0, low0, dd0 = attn_bwd(0, True, experts, gy0, h0, x0, first_weights, qkv0, p0, o0, b0, wrt0, dback0, n0.dgate, rt, rt_theirs, cos, sin)

    dense, got, *sums = finish(5, dd0, dd1, low0, gy0, (n0.even, n0.odd, n0.even_dn, n0.odd_dn), (m1.even, m1.odd, m1.even_dn, m1.odd_dn))
    dense, late = lax.optimization_barrier((dense, h1))
    y1 = (late + jnp.sum(back1.astype(F32), axis=0)).astype(BF)

    kept_out = jnp.where(at_zero, x1, y1)
    swapped_out = swap_sections(jnp.where(at_zero, y1, x1))
    layer_out = jnp.where(at_zero, jnp.stack([kept_out, swapped_out]), jnp.stack([swapped_out, kept_out]))
    gate_grad, up_grad, down_grad, *dense_grads, out_grad, router_grad, attn_grad, moe_grad, input_grad = last(
        experts, dense, dx0, dx1, got, *sums
    )
    return (
        layer_out[None, :, None],
        input_grad[None, :, None],
        attn_grad,
        moe_grad,
        *(v[None] for v in dense_grads),
        out_grad.T[None],
        jnp.transpose(router_grad, (1, 2, 0)),
        gate_grad[None],
        up_grad[None],
        down_grad[None],
    )


def solution(mesh):
    return jax.shard_map(
        local,
        mesh=mesh,
        in_specs=(
            P(None, ("group", "expert"), None, None),
            P(None, ("group", "expert"), None, None),
            P(None, ("group", "expert"), None),
            P(None, ("group", "expert"), None),
            P("section", None, ("group", "expert"), None, None),
            P("section", ("group", "expert")),
            P("section", ("group", "expert")),
            P("section", ("group", "expert"), None),
            P("section", ("group", "expert"), None),
            P("section", ("group", "expert"), None),
            P("section", None, ("group", "expert")),
            P("section", ("group", "expert"), None),
            P("section", "expert", None, None),
            P("section", "expert", None, None),
            P("section", "expert", None, None),
        ),
        out_specs=(
            P("section", None, ("group", "expert"), None, None),
            P("section", None, ("group", "expert"), None, None),
            P("section", ("group", "expert")),
            P("section", ("group", "expert")),
            P("section", ("group", "expert"), None),
            P("section", ("group", "expert"), None),
            P("section", ("group", "expert"), None),
            P("section", None, ("group", "expert")),
            P("section", ("group", "expert"), None),
            P("section", "expert", "group", None),
            P("section", "expert", "group", None),
            P("section", "expert", None, "group"),
        ),
        check_vma=False,
    )
```

```python
import functools
import types

import jax
import jax.numpy as jnp
import numpy as np
from jax import lax
from jax.experimental import pallas as pl
from jax.experimental.pallas import tpu as pltpu
from jax.sharding import PartitionSpec as P

QUERY_HEADS = 24
KEY_VALUE_HEADS = 8
HEAD_SIZE = 64
BLK = 64
EPS = 1e-06
THETA = 10000.0
NEG_FILL = -1e30
BF = jnp.bfloat16
F32 = jnp.float32
MESH = pl.DeviceIdType.MESH
LANES = 128
TILE = 512
QW = QUERY_HEADS * HEAD_SIZE
KW = KEY_VALUE_HEADS * HEAD_SIZE
QKV = QW + 2 * KW
GAIN_MOE_ROW = 126
GAIN_ATTN_ROW = 127
VMEM_LIMIT = 60 * 1024 * 1024
HEAD_PAIRS = KEY_VALUE_HEADS // 2
TILES_PER_PAIR = QUERY_HEADS // KEY_VALUE_HEADS


def dot(a, b, ca=1, cb=0):
    return lax.dot_general(a, b, (((ca,), (cb,)), ((), ())), preferred_element_type=F32)


def iota(shape, axis):
    return lax.broadcasted_iota(jnp.int32, shape, axis)


def rope(z, cos, sin, direction):
    width = z.shape[1]
    half = HEAD_SIZE // 2
    first = iota(z.shape, 1) % HEAD_SIZE < half
    partner = jnp.where(first, pltpu.roll(z, width - half, 1), pltpu.roll(z, half, 1))
    signed = jnp.where(first, -direction, direction) * partner
    reps = width // LANES
    return z * jnp.concatenate([cos] * reps, axis=1) + signed * jnp.concatenate([sin] * reps, axis=1)


def lane_masks(t):
    low = iota((t, LANES), 1) < HEAD_SIZE
    return low, jnp.logical_not(low)


def swapped(z):
    return pltpu.roll(z.astype(F32), HEAD_SIZE, 1).astype(BF)


def head_plan():
    return [(r, half, (2 * r + half) // TILES_PER_PAIR != half) for r in range(TILES_PER_PAIR) for half in range(2)]


def pick(z, half, masks):
    return jnp.where(masks[half], z, jnp.zeros_like(z))


def weight_pieces(d, order):
    aux = [(pl.ds(0, d), pl.ds(QKV + QW, LANES))]
    qkv = [(pl.ds(0, d), pl.ds(n * TILE, TILE)) for n in range(QKV // TILE)]
    out = [(pl.ds(n * TILE, TILE), pl.ds(QKV, QW)) for n in range(d // TILE)]
    down = [(pl.ds(0, d), pl.ds(QKV + n * TILE, TILE)) for n in range(QW // TILE)]
    rows = [(pl.ds(n * TILE, TILE), pl.ds(0, QKV)) for n in range(d // TILE)]
    return aux + qkv + out if order == "forward" else down + rows


def arriving(w_hbm, w_ref, sem, order):
    copies = [
        pltpu.make_async_copy(w_hbm.at[rows, cols], w_ref.at[rows, cols], sem.at[i])
        for i, (rows, cols) in enumerate(weight_pieces(w_ref.shape[0], order))
    ]
    for c in copies:
        c.start()
    return copies


def attn_fwd_kernel(
    blocks, below_ref, *refs,
):
    back_ref = refs[0] if blocks else None
    (
        w_hbm, cos_ref, sin_ref, seg_ref, live_ref,
        qkv_ref, p_ref, o_ref, h_ref, b_ref, wrt_ref, x_ref, w_ref, w_sem,
    ) = refs[1 if blocks else 0 :]
    t, d = x_ref.shape
    pieces = arriving(w_hbm, w_ref, w_sem, "forward")
    mine = lax.axis_index("section")
    entering = (below_ref[mine] if len(below_ref.shape) == 3 else below_ref[...]).astype(F32)
    for z in range(blocks):
        entering = entering + back_ref[z].astype(F32)
    x_ref[...] = entering.astype(BF)
    pieces.pop(0).wait()
    aux = jnp.transpose(w_ref[:, QKV + QW :].astype(F32))
    wrt_ref[...] = aux.astype(BF)
    gain_attn = aux[GAIN_ATTN_ROW : GAIN_ATTN_ROW + 1]
    gain_moe = aux[GAIN_MOE_ROW : GAIN_MOE_ROW + 1]
    x = x_ref[...].astype(F32)
    r1 = lax.rsqrt(jnp.mean(x * x, axis=1, keepdims=True) + EPS)
    a = (x * r1 * gain_attn).astype(BF)
    cos, sin = cos_ref[...], sin_ref[...]
    for n in range(QKV // TILE):
        cols = slice(n * TILE, (n + 1) * TILE)
        pieces.pop(0).wait()
        y = dot(a, w_ref[:, cols])
        if n * TILE < QW + KW:
            y = rope(y, cos, sin, 1.0)
        qkv_ref[:, cols] = y.astype(BF)
    i, j = iota((t, t), 0), iota((t, t), 1)
    segments = jnp.broadcast_to(seg_ref[pl.ds(mine, 1), :].astype(F32), (t, t))
    first_block = jnp.zeros((t, t), jnp.int32)
    for block in range(t // BLK):
        first_block = jnp.where(i // BLK == block, live_ref[mine, block], first_block)
    allowed = (j <= i) & (jnp.transpose(segments) == segments) & (j // BLK >= first_block)
    masks = lane_masks(t)

    def pair(m, carry):
        def lanes(base):
            return pl.ds(pl.multiple_of(base, LANES), LANES)

        kp = qkv_ref[:, lanes(QW + m * LANES)]
        vp = qkv_ref[:, lanes(QW + KW + m * LANES)]
        ks, vs = swapped(kp), swapped(vp)
        plan = head_plan()
        scores = []
        for r, half, swap in plan:
            q = pick(qkv_ref[:, lanes((m * TILES_PER_PAIR + r) * LANES)], half, masks)
            s = dot(q, ks if swap else kp, 1, 1) * HEAD_SIZE ** (-0.5)
            scores.append(jnp.where(allowed, s, NEG_FILL))
        tops = [jnp.max(s, axis=1, keepdims=True) for s in scores]
        exps = [jnp.exp(s - top) for s, top in zip(scores, tops)]
        sums = [1.0 / jnp.sum(e, axis=1, keepdims=True) for e in exps]
        probs = [e * u for e, u in zip(exps, sums)]
        for (r, half, swap), p in zip(plan, probs):
            p_ref[m * 2 * TILES_PER_PAIR + 2 * r + half] = p
        parts = [dot(p.astype(BF), pick(vs if swap else vp, half, masks)) for (r, half, swap), p in zip(plan, probs)]
        for r in range(TILES_PER_PAIR):
            o_ref[:, lanes((m * TILES_PER_PAIR + r) * LANES)] = (parts[2 * r] + parts[2 * r + 1]).astype(BF)
        return carry

    lax.fori_loop(0, HEAD_PAIRS, pair, 0, unroll=True)
    o = o_ref[...]
    for n in range(d // TILE):
        rows = slice(n * TILE, (n + 1) * TILE)
        pieces.pop(0).wait()
        h_ref[:, rows] = x_ref[:, rows].astype(F32) + dot(o, w_ref[rows, QKV : QKV + QW], 1, 1)
    h = h_ref[...]
    r2 = lax.rsqrt(jnp.mean(h * h, axis=1, keepdims=True) + EPS)
    b_ref[...] = (h * r2 * gain_moe).astype(BF)


def vmem(n):
    return [pl.BlockSpec(memory_space=pltpu.VMEM)] * n


def attn_fwd(below, back, w, cos, sin, seg, live):
    t, d = below.shape[-2:]
    sds = jax.ShapeDtypeStruct
    return pl.pallas_call(
        functools.partial(attn_fwd_kernel, len(back)),
        out_shape=(
            sds((t, QKV), BF),
            sds((QUERY_HEADS, t, t), F32),
            sds((t, QW), BF),
            sds((t, d), F32),
            sds((t, d), BF),
            sds((LANES, d), BF),
            sds((t, d), BF),
        ),
        in_specs=vmem(2 if len(back) else 1) + [any_spec()] + vmem(3) + [pl.BlockSpec(memory_space=pltpu.SMEM)],
        out_specs=tuple(vmem(7)),
        scratch_shapes=[pltpu.VMEM(w.shape, BF), pltpu.SemaphoreType.DMA((1 + QKV // TILE + d // TILE,))],
        compiler_params=pltpu.CompilerParams(vmem_limit_bytes=VMEM_LIMIT),
        cost_estimate=pl.CostEstimate(flops=2 * t * d * 4096, bytes_accessed=w.size * 2, transcendentals=QUERY_HEADS * t * t),
    )(below, *((back,) if len(back) else ()), w, cos, sin, seg, live)


def gates_of(rt, wrt, b, e_pad):
    t = rt.shape[1]
    experts = iota((e_pad, t), 0)
    chosen = experts == rt[0:1]
    for k in range(1, rt.shape[0]):
        chosen = chosen | (experts == rt[k : k + 1])
    logits = jnp.where(chosen, dot(wrt[0:e_pad], b, 1, 1), NEG_FILL)
    e = jnp.where(chosen, jnp.exp(logits - jnp.max(logits, axis=0, keepdims=True)), 0.0)
    return e / jnp.sum(e, axis=0, keepdims=True)


def attn_bwd_kernel(
    layer, now, e_pad, e_real, gy_ref, h_ref, x_ref, w_hbm, qkv_ref, p_ref, o_ref, b_ref, wrt_ref, back_ref, dg_ref, rt_ref, side_ref, cos_ref, sin_ref,
    dx_ref, dxb_ref, *rest,
):
    t, d = x_ref.shape
    if now:
        dd_hbm, do_ref, dqkv_ref, dh_ref, w_ref, w_sem, lt_ref, dd_ref, dd_sem = rest
    else:
        dqkv_ref, at_ref, dht_ref, daux_ref, do_ref, dh_ref, w_ref, w_sem = rest
    pieces = arriving(w_hbm, w_ref, w_sem, "backward")
    last_tile = (QKV + QW) // TILE

    def leave(n, width):
        cols = pl.ds(pl.multiple_of(n * TILE, LANES), width)
        return pltpu.make_async_copy(dd_ref.at[:, cols], dd_hbm.at[:, cols], dd_sem.at[n])

    gain_attn = wrt_ref[GAIN_ATTN_ROW - 7 :, :].astype(F32)[7:8]
    gain_moe = wrt_ref[GAIN_ATTN_ROW - 7 :, :].astype(F32)[6:7]
    b = b_ref[...]
    mine = lax.axis_index("section")
    gates = gates_of(jnp.where(mine == layer, rt_ref[mine], side_ref[...]), wrt_ref, b, e_pad)
    per = e_real // dg_ref.shape[0]
    dg = [dg_ref[z][0:per] for z in range(dg_ref.shape[0])]
    if e_pad > e_real:
        dg.append(jnp.zeros((e_pad - e_real, t), F32))
    dg = jnp.concatenate(dg, axis=0)
    dl = (gates * (dg - jnp.sum(gates * dg, axis=0, keepdims=True)))
    dlb = dl.astype(BF)
    db = dot(dlb, wrt_ref[0:e_pad, :], 0, 0)
    for z in range(back_ref.shape[0]):
        db = db + back_ref[z].astype(F32)
    h = h_ref[...]
    r2 = lax.rsqrt(jnp.mean(h * h, axis=1, keepdims=True) + EPS)
    grad_moe = jnp.sum(db * h * r2, axis=0, keepdims=True)
    dn = db * gain_moe
    gy = gy_ref[lax.axis_index("section")] if len(gy_ref.shape) == 3 else gy_ref[...]
    dh = gy.astype(F32) + r2 * dn - h * (r2 * r2 * r2) * jnp.mean(dn * h, axis=1, keepdims=True)
    dh_ref[...] = dh
    dhb = dh.astype(BF)
    for n in range(QW // TILE):
        cols = slice(n * TILE, (n + 1) * TILE)
        pieces.pop(0).wait()
        do_ref[:, cols] = dot(dhb, w_ref[:, QKV + n * TILE : QKV + (n + 1) * TILE]).astype(BF)
    masks = lane_masks(t)
    cos, sin = cos_ref[...], sin_ref[...]

    def pair(m, carry):
        def lanes(base):
            return pl.ds(pl.multiple_of(base, LANES), LANES)

        kp = qkv_ref[:, lanes(QW + m * LANES)]
        vp = qkv_ref[:, lanes(QW + KW + m * LANES)]
        ks, vs = swapped(kp), swapped(vp)
        plan = head_plan()
        tiles = [lanes((m * TILES_PER_PAIR + r) * LANES) for r in range(TILES_PER_PAIR)]
        qs = [pick(qkv_ref[:, tiles[r]], half, masks) for r, half, _ in plan]
        dos = [pick(do_ref[:, tiles[r]], half, masks) for r, half, _ in plan]
        ps = [p_ref[m * 2 * TILES_PER_PAIR + 2 * r + half] for r, half, _ in plan]
        dps = [dot(do, vs if swap else vp, 1, 1) for do, (_, _, swap) in zip(dos, plan)]
        dvs = [dot(p.astype(BF), do, 0, 0) for p, do in zip(ps, dos)]
        sums = [jnp.sum(p * dp, axis=1, keepdims=True) for p, dp in zip(ps, dps)]
        dts = [(p * (dp - total) * HEAD_SIZE ** (-0.5)).astype(BF) for p, dp, total in zip(ps, dps, sums)]
        dks = [dot(dt, q, 0, 0) for dt, q in zip(dts, qs)]
        dqs = [dot(dt, pick(ks if swap else kp, half, masks)) for dt, (_, half, swap) in zip(dts, plan)]
        for r in range(TILES_PER_PAIR):
            dqkv_ref[:, tiles[r]] = rope(dqs[2 * r] + dqs[2 * r + 1], cos, sin, -1.0).astype(BF)
        dk, dv = (
            {way: functools.reduce(jnp.add, [v for v, (_, _, swap) in zip(vals, plan) if swap == way]) for way in (False, True)}
            for vals in (dks, dvs)
        )
        dk_all = dk[False] + pltpu.roll(dk[True], HEAD_SIZE, 1)
        dv_all = dv[False] + pltpu.roll(dv[True], HEAD_SIZE, 1)
        dqkv_ref[:, lanes(QW + m * LANES)] = rope(dk_all, cos, sin, -1.0).astype(BF)
        dqkv_ref[:, lanes(QW + KW + m * LANES)] = dv_all.astype(BF)
        return carry

    lax.fori_loop(0, HEAD_PAIRS, pair, 0, unroll=True)
    x = x_ref[...].astype(F32)
    r1 = lax.rsqrt(jnp.mean(x * x, axis=1, keepdims=True) + EPS)
    dqkv = dqkv_ref[...]
    for n in range(d // TILE):
        rows = slice(n * TILE, (n + 1) * TILE)
        pieces.pop(0).wait()
        dx_ref[:, rows] = dot(dqkv, w_ref[rows, 0:QKV], 1, 1)
    da = dx_ref[...]
    grad_attn = jnp.sum(da * x * r1, axis=0, keepdims=True)
    dag = da * gain_attn
    dx = dh_ref[...] + r1 * dag - x * (r1 * r1 * r1) * jnp.mean(dag * x, axis=1, keepdims=True)
    dx_ref[...] = dx
    dxb_ref[...] = dx.astype(BF)
    row = iota((LANES, d), 0)
    grads = jnp.where(row == GAIN_MOE_ROW, grad_moe, jnp.where(row == GAIN_ATTN_ROW, grad_attn, 0.0))
    dl_full = jnp.concatenate([dl, jnp.zeros((LANES - e_pad, t), F32)], axis=0)
    dl_rows = jnp.transpose(dl_full).astype(BF)
    bt = jnp.transpose(b_ref[...].astype(F32)).astype(BF)
    daux = (dot(bt, dl_rows) + jnp.transpose(grads)).astype(BF)
    if not now:
        at_ref[...] = jnp.transpose(x * r1 * gain_attn).astype(BF)
        dht_ref[...] = jnp.transpose(dh_ref[...]).astype(BF)
        daux_ref[...] = daux
        return
    lt_ref[...] = jnp.transpose(x * r1 * gain_attn).astype(BF)

    @pl.loop(0, QKV // TILE)
    def _(n):
        cols = pl.ds(pl.multiple_of(n * TILE, LANES), TILE)
        dd_ref[:, cols] = dot(lt_ref[...], dqkv_ref[:, cols]).astype(BF)
        leave(n, TILE).start()

    lt_ref[...] = jnp.transpose(dh_ref[...]).astype(BF)

    @pl.loop(0, QW // TILE)
    def _(n):
        cols = pl.ds(pl.multiple_of(n * TILE, LANES), TILE)
        dd_ref[:, pl.ds(pl.multiple_of(QKV + n * TILE, LANES), TILE)] = dot(lt_ref[...], o_ref[:, cols]).astype(BF)
        leave(QKV // TILE + n, TILE).start()

    dd_ref[:, QKV + QW :] = daux
    leave(last_tile, LANES).start()

    @pl.loop(0, last_tile)
    def _(n):
        leave(n, TILE).wait()

    leave(last_tile, LANES).wait()


def attn_bwd(layer, now, experts, gy, h, x, w, qkv, p, o, b, wrt, back, dg, rt, side, cos, sin):
    t, d = x.shape
    sds = jax.ShapeDtypeStruct
    dma = pltpu.SemaphoreType.DMA
    outs = [sds((t, d), F32), sds((t, d), BF)]
    scratch = [pltpu.VMEM((t, QW), BF)]
    if now:
        outs.append(sds(w.shape, BF))
        scratch.append(pltpu.VMEM((t, QKV), BF))
    else:
        outs += [sds((t, QKV), BF), sds((d, t), BF), sds((d, t), BF), sds((d, LANES), BF)]
    scratch += [pltpu.VMEM((t, d), F32), pltpu.VMEM(w.shape, BF), dma((QW // TILE + d // TILE,))]
    if now:
        scratch += [pltpu.VMEM((d, t), BF), pltpu.VMEM(w.shape, BF), dma((1 + QKV // TILE + QW // TILE,))]
    return pl.pallas_call(
        functools.partial(attn_bwd_kernel, layer, now, -(-experts // 16) * 16, experts),
        out_shape=tuple(outs),
        in_specs=vmem(3) + [any_spec()] + vmem(11),
        out_specs=tuple(vmem(2) + [any_spec()] if now else vmem(6)),
        scratch_shapes=scratch,
        compiler_params=pltpu.CompilerParams(vmem_limit_bytes=VMEM_LIMIT),
        cost_estimate=pl.CostEstimate(flops=4 * t * d * 4096, bytes_accessed=w.size * 4, transcendentals=0),
    )(gy, h, x, w, qkv, p, o, b, wrt, back, dg, rt, side, cos, sin)


def one_hot(pos_row, cap):
    return jnp.where(iota((cap, pos_row.shape[1]), 0) == pos_row, 1.0, 0.0)


def all_hots(pos, per, cap):
    return jnp.concatenate([one_hot(pos[j : j + 1], cap) for j in range(per)], axis=0)


def all_hots_back(pos, per, cap):
    width = per * cap
    expert = jnp.where(iota((8, width), 1) // cap == iota((8, width), 0), 1.0, 0.0).astype(BF)
    wide = dot(pos.astype(F32).astype(BF), expert, 0, 0)
    slot = (iota((1, width), 1) % cap).astype(F32)
    return jnp.where(wide == slot, 1.0, 0.0).astype(BF)


def slots_of(rt, first, per):
    t = rt.shape[1]
    experts = iota((16, t), 0)
    mine = jnp.where(experts < per, experts + first, -1)
    chosen = mine == rt[0:1]
    for k in range(1, rt.shape[0]):
        chosen = chosen | (mine == rt[k : k + 1])
    earlier = jnp.where(iota((t, t), 0) < iota((t, t), 1), 1.0, 0.0).astype(BF)
    before = dot(jnp.where(chosen, 1.0, 0.0).astype(BF), earlier)
    return jnp.where(chosen, before.astype(jnp.int32), -1)[0:8]


def streamed(count, copies, body, primed=False):
    if not primed:
        for c in copies(0, 0):
            c.start()

    def step(b, carry):
        slot = lax.rem(b, 2)

        @pl.when(b + 1 < count)
        def _():
            for c in copies(b + 1, lax.rem(b + 1, 2)):
                c.start()

        for c in copies(b, slot):
            c.wait()
        body(b, slot)
        return carry

    lax.fori_loop(0, count, step, 0)


def combine(base, count, per, cap, pos_ref, rows_ref, out_hbm, obuf, osem):
    def copy(b, slot):
        return pltpu.make_async_copy(obuf.at[slot], out_hbm.at[b], osem.at[slot])

    def step(b, carry):
        slot = lax.rem(b, 2)

        @pl.when(b >= 2)
        def _():
            copy(b - 2, slot).wait()

        back = all_hots_back(pos_ref[base + b], per, cap)
        at = pl.ds(pl.multiple_of((base + b) * cap, cap), cap)
        rows = jnp.concatenate([rows_ref[j, at, :] for j in range(per)], axis=0)
        obuf[slot] = dot(back, rows).astype(BF)
        copy(b, slot).start()
        return carry

    lax.fori_loop(0, count, step, 0)
    copy(count - 2, (count - 2) % 2).wait()
    copy(count - 1, (count - 1) % 2).wait()


def chunk_gates(c, j, chunk, cap, pos_ref, gate_ref):
    hots, gates = [], []
    for bb in range(chunk // cap):
        b = c * (chunk // cap) + bb
        hot = one_hot(pos_ref[b, pl.ds(j, 1), :], cap)
        hots.append(hot)
        gates.append(jnp.sum(hot * gate_ref[b, pl.ds(j, 1), :], axis=1, keepdims=True))
    return hots, jnp.concatenate(gates, axis=0)


def any_spec():
    return pl.BlockSpec(memory_space=pl.ANY)


def put_rows(hots, block, b, per, cap, dest):
    at = pl.ds(pl.multiple_of(b * cap, cap), cap)
    rows = dot(hots, block).astype(BF)
    for k in range(per):
        dest[k, at, :] = rows[k * cap : (k + 1) * cap]


def gather_from(count, per, cap, pos, source, dest, buf, sem):
    def body(b, slot):
        put_rows(all_hots(pos[b], per, cap).astype(BF), buf[slot], b, per, cap, dest)

    streamed(count, lambda b, slot: [pltpu.make_async_copy(source.at[b], buf.at[slot], sem.at[slot])], body)


def weight_grads(r, per):
    parts, piece = r.even.shape[0], r.even.shape[3]
    g = lax.axis_index("group")
    parity, place = lax.rem(g, 2), g // 2

    def outgoing(j, at, slot):
        return [
            pltpu.make_async_copy(r.gu_buf.at[slot, 0], r.even.at[at, :, j], r.gu_sem.at[slot, 0]),
            pltpu.make_async_copy(r.gu_buf.at[slot, 1], r.odd.at[at, :, j], r.gu_sem.at[slot, 1]),
            pltpu.make_async_copy(r.dn_buf.at[slot, 0], r.even_dn.at[at, j], r.dn_sem.at[slot, 0]),
            pltpu.make_async_copy(r.dn_buf.at[slot, 1], r.odd_dn.at[at, j], r.dn_sem.at[slot, 1]),
        ]

    def finished(slot):
        for c in outgoing(0, 0, slot):
            c.wait()

    def body(i, carry):
        j, q = i // parts, lax.rem(i, parts)
        slot = lax.rem(i, 2)

        @pl.when(i >= 2)
        def _():
            finished(slot)

        cols = pl.ds(pl.multiple_of(2 * q * piece, LANES), 2 * piece)
        for m in range(2):
            full = dot(r.x_scr[j, :, cols], r.act[m, j], 0, 0).astype(BF)
            r.gu_buf[slot, parity, m] = full[:piece]
            r.gu_buf[slot, 1 - parity, m] = full[piece:]
        full = dot(r.act[2, j], r.y_scr[j, :, cols], 0, 0).astype(BF)
        r.dn_buf[slot, parity] = full[:, :piece]
        r.dn_buf[slot, 1 - parity] = full[:, piece:]
        for c in outgoing(j, lax.bitwise_xor(place, q), slot):
            c.start()
        return carry

    lax.fori_loop(0, per * parts, body, 0)
    for slot in range(2):
        finished(slot)


def meet(n, bits):
    s, g, z = lax.axis_index("section"), lax.axis_index("group"), lax.axis_index("expert")
    barrier = pltpu.get_barrier_semaphore()
    peers = [{"section": 1 - s}] + [{"expert": lax.rem(z + k, n)} for k in range(1, n)]
    peers += [{"group": lax.bitwise_xor(g, 1 << b)} for b in range(bits)]
    for peer in peers:
        pl.semaphore_signal(barrier, inc=1, device_id=peer, device_id_type=MESH)
    pl.semaphore_wait(barrier, len(peers))


def moe_kernel(layer, mode, n, e_pad, cap, names, *refs):
    r = types.SimpleNamespace(**dict(zip(names, refs)))
    forward, backward = mode != "bwd", mode != "fwd"
    s, z = lax.axis_index("section"), lax.axis_index("expert")
    here = s == layer
    count = 2 * n
    per, rows, d = r.y_scr.shape
    first = z * per
    chunk = n * cap
    remote = functools.partial(pltpu.make_async_remote_copy, device_id_type=MESH)
    other = {"section": 1 - s}
    g = lax.axis_index("group")
    riding = forward and not backward
    groups = r.dense_out.shape[0] // n if riding else 1
    bits = top_bit(groups)
    meet(n, bits)
    r.blk[s, z] = r.own[...]

    def over(q, b, zz):
        at = q | (1 << b)
        shard = r.dense_out.at[lax.bitwise_xor(g, q) * n + zz]
        return remote(
            src_ref=shard, dst_ref=shard, send_sem=r.s_over.at[at, zz], recv_sem=r.r_over.at[at, zz],
            device_id={"group": lax.bitwise_xor(g, 1 << b)},
        )

    def ride(bs):
        for b in bs:
            for zz in range(n):
                over(0, b, zz).start()

    def ride_on():
        for q in sorted(range(1, groups), key=lambda q: -low_bit(q)):
            for zz in range(n):
                over(q & (q - 1), low_bit(q), zz).wait_recv()
                for b in reversed(range(low_bit(q))):
                    over(q, b, zz).start()

    if riding:
        ride(reversed(range(1, bits)))

    def half(i):
        section = jnp.where(i < per, layer, 1 - layer)
        return lax.rem(i, per), section, pl.ds(pl.multiple_of(section * chunk, chunk), chunk)

    def weights(i, slot):
        j, _, at = half(i)
        both = [
            pltpu.make_async_copy(r.wg.at[j], r.wg_buf.at[slot], r.w_sem.at[slot, 0]),
            pltpu.make_async_copy(r.wu.at[j], r.wu_buf.at[slot], r.w_sem.at[slot, 1]),
            pltpu.make_async_copy(r.wd.at[j], r.wd_buf.at[slot], r.w_sem.at[slot, 2]),
        ]
        if mode == "bwd":
            both.append(pltpu.make_async_copy(r.gp.at[j, at], r.gp_buf.at[slot], r.gp_sem.at[slot, 0]))
            both.append(pltpu.make_async_copy(r.up.at[j, at], r.gp_buf.at[2 + slot], r.gp_sem.at[slot, 1]))
        return both

    def chain(to, zz, t, ssem, rsem):
        return remote(
            src_ref=r.blk.at[s, zz], dst_ref=r.blk.at[s, zz], send_sem=ssem.at[t], recv_sem=rsem.at[t], device_id={"expert": to}
        )

    def right(t):
        return chain(z + 1, z - t, t, r.s_right, r.r_right)

    def left(t):
        return chain(z - 1, z + t, t, r.s_left, r.r_left)

    def cross(zz):
        return remote(
            src_ref=r.blk.at[s, zz], dst_ref=r.blk.at[s, zz], send_sem=r.s_cross.at[zz], recv_sem=r.r_cross.at[zz], device_id=other
        )

    def prepare(section, zz):
        b = section * n + zz
        block = r.blk[section, zz]
        if forward:
            rt = r.rt[b]
            pos = slots_of(rt, first, per)
            r.pos[b] = pos
            r.gates[...] = gates_of(rt, r.wrt, block, e_pad)
            r.gate[b] = jnp.concatenate(
                [r.gates[pl.ds(first + k, 1), :] for k in range(per)] + [jnp.zeros((8 - per, rt.shape[1]), F32)], axis=0
            )
            put_rows(all_hots(pos, per, cap).astype(BF), block, b, per, cap, r.x_scr)
        else:
            put_rows(all_hots(r.pos[b], per, cap).astype(BF), block, b, per, cap, r.y_scr)

    @pl.when(here)
    def _():
        for c in weights(0, 0):
            c.start()

    def prepare_at(section, t):
        def candidate(m, carry):
            zz = jnp.where(m == 0, z - t, z + t)

            @pl.when((zz >= 0) & (zz < n) & ((m == 0) | (t > 0)))
            def _():
                prepare(section, zz)

            return carry

        lax.fori_loop(0, 2, candidate, 0)

    tiles = (("at", "dqkv", 0, QW), ("at", "dqkv", QW, 2 * KW), ("dht", "o", QKV, QW))

    def dense_copy(block, m):
        _, _, col, width = tiles[m]
        at = pl.ds(pl.multiple_of(block * rows, rows), rows)
        return pltpu.make_async_copy(
            r.x_scr.at[m, :, pl.ds(0, width)], r.dd.at[at, pl.ds(col, width)], r.dd_sem.at[m]
        )

    def aux_copy():
        return pltpu.make_async_copy(r.daux, r.dd.at[:, pl.ds(QKV + QW, LANES)], r.daux_sem)

    def dense_start(block):
        @pl.when(block == 0)
        def _():
            aux_copy().start()

        at = pl.ds(pl.multiple_of(block * rows, rows), rows)
        for m, (left, right, col, width) in enumerate(tiles):

            @pl.when(block > 0)
            def _():
                dense_copy(block - 1, m).wait()

            source = getattr(r, right)
            source = source[:, col : col + width] if right == "dqkv" else source[...]
            r.x_scr[m, :, 0:width] = dot(getattr(r, left)[at, :], source).astype(BF)
            dense_copy(block, m).start()

    def dense_wait():
        aux_copy().wait()
        for m in range(len(tiles)):
            dense_copy(d // rows - 1, m).wait()

    @pl.loop(0, n)
    def _(t):
        from_left = z >= t
        from_right = z + t < n

        @pl.when(from_left & (t > 0))
        def _():
            right(t - 1).wait_recv()

        @pl.when(from_left & (z < n - 1))
        def _():
            right(t).start()

        @pl.when(from_left & jnp.logical_not(here))
        def _():
            cross(z - t).start()

        @pl.when(from_right & (t > 0))
        def _():
            left(t - 1).wait_recv()

        @pl.when(from_right & (z > 0))
        def _():
            left(t).start()

        @pl.when(from_right & (t > 0) & jnp.logical_not(here))
        def _():
            cross(z + t).start()

        if mode == "bwd":

            @pl.when(t < d // rows)
            def _():
                dense_start(t)

        @pl.when(here)
        def _():
            if mode == "both":

                @pl.when(t == 0)
                def _():
                    @pl.loop(0, count)
                    def _(b):
                        r.pos[b] = slots_of(r.rt[b], first, per)

                    gather_from(count, per, cap, r.pos, r.gy, r.y_scr, r.row_buf, r.row_sem)

            prepare_at(layer, t)

            @pl.when(t == min(2, n - 1))
            def _():
                cross(z).wait_recv()
                prepare(1 - layer, z)

    def late_blocks():
        @pl.loop(1, n)
        def _(t):
            @pl.when(z >= t)
            def _():
                cross(z - t).wait_recv()

            @pl.when(z + t < n)
            def _():
                cross(z + t).wait_recv()

            prepare_at(1 - layer, t)

    if riding:
        ride((0,))

    def over_part(zz):
        return remote(
            src_ref=r.part.at[zz], dst_ref=r.part_out.at[zz], send_sem=r.s_part.at[zz], recv_sem=r.r_part.at[zz], device_id=other
        )

    if mode == "bwd":
        dense_wait()

        @pl.when(jnp.logical_not(here))
        def _():
            for zz in range(n):
                over_part(zz).start()
            pltpu.make_async_copy(r.part_own, r.pbuf.at[layer], r.part_sem.at[0]).start()

    def part_home():
        return pltpu.make_async_copy(r.pbuf.at[layer], r.part_out, r.part_sem.at[1])

    srcs = (r.pbuf, r.dg) if backward else (r.pbuf,)
    outs = (r.back, r.dgate) if backward else (r.back,)
    relays = (r.relay, r.dg_relay) if backward else (r.relay,)
    arrays = range(len(srcs))

    def hop(a, to):
        return remote(
            src_ref=srcs[a].at[1 - layer, to],
            dst_ref=relays[a].at[to],
            send_sem=r.s_hop.at[a, to],
            recv_sem=r.r_hop.at[a, to],
            device_id=other,
        )

    def give(a, source, k):
        return remote(
            src_ref=source,
            dst_ref=outs[a].at[z],
            send_sem=r.s_give.at[a, k],
            recv_sem=r.r_give.at[a, k],
            device_id={"expert": lax.rem(z + k, n)},
        )

    def keep(a, source):
        return pltpu.make_async_copy(source, outs[a].at[z], r.keep_sem.at[a])

    def saved(i, slot):
        j, _, at = half(i)
        return [
            pltpu.make_async_copy(r.gp_buf.at[slot], r.gp.at[j, at], r.gp_sem.at[slot, 0]),
            pltpu.make_async_copy(r.gp_buf.at[2 + slot], r.up.at[j, at], r.gp_sem.at[slot, 1]),
        ]

    def expert(i, slot):
        j, section, at = half(i)

        @pl.when(i == per)
        def _():
            late_blocks()

        if mode == "fwd":

            @pl.when(i >= 2)
            def _():
                for c in saved(i - 2, slot):
                    c.wait()

        if forward:
            x = r.x_scr[j, at, :]
            gp = dot(x, r.wg_buf[slot])
            up = dot(x, r.wu_buf[slot])
        else:
            gp, up = r.gp_buf[slot].astype(F32), r.gp_buf[2 + slot].astype(F32)
        sg = 1.0 / (1.0 + jnp.exp(-gp))
        silu = gp * sg
        hid = silu * up
        hots, gate = chunk_gates(section, j, chunk, cap, r.pos, r.gate)
        if not backward:
            r.gp_buf[slot] = gp.astype(BF)
            r.gp_buf[2 + slot] = up.astype(BF)
            r.y_scr[j, at, :] = (dot(hid.astype(BF), r.wd_buf[slot]) * gate).astype(BF)
            for c in saved(i, slot):
                c.start()
            return
        raw = dot(r.y_scr[j, at, :], r.wd_buf[slot], 1, 1)
        dgate = jnp.sum(hid.astype(BF).astype(F32) * raw, axis=1, keepdims=True)
        for bb in range(n):
            r.dg[section, bb, pl.ds(j, 1), :] = jnp.sum(hots[bb] * dgate[bb * cap : (bb + 1) * cap], axis=0, keepdims=True)
        dh = raw * gate
        dgp = (dh * up * sg * (1.0 + gp * (1.0 - sg))).astype(BF)
        dup = (dh * silu).astype(BF)
        r.act[0, j, at, :] = dgp
        r.act[1, j, at, :] = dup
        r.act[2, j, at, :] = (hid * gate).astype(BF)
        r.y_scr[j, at, :] = (dot(dgp, r.wg_buf[slot], 1, 1) + dot(dup, r.wu_buf[slot], 1, 1)).astype(BF)

    def summed(b, source):
        at = pl.ds(pl.multiple_of(b * cap, cap), cap)
        stacked = jnp.concatenate([source[j, at, :] for j in range(per)], axis=0)
        return dot(all_hots_back(r.pos[b], per, cap), stacked).astype(BF)

    @pl.when(here)
    def _():
        if backward:
            r.dg[...] = jnp.zeros_like(r.dg)
        if mode == "fwd":
            keep_blocks = pltpu.make_async_copy(r.blk, r.blocks, r.row_sem.at[0])
        streamed(2 * per, weights, expert, primed=True)
        if mode == "fwd":
            keep_blocks.start()

        def emit(i, carry):
            to = lax.rem(z + i + 1, n)
            section = jnp.where(i < n, 1 - layer, layer)
            r.pbuf[section, to] = summed(section * n + to, r.y_scr)

            @pl.when(i < n)
            def _():
                for a in arrays:
                    hop(a, to).start()

            @pl.when((i >= n) & (to != z))
            def _():
                for a in arrays:
                    give(a, srcs[a].at[layer, to], i + 1 - n).start()

            return carry

        lax.fori_loop(0, 2 * n, emit, 0)
        for a in arrays:
            keep(a, srcs[a].at[layer, z]).start()
        if mode == "fwd":
            for i in (2 * per - 2, 2 * per - 1):
                for c in saved(i, i % 2):
                    c.wait()
            keep_blocks.wait()
        if mode == "bwd":

            @pl.loop(0, count)
            def _(b):
                put_rows(all_hots(r.pos[b], per, cap).astype(BF), r.blk[b // n, lax.rem(b, n)], b, per, cap, r.y_scr)

            gather_from(count, per, cap, r.pos, r.blocks, r.x_scr, r.row_buf, r.row_sem)
        if mode == "both":
            gather_from(count, per, cap, r.pos, r.gy, r.y_scr, r.row_buf, r.row_sem)
        if backward:
            weight_grads(r, per)
        if mode == "both":
            def output(j, slot):
                @pl.loop(0, 2)
                def _(c):
                    at = pl.ds(pl.multiple_of(c * chunk, chunk), chunk)
                    r.x_scr[j, at, :] = dot(r.act[2, j, at, :], r.wd_buf[slot]).astype(BF)

            streamed(per, lambda j, slot: weights(j, slot)[2:], output)
            combine(0, n, per, cap, r.pos, r.x_scr, r.part0, r.row_buf, r.row_sem)
            combine(n, n, per, cap, r.pos, r.x_scr, r.part1, r.row_buf, r.row_sem)
        for to in range(n):
            for a in arrays:
                hop(a, to).wait_send()

    @pl.when(jnp.logical_not(here))
    def _():
        @pl.loop(1, n + 1)
        def _(k):
            to = lax.rem(lax.rem(k, n) + z, n)
            for a in arrays:
                hop(a, to).wait_recv()

            @pl.when(k < n)
            def _():
                for a in arrays:
                    give(a, relays[a].at[to], k).start()

        for a in arrays:
            keep(a, relays[a].at[z]).start()
        for zz in range(n):
            cross(zz).wait_send()

    if mode == "bwd":

        @pl.when(here)
        def _():
            for zz in range(n):
                over_part(zz).wait_recv()

        @pl.when(jnp.logical_not(here))
        def _():
            pltpu.make_async_copy(r.part_own, r.pbuf.at[layer], r.part_sem.at[0]).wait()
            part_home().start()
            part_home().wait()
            for zz in range(n):
                over_part(zz).wait_send()

    if riding:
        ride_on()
        for q in range(1, groups):
            for zz in range(n):
                over(q & (q - 1), low_bit(q), zz).wait_send()
    for a in arrays:
        keep(a, relays[a].at[z]).wait()
        for k in range(1, n):
            give(a, relays[a].at[lax.rem(z + k, n)], k).wait()
    for t in range(n):

        @pl.when((z >= t) & (z < n - 1))
        def _():
            right(t).wait_send()

        @pl.when((z + t < n) & (z > 0))
        def _():
            left(t).wait_send()


def moe(layer, mode, cid, e_pad, cap, own, wg, wu, wd, **given):
    n, groups = lax.axis_size("expert"), lax.axis_size("group")
    count = 2 * n
    t, d = own.shape
    per, _, f = wg.shape
    rows = count * cap
    piece = d // groups
    sds = jax.ShapeDtypeStruct
    dma = pltpu.SemaphoreType.DMA
    vm, hbm = pl.BlockSpec(memory_space=pltpu.VMEM), any_spec()
    on_chip = ("own", "rt", "wrt", "pos", "gate", "dqkv", "at", "dht", "daux", "o")
    ins = dict(own=own, wg=wg, wu=wu, wd=wd, **given)
    outs = dict(back=sds((n, t, d), BF))
    scratch = dict(
        blk=pltpu.VMEM((2, n, t, d), BF),
        y_scr=pltpu.VMEM((per, rows, d), BF),
        wg_buf=pltpu.VMEM((2, d, f), BF),
        wu_buf=pltpu.VMEM((2, d, f), BF),
        wd_buf=pltpu.VMEM((2, f, d), BF),
        pbuf=pltpu.VMEM((2, n, t, d), BF),
        relay=pltpu.VMEM((n, t, d), BF),
        x_scr=pltpu.VMEM((per, rows, d), BF),
        row_buf=pltpu.VMEM((2, t, d), BF),
        row_sem=dma((2,)),
        w_sem=dma((2, 3)),
        keep_sem=dma((2,)),
    )
    for name in ("right", "left", "cross"):
        scratch["s_" + name] = dma((n,))
        scratch["r_" + name] = dma((n,))
    for name in ("hop", "give"):
        scratch["s_" + name] = dma((2, n))
        scratch["r_" + name] = dma((2, n))
    if mode != "both":
        scratch["gp_buf"] = pltpu.VMEM((4, n * cap, f), BF)
        scratch["gp_sem"] = dma((2, 2))
    if mode != "bwd":
        scratch["gates"] = pltpu.VMEM((e_pad, t), F32)
    if mode == "fwd":
        del scratch["row_buf"]
        outs.update(pos=sds((count, 8, t), jnp.int32), gate=sds((count, 8, t), F32))
        outs.update(gp=sds((per, rows, f), BF), up=sds((per, rows, f), BF), blocks=sds((2, n, t, d), BF))
        outs["dense_out"] = sds(given["dense"].shape, BF)
        scratch.update(s_over=dma((groups, n)), r_over=dma((groups, n)))
    else:
        outs["dgate"] = sds((n, 8, t), F32)
        outs["even"] = outs["odd"] = sds((groups // 2, 2, per, piece, f), BF)
        outs["even_dn"] = outs["odd_dn"] = sds((groups // 2, per, f, piece), BF)
        scratch.update(
            dg=pltpu.VMEM((2, n, 8, t), F32),
            dg_relay=pltpu.VMEM((n, 8, t), F32),
            act=pltpu.VMEM((3, per, rows, f), BF),
            gu_buf=pltpu.VMEM((2, 2, 2, piece, f), BF),
            dn_buf=pltpu.VMEM((2, 2, f, piece), BF),
            gu_sem=dma((2, 2)),
            dn_sem=dma((2, 2)),
        )
    if mode == "bwd":
        outs["dd"] = sds((d, QKV + QW + LANES), BF)
        outs["part_out"] = sds((n, t, d), BF)
        scratch.update(s_part=dma((n,)), r_part=dma((n,)), part_sem=dma((2,)))
        scratch.update(dd_sem=dma((3,)), daux_sem=dma)
    if mode == "both":
        outs["part0"] = outs["part1"] = sds((n, t, d), BF)
        scratch.update(pos=pltpu.VMEM((count, 8, t), jnp.int32), gate=pltpu.VMEM((count, 8, t), F32))
    names = tuple(ins) + tuple(outs) + tuple(scratch)
    results = pl.pallas_call(
        functools.partial(moe_kernel, layer, mode, n, e_pad, cap, names),
        out_shape=tuple(outs.values()),
        in_specs=[vm if name in on_chip else hbm for name in ins],
        out_specs=tuple(vm if name in on_chip else hbm for name in outs),
        scratch_shapes=list(scratch.values()),
        input_output_aliases={list(ins).index("dense"): list(outs).index("dense_out")} if mode == "fwd" else {},
        compiler_params=pltpu.CompilerParams(collective_id=cid, has_side_effects=True, vmem_limit_bytes=VMEM_LIMIT),
    )(*ins.values())
    return types.SimpleNamespace(**dict(zip(outs, results)))


def top_bit(q):
    return q.bit_length() - 1


def finish_kernel(
    n, dd0, dd1, dx0, dx1, egu0, ogu0, ed0, od0, egu1, ogu1, ed1, od1,
    dense_out, dx_out, gate_out, up_out, down_out,
    core_gu, core_dn, hop_gu, hop_dn, core_dd, hop_y, hop_z, hop_x, dd_buf, gu_buf, dn_buf, gu_res, dn_res,
    s_core_gu, r_core_gu, s_core_dn, r_core_dn, s_hop_gu, r_hop_gu, s_hop_dn, r_hop_dn,
    s_core_dd, r_core_dd, s_y, r_y, s_z, r_z, s_x, r_x, l_dd, l_gu, l_dn, o_gu, o_dn, s_dx, r_dx,
):
    s, g, z = lax.axis_index("section"), lax.axis_index("group"), lax.axis_index("expert")
    pairs, cgu = core_gu.shape[:2]
    cdn = core_dn.shape[1]
    levels = top_bit(pairs)
    units = pairs * n
    remote = functools.partial(pltpu.make_async_remote_copy, device_id_type=MESH)
    twin = {"group": lax.bitwise_xor(g, 1)}
    other = {"section": 1 - s}

    def across(k):
        return {"group": lax.bitwise_xor(g, 2 << k)}

    barrier = pltpu.get_barrier_semaphore()
    peers = [twin, other] + [across(k) for k in range(levels)] + [{"expert": lax.rem(z + k, n)} for k in range(1, n)]
    for peer in peers:
        pl.semaphore_signal(barrier, inc=1, device_id=peer, device_id_type=MESH)
    pl.semaphore_wait(barrier, len(peers))

    def by_section(action):
        @pl.when(s == 0)
        def _():
            action(dd0, dd1, egu0, ogu0, ed0, od0)

        @pl.when(s != 0)
        def _():
            action(dd1, dd0, egu1, ogu1, ed1, od1)

    def unit(i):
        return pairs - 1 - i // n, lax.rem(z + 1 + lax.rem(i, n), n)

    def shard(i, core):
        q, place = unit(i)
        return (lax.bitwise_xor(g // 2, q) * 2 + core) * n + place

    core = lax.rem(g, 2)

    def core_dd_copy(kind, i, source):
        return remote(
            src_ref=source.at[shard(i, 1 - core)],
            dst_ref=core_dd.at[kind, i],
            send_sem=s_core_dd.at[kind, i],
            recv_sem=r_core_dd.at[kind, i],
            device_id=twin,
        )

    def core_chunk(source, dest, ssem, rsem, q, c):
        return remote(
            src_ref=source.at[q, c], dst_ref=dest.at[q, c], send_sem=ssem.at[q, c], recv_sem=rsem.at[q, c], device_id=twin
        )

    def core_gu_copy(source, q, c):
        return core_chunk(source, core_gu, s_core_gu, r_core_gu, q, c)

    def core_dn_copy(source, q, c):
        return core_chunk(source, core_dn, s_core_dn, r_core_dn, q, c)

    def send_first(own, away, egu, ogu, ed, od):
        @pl.loop(0, units)
        def _(i):
            core_dd_copy(0, i, away).start()

            @pl.when(i < cgu)
            def _():
                core_gu_copy(ogu, pairs - 1, i).start()

            @pl.when(i < cdn)
            def _():
                core_dn_copy(od, pairs - 1, i).start()

        for i in range(units, max(cgu, cdn)):
            if i < cgu:
                core_gu_copy(ogu, pairs - 1, i).start()
            if i < cdn:
                core_dn_copy(od, pairs - 1, i).start()

    def send_rest(own, away, egu, ogu, ed, od):
        @pl.loop(0, units)
        def _(i):
            core_dd_copy(1, i, own).start()

        for q in reversed(range(pairs - 1)):

            @pl.loop(0, cgu)
            def _(c):
                core_gu_copy(ogu, q, c).start()

            @pl.loop(0, cdn)
            def _(c):
                core_dn_copy(od, q, c).start()

    by_section(send_first)

    def dx_copy(source):
        return remote(src_ref=source, dst_ref=dx_out, send_sem=s_dx, recv_sem=r_dx, device_id=other)

    def load(buf, sem, slot, source):
        return pltpu.make_async_copy(source, buf.at[slot], sem.at[slot])

    def dd_load(i, slot, source):
        return load(dd_buf, l_dd, slot, source.at[shard(i, core)])

    def hop(dest, ssem, rsem, source, k, q, c):
        return remote(
            src_ref=source.at[q, c],
            dst_ref=dest.at[k, q - (1 << k), c],
            send_sem=ssem.at[k, q - (1 << k), c],
            recv_sem=rsem.at[k, q - (1 << k), c],
            device_id=across(k),
        )

    def gu_hop(k, q, c):
        return hop(hop_gu, s_hop_gu, r_hop_gu, core_gu, k, q, c)

    def dn_hop(k, q, c):
        return hop(hop_dn, s_hop_dn, r_hop_dn, core_dn, k, q, c)

    def y_copy(i):
        return remote(src_ref=core_dd.at[0, i], dst_ref=hop_y.at[i], send_sem=s_y.at[i], recv_sem=r_y.at[i], device_id=other)

    def z_copy(q, k, i):
        return remote(
            src_ref=core_dd.at[1, i],
            dst_ref=hop_z.at[k - 1, q],
            send_sem=s_z.at[k - 1, q],
            recv_sem=r_z.at[k - 1, q],
            device_id={"expert": lax.rem(z + k, n)},
        )

    def x_copy(k, q, i):
        return remote(
            src_ref=core_dd.at[1, i],
            dst_ref=hop_x.at[k, q - (1 << k)],
            send_sem=s_x.at[k, q - (1 << k)],
            recv_sem=r_x.at[k, q - (1 << k)],
            device_id=across(k),
        )

    def chunk_start(i, slot, q, egu, ed):
        @pl.when(i < cgu)
        def _():
            load(gu_buf, l_gu, slot, egu.at[q, i]).start()

        @pl.when(i < cdn)
        def _():
            load(dn_buf, l_dn, slot, ed.at[q, i]).start()

    def expert_sum(hops, rsem, dest, core_r, buf, sem, slot, even, q, c, hop_copy):
        load(buf, sem, slot, even.at[q, c]).wait()
        core_r(q, c).wait_recv()
        total = buf[slot].astype(F32) + dest[q, c].astype(F32)
        for k in range(top_bit(q) + 1 if q else 0, levels):
            hop_copy(k, q + (1 << k), c).wait_recv()
            total = total + hops[k, q, c].astype(F32)
        return total

    def gu_sum(slot, q, c):
        return expert_sum(hop_gu, r_hop_gu, core_gu, functools.partial(core_gu_copy, ogu0), gu_buf, l_gu, slot, egu0, q, c, gu_hop)

    def dn_sum(slot, q, c):
        return expert_sum(hop_dn, r_hop_dn, core_dn, functools.partial(core_dn_copy, od0), dn_buf, l_dn, slot, ed0, q, c, dn_hop)

    def stepped(count, start, body):
        start(0, 0)

        def step(i, carry):
            @pl.when(i + 1 < count)
            def _():
                start(i + 1, lax.rem(i + 1, 2))

            body(i, lax.rem(i, 2))
            return carry

        lax.fori_loop(0, count, step, 0)

    for q in reversed(range(1, pairs)):
        dense_too = q == pairs - 1
        if not dense_too and q == pairs - 2:
            by_section(send_rest)
        steps = max(units, cgu, cdn) if dense_too else max(cgu, cdn)

        def start(i, slot):
            def go(own, away, egu, ogu, ed, od):
                if dense_too:

                    @pl.when(i < units)
                    def _():
                        dd_load(i, slot, away).start()

                chunk_start(i, slot, q, egu, ed)

            by_section(go)

        def body(i, slot):
            if dense_too:

                @pl.when(i < units)
                def _():
                    dd_load(i, slot, dd0).wait()
                    core_dd_copy(0, i, dd0).wait_recv()
                    core_dd[0, i] = core_dd[0, i] + dd_buf[slot]
                    y_copy(i).start()

            @pl.when(i < cgu)
            def _():
                core_gu[q, i] = gu_sum(slot, q, i).astype(BF)
                gu_hop(top_bit(q), q, i).start()

            @pl.when(i < cdn)
            def _():
                core_dn[q, i] = dn_sum(slot, q, i).astype(BF)
                dn_hop(top_bit(q), q, i).start()

        stepped(steps, start, body)

    if pairs == 2:
        by_section(send_rest)

    @pl.when(s == 0)
    def _():
        dx_copy(dx1).start()

    @pl.when(s != 0)
    def _():
        dx_copy(dx0).start()

    def gu_out_copy(c, slot, to=gate_out):
        return pltpu.make_async_copy(gu_res.at[slot], to.at[lax.rem(c, cgu // 2)], o_gu.at[slot])

    def dn_out_copy(c, slot):
        return pltpu.make_async_copy(dn_res.at[slot], down_out.at[c], o_dn.at[slot])

    def dense_sum(q):
        i = (pairs - 1 - q) * n + n - 1
        total = core_dd[1, i].astype(F32)
        for k in range(1, n):
            z_copy(q, k, i).wait_recv()
            total = total + hop_z[k - 1, q].astype(F32)
        for k in range(top_bit(q) + 1 if q else 0, levels):
            x_copy(k, q + (1 << k), i).wait_recv()
            total = total + hop_x[k, q].astype(F32)
        return i, total

    def pass_on(q):
        i, total = dense_sum(q)
        core_dd[1, i] = total.astype(BF)
        x_copy(top_bit(q), q, i).start()

    def core_sent():
        @pl.loop(0, units)
        def _(i):
            core_dd_copy(0, i, dd0).wait_send()
            core_dd_copy(1, i, dd0).wait_send()

        for q in range(pairs):

            @pl.loop(0, cgu)
            def _(c):
                core_gu_copy(ogu0, q, c).wait_send()

            @pl.loop(0, cdn)
            def _(c):
                core_dn_copy(od0, q, c).wait_send()

    steps = max(units, cgu, cdn)

    def start(i, slot):
        def go(own, away, egu, ogu, ed, od):
            @pl.when(i < units)
            def _():
                dd_load(i, slot, own).start()

            chunk_start(i, slot, 0, egu, ed)

        by_section(go)

    def body(i, slot):
        @pl.when(i < units)
        def _():
            dd_load(i, slot, dd0).wait()
            core_dd_copy(1, i, dd0).wait_recv()
            y_copy(i).wait_recv()
            core_dd[1, i] = (core_dd[1, i].astype(F32) + dd_buf[slot].astype(F32) + hop_y[i].astype(F32)).astype(BF)
            q, _ = unit(i)
            k = lax.rem(i, n) + 1

            @pl.when(k < n)
            def _():
                z_copy(q, k, i).start()

        for q in range(1, pairs):

            @pl.when(i == (pairs - q) * n)
            def _():
                pass_on(q)

        @pl.when(i == units - 2)
        def _():
            core_sent()

        @pl.when(i < cgu)
        def _():
            @pl.when(i >= 2)
            def _():
                gu_out_copy(i - 2, slot).wait()

            gu_res[slot] = gu_sum(slot, 0, i).astype(BF)

            @pl.when(i < cgu // 2)
            def _():
                gu_out_copy(i, slot).start()

            @pl.when(i >= cgu // 2)
            def _():
                gu_out_copy(i, slot, up_out).start()

        @pl.when(i < cdn)
        def _():
            @pl.when(i >= 2)
            def _():
                dn_out_copy(i - 2, slot).wait()

            dn_res[slot] = dn_sum(slot, 0, i).astype(BF)
            dn_out_copy(i, slot).start()

    stepped(steps, start, body)
    _, total = dense_sum(0)
    dense_out[...] = total
    for c in (cgu - 2, cgu - 1):
        gu_out_copy(c, c % 2).wait()
    for c in (cdn - 2, cdn - 1):
        dn_out_copy(c, c % 2).wait()

    dx_copy(dx0).wait()

    @pl.loop(0, units)
    def _(i):
        y_copy(i).wait_send()
        q, _ = unit(i)
        k = lax.rem(i, n) + 1

        @pl.when(k < n)
        def _():
            z_copy(q, k, i).wait_send()

    for q in range(1, pairs):
        x_copy(top_bit(q), q, (pairs - 1 - q) * n + n - 1).wait_send()

        @pl.loop(0, cgu)
        def _(c):
            gu_hop(top_bit(q), q, c).wait_send()

        @pl.loop(0, cdn)
        def _(c):
            dn_hop(top_bit(q), q, c).wait_send()


def finish(cid, dd0, dd1, dx0, dx1, experts0, experts1):
    n, groups = lax.axis_size("expert"), lax.axis_size("group")
    pairs, levels = groups // 2, top_bit(groups // 2)
    width = dd0.shape[1]
    rows = dd0.shape[0] // (groups * n)
    dd0, dd1 = (v.reshape(groups * n, rows, width) for v in (dd0, dd1))

    def chunked(arrays):
        gu_even, gu_odd, dn_even, dn_odd = arrays
        flat = (pairs, -1) + gu_even.shape[3:]
        return gu_even.reshape(flat), gu_odd.reshape(flat), dn_even, dn_odd

    experts0, experts1 = chunked(experts0), chunked(experts1)
    gu, dn = experts0[0].shape[1:], experts0[2].shape[1:]
    units = pairs * n
    dma = pltpu.SemaphoreType.DMA
    sds = jax.ShapeDtypeStruct
    half = max(1, pairs // 2)

    def both(shape):
        return [dma(shape), dma(shape)]

    return pl.pallas_call(
        functools.partial(finish_kernel, n),
        out_shape=(
            sds((rows, width), F32),
            sds(dx0.shape, dx0.dtype),
            sds((gu[0] // 2,) + gu[1:], BF),
            sds((gu[0] // 2,) + gu[1:], BF),
            sds(dn, BF),
        ),
        in_specs=[any_spec()] * 12,
        out_specs=tuple(vmem(1) + [any_spec()] * 4),
        scratch_shapes=[
            pltpu.VMEM((pairs,) + gu, BF),
            pltpu.VMEM((pairs,) + dn, BF),
            pltpu.VMEM((levels, half) + gu, BF),
            pltpu.VMEM((levels, half) + dn, BF),
            pltpu.VMEM((2, units, rows, width), BF),
            pltpu.VMEM((units, rows, width), BF),
            pltpu.VMEM((n - 1, pairs, rows, width), BF),
            pltpu.VMEM((levels, half, rows, width), BF),
            pltpu.VMEM((2, rows, width), BF),
            pltpu.VMEM((2,) + gu[1:], BF),
            pltpu.VMEM((2,) + dn[1:], BF),
            pltpu.VMEM((2,) + gu[1:], BF),
            pltpu.VMEM((2,) + dn[1:], BF),
        ]
        + both((pairs, gu[0]))
        + both((pairs, dn[0]))
        + both((levels, half, gu[0]))
        + both((levels, half, dn[0]))
        + both((2, units))
        + both((units,))
        + both((n - 1, pairs))
        + both((levels, half))
        + [dma((2,))] * 5
        + [dma, dma],
        compiler_params=pltpu.CompilerParams(collective_id=cid, has_side_effects=True, vmem_limit_bytes=VMEM_LIMIT),
    )(dd0, dd1, dx0, dx1, *experts0, *experts1)


def last_kernel(
    experts, dense_ref, dx0_ref, dx1_ref, got_ref, gate_ref, up_ref, down_ref,
    gate_out, up_out, down_out, q_out, k_out, v_out, o_out, router_out, attn_out, moe_out, dx_out,
):
    gate_out[...] = gate_ref[...].astype(F32)
    up_out[...] = up_ref[...].astype(F32)
    down_out[...] = down_ref[...].astype(F32)

    @pl.when(pl.program_id(0) == 0)
    def _():
        s = lax.axis_index("section")
        q_out[...] = dense_ref[:, 0:QW]
        k_out[...] = dense_ref[:, QW : QW + KW]
        v_out[...] = dense_ref[:, QW + KW : QKV]
        o_out[...] = dense_ref[:, QKV : QKV + QW]
        aux_rows = jnp.transpose(dense_ref[:, QKV + QW :])
        for e in range(experts):
            router_out[e] = aux_rows[e : e + 1]
        moe_out[...] = aux_rows[GAIN_MOE_ROW : GAIN_MOE_ROW + 1]
        attn_out[...] = aux_rows[GAIN_ATTN_ROW : GAIN_ATTN_ROW + 1]
        dx_out[s] = jnp.where(s == 0, dx0_ref[...], dx1_ref[...])
        dx_out[1 - s] = got_ref[...].astype(F32)


def last(experts, dense, dx0, dx1, got, gate, up, down):
    sh = dense.shape[0]
    t, d = dx0.shape
    per, piece, f = gate.shape
    sds = jax.ShapeDtypeStruct

    def whole(shape):
        return pl.BlockSpec(shape, lambda j: (0,) * len(shape))

    wide = pl.BlockSpec((1, piece, f), lambda j: (j, 0, 0))
    tall = pl.BlockSpec((1, f, piece), lambda j: (j, 0, 0))
    small = [(sh, QW), (sh, KW), (sh, KW), (sh, QW), (experts, 1, sh), (1, sh), (1, sh), (2, t, d)]
    return pl.pallas_call(
        functools.partial(last_kernel, experts),
        grid=(per,),
        out_shape=tuple(sds(v.shape, F32) for v in (gate, up, down)) + tuple(sds(shape, F32) for shape in small),
        in_specs=[whole(v.shape) for v in (dense, dx0, dx1, got)] + [wide, wide, tall],
        out_specs=tuple([wide, wide, tall] + [whole(shape) for shape in small]),
        compiler_params=pltpu.CompilerParams(vmem_limit_bytes=VMEM_LIMIT),
    )(dense, dx0, dx1, got, gate, up, down)


def low_bit(q):
    return top_bit(q & -q)


def open_kernel(
    n, groups, pieces, wq_ref, wk_ref, wv_ref, wo_ref, wr_ref, ga_ref, gm_ref, cot_ref, rt_ref, w0_out, w1_out, gy_out, rt_out, rt_side,
    w_ref, s_right, r_right, s_left, r_left, s_group, r_group, s_y, r_y, s_cross, r_cross, s_rt, r_rt, s_side, r_side, local_sem,
):
    s, g, z = lax.axis_index("section"), lax.axis_index("group"), lax.axis_index("expert")
    remote = functools.partial(pltpu.make_async_remote_copy, device_id_type=MESH)
    rows = w_ref.shape[0] // pieces
    bits = top_bit(groups)
    other = {"section": 1 - s}
    w_ref[:, 0:QW] = wq_ref[...]
    w_ref[:, QW : QW + KW] = wk_ref[...]
    w_ref[:, QW + KW : QKV] = wv_ref[...]
    w_ref[:, QKV : QKV + QW] = wo_ref[...]
    experts, sh = wr_ref.shape
    gap = jnp.zeros((GAIN_MOE_ROW - experts, sh), F32)
    aux = jnp.concatenate([wr_ref[...].astype(F32), gap, gm_ref[...].astype(F32), ga_ref[...].astype(F32)], axis=0)
    w_ref[:, QKV + QW :] = jnp.transpose(aux).astype(BF)
    barrier = pltpu.get_barrier_semaphore()
    peers = [other] + [{"group": lax.bitwise_xor(g, 1 << b)} for b in range(bits)] + [{"expert": lax.rem(z + k, n)} for k in range(1, n)]
    for peer in peers:
        pl.semaphore_signal(barrier, inc=1, device_id=peer, device_id_type=MESH)
    pl.semaphore_wait(barrier, len(peers))
    sent = []

    def launch(cond, make):
        sent.append((cond, make))
        if cond is None:
            make().start()
        else:

            @pl.when(cond)
            def _():
                make().start()

    def part(q, zz, c):
        if c == 2 * pieces:
            return gy_out.at[s, zz]
        return (w0_out, w1_out)[c // pieces].at[lax.bitwise_xor(g, q) * n + zz, pl.ds(c % pieces * rows, rows)]

    def chain(to, zz, t, c, ssem, rsem):
        return remote(src_ref=part(0, zz, c), dst_ref=part(0, zz, c), send_sem=ssem.at[t, c], recv_sem=rsem.at[t, c], device_id={"expert": to})

    def right(t, c):
        return chain(z + 1, z - t, t, c, s_right, r_right)

    def left(t, c):
        return chain(z - 1, z + t, t, c, s_left, r_left)

    def over(q, b, zz, c):
        at = q | (1 << b)
        return remote(
            src_ref=part(q, zz, c), dst_ref=part(q, zz, c), send_sem=s_group.at[at, zz, c], recv_sem=r_group.at[at, zz, c],
            device_id={"group": lax.bitwise_xor(g, 1 << b)},
        )

    def hop(c, to=w0_out):
        at = pl.ds(c * rows, rows)
        return remote(src_ref=w_ref.at[at], dst_ref=to.at[g * n + z, at], send_sem=s_y.at[c], recv_sem=r_y.at[c], device_id=other)

    def by_layer(action):
        for layer, to in enumerate((w0_out, w1_out)):

            @pl.when(s == layer)
            def _(to=to):
                action(to)

    def cross(zz):
        return remote(src_ref=gy_out.at[0, zz], dst_ref=gy_out.at[0, zz], send_sem=s_cross.at[zz], recv_sem=r_cross.at[zz], device_id=other)

    def route(m, k):
        return remote(
            src_ref=rt_ref.at[m], dst_ref=rt_out.at[m, z], send_sem=s_rt.at[m, k], recv_sem=r_rt.at[m, k],
            device_id={"expert": lax.rem(z + k, n)},
        )

    def side():
        return remote(src_ref=rt_ref.at[1 - s], dst_ref=rt_side, send_sem=s_side, recv_sem=r_side, device_id=other)

    by_layer(lambda to: hop(0, to).start())
    launch(None, side)
    own = [pltpu.make_async_copy(cot_ref.at[s], gy_out.at[s, z], local_sem.at[0])]
    own += [pltpu.make_async_copy(rt_ref.at[m], rt_out.at[m, z], local_sem.at[1 + m]) for m in range(2)]

    def keep(to=w0_out):
        return pltpu.make_async_copy(w_ref, to.at[g * n + z], local_sem.at[3])

    for copy in own:
        copy.start()

    by_layer(lambda to: keep(to).start())
    keep().wait()

    def spread_out(cond, zz, c):
        if c < pieces:
            for b in reversed(range(bits)):
                launch(cond, functools.partial(over, 0, b, zz, c))
        elif c == 2 * pieces:
            launch((s == 0) if cond is None else ((s == 0) & cond), functools.partial(cross, zz))

    def pass_along(t, c):
        if t == 0:
            if c < 2 * pieces:

                @pl.when(s != c // pieces)
                def _():
                    hop(c % pieces).wait_recv()
            else:
                own[0].wait()
            launch(z < n - 1, functools.partial(right, t, c))
            launch(z > 0, functools.partial(left, t, c))
            spread_out(None, z, c)
            if c + 1 < pieces:
                hop(c).wait_send()
                by_layer(lambda to: hop(c + 1, to).start())
        else:
            from_left, from_right = z >= t, z + t < n

            @pl.when(from_left)
            def _():
                right(t - 1, c).wait_recv()

            launch(from_left & (z < n - 1), functools.partial(right, t, c))
            spread_out(from_left, z - t, c)

            @pl.when(from_right)
            def _():
                left(t - 1, c).wait_recv()

            launch(from_right & (z > 0), functools.partial(left, t, c))
            spread_out(from_right, z + t, c)

    def forward(q, k):
        zz = lax.rem(z + k, n)
        for c in range(pieces):
            over(q & (q - 1), low_bit(q), zz, c).wait_recv()
            for b in reversed(range(low_bit(q))):
                launch(None, functools.partial(over, q, b, zz, c))

    for t in range(n):
        for c in range(pieces):
            pass_along(t, c)
        if t == 0:
            for m in range(2):
                for k in range(1, n):
                    launch(None, functools.partial(route, m, k))
    pending = [(q, k) for q in sorted(range(1, groups), key=lambda q: -low_bit(q)) for k in range(n)]
    for t in range(n):
        pass_along(t, 2 * pieces)
        forward(*pending.pop(0))
    for t in range(n):
        for c in range(pieces, 2 * pieces):
            pass_along(t, c)
    for q, k in pending:
        forward(q, k)

    @pl.when(s != 0)
    def _():
        for zz in range(n):
            cross(zz).wait_recv()

    side().wait_recv()
    for m in range(2):
        own[1 + m].wait()
        for k in range(1, n):
            route(m, k).wait_recv()
    hop(pieces - 1).wait_send()
    for cond, make in sent:
        if cond is None:
            make().wait_send()
        else:

            @pl.when(cond)
            def _(make=make):
                make().wait_send()


def open_up(cid, weights, cot, rt):
    n, groups = lax.axis_size("expert"), lax.axis_size("group")
    sh = weights[0].shape[0]
    packed = (sh, QKV + QW + LANES)
    pieces = 3 if sh % 48 == 0 else 1
    dma = pltpu.SemaphoreType.DMA
    sds = jax.ShapeDtypeStruct

    def both(shape):
        return [dma(shape), dma(shape)]

    w0, w1, gy, rt_all, rt_side = pl.pallas_call(
        functools.partial(open_kernel, n, groups, pieces),
        out_shape=(sds((groups * n,) + packed, BF),) * 2 + (sds((2, n) + cot.shape[1:], BF), sds((2, n) + rt.shape[1:], rt.dtype), sds(rt.shape[1:], rt.dtype)),
        in_specs=vmem(9),
        out_specs=tuple([any_spec()] * 5),
        scratch_shapes=[pltpu.VMEM(packed, BF)] + both((n, 2 * pieces + 1)) + both((n, 2 * pieces + 1)) + both((groups, n, pieces)) + both((pieces,)) + both((n,)) + both((2, n)) + [dma, dma] + [dma((4,))],
        compiler_params=pltpu.CompilerParams(collective_id=cid, has_side_effects=True),
    )(*weights, cot, rt)
    return w0.reshape(groups * n * sh, -1), w1, gy, rt_all, rt_side


def swap_sections(value):
    return lax.ppermute(value, "section", [(0, 1), (1, 0)])


def rope_tables(t):
    half = HEAD_SIZE // 2
    frequency = THETA ** (-np.arange(half) * 2.0 / HEAD_SIZE)
    angles = np.arange(t)[:, None] * frequency[None, :]
    reps = LANES // half
    return (jnp.asarray(np.tile(f(angles), (1, reps)).astype(np.float32)) for f in (np.cos, np.sin))


def local(
    inputs, cotangent, segment_ids, live_first, routes, gain_attn, gain_moe,
    w_query, key_weight, value_weight, w_out, w_router, w_gate, w_up, w_down,
):
    s = lax.axis_index("section")
    n = lax.axis_size("expert")
    groups = lax.axis_size("group")
    t, d = inputs.shape[2:]
    top = routes.shape[-1]
    per = w_gate.shape[1]
    experts = per * n
    e_pad = -(-experts // 16) * 16
    cap = t * top * 5 // (4 * experts)
    wg, wu, wd = w_gate[0], w_up[0], w_down[0]
    at_zero = s == 0

    dense_shards = (w_query[0], key_weight[0], value_weight[0], w_out[0].T, w_router[0].T, gain_attn, gain_moe)

    seg, live, cot = segment_ids[:, 0], live_first[:, 0], cotangent[:, 0]
    cos, sin = rope_tables(t)

    rt = jnp.swapaxes(routes[0, :, 0], 1, 2)

    def flat(z):
        return z.reshape((2 * n,) + z.shape[2:])

    def paired(z):
        return z.reshape((2, n) + z.shape[1:])

    first_weights, second_weights, gy1, rt_all, rt_theirs = open_up(1, dense_shards, cot, rt)
    gy1, rt_all = flat(gy1), flat(rt_all)

    qkv0, p0, o0, h0, b0, wrt0, x0 = attn_fwd(inputs[:, 0], (), first_weights, cos, sin, seg, live)
    m0 = moe(0, "fwd", 2, e_pad, cap, b0, wg, wu, wd, rt=rt_all, wrt=wrt0, dense=second_weights)
    second_weights = m0.dense_out.reshape(first_weights.shape)

    qkv1, p1, o1, h1, b1, wrt1, x1 = attn_fwd(h0, m0.back, second_weights, cos, sin, seg, live)
    m1 = moe(1, "both", 3, e_pad, cap, b1, wg, wu, wd, rt=rt_all, wrt=wrt1, gy=gy1)

    dx1, gy0, dqkv1, at1, dht1, daux1 = attn_bwd(1, False, experts, cot, h1, x1, second_weights, qkv1, p1, o1, b1, wrt1, m1.back, m1.dgate, rt, rt_theirs, cos, sin)

    n0 = moe(0, "bwd", 4, e_pad, cap, gy0, wg, wu, wd, pos=m0.pos, gate=m0.gate, gp=m0.gp, up=m0.up, blocks=flat(m0.blocks),
             dqkv=dqkv1, at=at1, dht=dht1, daux=daux1, o=o1, part=m1.part0, part_own=m1.part1)
    dd1 = n0.dd
    dback0 = n0.back
    back1 = lax.all_to_all(n0.part_out, "expert", split_axis=0, concat_axis=0, tiled=True)
    dx0, low0, dd0 = attn_bwd(0, True, experts, gy0, h0, x0, first_weights, qkv0, p0, o0, b0, wrt0, dback0, n0.dgate, rt, rt_theirs, cos, sin)

    dense, got, *sums = finish(5, dd0, dd1, low0, gy0, (n0.even, n0.odd, n0.even_dn, n0.odd_dn), (m1.even, m1.odd, m1.even_dn, m1.odd_dn))
    dense, late = lax.optimization_barrier((dense, h1))
    y1 = (late + jnp.sum(back1.astype(F32), axis=0)).astype(BF)

    kept_out = jnp.where(at_zero, x1, y1)
    swapped_out = swap_sections(jnp.where(at_zero, y1, x1))
    layer_out = jnp.where(at_zero, jnp.stack([kept_out, swapped_out]), jnp.stack([swapped_out, kept_out]))
    gate_grad, up_grad, down_grad, *dense_grads, out_grad, router_grad, attn_grad, moe_grad, input_grad = last(
        experts, dense, dx0, dx1, got, *sums
    )
    return (
        layer_out[None, :, None],
        input_grad[None, :, None],
        attn_grad,
        moe_grad,
        *(v[None] for v in dense_grads),
        out_grad.T[None],
        jnp.transpose(router_grad, (1, 2, 0)),
        gate_grad[None],
        up_grad[None],
        down_grad[None],
    )


def solution(mesh):
    return jax.shard_map(
        local,
        mesh=mesh,
        in_specs=(
            P(None, ("group", "expert"), None, None),
            P(None, ("group", "expert"), None, None),
            P(None, ("group", "expert"), None),
            P(None, ("group", "expert"), None),
            P("section", None, ("group", "expert"), None, None),
            P("section", ("group", "expert")),
            P("section", ("group", "expert")),
            P("section", ("group", "expert"), None),
            P("section", ("group", "expert"), None),
            P("section", ("group", "expert"), None),
            P("section", None, ("group", "expert")),
            P("section", ("group", "expert"), None),
            P("section", "expert", None, None),
            P("section", "expert", None, None),
            P("section", "expert", None, None),
        ),
        out_specs=(
            P("section", None, ("group", "expert"), None, None),
            P("section", None, ("group", "expert"), None, None),
            P("section", ("group", "expert")),
            P("section", ("group", "expert")),
            P("section", ("group", "expert"), None),
            P("section", ("group", "expert"), None),
            P("section", ("group", "expert"), None),
            P("section", None, ("group", "expert")),
            P("section", ("group", "expert"), None),
            P("section", "expert", "group", None),
            P("section", "expert", "group", None),
            P("section", "expert", None, "group"),
        ),
        check_vma=False,
    )
```
